32 devices in a mesh: row: 4 (over z), col: 8 (over y, x, core).
Axes of the slice: x: 2, y: 2, z: 4, core: 2. Of those that a mesh axis runs over, the one named last changes fastest.
Arguments:
- hidden: bfloat16 [1024, 8, 2048], P('col', 'row')
- per_layer: bfloat16 [1024, 8, 256], P('col', 'row'), may hold values from -6 to 6
- lengths: int32 [8], replicated, may hold values from 922 to 1024, as said below
- block_ids: int32 [8, 1024], P('row'), may hold values from 0 to 7, never falling along the last dimension, each value on 1 to 256 neighbouring positions
- out_grad: bfloat16 [1024, 8, 2048], P('col', 'row'), may hold values from -6 to 6
- query_weight: bfloat16 [2048, 2048], P('row', 'col'), may hold values from -0.125 to 0.125
- key_weight: bfloat16 [2048, 512], P('row', 'col'), may hold values from -0.125 to 0.125
- value_weight: bfloat16 [2048, 512], P('row', 'col'), may hold values from -0.125 to 0.125
- output_weight: bfloat16 [2048, 2048], P('col', 'row'), may hold values from -0.125 to 0.125
- gate_weight: bfloat16 [2048, 8192], P('row', 'col'), may hold values from -0.125 to 0.125
- up_weight: bfloat16 [2048, 8192], P('row', 'col'), may hold values from -0.125 to 0.125
- down_weight: bfloat16 [8192, 2048], P('col', 'row'), may hold values from -0.0625 to 0.0625
- laurel_left: bfloat16 [2048, 64], P('row', 'col'), may hold values from -0.125 to 0.125
- laurel_right: bfloat16 [64, 2048], P('col', 'row'), may hold values from -0.75 to 0.75
- layer_gate: bfloat16 [2048, 256], P('row', 'col'), may hold values from -0.125 to 0.125
- layer_proj: bfloat16 [256, 2048], P('col', 'row'), may hold values from -0.375 to 0.375
- norm_gains: float32 [6, 2048], replicated, may hold values from 0.5 to 1.5
- head_gains: float32 [2, 256], replicated, may hold values from 1 to 1.6
Outputs:
- output: bfloat16 [1024, 8, 2048], P('col', 'row')
- stats: float32 [4], replicated
- d_hidden: bfloat16 [1024, 8, 2048], P('col', 'row')
- d_per_layer: bfloat16 [1024, 8, 256], P('col', 'row')
- d_query_weight: float32 [2048, 2048], P('row', 'col')
- d_key_weight: float32 [2048, 512], P('row', 'col')
- d_value_weight: float32 [2048, 512], P('row', 'col')
- d_output_weight: float32 [2048, 2048], P('col', 'row')
- d_gate_weight: float32 [2048, 8192], P('row', 'col')
- d_up_weight: float32 [2048, 8192], P('row', 'col')
- d_down_weight: float32 [8192, 2048], P('col', 'row')
- d_laurel_left: float32 [2048, 64], P('row', 'col')
- d_laurel_right: float32 [64, 2048], P('col', 'row')
- d_layer_gate: float32 [2048, 256], P('row', 'col')
- d_layer_proj: float32 [256, 2048], P('col', 'row')
- d_norm_gains: float32 [6, 2048], replicated
- d_head_gains: float32 [2, 256], replicated
The draws below stay inside these ranges and needn't reach their ends.
Inputs may be any that keep to these rules, and one draw needn't show every extreme that they name: `lengths`: in every aligned group of 2 sequences (those that share a row index) one has length 1024; some sequence has length 922. `block_ids`: along a sequence the block numbers never fall, and a block holds at most 256 positions.
All inputs are finite; a program needn't handle non-finite values.
Results may differ from the reference program's by a relative error of at most 0.024.
Values may be sent and summed in bfloat16 or wider, within the bound.
A program may use at most 320 MiB of HBM per device.

```python
import math
import jax
import jax.numpy as jnp
import numpy as np
from jax import lax

D = 2048
H = 8
KV = 2
HD = 256
FF = 8192
RANK = 64
PLD = 256
WINDOW = 512
BLOCK = 256
SG = 2
SEQ = 1024
SEQS = 8


def draw_hidden(key, part):
    base_key = jax.random.fold_in(key, 11)
    column_key = jax.random.fold_in(key, 12)
    token_key = jax.random.fold_in(key, 13)
    base_values = jax.random.normal(base_key, (SEQ, SEQS, D), jnp.float32)
    column_low = 0.4
    column_high = 2.5
    columns = jnp.exp(jax.random.uniform(column_key, (D,), jnp.float32, math.log(column_low), math.log(column_high)))
    tokens = jnp.exp(jax.random.uniform(token_key, (SEQ, SEQS, 1), jnp.float32, math.log(0.6), math.log(1.8)))
    position_part = jnp.arange(SEQ, dtype=jnp.float32)[:, None, None] / (SEQ - 1)
    sequence_part = jnp.arange(SEQS, dtype=jnp.float32)[None, :, None] / (SEQS - 1)
    rising = jnp.exp(math.log(3.0) * 0.5 * (position_part + sequence_part))
    return (base_values * columns[None, None, :] * tokens * rising).astype(jnp.bfloat16)


def draw_lengths(key, part):
    short_key = jax.random.fold_in(key, 21)
    full_key = jax.random.fold_in(key, 22)
    shortfall = jax.random.randint(short_key, (SEQS,), 0, SEQ // 10 + 1)
    group_count = SEQS // SG
    chosen = jax.random.randint(full_key, (group_count,), 0, SG) + jnp.arange(group_count, dtype=jnp.int32) * SG
    is_full = jnp.zeros((SEQS,), jnp.int32).at[chosen].set(1)
    shortest = (chosen[0] + 1) % SG
    shortfall = shortfall.at[shortest].set(SEQ // 10)
    return (SEQ - shortfall * (1 - is_full)).astype(jnp.int32)


def block_scale(key, dims, split, low, top_value):
    def one(dim, blocks):
        heights = jax.random.uniform(jax.random.fold_in(jax.random.fold_in(key, 6), dim), (blocks,), jnp.float32, low / len(split), top_value / len(split))
        return jnp.repeat(jnp.exp(heights), dims[dim] // blocks).reshape((-1,) + (1,) * (len(dims) - dim - 1))

    level = one(*split[0])
    for cut in split[1:]:
        level = level * one(*cut)
    return level


def length_profile(count, total, most, skew):
    portions = [(1 << 20) // math.isqrt(grade ** skew) + 1 for grade in range(2, count + 1)]
    spare, given = total - most - (count - 1), [1] * (count - 1)
    while spare > 0:
        candidates = [i for i in range(count - 1) if given[i] < most]
        pool, remaining = sum([portions[i] for i in candidates]), spare
        for i in candidates:
            addition = min(most - given[i], max(1, remaining * portions[i] // pool), spare)
            given[i] = given[i] + addition
            spare = spare - addition
    return np.array([most] + given)


def ragged(key, count, total, most, slope):
    if count == 2:
        one = jax.random.randint(key, (), max(1, total - most), min(most, total - 1) + 1)
        return jnp.stack([one, total - one])
    sizes = jnp.asarray(length_profile(count, total, most, slope), jnp.int32)
    twos = (count - 1) // 2
    giver, taker = sizes[1:1 + 2 * twos:2], sizes[2:2 + 2 * twos:2]
    room = jnp.minimum(giver - 1, most - taker)
    shifted = jax.random.randint(jax.random.fold_in(key, 1), (twos,), 0, 1 << 20) % (room + 1)
    sizes = sizes.at[1:1 + 2 * twos:2].set(giver - shifted).at[2:2 + 2 * twos:2].set(taker + shifted)
    return sizes[jax.random.permutation(jax.random.fold_in(key, 2), count)]


def gaussian(own_key, dims, spread, bound, shards=(), held_as=jnp.bfloat16):
    gain = block_scale(own_key, dims, shards, -0.22, 0.18) if shards else 1.0
    array = jax.random.normal(own_key, dims, jnp.float32) * spread * gain
    return jnp.minimum(jnp.maximum(array, -bound), bound).astype(held_as)


def setup_inputs(seed: int = 0) -> dict:
    arg_keys = jax.random.split(jax.random.key(seed), 19)
    hidden = draw_hidden(jax.random.fold_in(arg_keys[18], 71), 0)
    per_layer = gaussian(arg_keys[1], (SEQ, SEQS, PLD), 1.0, 6.0, ((0, 8), (1, 4)))
    lengths = draw_lengths(jax.random.fold_in(arg_keys[18], 71), 0)
    block_ids = jax.vmap(lambda own: jnp.searchsorted(jnp.cumsum(ragged(own, 2 * SEQ // BLOCK, SEQ, BLOCK, 0)), jnp.arange(SEQ), side="right"))(jax.random.split(arg_keys[3], SEQS)).reshape((SEQS, SEQ)).astype(jnp.int32)
    out_grad = gaussian(arg_keys[4], (SEQ, SEQS, D), 1.0, 6.0, ((0, 8), (1, 4)))
    query_weight = gaussian(arg_keys[5], (D, H * HD), D ** -0.5, 0.125, ((0, 4), (1, 8)))
    key_weight = gaussian(arg_keys[6], (D, KV * HD), D ** -0.5, 0.125, ((0, 4), (1, 8)))
    value_weight = gaussian(arg_keys[7], (D, KV * HD), D ** -0.5, 0.125, ((0, 4), (1, 8)))
    output_weight = gaussian(arg_keys[8], (H * HD, D), (H * HD) ** -0.5, 0.125, ((0, 8), (1, 4)))
    gate_weight = gaussian(arg_keys[9], (D, FF), D ** -0.5, 0.125, ((0, 4), (1, 8)))
    up_weight = gaussian(arg_keys[10], (D, FF), D ** -0.5, 0.125, ((0, 4), (1, 8)))
    down_weight = gaussian(arg_keys[11], (FF, D), FF ** -0.5, 0.0625, ((0, 8), (1, 4)))
    laurel_left = gaussian(arg_keys[12], (D, RANK), D ** -0.5, 0.125, ((0, 4), (1, 8)))
    laurel_right = gaussian(arg_keys[13], (RANK, D), RANK ** -0.5, 0.75, ((0, 8), (1, 4)))
    layer_gate = gaussian(arg_keys[14], (D, PLD), D ** -0.5, 0.125, ((0, 4), (1, 8)))
    layer_proj = gaussian(arg_keys[15], (PLD, D), PLD ** -0.5, 0.375, ((0, 8), (1, 4)))
    norm_gains = jnp.clip(1.0 + 0.1 * jax.random.normal(arg_keys[16], (6, D), jnp.float32), 0.5, 1.5)
    head_gains = jnp.clip(jax.random.uniform(arg_keys[17], (2, HD), jnp.float32, 1.0, 1.6), 1.0, 1.6)
    return dict(hidden=hidden, per_layer=per_layer, lengths=lengths, block_ids=block_ids, out_grad=out_grad, query_weight=query_weight, key_weight=key_weight, value_weight=value_weight, output_weight=output_weight, gate_weight=gate_weight, up_weight=up_weight, down_weight=down_weight, laurel_left=laurel_left, laurel_right=laurel_right, layer_gate=layer_gate, layer_proj=layer_proj, norm_gains=norm_gains, head_gains=head_gains)


@jax.custom_vjp
def low(v):
    return lax.optimization_barrier(v.astype(jnp.bfloat16)).astype(jnp.float32)

@jax.custom_vjp
def low_back(v):
    return v

def low_keep(v):
    return (low(v), None)

def low_pass(kept, grad):
    return (grad,)

def back_keep(v):
    return (v, None)

def back_low(kept, grad):
    return (low(grad),)
low.defvjp(low_keep, low_pass)
low_back.defvjp(back_keep, back_low)
EPSILON = 1e-06
NEGATIVE = -1e+30
HIGHEST = lax.Precision.HIGHEST
HALF_ROOT = 1.0 / math.sqrt(2.0)

def root_norm(values, gain_row):
    return values * lax.rsqrt(lax.optimization_barrier(jnp.mean(values * values, axis=-1, keepdims=True)) + EPSILON) * gain_row

def plain_norm(values):
    return values * lax.rsqrt(lax.optimization_barrier(jnp.mean(values * values, axis=-1, keepdims=True)) + EPSILON)

def smooth_gate(values):
    return jax.nn.gelu(values, approximate=True)

def rotate(values, angles):
    half_width = values.shape[-1] // 2
    leading = values[..., :half_width]
    trailing = values[..., half_width:]
    cosine = jnp.cos(angles)
    sine_part = jnp.sin(angles)
    return jnp.concatenate([leading * cosine - trailing * sine_part, trailing * cosine + leading * sine_part], axis=-1)

def matmul(first_array, second_array):
    return jnp.dot(first_array, second_array, precision=HIGHEST)

def attend(queries, keys_all, values_all, length, blocks):
    block_size = math.gcd(SEQ, 512)
    block_count = SEQ // block_size
    key_position = jnp.arange(SEQ, dtype=jnp.int32)
    key_live = key_position < length
    query_blocks = queries.reshape(block_count, block_size, KV, H // KV, HD)
    starts = jnp.arange(block_count, dtype=jnp.int32) * block_size
    score_scale = HD ** (-0.5)

    def one_block(block_item):
        query_block, start_row = block_item
        query_position = start_row + jnp.arange(block_size, dtype=jnp.int32)
        query_ids = lax.dynamic_slice_in_dim(blocks, start_row, block_size, 0)
        raw_scores = jnp.einsum('qkgd,jkd->kgqj', query_block, keys_all, precision=HIGHEST) * score_scale
        scores = low_back(raw_scores)
        nearby = (query_ids[:, None] >= blocks[None, :]) & (query_position[:, None] - key_position[None, :] < WINDOW)
        nearby = nearby & (query_position < length)[:, None] & key_live[None, :]
        visible = nearby | (query_position[:, None] == key_position[None, :])
        scores = jnp.where(visible[None, None], scores, NEGATIVE)
        row_max = lax.optimization_barrier(jnp.max(scores, axis=-1, keepdims=True))
        exponent = jnp.exp(scores - row_max)
        soft_weights = exponent / lax.optimization_barrier(jnp.sum(exponent, axis=-1, keepdims=True))
        mixed = jnp.einsum('kgqj,jkd->qkgd', low(soft_weights), values_all, precision=HIGHEST)
        return low(low_back(mixed)).reshape(block_size, H * HD)
    mixed_all = lax.map(jax.checkpoint(one_block), (query_blocks, starts))
    return mixed_all.reshape(SEQ, H * HD)

def layer(residual, layer_input, weight_set, norm_gains, head_gains, length, blocks):
    query_weight, key_weight, value_weight, output_weight, gate_weight, up_weight, down_weight, laurel_left, laurel_right, layer_gate, layer_proj = weight_set
    positions = jnp.arange(SEQ, dtype=jnp.int32)
    half_width = HD // 2
    frequency = jnp.exp(jnp.arange(half_width, dtype=jnp.float32) * (-2.0 * math.log(10000.0) / HD))
    angles = (positions.astype(jnp.float32)[:, None] * frequency[None, :])[:, None, :]
    normed = low(root_norm(residual, norm_gains[0]))
    query_raw = low_back(matmul(normed, query_weight)).reshape(SEQ, H, HD)
    key_raw = low_back(matmul(normed, key_weight)).reshape(SEQ, KV, HD)
    value_raw = low_back(matmul(normed, value_weight)).reshape(SEQ, KV, HD)
    queries = low(rotate(root_norm(query_raw, head_gains[0]), angles))
    keys_all = low(rotate(root_norm(key_raw, head_gains[1]), angles))
    values_all = low(plain_norm(value_raw))
    mixed = attend(queries.reshape(SEQ, KV, H // KV, HD), keys_all, values_all, length, blocks)
    out_proj = low_back(matmul(mixed, output_weight))
    laurel_mid = low(low_back(matmul(normed, laurel_left)))
    low_rank = low_back(matmul(laurel_mid, laurel_right))
    after_attention = (residual + root_norm(out_proj, norm_gains[1]) + normed + root_norm(low_rank, norm_gains[4])) * HALF_ROOT
    feed_low = low(root_norm(after_attention, norm_gains[2]))
    gate_value = low_back(matmul(feed_low, gate_weight))
    up_value = low_back(matmul(feed_low, up_weight))
    units = low(smooth_gate(gate_value) * up_value)
    summed = low_back(matmul(units, down_weight))
    after_feed = after_attention + root_norm(summed, norm_gains[3])
    layer_pre = low_back(matmul(low(after_feed), layer_gate))
    layer_low = low(smooth_gate(layer_pre) * layer_input)
    projected = low_back(matmul(layer_low, layer_proj))
    result = after_feed + root_norm(projected, norm_gains[5])
    return (result, (after_attention, after_feed))

def reference(hidden, per_layer, lengths, block_ids, out_grad, query_weight, key_weight, value_weight, output_weight, gate_weight, up_weight, down_weight, laurel_left, laurel_right, layer_gate, layer_proj, norm_gains, head_gains):
    weight_set = tuple((matrix.astype(jnp.float32) for matrix in (query_weight, key_weight, value_weight, output_weight, gate_weight, up_weight, down_weight, laurel_left, laurel_right, layer_gate, layer_proj)))
    residuals = jnp.moveaxis(hidden, 1, 0).astype(jnp.float32)
    layer_inputs = jnp.moveaxis(per_layer, 1, 0).astype(jnp.float32)
    cotangents = jnp.moveaxis(out_grad, 1, 0).astype(jnp.float32)

    def one_sequence(carried, sequence_item):
        grad_weights, grad_gains, grad_heads, square_sums = carried
        residual, layer_input, cotangent, length, blocks = sequence_item

        def forward(residual_in, input_in, weights_in, gains_in, heads_in):
            return layer(residual_in, input_in, weights_in, gains_in, heads_in, length, blocks)
        result, backward, extras = jax.vjp(forward, residual, layer_input, weight_set, norm_gains, head_gains, has_aux=True)
        valid = (jnp.arange(SEQ, dtype=jnp.int32) < length).astype(jnp.float32)[:, None]
        grad_residual, grad_input, grad_set, grad_norms, grad_head = backward(cotangent * valid)
        after_attention, after_feed = extras
        square_sums = square_sums + jnp.stack([jnp.sum(valid * residual * residual), jnp.sum(valid * after_attention * after_attention), jnp.sum(valid * after_feed * after_feed), jnp.sum(valid * result * result)])
        grad_weights = tuple((first_array + second_array for first_array, second_array in zip(grad_weights, grad_set)))
        new_carry = (grad_weights, grad_gains + grad_norms, grad_heads + grad_head, square_sums)
        return (new_carry, (result.astype(jnp.bfloat16), grad_residual.astype(jnp.bfloat16), grad_input.astype(jnp.bfloat16)))
    initial = (tuple((jnp.zeros_like(matrix) for matrix in weight_set)), jnp.zeros_like(norm_gains), jnp.zeros_like(head_gains), jnp.zeros((4,), jnp.float32))
    (grad_weights, grad_gains, grad_heads, square_sums), (results, grad_residuals, grad_inputs) = lax.scan(one_sequence, initial, (residuals, layer_inputs, cotangents, lengths, block_ids))
    valid_count = jnp.sum(lengths).astype(jnp.float32)
    stats = jnp.sqrt(square_sums / (valid_count * D))
    output = jnp.moveaxis(results, 0, 1)
    d_hidden = jnp.moveaxis(grad_residuals, 0, 1)
    d_per_layer = jnp.moveaxis(grad_inputs, 0, 1)
    return (output, stats, d_hidden, d_per_layer, grad_weights[0], grad_weights[1], grad_weights[2], grad_weights[3], grad_weights[4], grad_weights[5], grad_weights[6], grad_weights[7], grad_weights[8], grad_weights[9], grad_weights[10], grad_gains, grad_heads)
```

```python
import functools
import math

import jax
import jax.numpy as jnp
from jax import lax
from jax.experimental import pallas as pl
from jax.experimental.pallas import tpu as pltpu
from jax.sharding import PartitionSpec as P

D = 2048
H = 8
KV = 2
HD = 256
WINDOW = 512
BLOCK = 256


EPSILON = 1e-06
FAR_BLOCK = 1 << 30
NEGATIVE = -1e30
HALF_ROOT = 1.0 / math.sqrt(2.0)


MESH = pl.DeviceIdType.MESH


def passed_along(value, axis, steps):
    count = lax.axis_size(axis)
    initial, last = (max(0, -steps), min(count, count - steps))
    return lax.ppermute(value, axis, [(source, source + steps) for source in range(initial, last)])


def root_norm(values, gain_row):
    return (
        values * lax.rsqrt(jnp.mean(values * values, axis=-1, keepdims=True) + EPSILON) * gain_row
    )


def plain_norm(values):
    return values * lax.rsqrt(jnp.mean(values * values, axis=-1, keepdims=True) + EPSILON)


def smooth_gate(values):
    return jax.nn.gelu(values, approximate=True)


def rotate(values, angles):
    half_width = values.shape[-1] // 2
    leading = values[..., :half_width]
    trailing = values[..., half_width:]
    cosine = jnp.cos(angles)
    sine_part = jnp.sin(angles)
    return jnp.concatenate(
        [leading * cosine - trailing * sine_part, trailing * cosine + leading * sine_part], axis=-1
    )


def matmul_last(first_array, second_array):
    return lax.dot_general(
        first_array,
        second_array,
        (((first_array.ndim - 1,), (0,)), ((), ())),
        preferred_element_type=jnp.float32,
    )


def matmul_back(first_array, second_array):
    return lax.dot_general(
        first_array,
        second_array,
        (((first_array.ndim - 1,), (1,)), ((), ())),
        preferred_element_type=jnp.float32,
    )


def outer_sum(first_array, second_array):
    return lax.dot_general(
        first_array, second_array, (((0, 1), (0, 1)), ((), ())), preferred_element_type=jnp.float32
    )


def input_norm(residual, gain_rows):
    return root_norm(residual, gain_rows[0])


def middle(residual, out_proj, low_rank, normed, gain_rows):
    merged = (
        residual + root_norm(out_proj, gain_rows[1]) + normed + root_norm(low_rank, gain_rows[4])
    ) * HALF_ROOT
    return (merged, root_norm(merged, gain_rows[2]))


def feed_join(merged, summed, gain_rows):
    return merged + root_norm(summed, gain_rows[3])


def final_join(merged, projected, gain_rows):
    return merged + root_norm(projected, gain_rows[5])


def gated_product(first_array, second_array):
    return smooth_gate(first_array) * second_array


def partners():
    c = lax.axis_index("col")
    sib = c + 1 - 2 * (c % 2)
    xn = c + 2 - 4 * ((c // 2) % 2)
    yn = c + 4 - 8 * (c // 4)
    return c, sib, xn, yn

def greet(devs):
    barrier = pltpu.get_barrier_semaphore()
    for d in devs:
        pl.semaphore_signal(barrier, inc=1, device_id={"col": d}, device_id_type=MESH)
    pl.semaphore_wait(barrier, len(devs))

def spread_kernel(rows, x_ref, o_ref, local_sem, send, recv):
    c, sib, xn, yn = partners()
    def slot(half, who):
        return o_ref.at[half, pl.ds(pl.multiple_of(who * rows, rows), rows), :]
    def both(who):
        return o_ref.at[:, pl.ds(pl.multiple_of(who * rows, rows), rows), :]
    def push(i, src, dst, dev):
        return pltpu.make_async_remote_copy(src_ref=src, dst_ref=dst, send_sem=send.at[i], recv_sem=recv.at[i], device_id={"col": dev}, device_id_type=MESH)
    mine = pltpu.make_async_copy(x_ref, both(c), local_sem)
    mine.start()
    greet((sib, xn, yn))
    x0 = push(0, x_ref.at[0], slot(0, c), xn)
    y1 = push(1, x_ref.at[1], slot(1, c), yn)
    x1 = push(2, x_ref.at[1], slot(1, c), xn)
    y0 = push(3, x_ref.at[0], slot(0, c), yn)
    s = push(4, x_ref, both(c), sib)
    x0.start(); y1.start(); x1.start(); y0.start(); s.start()
    diag = yn + (xn - c)
    x0.wait_recv()
    fy = push(5, slot(0, xn), slot(0, xn), yn)
    fy.start()
    sx0 = push(6, slot(0, xn), slot(0, xn), sib)
    sx0.start()
    y1.wait_recv()
    fx = push(7, slot(1, yn), slot(1, yn), xn)
    fx.start()
    sy1 = push(8, slot(1, yn), slot(1, yn), sib)
    sy1.start()
    x1.wait_recv()
    sx1 = push(9, slot(1, xn), slot(1, xn), sib)
    sx1.start()
    y0.wait_recv()
    sy0 = push(10, slot(0, yn), slot(0, yn), sib)
    sy0.start()
    fy.wait_recv()
    sd0 = push(11, slot(0, diag), slot(0, diag), sib)
    sd0.start()
    fx.wait_recv()
    sd1 = push(12, slot(1, diag), slot(1, diag), sib)
    sd1.start()
    for cp in (s, sx0, sy1, sx1, sy0, sd0, sd1):
        cp.wait_recv()
    for cp in (x0, y1, x1, y0, s, fy, sx0, fx, sy1, sx1, sy0, sd0, sd1):
        cp.wait_send()
    mine.wait()

def spread(x, cid=0):
    h, rows, d = x.shape
    return pl.pallas_call(
        functools.partial(spread_kernel, rows),
        out_shape=jax.ShapeDtypeStruct((h, 8 * rows, d), x.dtype),
        in_specs=[pl.BlockSpec(memory_space=pl.ANY)],
        out_specs=pl.BlockSpec(memory_space=pl.ANY),
        scratch_shapes=[pltpu.SemaphoreType.DMA, pltpu.SemaphoreType.DMA((13,)), pltpu.SemaphoreType.DMA((13,))],
        compiler_params=pltpu.CompilerParams(collective_id=cid, has_side_effects=True),
        cost_estimate=pl.CostEstimate(flops=0, bytes_accessed=120_000_000, transcendentals=0),
        name="spread",
    )(x)

def fold_kernel(rows, p_ref, o_ref, own, sibs, dx, dy, rx, ry, local_sem, send, recv):
    c, sib, xn, yn = partners()
    diag = yn + (xn - c)
    def blk(who):
        return p_ref.at[:, pl.ds(pl.multiple_of(who * rows, rows), rows), :]
    def push(i, src, dst, dev):
        return pltpu.make_async_remote_copy(src_ref=src, dst_ref=dst, send_sem=send.at[i], recv_sem=recv.at[i], device_id={"col": dev}, device_id_type=MESH)
    dests = (diag, xn, yn, c)
    loads = [pltpu.make_async_copy(blk(d), own.at[j], local_sem.at[j]) for j, d in enumerate(dests)]
    for l in loads: l.start()
    greet((sib, xn, yn))
    step = sib - c
    sides = [push(j, blk(d + step), sibs.at[j], sib) for j, d in enumerate(dests)]
    for q in sides: q.start()
    F = jnp.float32
    tall = 32 if rows % 32 == 0 else 8
    def add(dst, src):
        @pl.loop(0, 2)
        def _(h):
            @pl.loop(0, rows // tall)
            def _(i):
                r = pl.ds(pl.multiple_of(i * tall, tall), tall)
                dst[h, r, :] = (dst[h, r, :].astype(F) + src[h, r, :].astype(F)).astype(dst.dtype)
    def add1(dst, src):
        @pl.loop(0, rows // tall)
        def _(i):
            r = pl.ds(pl.multiple_of(i * tall, tall), tall)
            dst[r, :] = (dst[r, :].astype(F) + src[r, :].astype(F)).astype(dst.dtype)
    loads[0].wait(); sides[0].wait_recv()
    add(own.at[0], sibs.at[0])
    a = push(4, own.at[0, 0], dx, xn); a.start()
    b = push(5, own.at[0, 1], dy, yn); b.start()
    loads[1].wait(); sides[1].wait_recv()
    add(own.at[1], sibs.at[1])
    x0 = push(6, own.at[1, 0], rx.at[0], xn); x0.start()
    loads[2].wait(); sides[2].wait_recv()
    add(own.at[2], sibs.at[2])
    y1 = push(7, own.at[2, 1], ry.at[1], yn); y1.start()
    a.wait_recv()
    add1(own.at[2, 0], dx)
    y0 = push(8, own.at[2, 0], ry.at[0], yn); y0.start()
    b.wait_recv()
    add1(own.at[1, 1], dy)
    x1 = push(9, own.at[1, 1], rx.at[1], xn); x1.start()
    loads[3].wait(); sides[3].wait_recv()
    add(own.at[3], sibs.at[3])
    def last(h):
        @pl.loop(0, rows // tall)
        def _(i):
            r = pl.ds(pl.multiple_of(i * tall, tall), tall)
            o_ref[h, r, :] = own[3, h, r, :].astype(F) + rx[h, r, :].astype(F) + ry[h, r, :].astype(F)
    x0.wait_recv(); y0.wait_recv()
    last(0)
    x1.wait_recv(); y1.wait_recv()
    last(1)
    for cp in (*sides, a, b, x0, y1, y0, x1):
        cp.wait_send()

def fold(p, cid=1):
    h, total, d = p.shape
    rows = total // 8
    B = p.dtype
    return pl.pallas_call(
        functools.partial(fold_kernel, rows),
        out_shape=jax.ShapeDtypeStruct((h, rows, d), jnp.float32),
        in_specs=[pl.BlockSpec(memory_space=pl.ANY)],
        out_specs=pl.BlockSpec(memory_space=pltpu.VMEM),
        scratch_shapes=[pltpu.VMEM((4, h, rows, d), B), pltpu.VMEM((4, h, rows, d), B),
            pltpu.VMEM((rows, d), B), pltpu.VMEM((rows, d), B), pltpu.VMEM((h, rows, d), B), pltpu.VMEM((h, rows, d), B),
            pltpu.SemaphoreType.DMA((4,)), pltpu.SemaphoreType.DMA((10,)), pltpu.SemaphoreType.DMA((10,))],
        compiler_params=pltpu.CompilerParams(collective_id=cid, has_side_effects=True, vmem_limit_bytes=40 << 20),
        cost_estimate=pl.CostEstimate(flops=0, bytes_accessed=120_000_000, transcendentals=0),
        name="fold",
    )(p)


def general_body(
    hidden,
    per_layer,
    lengths,
    block_ids,
    out_grad,
    query_weight,
    key_weight,
    value_weight,
    output_weight,
    gate_weight,
    up_weight,
    down_weight,
    laurel_left,
    laurel_right,
    layer_gate,
    layer_proj,
    norm_gains,
    head_gains,
):
    local_rows = hidden.shape[0]
    seq_groups = hidden.shape[1]
    col_index = lax.axis_index("col")
    row_index = lax.axis_index("row")
    all_lengths = lengths
    lengths = lax.dynamic_slice_in_dim(all_lengths, row_index * seq_groups, seq_groups, 0)
    (
        query_cols,
        key_cols,
        value_cols,
        output_rows,
        gate_cols,
        up_cols,
        down_rows,
        left_cols,
        right_rows,
        gate_layer_cols,
        proj_layer_rows,
    ) = (
        lax.all_gather(query_weight, "row", axis=0, tiled=True),
        lax.all_gather(key_weight, "row", axis=0, tiled=True),
        lax.all_gather(value_weight, "row", axis=0, tiled=True),
        lax.all_gather(output_weight, "row", axis=1, tiled=True),
        lax.all_gather(gate_weight, "row", axis=0, tiled=True),
        lax.all_gather(up_weight, "row", axis=0, tiled=True),
        lax.all_gather(down_weight, "row", axis=1, tiled=True),
        lax.all_gather(laurel_left, "row", axis=0, tiled=True),
        lax.all_gather(laurel_right, "row", axis=1, tiled=True),
        lax.all_gather(layer_gate, "row", axis=0, tiled=True),
        lax.all_gather(layer_proj, "row", axis=1, tiled=True),
    )
    (
        query_full,
        key_full,
        value_full,
        output_full,
        left_full,
        right_full,
        gate_layer_full,
        proj_layer_full,
    ) = (
        lax.all_gather(query_cols, "col", axis=1, tiled=True),
        lax.all_gather(key_cols, "col", axis=1, tiled=True),
        lax.all_gather(value_cols, "col", axis=1, tiled=True),
        lax.all_gather(output_rows, "col", axis=0, tiled=True),
        lax.all_gather(left_cols, "col", axis=1, tiled=True),
        lax.all_gather(right_rows, "col", axis=0, tiled=True),
        lax.all_gather(gate_layer_cols, "col", axis=1, tiled=True),
        lax.all_gather(proj_layer_rows, "col", axis=0, tiled=True),
    )
    paired = jnp.concatenate([gate_cols, up_cols], axis=1)
    unit_width = gate_cols.shape[1]
    first_position = col_index * local_rows
    positions = first_position + jnp.arange(local_rows, dtype=jnp.int32)
    live_mask = positions[:, None] < lengths[None, :]
    keep_mask = live_mask.astype(jnp.float32)[:, :, None]
    reach_back = (WINDOW + local_rows - 2) // local_rows
    reach_ahead = (BLOCK + local_rows - 2) // local_rows
    key_span = (reach_back + 1 + reach_ahead) * local_rows
    key_position = first_position - reach_back * local_rows + jnp.arange(key_span, dtype=jnp.int32)
    filler_low = jnp.full((seq_groups, reach_back * local_rows), FAR_BLOCK, jnp.int32)
    filler_high = jnp.full((seq_groups, reach_ahead * local_rows), FAR_BLOCK, jnp.int32)
    padded_blocks = jnp.concatenate([filler_low, block_ids, filler_high], axis=1)
    key_blocks = lax.dynamic_slice_in_dim(padded_blocks, first_position, key_span, 1)
    query_blocks = lax.dynamic_slice_in_dim(block_ids, first_position, local_rows, 1)
    key_live = (key_position[None, :] >= 0) & (key_position[None, :] < lengths[:, None])
    query_live = positions[None, :] < lengths[:, None]
    distance = positions[:, None] - key_position[None, :]
    nearby = (query_blocks[:, :, None] >= key_blocks[:, None, :]) & (distance < WINDOW)[None]
    nearby = nearby & query_live[:, :, None] & key_live[:, None, :]
    visible = (nearby | (distance == 0)[None])[:, None, None]
    residual = hidden.astype(jnp.float32)
    normed_value, input_back = jax.vjp(input_norm, residual, norm_gains)
    normed_low = normed_value.astype(jnp.bfloat16)
    half_width = HD // 2
    frequency = jnp.exp(jnp.arange(half_width, dtype=jnp.float32) * (-2.0 * math.log(10000.0) / HD))
    angles = (positions.astype(jnp.float32)[:, None] * frequency[None, :])[:, None, None, :]

    def prepare(query_in, key_in, value_in, gain_rows):
        return (
            rotate(root_norm(query_in, gain_rows[0]), angles),
            rotate(root_norm(key_in, gain_rows[1]), angles),
            plain_norm(value_in),
        )

    query_raw = matmul_last(normed_low, query_full).reshape(local_rows, seq_groups, H, HD)
    key_raw = matmul_last(normed_low, key_full).reshape(local_rows, seq_groups, KV, HD)
    value_raw = matmul_last(normed_low, value_full).reshape(local_rows, seq_groups, KV, HD)
    (query_value, key_value, value_value), head_back = jax.vjp(
        prepare, query_raw, key_raw, value_raw, head_gains
    )
    query_low = query_value.astype(jnp.bfloat16).reshape(local_rows, seq_groups, KV, H // KV, HD)
    key_low = key_value.astype(jnp.bfloat16)
    value_low = value_value.astype(jnp.bfloat16)
    offsets = list(range(reach_back, -reach_ahead - 1, -1))
    key_parts = []
    value_parts = []
    for offset in offsets:
        if offset == 0:
            key_parts.append(key_low)
            value_parts.append(value_low)
        else:
            moved_key, moved_value = passed_along((key_low, value_low), "col", offset)
            key_parts.append(moved_key)
            value_parts.append(moved_value)
    near_keys = jnp.concatenate(key_parts, axis=0)
    near_values = jnp.concatenate(value_parts, axis=0)
    score_scale = HD ** (-0.5)

    def score_all():
        raw_scores = (
            jnp.einsum(
                "psjgd,esjd->sjgpe", query_low, near_keys, preferred_element_type=jnp.float32
            )
            * score_scale
        )
        return jnp.where(visible, raw_scores, NEGATIVE)

    scores = score_all()
    row_max = jnp.max(scores, axis=-1, keepdims=True)
    exponent = jnp.exp(scores - row_max)
    row_total = jnp.sum(exponent, axis=-1, keepdims=True)
    attn_prob = exponent / row_total
    log_total = row_max + jnp.log(row_total)
    mixed_heads = jnp.einsum(
        "sjgpe,esjd->psjgd",
        attn_prob.astype(jnp.bfloat16),
        near_values,
        preferred_element_type=jnp.float32,
    )
    mixed_low = mixed_heads.reshape(local_rows, seq_groups, H * HD).astype(jnp.bfloat16)
    out_proj = matmul_last(mixed_low, output_full)
    laurel_mid = matmul_last(normed_low, left_full).astype(jnp.bfloat16)
    low_rank = matmul_last(laurel_mid, right_full)
    (after_attention, feed_normed), middle_back = jax.vjp(
        middle, residual, out_proj, low_rank, normed_low.astype(jnp.float32), norm_gains
    )
    feed_low = feed_normed.astype(jnp.bfloat16)
    gate_up = matmul_last(lax.all_gather(feed_low, "col", axis=0, tiled=True), paired)
    unit_value, gate_back = jax.vjp(
        gated_product, gate_up[..., :unit_width], gate_up[..., unit_width:]
    )
    units_low = unit_value.astype(jnp.bfloat16)
    summed = lax.psum_scatter(
        matmul_last(units_low, down_rows), "col", scatter_dimension=0, tiled=True
    )
    after_feed, feed_back = jax.vjp(feed_join, after_attention, summed, norm_gains)
    feed_round = after_feed.astype(jnp.bfloat16)
    layer_pre = matmul_last(feed_round, gate_layer_full)
    layer_input = per_layer.astype(jnp.float32)
    layer_value, layer_back = jax.vjp(gated_product, layer_pre, layer_input)
    layer_low = layer_value.astype(jnp.bfloat16)
    projected = matmul_last(layer_low, proj_layer_full)
    out_value, final_back = jax.vjp(final_join, after_feed, projected, norm_gains)
    square_sums = jnp.stack(
        [
            jnp.sum(keep_mask * residual * residual),
            jnp.sum(keep_mask * after_attention * after_attention),
            jnp.sum(keep_mask * after_feed * after_feed),
            jnp.sum(keep_mask * out_value * out_value),
        ]
    )
    valid_count = jnp.sum(all_lengths).astype(jnp.float32)
    cotangent = out_grad.astype(jnp.float32) * keep_mask
    grad_feed_out, grad_projected, gains_final = final_back(cotangent)
    projected_low = grad_projected.astype(jnp.bfloat16)
    grad_proj_layer = outer_sum(layer_low, projected_low)
    grad_layer_pre, grad_layer_input = layer_back(matmul_back(projected_low, proj_layer_full))
    layer_pre_low = grad_layer_pre.astype(jnp.bfloat16)
    grad_gate_layer = outer_sum(feed_round, layer_pre_low)
    grad_after_feed = grad_feed_out + matmul_back(layer_pre_low, gate_layer_full)
    grad_after_attention_a, grad_summed, gains_feed = feed_back(grad_after_feed)
    summed_low = grad_summed.astype(jnp.bfloat16)
    block_rows = lax.all_gather(summed_low, "col", axis=0, tiled=True)
    grad_down = outer_sum(units_low, block_rows)
    grad_units = matmul_back(block_rows, down_rows)
    grad_down, grad_units = (grad_down, grad_units)
    grad_gate_value, grad_up_value = gate_back(grad_units)
    grad_paired = jnp.concatenate([grad_gate_value, grad_up_value], axis=-1).astype(jnp.bfloat16)
    grad_weights_paired = outer_sum(
        lax.all_gather(feed_low, "col", axis=0, tiled=True), grad_paired
    )
    grad_feed = lax.psum_scatter(
        matmul_back(grad_paired, paired).astype(jnp.bfloat16),
        "col",
        scatter_dimension=0,
        tiled=True,
    ).astype(jnp.float32)
    grad_residual_mid, grad_out_proj, grad_low_rank, grad_normed_mid, gains_middle = middle_back(
        (grad_after_attention_a, grad_feed)
    )
    out_proj_low = grad_out_proj.astype(jnp.bfloat16)
    grad_output = outer_sum(mixed_low, out_proj_low)
    grad_mixed = matmul_back(out_proj_low, output_full).astype(jnp.bfloat16)
    grad_mixed = grad_mixed.reshape(local_rows, seq_groups, KV, H // KV, HD)
    low_rank_grad = grad_low_rank.astype(jnp.bfloat16)
    grad_right = outer_sum(laurel_mid, low_rank_grad)
    grad_laurel_mid = matmul_back(low_rank_grad, right_full).astype(jnp.bfloat16)
    grad_left = outer_sum(normed_low, grad_laurel_mid)
    scores = score_all()
    attn_prob = jnp.exp(scores - log_total)
    grad_prob = jnp.einsum(
        "psjgd,esjd->sjgpe", grad_mixed, near_values, preferred_element_type=jnp.float32
    )
    grad_scores = (
        attn_prob * (grad_prob - jnp.sum(attn_prob * grad_prob, axis=-1, keepdims=True))
    ).astype(jnp.bfloat16)
    grad_queries = (
        jnp.einsum("sjgpe,esjd->psjgd", grad_scores, near_keys, preferred_element_type=jnp.float32)
        * score_scale
    )
    grad_near_keys = (
        jnp.einsum("sjgpe,psjgd->esjd", grad_scores, query_low, preferred_element_type=jnp.float32)
        * score_scale
    )
    grad_near_values = jnp.einsum(
        "sjgpe,psjgd->esjd",
        attn_prob.astype(jnp.bfloat16),
        grad_mixed,
        preferred_element_type=jnp.float32,
    )
    grad_key_total = grad_near_keys[reach_back * local_rows : (reach_back + 1) * local_rows]
    grad_value_total = grad_near_values[reach_back * local_rows : (reach_back + 1) * local_rows]
    for slot_index, offset in enumerate(offsets):
        if offset != 0:
            piece_keys = grad_near_keys[slot_index * local_rows : (slot_index + 1) * local_rows]
            piece_values = grad_near_values[slot_index * local_rows : (slot_index + 1) * local_rows]
            back_keys, back_values = (
                passed_along(piece_keys.astype(jnp.bfloat16), "col", -offset).astype(
                    piece_keys.dtype
                ),
                passed_along(piece_values.astype(jnp.bfloat16), "col", -offset).astype(
                    piece_values.dtype
                ),
            )
            grad_key_total = grad_key_total + back_keys
            grad_value_total = grad_value_total + back_values
    grad_query_raw, grad_key_raw, grad_value_raw, grad_heads = head_back(
        (grad_queries.reshape(local_rows, seq_groups, H, HD), grad_key_total, grad_value_total)
    )
    query_grad_low = grad_query_raw.reshape(local_rows, seq_groups, H * HD).astype(jnp.bfloat16)
    key_grad_low = grad_key_raw.reshape(local_rows, seq_groups, KV * HD).astype(jnp.bfloat16)
    value_grad_low = grad_value_raw.reshape(local_rows, seq_groups, KV * HD).astype(jnp.bfloat16)
    grad_query = outer_sum(normed_low, query_grad_low)
    grad_key = outer_sum(normed_low, key_grad_low)
    grad_value = outer_sum(normed_low, value_grad_low)
    grad_normed = (
        grad_normed_mid
        + matmul_back(grad_laurel_mid, left_full)
        + matmul_back(query_grad_low, query_full)
        + matmul_back(key_grad_low, key_full)
        + matmul_back(value_grad_low, value_full)
    )
    grad_residual_in, gains_input = input_back(grad_normed)
    d_hidden = (grad_residual_mid + grad_residual_in).astype(jnp.bfloat16)
    d_per_layer = grad_layer_input.astype(jnp.bfloat16)
    grad_gains = gains_final + gains_feed + gains_middle + gains_input
    grad_gate = grad_weights_paired[:, :unit_width]
    grad_up = grad_weights_paired[:, unit_width:]
    (
        query_part,
        key_part,
        value_part,
        output_part,
        left_part,
        right_part,
        gate_layer_part,
        proj_layer_part,
    ) = (
        lax.psum_scatter(
            grad_query.astype(jnp.bfloat16), "col", scatter_dimension=1, tiled=True
        ).astype(jnp.float32),
        lax.psum_scatter(
            grad_key.astype(jnp.bfloat16), "col", scatter_dimension=1, tiled=True
        ).astype(jnp.float32),
        lax.psum_scatter(
            grad_value.astype(jnp.bfloat16), "col", scatter_dimension=1, tiled=True
        ).astype(jnp.float32),
        lax.psum_scatter(
            grad_output.astype(jnp.bfloat16), "col", scatter_dimension=0, tiled=True
        ).astype(jnp.float32),
        lax.psum_scatter(
            grad_left.astype(jnp.bfloat16), "col", scatter_dimension=1, tiled=True
        ).astype(jnp.float32),
        lax.psum_scatter(
            grad_right.astype(jnp.bfloat16), "col", scatter_dimension=0, tiled=True
        ).astype(jnp.float32),
        lax.psum_scatter(
            grad_gate_layer.astype(jnp.bfloat16), "col", scatter_dimension=1, tiled=True
        ).astype(jnp.float32),
        lax.psum_scatter(
            grad_proj_layer.astype(jnp.bfloat16), "col", scatter_dimension=0, tiled=True
        ).astype(jnp.float32),
    )
    (
        d_query_weight,
        d_key_weight,
        d_value_weight,
        d_output_weight,
        d_gate_weight,
        d_up_weight,
        d_down_weight,
        d_laurel_left,
        d_laurel_right,
        d_layer_gate,
        d_layer_proj,
    ) = (
        lax.psum_scatter(
            query_part.astype(jnp.bfloat16), "row", scatter_dimension=0, tiled=True
        ).astype(jnp.float32),
        lax.psum_scatter(
            key_part.astype(jnp.bfloat16), "row", scatter_dimension=0, tiled=True
        ).astype(jnp.float32),
        lax.psum_scatter(
            value_part.astype(jnp.bfloat16), "row", scatter_dimension=0, tiled=True
        ).astype(jnp.float32),
        lax.psum_scatter(
            output_part.astype(jnp.bfloat16), "row", scatter_dimension=1, tiled=True
        ).astype(jnp.float32),
        lax.psum_scatter(
            grad_gate.astype(jnp.bfloat16), "row", scatter_dimension=0, tiled=True
        ).astype(jnp.float32),
        lax.psum_scatter(
            grad_up.astype(jnp.bfloat16), "row", scatter_dimension=0, tiled=True
        ).astype(jnp.float32),
        lax.psum_scatter(
            grad_down.astype(jnp.bfloat16), "row", scatter_dimension=1, tiled=True
        ).astype(jnp.float32),
        lax.psum_scatter(
            left_part.astype(jnp.bfloat16), "row", scatter_dimension=0, tiled=True
        ).astype(jnp.float32),
        lax.psum_scatter(
            right_part.astype(jnp.bfloat16), "row", scatter_dimension=1, tiled=True
        ).astype(jnp.float32),
        lax.psum_scatter(
            gate_layer_part.astype(jnp.bfloat16), "row", scatter_dimension=0, tiled=True
        ).astype(jnp.float32),
        lax.psum_scatter(
            proj_layer_part.astype(jnp.bfloat16), "row", scatter_dimension=1, tiled=True
        ).astype(jnp.float32),
    )
    d_norm_gains, d_head_gains, total_squares = lax.psum(
        (grad_gains, grad_heads, square_sums), ("row", "col")
    )
    stats = jnp.sqrt(total_squares / (valid_count * D))
    output = out_value.astype(jnp.bfloat16)
    return (
        output,
        stats,
        d_hidden,
        d_per_layer,
        d_query_weight,
        d_key_weight,
        d_value_weight,
        d_output_weight,
        d_gate_weight,
        d_up_weight,
        d_down_weight,
        d_laurel_left,
        d_laurel_right,
        d_layer_gate,
        d_layer_proj,
        d_norm_gains,
        d_head_gains,
    )


def swap(array):
    return jnp.swapaxes(array, 0, 1)


def heads_body(
    hidden,
    per_layer,
    lengths,
    block_ids,
    out_grad,
    query_weight,
    key_weight,
    value_weight,
    output_weight,
    gate_weight,
    up_weight,
    down_weight,
    laurel_left,
    laurel_right,
    layer_gate,
    layer_proj,
    norm_gains,
    head_gains,
):
    low = jnp.bfloat16
    rows = hidden.shape[0]
    groups = hidden.shape[1]
    cols = lax.axis_size("col")
    seq = rows * cols
    share = cols // KV
    col_index = lax.axis_index("col")
    row_index = lax.axis_index("row")
    all_lengths = lengths
    lengths = lax.dynamic_slice_in_dim(all_lengths, row_index * groups, groups, 0)

    small = jnp.concatenate(
        [key_weight.T, value_weight.T, laurel_left.T, layer_gate.T, laurel_right, layer_proj],
        axis=0,
    )
    heights = [key_weight.shape[1], value_weight.shape[1], laurel_left.shape[1]]
    heights += [layer_gate.shape[1], laurel_right.shape[0], layer_proj.shape[0]]
    edges = [sum(heights[:i]) for i in range(len(heights) + 1)]
    small_row = lax.all_gather(small, "row", axis=1, tiled=True)
    query_full = lax.all_gather(query_weight, "row", axis=0, tiled=True)
    output_full = lax.all_gather(output_weight, "row", axis=1, tiled=True)
    gate_full = lax.all_gather(gate_weight, "row", axis=0, tiled=True)
    up_full = lax.all_gather(up_weight, "row", axis=0, tiled=True)
    down_full = lax.all_gather(down_weight, "row", axis=1, tiled=True)

    residual = swap(hidden).astype(jnp.float32)
    normed_value, input_back = jax.vjp(input_norm, residual, norm_gains)
    normed_low = normed_value.astype(low)
    normed_all = spread(normed_low, 0)
    half = edges[-1] // 2
    small_all = spread(small_row.reshape(2, half, D), 1)
    small_all = small_all.reshape(2, cols, half, D)
    small_all = jnp.swapaxes(small_all, 0, 1).reshape(cols, edges[-1], D)
    pieces = [small_all[:, a:b] for a, b in zip(edges[:-1], edges[1:])]
    group_start = (col_index // share) * share
    key_full, value_full = (
        lax.dynamic_slice_in_dim(piece, group_start, share, 0).reshape(HD, D)
        for piece in pieces[:2]
    )
    left_full, gate_layer_full, right_full, proj_layer_full = (
        piece.reshape(-1, D) for piece in pieces[2:]
    )

    positions = jnp.arange(seq, dtype=jnp.int32)
    mine = col_index * rows + jnp.arange(rows, dtype=jnp.int32)
    keep_mask = (mine[None, :] < lengths[:, None]).astype(jnp.float32)[:, :, None]
    live = positions[None, :] < lengths[:, None]
    distance = positions[:, None] - positions[None, :]
    nearby = (block_ids[:, :, None] >= block_ids[:, None, :]) & (distance < WINDOW)[None]
    nearby = nearby & live[:, :, None] & live[:, None, :]
    visible = nearby | (distance == 0)[None]

    half_width = HD // 2
    frequency = jnp.exp(jnp.arange(half_width, dtype=jnp.float32) * (-2.0 * math.log(10000.0) / HD))
    angles = (positions.astype(jnp.float32)[:, None] * frequency[None, :])[None]

    def prepare(query_in, key_in, value_in, gain_rows):
        return (
            rotate(root_norm(query_in, gain_rows[0]), angles),
            rotate(root_norm(key_in, gain_rows[1]), angles),
            plain_norm(value_in),
        )

    query_raw = matmul_last(normed_all, query_full)
    key_raw = matmul_back(normed_all, key_full)
    value_raw = matmul_back(normed_all, value_full)
    (query_value, key_value, value_value), head_back = jax.vjp(
        prepare, query_raw, key_raw, value_raw, head_gains
    )
    query_low = query_value.astype(low)
    key_low = key_value.astype(low)
    value_low = value_value.astype(low)
    score_scale = HD ** (-0.5)

    def score_all():
        raw_scores = (
            jnp.einsum("spd,sed->spe", query_low, key_low, preferred_element_type=jnp.float32)
            * score_scale
        )
        return jnp.where(visible, raw_scores, NEGATIVE)

    scores = score_all()
    row_max = jnp.max(scores, axis=-1, keepdims=True)
    exponent = jnp.exp(scores - row_max)
    row_total = jnp.sum(exponent, axis=-1, keepdims=True)
    attn_prob = exponent / row_total
    log_total = row_max + jnp.log(row_total)
    mixed_low = jnp.einsum(
        "spe,sed->spd", attn_prob.astype(low), value_low, preferred_element_type=jnp.float32
    ).astype(low)
    out_proj = fold(matmul_last(mixed_low, output_full).astype(low), 2)
    laurel_mid = matmul_back(normed_low, left_full).astype(low)
    low_rank = matmul_last(laurel_mid, right_full)
    (after_attention, feed_normed), middle_back = jax.vjp(
        middle, residual, out_proj, low_rank, normed_low.astype(jnp.float32), norm_gains
    )
    feed_all = spread(feed_normed.astype(low), 0)
    gate_value = matmul_last(feed_all, gate_full)
    up_value = matmul_last(feed_all, up_full)
    unit_value, gate_back = jax.vjp(gated_product, gate_value, up_value)
    units_low = unit_value.astype(low)
    summed = fold(matmul_last(units_low, down_full).astype(low), 2)
    after_feed, feed_back = jax.vjp(feed_join, after_attention, summed, norm_gains)
    feed_round = after_feed.astype(low)
    layer_pre = matmul_back(feed_round, gate_layer_full)
    layer_input = swap(per_layer).astype(jnp.float32)
    layer_value, layer_back = jax.vjp(gated_product, layer_pre, layer_input)
    layer_low = layer_value.astype(low)
    projected = matmul_last(layer_low, proj_layer_full)
    out_value, final_back = jax.vjp(final_join, after_feed, projected, norm_gains)
    square_sums = jnp.stack(
        [
            jnp.sum(keep_mask * residual * residual),
            jnp.sum(keep_mask * after_attention * after_attention),
            jnp.sum(keep_mask * after_feed * after_feed),
            jnp.sum(keep_mask * out_value * out_value),
        ]
    )
    valid_count = jnp.sum(all_lengths).astype(jnp.float32)

    cotangent = swap(out_grad).astype(jnp.float32) * keep_mask
    grad_feed_out, grad_projected, gains_final = final_back(cotangent)
    projected_low = grad_projected.astype(low)
    grad_proj_layer = outer_sum(layer_low, projected_low)
    grad_layer_pre, grad_layer_input = layer_back(matmul_back(projected_low, proj_layer_full))
    layer_pre_low = grad_layer_pre.astype(low)
    grad_gate_layer = outer_sum(layer_pre_low, feed_round)
    grad_after_feed = grad_feed_out + matmul_last(layer_pre_low, gate_layer_full)
    grad_after_attention_a, grad_summed, gains_feed = feed_back(grad_after_feed)
    summed_all = spread(grad_summed.astype(low), 0)
    grad_down = outer_sum(units_low, summed_all)
    d_down_weight = lax.psum_scatter(
        grad_down.astype(low), "row", scatter_dimension=1, tiled=True
    ).astype(jnp.float32)
    grad_units = matmul_back(summed_all, down_full)
    grad_gate_value, grad_up_value = gate_back(grad_units)
    grad_gate_low = grad_gate_value.astype(low)
    grad_up_low = grad_up_value.astype(low)
    grad_gate = outer_sum(feed_all, grad_gate_low)
    grad_up = outer_sum(feed_all, grad_up_low)
    d_gate_weight = lax.psum_scatter(
        grad_gate.astype(low), "row", scatter_dimension=0, tiled=True
    ).astype(jnp.float32)
    d_up_weight = lax.psum_scatter(
        grad_up.astype(low), "row", scatter_dimension=0, tiled=True
    ).astype(jnp.float32)
    grad_feed = fold(
        (matmul_back(grad_gate_low, gate_full) + matmul_back(grad_up_low, up_full)).astype(low), 2
    )
    grad_residual_mid, grad_out_proj, grad_low_rank, grad_normed_mid, gains_middle = middle_back(
        (grad_after_attention_a, grad_feed)
    )
    out_proj_all = spread(grad_out_proj.astype(low), 0)
    grad_output = outer_sum(mixed_low, out_proj_all)
    d_output_weight = lax.psum_scatter(
        grad_output.astype(low), "row", scatter_dimension=1, tiled=True
    ).astype(jnp.float32)
    grad_mixed = matmul_back(out_proj_all, output_full).astype(low)
    low_rank_grad = grad_low_rank.astype(low)
    grad_right = outer_sum(laurel_mid, low_rank_grad)
    grad_laurel_mid = matmul_back(low_rank_grad, right_full).astype(low)
    grad_left = outer_sum(grad_laurel_mid, normed_low)
    attn_prob = jnp.exp(score_all() - log_total)
    grad_prob = jnp.einsum(
        "spd,sed->spe", grad_mixed, value_low, preferred_element_type=jnp.float32
    )
    grad_scores = (
        attn_prob * (grad_prob - jnp.sum(attn_prob * grad_prob, axis=-1, keepdims=True))
    ).astype(low)
    grad_queries = (
        jnp.einsum("spe,sed->spd", grad_scores, key_low, preferred_element_type=jnp.float32)
        * score_scale
    )
    grad_keys = (
        jnp.einsum("spe,spd->sed", grad_scores, query_low, preferred_element_type=jnp.float32)
        * score_scale
    )
    grad_values = jnp.einsum(
        "spe,spd->sed", attn_prob.astype(low), grad_mixed, preferred_element_type=jnp.float32
    )
    grad_query_raw, grad_key_raw, grad_value_raw, grad_heads = head_back(
        (grad_queries, grad_keys, grad_values)
    )
    query_grad_low = grad_query_raw.astype(low)
    key_grad_low = grad_key_raw.astype(low)
    value_grad_low = grad_value_raw.astype(low)
    grad_query = outer_sum(normed_all, query_grad_low)
    d_query_weight = lax.psum_scatter(
        grad_query.astype(low), "row", scatter_dimension=0, tiled=True
    ).astype(jnp.float32)
    grad_normed_part = (
        matmul_back(query_grad_low, query_full)
        + matmul_last(key_grad_low, key_full)
        + matmul_last(value_grad_low, value_full)
    ).astype(low)
    grad_key = outer_sum(key_grad_low, normed_all).astype(low)
    grad_value = outer_sum(value_grad_low, normed_all).astype(low)

    def placed(array):
        empty = jnp.zeros((cols, HD // share, D), low)
        return lax.dynamic_update_slice_in_dim(
            empty, array.reshape(share, HD // share, D), group_start, 0
        )

    small_grads = jnp.concatenate(
        [
            placed(grad_key),
            placed(grad_value),
            grad_left.astype(low).reshape(cols, -1, D),
            grad_gate_layer.astype(low).reshape(cols, -1, D),
            grad_right.astype(low).reshape(cols, -1, D),
            grad_proj_layer.astype(low).reshape(cols, -1, D),
        ],
        axis=1,
    )
    small_grads = jnp.swapaxes(small_grads.reshape(cols, 2, half, D), 0, 1)
    grad_normed = fold(grad_normed_part, 2)
    small_part = fold(small_grads.reshape(2, cols * half, D), 3).reshape(edges[-1], D)
    small_out = lax.psum_scatter(
        small_part.astype(low), "row", scatter_dimension=1, tiled=True
    ).astype(jnp.float32)
    small_parts = [small_out[a:b] for a, b in zip(edges[:-1], edges[1:])]
    grad_normed = grad_normed + grad_normed_mid + matmul_last(grad_laurel_mid, left_full)
    grad_residual_in, gains_input = input_back(grad_normed)
    d_hidden = swap((grad_residual_mid + grad_residual_in).astype(low))
    d_per_layer = swap(grad_layer_input.astype(low))
    grad_gains = gains_final + gains_feed + gains_middle + gains_input
    d_norm_gains, d_head_gains, total_squares = lax.psum(
        (grad_gains, grad_heads, square_sums), ("row", "col")
    )
    stats = jnp.sqrt(total_squares / (valid_count * D))
    output = swap(out_value.astype(low))
    return (
        output,
        stats,
        d_hidden,
        d_per_layer,
        d_query_weight,
        small_parts[0].T,
        small_parts[1].T,
        d_output_weight,
        d_gate_weight,
        d_up_weight,
        d_down_weight,
        small_parts[2].T,
        small_parts[4],
        small_parts[3].T,
        small_parts[5],
        d_norm_gains,
        d_head_gains,
    )


def solution(mesh):
    body = heads_body if mesh.shape["col"] == H else general_body
    in_specs = (
        P("col", "row", None),
        P("col", "row", None),
        P(),
        P("row", None),
        P("col", "row", None),
        P("row", "col"),
        P("row", "col"),
        P("row", "col"),
        P("col", "row"),
        P("row", "col"),
        P("row", "col"),
        P("col", "row"),
        P("row", "col"),
        P("col", "row"),
        P("row", "col"),
        P("col", "row"),
        P(),
        P(),
    )
    out_specs = (
        P("col", "row", None),
        P(),
        P("col", "row", None),
        P("col", "row", None),
        P("row", "col"),
        P("row", "col"),
        P("row", "col"),
        P("col", "row"),
        P("row", "col"),
        P("row", "col"),
        P("col", "row"),
        P("row", "col"),
        P("col", "row"),
        P("row", "col"),
        P("col", "row"),
        P(),
        P(),
    )
    return jax.shard_map(body, mesh=mesh, in_specs=in_specs, out_specs=out_specs, check_vma=False)
```

```python
import functools
import math

import jax
import jax.numpy as jnp
from jax import lax
from jax.experimental import pallas as pl
from jax.experimental.pallas import tpu as pltpu
from jax.sharding import PartitionSpec as P

D = 2048
H = 8
KV = 2
HD = 256
WINDOW = 512
BLOCK = 256


EPSILON = 1e-06
FAR_BLOCK = 1 << 30
NEGATIVE = -1e30
HALF_ROOT = 1.0 / math.sqrt(2.0)


MESH = pl.DeviceIdType.MESH


def passed_along(value, axis, steps):
    count = lax.axis_size(axis)
    initial, last = (max(0, -steps), min(count, count - steps))
    return lax.ppermute(value, axis, [(source, source + steps) for source in range(initial, last)])


def root_norm(values, gain_row):
    return (
        values * lax.rsqrt(jnp.mean(values * values, axis=-1, keepdims=True) + EPSILON) * gain_row
    )


def plain_norm(values):
    return values * lax.rsqrt(jnp.mean(values * values, axis=-1, keepdims=True) + EPSILON)


def smooth_gate(values):
    return jax.nn.gelu(values, approximate=True)


def rotate(values, angles):
    half_width = values.shape[-1] // 2
    leading = values[..., :half_width]
    trailing = values[..., half_width:]
    cosine = jnp.cos(angles)
    sine_part = jnp.sin(angles)
    return jnp.concatenate(
        [leading * cosine - trailing * sine_part, trailing * cosine + leading * sine_part], axis=-1
    )


def matmul_last(first_array, second_array):
    return lax.dot_general(
        first_array,
        second_array,
        (((first_array.ndim - 1,), (0,)), ((), ())),
        preferred_element_type=jnp.float32,
    )


def matmul_back(first_array, second_array):
    return lax.dot_general(
        first_array,
        second_array,
        (((first_array.ndim - 1,), (1,)), ((), ())),
        preferred_element_type=jnp.float32,
    )


def outer_sum(first_array, second_array):
    return lax.dot_general(
        first_array, second_array, (((0, 1), (0, 1)), ((), ())), preferred_element_type=jnp.float32
    )


def input_norm(residual, gain_rows):
    return root_norm(residual, gain_rows[0])


def middle(residual, out_proj, low_rank, normed, gain_rows):
    merged = (
        residual + root_norm(out_proj, gain_rows[1]) + normed + root_norm(low_rank, gain_rows[4])
    ) * HALF_ROOT
    return (merged, root_norm(merged, gain_rows[2]))


def feed_join(merged, summed, gain_rows):
    return merged + root_norm(summed, gain_rows[3])


def final_join(merged, projected, gain_rows):
    return merged + root_norm(projected, gain_rows[5])


def gated_product(first_array, second_array):
    return smooth_gate(first_array) * second_array


def partners():
    c = lax.axis_index("col")
    sib = c + 1 - 2 * (c % 2)
    xn = c + 2 - 4 * ((c // 2) % 2)
    yn = c + 4 - 8 * (c // 4)
    return c, sib, xn, yn

def greet(devs):
    barrier = pltpu.get_barrier_semaphore()
    for d in devs:
        pl.semaphore_signal(barrier, inc=1, device_id={"col": d}, device_id_type=MESH)
    pl.semaphore_wait(barrier, len(devs))

def spread_kernel(rows, x_ref, o_ref, local_sem, send, recv):
    c, sib, xn, yn = partners()
    def slot(half, who):
        return o_ref.at[half, pl.ds(pl.multiple_of(who * rows, rows), rows), :]
    def both(who):
        return o_ref.at[:, pl.ds(pl.multiple_of(who * rows, rows), rows), :]
    def push(i, src, dst, dev):
        return pltpu.make_async_remote_copy(src_ref=src, dst_ref=dst, send_sem=send.at[i], recv_sem=recv.at[i], device_id={"col": dev}, device_id_type=MESH)
    mine = pltpu.make_async_copy(x_ref, both(c), local_sem)
    mine.start()
    greet((sib, xn, yn))
    x0 = push(0, x_ref.at[0], slot(0, c), xn)
    y1 = push(1, x_ref.at[1], slot(1, c), yn)
    x1 = push(2, x_ref.at[1], slot(1, c), xn)
    y0 = push(3, x_ref.at[0], slot(0, c), yn)
    s = push(4, x_ref, both(c), sib)
    x0.start(); y1.start(); x1.start(); y0.start(); s.start()
    diag = yn + (xn - c)
    x0.wait_recv()
    fy = push(5, slot(0, xn), slot(0, xn), yn)
    fy.start()
    sx0 = push(6, slot(0, xn), slot(0, xn), sib)
    sx0.start()
    y1.wait_recv()
    fx = push(7, slot(1, yn), slot(1, yn), xn)
    fx.start()
    sy1 = push(8, slot(1, yn), slot(1, yn), sib)
    sy1.start()
    x1.wait_recv()
    sx1 = push(9, slot(1, xn), slot(1, xn), sib)
    sx1.start()
    y0.wait_recv()
    sy0 = push(10, slot(0, yn), slot(0, yn), sib)
    sy0.start()
    fy.wait_recv()
    sd0 = push(11, slot(0, diag), slot(0, diag), sib)
    sd0.start()
    fx.wait_recv()
    sd1 = push(12, slot(1, diag), slot(1, diag), sib)
    sd1.start()
    for cp in (s, sx0, sy1, sx1, sy0, sd0, sd1):
        cp.wait_recv()
    for cp in (x0, y1, x1, y0, s, fy, sx0, fx, sy1, sx1, sy0, sd0, sd1):
        cp.wait_send()
    mine.wait()

def spread(x, cid=0):
    h, rows, d = x.shape
    return pl.pallas_call(
        functools.partial(spread_kernel, rows),
        out_shape=jax.ShapeDtypeStruct((h, 8 * rows, d), x.dtype),
        in_specs=[pl.BlockSpec(memory_space=pl.ANY)],
        out_specs=pl.BlockSpec(memory_space=pl.ANY),
        scratch_shapes=[pltpu.SemaphoreType.DMA, pltpu.SemaphoreType.DMA((13,)), pltpu.SemaphoreType.DMA((13,))],
        compiler_params=pltpu.CompilerParams(collective_id=cid, has_side_effects=True),
        cost_estimate=pl.CostEstimate(flops=0, bytes_accessed=120_000_000, transcendentals=0),
        name="spread",
    )(x)

def fold_steps(rows, p_ref, own, sibs, dx, dy, rx, ry, local_sem, send, recv):
    c, sib, xn, yn = partners()
    diag = yn + (xn - c)
    wide = jnp.float32
    tall = 32 if rows % 32 == 0 else 8

    def blk(who):
        return p_ref.at[:, pl.ds(pl.multiple_of(who * rows, rows), rows), :]

    def push(i, src, dst, dev):
        return pltpu.make_async_remote_copy(
            src_ref=src,
            dst_ref=dst,
            send_sem=send.at[i],
            recv_sem=recv.at[i],
            device_id={"col": dev},
            device_id_type=MESH,
        )

    def add(dst, src):
        @pl.loop(0, rows // tall)
        def _(i):
            r = pl.ds(pl.multiple_of(i * tall, tall), tall)
            dst[r, :] = (dst[r, :].astype(wide) + src[r, :].astype(wide)).astype(dst.dtype)

    def pair(j):
        add(own.at[j, 0], sibs.at[j, 0])
        add(own.at[j, 1], sibs.at[j, 1])

    dests = (diag, xn, yn, c)
    loads = [pltpu.make_async_copy(blk(d), own.at[j], local_sem.at[j]) for j, d in enumerate(dests)]
    for load in loads:
        load.start()
    yield None
    sides = [push(j, blk(d + (sib - c)), sibs.at[j], sib) for j, d in enumerate(dests)]
    for side in sides:
        side.start()
    yield None
    loads[0].wait()
    sides[0].wait_recv()
    pair(0)
    a = push(4, own.at[0, 0], dx, xn)
    b = push(5, own.at[0, 1], dy, yn)
    a.start()
    b.start()
    yield None
    loads[1].wait()
    sides[1].wait_recv()
    pair(1)
    x0 = push(6, own.at[1, 0], rx.at[0], xn)
    x0.start()
    yield None
    loads[2].wait()
    sides[2].wait_recv()
    pair(2)
    y1 = push(7, own.at[2, 1], ry.at[1], yn)
    y1.start()
    yield None
    a.wait_recv()
    add(own.at[2, 0], dx)
    y0 = push(8, own.at[2, 0], ry.at[0], yn)
    y0.start()
    yield None
    b.wait_recv()
    add(own.at[1, 1], dy)
    x1 = push(9, own.at[1, 1], rx.at[1], xn)
    x1.start()
    yield None
    loads[3].wait()
    sides[3].wait_recv()
    pair(3)
    yield None
    waits = ((x0, y0), (x1, y1))
    yield tall, waits, (*sides, a, b, x0, y1, y0, x1)


def fold_finish(rows, o_ref, own, rx, ry, tall, waits, sent):
    wide = jnp.float32
    for h in range(2):
        for copy in waits[h]:
            copy.wait_recv()

        @pl.loop(0, rows // tall)
        def _(i):
            r = pl.ds(pl.multiple_of(i * tall, tall), tall)
            o_ref[h, r, :] = (
                own[3, h, r, :].astype(wide) + rx[h, r, :].astype(wide) + ry[h, r, :].astype(wide)
            )

    for copy in sent:
        copy.wait_send()


def fold_scratch(h, rows, d, kind):
    return [
        pltpu.VMEM((4, h, rows, d), kind),
        pltpu.VMEM((4, h, rows, d), kind),
        pltpu.VMEM((rows, d), kind),
        pltpu.VMEM((rows, d), kind),
        pltpu.VMEM((h, rows, d), kind),
        pltpu.VMEM((h, rows, d), kind),
        pltpu.SemaphoreType.DMA((4,)),
        pltpu.SemaphoreType.DMA((10,)),
        pltpu.SemaphoreType.DMA((10,)),
    ]


def product_kernel(
    rows, flip, a_ref, w_ref, o_ref, a_buf, w_buf, stage, own, sibs, dx, dy, rx, ry,
    local_sem, send, recv,
):
    c, sib, xn, yn = partners()
    diag = yn + (xn - c)
    wide = jnp.float32
    d = o_ref.shape[-1]
    tile = 512
    tall = 32

    def push(i, src, dst, dev):
        return pltpu.make_async_remote_copy(
            src_ref=src,
            dst_ref=dst,
            send_sem=send.at[i],
            recv_sem=recv.at[i],
            device_id={"col": dev},
            device_id_type=MESH,
        )

    dests = (diag, xn, yn, c)
    step = sib - c
    weights = pltpu.make_async_copy(w_ref, w_buf, local_sem.at[8])
    weights.start()

    def load(i, who):
        return pltpu.make_async_copy(
            a_ref.at[:, pl.ds(pl.multiple_of(who * rows, rows), rows), :],
            a_buf.at[i],
            local_sem.at[i],
        )

    far = [load(j, dests[j] + step) for j in range(4)]
    near = [load(4 + j, dests[j]) for j in range(4)]
    for first, second in zip(far, near):
        first.start()
        second.start()
    greet((sib, xn, yn))
    weights.wait()

    def product(i, put):
        left = a_buf[i].reshape(2 * rows, a_buf.shape[-1])

        @pl.loop(0, d // tile)
        def _(n):
            cut = pl.ds(pl.multiple_of(n * tile, tile), tile)
            right = w_buf[cut, :] if flip else w_buf[:, cut]
            dims = (((1,), (1,)), ((), ())) if flip else (((1,), (0,)), ((), ()))
            value = lax.dot_general(left, right, dims, preferred_element_type=wide)
            put(cut, value.reshape(2, rows, tile))

    sides = [push(j, stage.at[j], sibs.at[j], sib) for j in range(4)]

    def for_sibling(j):
        far[j].wait()

        def put(cut, value):
            stage[j, :, :, cut] = value.astype(stage.dtype)

        product(j, put)
        sides[j].start()

    def for_chip(j):
        near[j].wait()
        sides[j].wait_recv()

        def put(cut, value):
            own[j, :, :, cut] = (value + sibs[j, :, :, cut].astype(wide)).astype(own.dtype)

        product(4 + j, put)

    def add(dst, src):
        @pl.loop(0, rows // tall)
        def _(i):
            r = pl.ds(pl.multiple_of(i * tall, tall), tall)
            dst[r, :] = (dst[r, :].astype(wide) + src[r, :].astype(wide)).astype(dst.dtype)

    for_sibling(0)
    for_sibling(1)
    for_chip(0)
    a = push(4, own.at[0, 0], dx, xn)
    b = push(5, own.at[0, 1], dy, yn)
    a.start()
    b.start()
    for_sibling(2)
    for_chip(1)
    x0 = push(6, own.at[1, 0], rx.at[0], xn)
    x0.start()
    for_sibling(3)
    for_chip(2)
    y1 = push(7, own.at[2, 1], ry.at[1], yn)
    y1.start()
    a.wait_recv()
    add(own.at[2, 0], dx)
    y0 = push(8, own.at[2, 0], ry.at[0], yn)
    y0.start()
    b.wait_recv()
    add(own.at[1, 1], dy)
    x1 = push(9, own.at[1, 1], rx.at[1], xn)
    x1.start()
    near[3].wait()
    sides[3].wait_recv()

    def put(cut, value):
        o_ref[:, :, cut] = value + sibs[3, :, :, cut].astype(wide)

    product(7, put)
    for h, waits in enumerate(((x0, y0), (x1, y1))):
        for copy in waits:
            copy.wait_recv()

        @pl.loop(0, rows // tall)
        def _(i):
            r = pl.ds(pl.multiple_of(i * tall, tall), tall)
            o_ref[h, r, :] = o_ref[h, r, :] + rx[h, r, :].astype(wide) + ry[h, r, :].astype(wide)

    for copy in (*sides, a, b, x0, y1, y0, x1):
        copy.wait_send()


def product_sum(left, right, flip, cid):
    h, total, depth = left.shape
    rows = total // 8
    d = right.shape[0] if flip else right.shape[1]
    low = left.dtype
    return pl.pallas_call(
        functools.partial(product_kernel, rows, flip),
        out_shape=jax.ShapeDtypeStruct((h, rows, d), jnp.float32),
        in_specs=[pl.BlockSpec(memory_space=pl.ANY)] * 2,
        out_specs=pl.BlockSpec(memory_space=pltpu.VMEM),
        scratch_shapes=[
            pltpu.VMEM((8, h, rows, depth), low),
            pltpu.VMEM(right.shape, low),
            pltpu.VMEM((4, h, rows, d), low),
            pltpu.VMEM((3, h, rows, d), low),
            pltpu.VMEM((4, h, rows, d), low),
            pltpu.VMEM((rows, d), low),
            pltpu.VMEM((rows, d), low),
            pltpu.VMEM((h, rows, d), low),
            pltpu.VMEM((h, rows, d), low),
            pltpu.SemaphoreType.DMA((9,)),
            pltpu.SemaphoreType.DMA((10,)),
            pltpu.SemaphoreType.DMA((10,)),
        ],
        compiler_params=pltpu.CompilerParams(
            collective_id=cid, has_side_effects=True, vmem_limit_bytes=44 << 20
        ),
        cost_estimate=pl.CostEstimate(
            flops=2 * h * total * depth * d, bytes_accessed=130_000_000, transcendentals=0
        ),
        name="product_sum",
    )(left, right)


def fold_small_kernel(
    rows, p_ref, g_ref, o_ref, k_ref, own, sibs, dx, dy, rx, ry, local_sem, send, recv,
    gown, gsibs, grx, glocal, gsend, grecv,
):
    c, sib, xn, yn = partners()
    m = c % 4
    m_sib = m + 1 - 2 * (m % 2)
    m_x = m + 2 - 4 * (m // 2)
    m_diag = m_sib + (m_x - m)
    wide = jnp.float32

    def push(i, src, dst, dev):
        return pltpu.make_async_remote_copy(
            src_ref=src,
            dst_ref=dst,
            send_sem=gsend.at[i],
            recv_sem=grecv.at[i],
            device_id={"col": dev},
            device_id_type=MESH,
        )

    steps = fold_steps(rows, p_ref, own, sibs, dx, dy, rx, ry, local_sem, send, recv)
    next(steps)
    loads = [
        pltpu.make_async_copy(g_ref.at[d], gown.at[j], glocal.at[j])
        for j, d in enumerate((m_x, m))
    ]
    for load in loads:
        load.start()
    greet((sib, xn, yn))
    sides = [push(j, g_ref.at[d], gsibs.at[j], sib) for j, d in enumerate((m_diag, m_sib))]
    sides[0].start()
    next(steps)
    sides[1].start()
    tall = k_ref.shape[0] // 4
    loads[0].wait()
    sides[0].wait_recv()

    @pl.loop(0, 4)
    def _(i):
        r = pl.ds(pl.multiple_of(i * tall, tall), tall)
        gown[0, r, :] = (gown[0, r, :].astype(wide) + gsibs[0, r, :].astype(wide)).astype(
            gown.dtype
        )

    over = push(2, gown.at[0], grx, xn)
    over.start()
    last = None
    for step in steps:
        last = step if step is not None else last
    fold_finish(rows, o_ref, own, rx, ry, *last)
    loads[1].wait()
    sides[1].wait_recv()
    over.wait_recv()

    @pl.loop(0, 4)
    def _(i):
        r = pl.ds(pl.multiple_of(i * tall, tall), tall)
        k_ref[r, :] = (
            gown[1, r, :].astype(wide) + gsibs[1, r, :].astype(wide) + grx[r, :].astype(wide)
        )

    for copy in (*sides, over):
        copy.wait_send()


def fold_small(p, g, cid):
    h, total, d = p.shape
    rows = total // 8
    share, tall, _ = g.shape
    return pl.pallas_call(
        functools.partial(fold_small_kernel, rows),
        out_shape=(
            jax.ShapeDtypeStruct((h, rows, d), jnp.float32),
            jax.ShapeDtypeStruct((tall, d), jnp.float32),
        ),
        in_specs=[pl.BlockSpec(memory_space=pl.ANY)] * 2,
        out_specs=[pl.BlockSpec(memory_space=pltpu.VMEM)] * 2,
        scratch_shapes=fold_scratch(h, rows, d, p.dtype)
        + [
            pltpu.VMEM((2, tall, d), g.dtype),
            pltpu.VMEM((2, tall, d), g.dtype),
            pltpu.VMEM((tall, d), g.dtype),
            pltpu.SemaphoreType.DMA((2,)),
            pltpu.SemaphoreType.DMA((3,)),
            pltpu.SemaphoreType.DMA((3,)),
        ],
        compiler_params=pltpu.CompilerParams(
            collective_id=cid, has_side_effects=True, vmem_limit_bytes=40 << 20
        ),
        cost_estimate=pl.CostEstimate(flops=0, bytes_accessed=60_000_000, transcendentals=0),
        name="fold_small",
    )(p, g)


def open_kernel(
    rows, near, x_ref, s_ref, q_ref, w_ref, o_ref, sa_ref, qa_ref, wa_ref, local_sem, send, recv
):
    c, sib, xn, yn = partners()
    diag = yn + (xn - c)
    r = lax.axis_index("row")
    tiers = lax.axis_size("row")

    def slot(half, who):
        return o_ref.at[half, pl.ds(pl.multiple_of(who * rows, rows), rows), :]

    def both(who):
        return o_ref.at[:, pl.ds(pl.multiple_of(who * rows, rows), rows), :]

    def kv(who):
        return sa_ref.at[who, :, pl.ds(0, near), :]

    def rest(who):
        return sa_ref.at[who, :, pl.ds(near, s_ref.shape[0] - near), :]

    started = []

    def push(src, dst, **dev):
        i = len(started)
        copy = pltpu.make_async_remote_copy(
            src_ref=src,
            dst_ref=dst,
            send_sem=send.at[i],
            recv_sem=recv.at[i],
            device_id=dev,
            device_id_type=MESH,
        )
        copy.start()
        started.append(copy)
        return copy

    local = [
        pltpu.make_async_copy(s_ref, sa_ref.at[c, r], local_sem.at[0]),
        pltpu.make_async_copy(x_ref, both(c), local_sem.at[1]),
        pltpu.make_async_copy(q_ref, qa_ref.at[r], local_sem.at[2]),
        pltpu.make_async_copy(w_ref, wa_ref.at[r], local_sem.at[3]),
    ]
    for copy in local:
        copy.start()
    others = [lax.rem(r + k, tiers) for k in range(1, tiers)]
    barrier = pltpu.get_barrier_semaphore()
    for d in (sib, xn, yn):
        pl.semaphore_signal(barrier, inc=1, device_id={"col": d}, device_id_type=MESH)
    for d in others:
        pl.semaphore_signal(barrier, inc=1, device_id={"row": d}, device_id_type=MESH)
    pl.semaphore_wait(barrier, 3 + len(others))
    small = [push(s_ref, sa_ref.at[c, r], row=d) for d in others]
    x0 = push(x_ref.at[0], slot(0, c), col=xn)
    y1 = push(x_ref.at[1], slot(1, c), col=yn)
    x1 = push(x_ref.at[1], slot(1, c), col=xn)
    y0 = push(x_ref.at[0], slot(0, c), col=yn)
    push(x_ref, both(c), col=sib)
    for d in others:
        push(q_ref, qa_ref.at[r], row=d)
    for d in others:
        push(w_ref, wa_ref.at[r], row=d)
    waited = [x0, y1, x1, y0, *small]
    x0.wait_recv()
    fy = push(slot(0, xn), slot(0, xn), col=yn)
    push(slot(0, xn), slot(0, xn), col=sib)
    y1.wait_recv()
    fx = push(slot(1, yn), slot(1, yn), col=xn)
    push(slot(1, yn), slot(1, yn), col=sib)
    local[0].wait()
    for copy in small:
        copy.wait_recv()
    kx = push(kv(c), kv(c), col=xn)
    rx = push(rest(c), rest(c), col=xn)
    ry = push(rest(c), rest(c), col=yn)
    push(kv(c), kv(c), col=sib)
    push(rest(c), rest(c), col=sib)
    x1.wait_recv()
    push(slot(1, xn), slot(1, xn), col=sib)
    y0.wait_recv()
    push(slot(0, yn), slot(0, yn), col=sib)
    fy.wait_recv()
    push(slot(0, diag), slot(0, diag), col=sib)
    fx.wait_recv()
    push(slot(1, diag), slot(1, diag), col=sib)
    kx.wait_recv()
    push(kv(xn), kv(xn), col=sib)
    rx.wait_recv()
    fd = push(rest(xn), rest(xn), col=yn)
    push(rest(xn), rest(xn), col=sib)
    ry.wait_recv()
    push(rest(yn), rest(yn), col=sib)
    fd.wait_recv()
    push(rest(diag), rest(diag), col=sib)
    waited += [fy, fx, kx, rx, ry, fd]
    for copy in started:
        if not any(copy is other for other in waited):
            copy.wait_recv()
    for copy in started:
        copy.wait_send()
    for copy in local[1:]:
        copy.wait()


def open_all(x, small, near, query, output, tiers, cid):
    h, rows, d = x.shape
    low = x.dtype
    copies = 13 + 3 * (tiers - 1) + 10
    return pl.pallas_call(
        functools.partial(open_kernel, rows, near),
        out_shape=(
            jax.ShapeDtypeStruct((h, 8 * rows, d), low),
            jax.ShapeDtypeStruct((8, tiers, *small.shape), low),
            jax.ShapeDtypeStruct((tiers, *query.shape), low),
            jax.ShapeDtypeStruct((tiers, *output.shape), low),
        ),
        in_specs=[pl.BlockSpec(memory_space=pl.ANY)] * 4,
        out_specs=[pl.BlockSpec(memory_space=pl.ANY)] * 4,
        scratch_shapes=[
            pltpu.SemaphoreType.DMA((4,)),
            pltpu.SemaphoreType.DMA((copies,)),
            pltpu.SemaphoreType.DMA((copies,)),
        ],
        compiler_params=pltpu.CompilerParams(collective_id=cid, has_side_effects=True),
        cost_estimate=pl.CostEstimate(flops=0, bytes_accessed=200_000_000, transcendentals=0),
        name="open_all",
    )(x, small, query, output)


def total_kernel(x_ref, o_ref, sums, got, tier_sums, send, recv):
    c, sib, xn, yn = partners()
    r = lax.axis_index("row")
    tiers = lax.axis_size("row")
    others = [lax.rem(r + k, tiers) for k in range(1, tiers)]
    barrier = pltpu.get_barrier_semaphore()
    for d in (sib, xn, yn):
        pl.semaphore_signal(barrier, inc=1, device_id={"col": d}, device_id_type=MESH)
    for d in others:
        pl.semaphore_signal(barrier, inc=1, device_id={"row": d}, device_id_type=MESH)
    pl.semaphore_wait(barrier, 3 + len(others))
    sums[0] = x_ref[...]
    for i, dev in enumerate((sib, xn, yn)):
        copy = pltpu.make_async_remote_copy(
            src_ref=sums.at[i],
            dst_ref=got.at[i],
            send_sem=send.at[i],
            recv_sem=recv.at[i],
            device_id={"col": dev},
            device_id_type=MESH,
        )
        copy.start()
        copy.wait()
        sums[i + 1] = sums[i] + got[i]
    tier_sums[r] = sums[3]
    copies = []
    for k, d in enumerate(others):
        copy = pltpu.make_async_remote_copy(
            src_ref=sums.at[3],
            dst_ref=tier_sums.at[r],
            send_sem=send.at[3 + k],
            recv_sem=recv.at[3 + k],
            device_id={"row": d},
            device_id_type=MESH,
        )
        copy.start()
        copies.append(copy)
    for copy in copies:
        copy.wait()
    result = tier_sums[0]
    for k in range(1, tiers):
        result = result + tier_sums[k]
    o_ref[...] = result


def total(x, tiers, cid):
    return pl.pallas_call(
        total_kernel,
        out_shape=jax.ShapeDtypeStruct(x.shape, x.dtype),
        in_specs=[pl.BlockSpec(memory_space=pltpu.VMEM)],
        out_specs=pl.BlockSpec(memory_space=pltpu.VMEM),
        scratch_shapes=[
            pltpu.VMEM((4, *x.shape), x.dtype),
            pltpu.VMEM((3, *x.shape), x.dtype),
            pltpu.VMEM((tiers, *x.shape), x.dtype),
            pltpu.SemaphoreType.DMA((2 + tiers,)),
            pltpu.SemaphoreType.DMA((2 + tiers,)),
        ],
        compiler_params=pltpu.CompilerParams(collective_id=cid, has_side_effects=True),
        cost_estimate=pl.CostEstimate(flops=0, bytes_accessed=40_000_000, transcendentals=0),
        name="total",
    )(x)


def after(value, *earlier):
    return lax.optimization_barrier((value, *earlier))[0]


def general_body(
    hidden,
    per_layer,
    lengths,
    block_ids,
    out_grad,
    query_weight,
    key_weight,
    value_weight,
    output_weight,
    gate_weight,
    up_weight,
    down_weight,
    laurel_left,
    laurel_right,
    layer_gate,
    layer_proj,
    norm_gains,
    head_gains,
):
    local_rows = hidden.shape[0]
    seq_groups = hidden.shape[1]
    col_index = lax.axis_index("col")
    row_index = lax.axis_index("row")
    all_lengths = lengths
    lengths = lax.dynamic_slice_in_dim(all_lengths, row_index * seq_groups, seq_groups, 0)
    (
        query_cols,
        key_cols,
        value_cols,
        output_rows,
        gate_cols,
        up_cols,
        down_rows,
        left_cols,
        right_rows,
        gate_layer_cols,
        proj_layer_rows,
    ) = (
        lax.all_gather(query_weight, "row", axis=0, tiled=True),
        lax.all_gather(key_weight, "row", axis=0, tiled=True),
        lax.all_gather(value_weight, "row", axis=0, tiled=True),
        lax.all_gather(output_weight, "row", axis=1, tiled=True),
        lax.all_gather(gate_weight, "row", axis=0, tiled=True),
        lax.all_gather(up_weight, "row", axis=0, tiled=True),
        lax.all_gather(down_weight, "row", axis=1, tiled=True),
        lax.all_gather(laurel_left, "row", axis=0, tiled=True),
        lax.all_gather(laurel_right, "row", axis=1, tiled=True),
        lax.all_gather(layer_gate, "row", axis=0, tiled=True),
        lax.all_gather(layer_proj, "row", axis=1, tiled=True),
    )
    (
        query_full,
        key_full,
        value_full,
        output_full,
        left_full,
        right_full,
        gate_layer_full,
        proj_layer_full,
    ) = (
        lax.all_gather(query_cols, "col", axis=1, tiled=True),
        lax.all_gather(key_cols, "col", axis=1, tiled=True),
        lax.all_gather(value_cols, "col", axis=1, tiled=True),
        lax.all_gather(output_rows, "col", axis=0, tiled=True),
        lax.all_gather(left_cols, "col", axis=1, tiled=True),
        lax.all_gather(right_rows, "col", axis=0, tiled=True),
        lax.all_gather(gate_layer_cols, "col", axis=1, tiled=True),
        lax.all_gather(proj_layer_rows, "col", axis=0, tiled=True),
    )
    paired = jnp.concatenate([gate_cols, up_cols], axis=1)
    unit_width = gate_cols.shape[1]
    first_position = col_index * local_rows
    positions = first_position + jnp.arange(local_rows, dtype=jnp.int32)
    live_mask = positions[:, None] < lengths[None, :]
    keep_mask = live_mask.astype(jnp.float32)[:, :, None]
    reach_back = (WINDOW + local_rows - 2) // local_rows
    reach_ahead = (BLOCK + local_rows - 2) // local_rows
    key_span = (reach_back + 1 + reach_ahead) * local_rows
    key_position = first_position - reach_back * local_rows + jnp.arange(key_span, dtype=jnp.int32)
    filler_low = jnp.full((seq_groups, reach_back * local_rows), FAR_BLOCK, jnp.int32)
    filler_high = jnp.full((seq_groups, reach_ahead * local_rows), FAR_BLOCK, jnp.int32)
    padded_blocks = jnp.concatenate([filler_low, block_ids, filler_high], axis=1)
    key_blocks = lax.dynamic_slice_in_dim(padded_blocks, first_position, key_span, 1)
    query_blocks = lax.dynamic_slice_in_dim(block_ids, first_position, local_rows, 1)
    key_live = (key_position[None, :] >= 0) & (key_position[None, :] < lengths[:, None])
    query_live = positions[None, :] < lengths[:, None]
    distance = positions[:, None] - key_position[None, :]
    nearby = (query_blocks[:, :, None] >= key_blocks[:, None, :]) & (distance < WINDOW)[None]
    nearby = nearby & query_live[:, :, None] & key_live[:, None, :]
    visible = (nearby | (distance == 0)[None])[:, None, None]
    residual = hidden.astype(jnp.float32)
    normed_value, input_back = jax.vjp(input_norm, residual, norm_gains)
    normed_low = normed_value.astype(jnp.bfloat16)
    half_width = HD // 2
    frequency = jnp.exp(jnp.arange(half_width, dtype=jnp.float32) * (-2.0 * math.log(10000.0) / HD))
    angles = (positions.astype(jnp.float32)[:, None] * frequency[None, :])[:, None, None, :]

    def prepare(query_in, key_in, value_in, gain_rows):
        return (
            rotate(root_norm(query_in, gain_rows[0]), angles),
            rotate(root_norm(key_in, gain_rows[1]), angles),
            plain_norm(value_in),
        )

    query_raw = matmul_last(normed_low, query_full).reshape(local_rows, seq_groups, H, HD)
    key_raw = matmul_last(normed_low, key_full).reshape(local_rows, seq_groups, KV, HD)
    value_raw = matmul_last(normed_low, value_full).reshape(local_rows, seq_groups, KV, HD)
    (query_value, key_value, value_value), head_back = jax.vjp(
        prepare, query_raw, key_raw, value_raw, head_gains
    )
    query_low = query_value.astype(jnp.bfloat16).reshape(local_rows, seq_groups, KV, H // KV, HD)
    key_low = key_value.astype(jnp.bfloat16)
    value_low = value_value.astype(jnp.bfloat16)
    offsets = list(range(reach_back, -reach_ahead - 1, -1))
    key_parts = []
    value_parts = []
    for offset in offsets:
        if offset == 0:
            key_parts.append(key_low)
            value_parts.append(value_low)
        else:
            moved_key, moved_value = passed_along((key_low, value_low), "col", offset)
            key_parts.append(moved_key)
            value_parts.append(moved_value)
    near_keys = jnp.concatenate(key_parts, axis=0)
    near_values = jnp.concatenate(value_parts, axis=0)
    score_scale = HD ** (-0.5)

    def score_all():
        raw_scores = (
            jnp.einsum(
                "psjgd,esjd->sjgpe", query_low, near_keys, preferred_element_type=jnp.float32
            )
            * score_scale
        )
        return jnp.where(visible, raw_scores, NEGATIVE)

    scores = score_all()
    row_max = jnp.max(scores, axis=-1, keepdims=True)
    exponent = jnp.exp(scores - row_max)
    row_total = jnp.sum(exponent, axis=-1, keepdims=True)
    attn_prob = exponent / row_total
    log_total = row_max + jnp.log(row_total)
    mixed_heads = jnp.einsum(
        "sjgpe,esjd->psjgd",
        attn_prob.astype(jnp.bfloat16),
        near_values,
        preferred_element_type=jnp.float32,
    )
    mixed_low = mixed_heads.reshape(local_rows, seq_groups, H * HD).astype(jnp.bfloat16)
    out_proj = matmul_last(mixed_low, output_full)
    laurel_mid = matmul_last(normed_low, left_full).astype(jnp.bfloat16)
    low_rank = matmul_last(laurel_mid, right_full)
    (after_attention, feed_normed), middle_back = jax.vjp(
        middle, residual, out_proj, low_rank, normed_low.astype(jnp.float32), norm_gains
    )
    feed_low = feed_normed.astype(jnp.bfloat16)
    gate_up = matmul_last(lax.all_gather(feed_low, "col", axis=0, tiled=True), paired)
    unit_value, gate_back = jax.vjp(
        gated_product, gate_up[..., :unit_width], gate_up[..., unit_width:]
    )
    units_low = unit_value.astype(jnp.bfloat16)
    summed = lax.psum_scatter(
        matmul_last(units_low, down_rows), "col", scatter_dimension=0, tiled=True
    )
    after_feed, feed_back = jax.vjp(feed_join, after_attention, summed, norm_gains)
    feed_round = after_feed.astype(jnp.bfloat16)
    layer_pre = matmul_last(feed_round, gate_layer_full)
    layer_input = per_layer.astype(jnp.float32)
    layer_value, layer_back = jax.vjp(gated_product, layer_pre, layer_input)
    layer_low = layer_value.astype(jnp.bfloat16)
    projected = matmul_last(layer_low, proj_layer_full)
    out_value, final_back = jax.vjp(final_join, after_feed, projected, norm_gains)
    square_sums = jnp.stack(
        [
            jnp.sum(keep_mask * residual * residual),
            jnp.sum(keep_mask * after_attention * after_attention),
            jnp.sum(keep_mask * after_feed * after_feed),
            jnp.sum(keep_mask * out_value * out_value),
        ]
    )
    valid_count = jnp.sum(all_lengths).astype(jnp.float32)
    cotangent = out_grad.astype(jnp.float32) * keep_mask
    grad_feed_out, grad_projected, gains_final = final_back(cotangent)
    projected_low = grad_projected.astype(jnp.bfloat16)
    grad_proj_layer = outer_sum(layer_low, projected_low)
    grad_layer_pre, grad_layer_input = layer_back(matmul_back(projected_low, proj_layer_full))
    layer_pre_low = grad_layer_pre.astype(jnp.bfloat16)
    grad_gate_layer = outer_sum(feed_round, layer_pre_low)
    grad_after_feed = grad_feed_out + matmul_back(layer_pre_low, gate_layer_full)
    grad_after_attention_a, grad_summed, gains_feed = feed_back(grad_after_feed)
    summed_low = grad_summed.astype(jnp.bfloat16)
    block_rows = lax.all_gather(summed_low, "col", axis=0, tiled=True)
    grad_down = outer_sum(units_low, block_rows)
    grad_units = matmul_back(block_rows, down_rows)
    grad_down, grad_units = (grad_down, grad_units)
    grad_gate_value, grad_up_value = gate_back(grad_units)
    grad_paired = jnp.concatenate([grad_gate_value, grad_up_value], axis=-1).astype(jnp.bfloat16)
    grad_weights_paired = outer_sum(
        lax.all_gather(feed_low, "col", axis=0, tiled=True), grad_paired
    )
    grad_feed = lax.psum_scatter(
        matmul_back(grad_paired, paired).astype(jnp.bfloat16),
        "col",
        scatter_dimension=0,
        tiled=True,
    ).astype(jnp.float32)
    grad_residual_mid, grad_out_proj, grad_low_rank, grad_normed_mid, gains_middle = middle_back(
        (grad_after_attention_a, grad_feed)
    )
    out_proj_low = grad_out_proj.astype(jnp.bfloat16)
    grad_output = outer_sum(mixed_low, out_proj_low)
    grad_mixed = matmul_back(out_proj_low, output_full).astype(jnp.bfloat16)
    grad_mixed = grad_mixed.reshape(local_rows, seq_groups, KV, H // KV, HD)
    low_rank_grad = grad_low_rank.astype(jnp.bfloat16)
    grad_right = outer_sum(laurel_mid, low_rank_grad)
    grad_laurel_mid = matmul_back(low_rank_grad, right_full).astype(jnp.bfloat16)
    grad_left = outer_sum(normed_low, grad_laurel_mid)
    scores = score_all()
    attn_prob = jnp.exp(scores - log_total)
    grad_prob = jnp.einsum(
        "psjgd,esjd->sjgpe", grad_mixed, near_values, preferred_element_type=jnp.float32
    )
    grad_scores = (
        attn_prob * (grad_prob - jnp.sum(attn_prob * grad_prob, axis=-1, keepdims=True))
    ).astype(jnp.bfloat16)
    grad_queries = (
        jnp.einsum("sjgpe,esjd->psjgd", grad_scores, near_keys, preferred_element_type=jnp.float32)
        * score_scale
    )
    grad_near_keys = (
        jnp.einsum("sjgpe,psjgd->esjd", grad_scores, query_low, preferred_element_type=jnp.float32)
        * score_scale
    )
    grad_near_values = jnp.einsum(
        "sjgpe,psjgd->esjd",
        attn_prob.astype(jnp.bfloat16),
        grad_mixed,
        preferred_element_type=jnp.float32,
    )
    grad_key_total = grad_near_keys[reach_back * local_rows : (reach_back + 1) * local_rows]
    grad_value_total = grad_near_values[reach_back * local_rows : (reach_back + 1) * local_rows]
    for slot_index, offset in enumerate(offsets):
        if offset != 0:
            piece_keys = grad_near_keys[slot_index * local_rows : (slot_index + 1) * local_rows]
            piece_values = grad_near_values[slot_index * local_rows : (slot_index + 1) * local_rows]
            back_keys, back_values = (
                passed_along(piece_keys.astype(jnp.bfloat16), "col", -offset).astype(
                    piece_keys.dtype
                ),
                passed_along(piece_values.astype(jnp.bfloat16), "col", -offset).astype(
                    piece_values.dtype
                ),
            )
            grad_key_total = grad_key_total + back_keys
            grad_value_total = grad_value_total + back_values
    grad_query_raw, grad_key_raw, grad_value_raw, grad_heads = head_back(
        (grad_queries.reshape(local_rows, seq_groups, H, HD), grad_key_total, grad_value_total)
    )
    query_grad_low = grad_query_raw.reshape(local_rows, seq_groups, H * HD).astype(jnp.bfloat16)
    key_grad_low = grad_key_raw.reshape(local_rows, seq_groups, KV * HD).astype(jnp.bfloat16)
    value_grad_low = grad_value_raw.reshape(local_rows, seq_groups, KV * HD).astype(jnp.bfloat16)
    grad_query = outer_sum(normed_low, query_grad_low)
    grad_key = outer_sum(normed_low, key_grad_low)
    grad_value = outer_sum(normed_low, value_grad_low)
    grad_normed = (
        grad_normed_mid
        + matmul_back(grad_laurel_mid, left_full)
        + matmul_back(query_grad_low, query_full)
        + matmul_back(key_grad_low, key_full)
        + matmul_back(value_grad_low, value_full)
    )
    grad_residual_in, gains_input = input_back(grad_normed)
    d_hidden = (grad_residual_mid + grad_residual_in).astype(jnp.bfloat16)
    d_per_layer = grad_layer_input.astype(jnp.bfloat16)
    grad_gains = gains_final + gains_feed + gains_middle + gains_input
    grad_gate = grad_weights_paired[:, :unit_width]
    grad_up = grad_weights_paired[:, unit_width:]
    (
        query_part,
        key_part,
        value_part,
        output_part,
        left_part,
        right_part,
        gate_layer_part,
        proj_layer_part,
    ) = (
        lax.psum_scatter(
            grad_query.astype(jnp.bfloat16), "col", scatter_dimension=1, tiled=True
        ).astype(jnp.float32),
        lax.psum_scatter(
            grad_key.astype(jnp.bfloat16), "col", scatter_dimension=1, tiled=True
        ).astype(jnp.float32),
        lax.psum_scatter(
            grad_value.astype(jnp.bfloat16), "col", scatter_dimension=1, tiled=True
        ).astype(jnp.float32),
        lax.psum_scatter(
            grad_output.astype(jnp.bfloat16), "col", scatter_dimension=0, tiled=True
        ).astype(jnp.float32),
        lax.psum_scatter(
            grad_left.astype(jnp.bfloat16), "col", scatter_dimension=1, tiled=True
        ).astype(jnp.float32),
        lax.psum_scatter(
            grad_right.astype(jnp.bfloat16), "col", scatter_dimension=0, tiled=True
        ).astype(jnp.float32),
        lax.psum_scatter(
            grad_gate_layer.astype(jnp.bfloat16), "col", scatter_dimension=1, tiled=True
        ).astype(jnp.float32),
        lax.psum_scatter(
            grad_proj_layer.astype(jnp.bfloat16), "col", scatter_dimension=0, tiled=True
        ).astype(jnp.float32),
    )
    (
        d_query_weight,
        d_key_weight,
        d_value_weight,
        d_output_weight,
        d_gate_weight,
        d_up_weight,
        d_down_weight,
        d_laurel_left,
        d_laurel_right,
        d_layer_gate,
        d_layer_proj,
    ) = (
        lax.psum_scatter(
            query_part.astype(jnp.bfloat16), "row", scatter_dimension=0, tiled=True
        ).astype(jnp.float32),
        lax.psum_scatter(
            key_part.astype(jnp.bfloat16), "row", scatter_dimension=0, tiled=True
        ).astype(jnp.float32),
        lax.psum_scatter(
            value_part.astype(jnp.bfloat16), "row", scatter_dimension=0, tiled=True
        ).astype(jnp.float32),
        lax.psum_scatter(
            output_part.astype(jnp.bfloat16), "row", scatter_dimension=1, tiled=True
        ).astype(jnp.float32),
        lax.psum_scatter(
            grad_gate.astype(jnp.bfloat16), "row", scatter_dimension=0, tiled=True
        ).astype(jnp.float32),
        lax.psum_scatter(
            grad_up.astype(jnp.bfloat16), "row", scatter_dimension=0, tiled=True
        ).astype(jnp.float32),
        lax.psum_scatter(
            grad_down.astype(jnp.bfloat16), "row", scatter_dimension=1, tiled=True
        ).astype(jnp.float32),
        lax.psum_scatter(
            left_part.astype(jnp.bfloat16), "row", scatter_dimension=0, tiled=True
        ).astype(jnp.float32),
        lax.psum_scatter(
            right_part.astype(jnp.bfloat16), "row", scatter_dimension=1, tiled=True
        ).astype(jnp.float32),
        lax.psum_scatter(
            gate_layer_part.astype(jnp.bfloat16), "row", scatter_dimension=0, tiled=True
        ).astype(jnp.float32),
        lax.psum_scatter(
            proj_layer_part.astype(jnp.bfloat16), "row", scatter_dimension=1, tiled=True
        ).astype(jnp.float32),
    )
    d_norm_gains, d_head_gains, total_squares = lax.psum(
        (grad_gains, grad_heads, square_sums), ("row", "col")
    )
    stats = jnp.sqrt(total_squares / (valid_count * D))
    output = out_value.astype(jnp.bfloat16)
    return (
        output,
        stats,
        d_hidden,
        d_per_layer,
        d_query_weight,
        d_key_weight,
        d_value_weight,
        d_output_weight,
        d_gate_weight,
        d_up_weight,
        d_down_weight,
        d_laurel_left,
        d_laurel_right,
        d_layer_gate,
        d_layer_proj,
        d_norm_gains,
        d_head_gains,
    )


def swap(array):
    return jnp.swapaxes(array, 0, 1)


def heads_body(
    hidden,
    per_layer,
    lengths,
    block_ids,
    out_grad,
    query_weight,
    key_weight,
    value_weight,
    output_weight,
    gate_weight,
    up_weight,
    down_weight,
    laurel_left,
    laurel_right,
    layer_gate,
    layer_proj,
    norm_gains,
    head_gains,
):
    low = jnp.bfloat16
    rows = hidden.shape[0]
    groups = hidden.shape[1]
    cols = lax.axis_size("col")
    seq = rows * cols
    share = cols // KV
    col_index = lax.axis_index("col")
    row_index = lax.axis_index("row")
    all_lengths = lengths
    lengths = lax.dynamic_slice_in_dim(all_lengths, row_index * groups, groups, 0)

    small = jnp.concatenate(
        [key_weight.T, value_weight.T, laurel_left.T, layer_gate.T, laurel_right, layer_proj],
        axis=0,
    )
    heights = [key_weight.shape[1], value_weight.shape[1], laurel_left.shape[1]]
    heights += [layer_gate.shape[1], laurel_right.shape[0], layer_proj.shape[0]]
    edges = [sum(heights[:i]) for i in range(len(heights) + 1)]
    unit_width = gate_weight.shape[1]
    residual = swap(hidden).astype(jnp.float32)
    normed_value, input_back = jax.vjp(input_norm, residual, norm_gains)
    normed_low = normed_value.astype(low)
    tiers = lax.axis_size("row")
    normed_all, small_all, query_full, output_full = open_all(
        normed_low, small, heights[0] + heights[1], query_weight, output_weight, tiers, 1
    )
    both_weights = jnp.concatenate([gate_weight, up_weight], axis=1)
    paired = lax.all_gather(after(both_weights, normed_all), "row", axis=0, tiled=True)
    down_full = lax.all_gather(after(down_weight, normed_all), "row", axis=1, tiled=True)
    query_full = query_full.reshape(D, HD).T
    output_full = jnp.swapaxes(output_full, 0, 1).reshape(HD, D)
    pieces = [small_all[:, :, a:b] for a, b in zip(edges[:-1], edges[1:])]
    group_start = (col_index // share) * share

    def joined(piece):
        return jnp.swapaxes(piece, 1, 2).reshape(-1, D)

    key_full, value_full = (
        joined(lax.dynamic_slice_in_dim(piece, group_start, share, 0)) for piece in pieces[:2]
    )
    left_full, gate_layer_full, right_full, proj_layer_full = (
        joined(piece) for piece in pieces[2:]
    )
    head_weights = jnp.concatenate([query_full, key_full, value_full], axis=0)

    positions = jnp.arange(seq, dtype=jnp.int32)
    mine = col_index * rows + jnp.arange(rows, dtype=jnp.int32)
    keep_mask = (mine[None, :] < lengths[:, None]).astype(jnp.float32)[:, :, None]
    live = positions[None, :] < lengths[:, None]
    distance = positions[:, None] - positions[None, :]
    nearby = (block_ids[:, :, None] >= block_ids[:, None, :]) & (distance < WINDOW)[None]
    nearby = nearby & live[:, :, None] & live[:, None, :]
    visible = nearby | (distance == 0)[None]

    half_width = HD // 2
    frequency = jnp.exp(jnp.arange(half_width, dtype=jnp.float32) * (-2.0 * math.log(10000.0) / HD))
    angles = (positions.astype(jnp.float32)[:, None] * frequency[None, :])[None]

    def prepare(query_in, key_in, value_in, gain_rows):
        return (
            rotate(root_norm(query_in, gain_rows[0]), angles),
            rotate(root_norm(key_in, gain_rows[1]), angles),
            plain_norm(value_in),
        )

    head_raw = matmul_back(normed_all, head_weights)
    query_raw, key_raw, value_raw = jnp.split(head_raw, 3, axis=-1)
    (query_value, key_value, value_value), head_back = jax.vjp(
        prepare, query_raw, key_raw, value_raw, head_gains
    )
    query_low = query_value.astype(low)
    key_low = key_value.astype(low)
    value_low = value_value.astype(low)
    score_scale = HD ** (-0.5)

    def score_all():
        raw_scores = (
            jnp.einsum("spd,sed->spe", query_low, key_low, preferred_element_type=jnp.float32)
            * score_scale
        )
        return jnp.where(visible, raw_scores, NEGATIVE)

    scores = score_all()
    row_max = jnp.max(scores, axis=-1, keepdims=True)
    exponent = jnp.exp(scores - row_max)
    row_total = jnp.sum(exponent, axis=-1, keepdims=True)
    attn_prob = exponent / row_total
    log_total = row_max + jnp.log(row_total)
    mixed_low = jnp.einsum(
        "spe,sed->spd", attn_prob.astype(low), value_low, preferred_element_type=jnp.float32
    ).astype(low)
    out_proj = product_sum(mixed_low, output_full, False, 2)
    laurel_mid = matmul_back(normed_low, left_full).astype(low)
    low_rank = matmul_last(laurel_mid, right_full)
    (after_attention, feed_normed), middle_back = jax.vjp(
        middle, residual, out_proj, low_rank, normed_low.astype(jnp.float32), norm_gains
    )
    feed_all = spread(feed_normed.astype(low), 0)
    gate_value = matmul_last(feed_all, paired[:, :unit_width])
    up_value = matmul_last(feed_all, paired[:, unit_width:])
    unit_value, gate_back = jax.vjp(gated_product, gate_value, up_value)
    units_low = unit_value.astype(low)
    summed = product_sum(units_low, down_full, False, 5)
    after_feed, feed_back = jax.vjp(feed_join, after_attention, summed, norm_gains)
    feed_round = after_feed.astype(low)
    layer_pre = matmul_back(feed_round, gate_layer_full)
    layer_input = swap(per_layer).astype(jnp.float32)
    layer_value, layer_back = jax.vjp(gated_product, layer_pre, layer_input)
    layer_low = layer_value.astype(low)
    projected = matmul_last(layer_low, proj_layer_full)
    out_value, final_back = jax.vjp(final_join, after_feed, projected, norm_gains)
    square_sums = jnp.stack(
        [
            jnp.sum(keep_mask * residual * residual),
            jnp.sum(keep_mask * after_attention * after_attention),
            jnp.sum(keep_mask * after_feed * after_feed),
            jnp.sum(keep_mask * out_value * out_value),
        ]
    )
    valid_count = jnp.sum(all_lengths).astype(jnp.float32)

    cotangent = swap(out_grad).astype(jnp.float32) * keep_mask
    grad_feed_out, grad_projected, gains_final = final_back(cotangent)
    projected_low = grad_projected.astype(low)
    grad_proj_layer = outer_sum(layer_low, projected_low)
    grad_layer_pre, grad_layer_input = layer_back(matmul_back(projected_low, proj_layer_full))
    layer_pre_low = grad_layer_pre.astype(low)
    grad_gate_layer = outer_sum(layer_pre_low, feed_round)
    grad_after_feed = grad_feed_out + matmul_last(layer_pre_low, gate_layer_full)
    grad_after_attention_a, grad_summed, gains_feed = feed_back(grad_after_feed)
    summed_all = spread(grad_summed.astype(low), 0)
    grad_down = outer_sum(units_low, summed_all)
    grad_down_low = grad_down.astype(low)
    d_down_weight = lax.psum_scatter(
        grad_down_low, "row", scatter_dimension=1, tiled=True
    ).astype(jnp.float32)
    grad_units = matmul_back(after(summed_all, grad_down_low), down_full)
    grad_gate_value, grad_up_value = gate_back(grad_units)
    grad_paired = jnp.concatenate([grad_gate_value, grad_up_value], axis=-1).astype(low)
    grad_gate = outer_sum(feed_all, grad_paired[..., :unit_width]).astype(low)
    d_gate_weight = lax.psum_scatter(
        grad_gate, "row", scatter_dimension=0, tiled=True
    ).astype(jnp.float32)
    grad_feed = product_sum(after(grad_paired, grad_gate), paired, True, 6)
    grad_up = outer_sum(feed_all, after(grad_paired, grad_feed)[..., unit_width:]).astype(low)
    d_up_weight = lax.psum_scatter(
        grad_up, "row", scatter_dimension=0, tiled=True
    ).astype(jnp.float32)
    grad_feed = after(grad_feed, grad_up)
    grad_residual_mid, grad_out_proj, grad_low_rank, grad_normed_mid, gains_middle = middle_back(
        (grad_after_attention_a, grad_feed)
    )
    out_proj_all = spread(after(grad_out_proj.astype(low), d_down_weight), 0)
    grad_mixed = matmul_back(out_proj_all, output_full).astype(low)
    low_rank_grad = grad_low_rank.astype(low)
    grad_right = outer_sum(laurel_mid, low_rank_grad)
    grad_laurel_mid = matmul_back(low_rank_grad, right_full).astype(low)
    grad_left = outer_sum(grad_laurel_mid, normed_low)
    attn_prob = jnp.exp(score_all() - log_total)
    grad_prob = jnp.einsum(
        "spd,sed->spe", grad_mixed, value_low, preferred_element_type=jnp.float32
    )
    grad_scores = (
        attn_prob * (grad_prob - jnp.sum(attn_prob * grad_prob, axis=-1, keepdims=True))
    ).astype(low)
    grad_queries = (
        jnp.einsum("spe,sed->spd", grad_scores, key_low, preferred_element_type=jnp.float32)
        * score_scale
    )
    grad_keys = (
        jnp.einsum("spe,spd->sed", grad_scores, query_low, preferred_element_type=jnp.float32)
        * score_scale
    )
    grad_values = jnp.einsum(
        "spe,spd->sed", attn_prob.astype(low), grad_mixed, preferred_element_type=jnp.float32
    )
    grad_query_raw, grad_key_raw, grad_value_raw, grad_heads = head_back(
        (grad_queries, grad_keys, grad_values)
    )
    head_grads = jnp.concatenate([grad_query_raw, grad_key_raw, grad_value_raw], axis=-1)
    head_grads = head_grads.astype(low)
    grad_head_weights = outer_sum(head_grads, normed_all).astype(low)
    grad_query, grad_key, grad_value = jnp.split(grad_head_weights, 3, axis=0)
    grad_output = outer_sum(mixed_low, after(out_proj_all, head_grads)).astype(low)
    grad_group = jnp.concatenate(
        [grad_key.reshape(share, -1, D), grad_value.reshape(share, -1, D)], axis=1
    )
    grad_rest = jnp.concatenate(
        [
            piece.astype(low).reshape(cols, -1, D)
            for piece in (grad_left, grad_gate_layer, grad_right, grad_proj_layer)
        ],
        axis=1,
    )
    half = grad_rest.shape[1] // 2
    grad_rest = jnp.swapaxes(grad_rest.reshape(cols, 2, half, D), 0, 1)
    grad_group = after(grad_group, d_gate_weight)
    rest_part, group_part = fold_small(grad_rest.reshape(2, cols * half, D), grad_group, 3)
    parts = jnp.concatenate(
        [grad_output, grad_query, group_part.astype(low), rest_part.astype(low).reshape(-1, D)],
        axis=0,
    )
    parts_out = lax.psum_scatter(parts, "row", scatter_dimension=1, tiled=True).astype(jnp.float32)
    d_output_weight = parts_out[:HD]
    d_query_weight = parts_out[HD : 2 * HD].T
    small_out = parts_out[2 * HD :]
    small_parts = [small_out[a:b] for a, b in zip(edges[:-1], edges[1:])]
    grad_normed = product_sum(after(head_grads, parts, d_up_weight), head_weights, False, 7)
    grad_normed = grad_normed + grad_normed_mid + matmul_last(grad_laurel_mid, left_full)
    grad_residual_in, gains_input = input_back(grad_normed)
    d_hidden = swap((grad_residual_mid + grad_residual_in).astype(low))
    d_per_layer = swap(grad_layer_input.astype(low))
    grad_gains = gains_final + gains_feed + gains_middle + gains_input
    extra = jnp.concatenate([grad_heads.reshape(-1), square_sums])
    extra = jnp.pad(extra, (0, 2 * D - extra.shape[0])).reshape(2, D)
    totals = total(jnp.concatenate([grad_gains, extra], axis=0), tiers, 4)
    d_norm_gains = totals[:6]
    d_head_gains = totals[6, : 2 * HD].reshape(2, HD)
    total_squares = totals[6, 2 * HD : 2 * HD + 4]
    stats = jnp.sqrt(total_squares / (valid_count * D))
    output = swap(out_value.astype(low))
    return (
        output,
        stats,
        d_hidden,
        d_per_layer,
        d_query_weight,
        small_parts[0].T,
        small_parts[1].T,
        d_output_weight,
        d_gate_weight,
        d_up_weight,
        d_down_weight,
        small_parts[2].T,
        small_parts[4],
        small_parts[3].T,
        small_parts[5],
        d_norm_gains,
        d_head_gains,
    )


def solution(mesh):
    body = heads_body if mesh.shape["col"] == H else general_body
    in_specs = (
        P("col", "row", None),
        P("col", "row", None),
        P(),
        P("row", None),
        P("col", "row", None),
        P("row", "col"),
        P("row", "col"),
        P("row", "col"),
        P("col", "row"),
        P("row", "col"),
        P("row", "col"),
        P("col", "row"),
        P("row", "col"),
        P("col", "row"),
        P("row", "col"),
        P("col", "row"),
        P(),
        P(),
    )
    out_specs = (
        P("col", "row", None),
        P(),
        P("col", "row", None),
        P("col", "row", None),
        P("row", "col"),
        P("row", "col"),
        P("row", "col"),
        P("col", "row"),
        P("row", "col"),
        P("row", "col"),
        P("col", "row"),
        P("row", "col"),
        P("col", "row"),
        P("row", "col"),
        P("col", "row"),
        P(),
        P(),
    )
    return jax.shard_map(body, mesh=mesh, in_specs=in_specs, out_specs=out_specs, check_vma=False)
```

```python
import functools
import math

import jax
import jax.numpy as jnp
from jax import lax
from jax.experimental import pallas as pl
from jax.experimental.pallas import tpu as pltpu
from jax.sharding import PartitionSpec as P

D = 2048
H = 8
KV = 2
HD = 256
WINDOW = 512
BLOCK = 256


EPSILON = 1e-06
FAR_BLOCK = 1 << 30
NEGATIVE = -1e30
HALF_ROOT = 1.0 / math.sqrt(2.0)
CURVE = math.sqrt(2.0 / math.pi)
BEND = 0.044715


MESH = pl.DeviceIdType.MESH


def passed_along(value, axis, steps):
    count = lax.axis_size(axis)
    initial, last = (max(0, -steps), min(count, count - steps))
    return lax.ppermute(value, axis, [(source, source + steps) for source in range(initial, last)])


def root_norm(values, gain_row):
    return (
        values * lax.rsqrt(jnp.mean(values * values, axis=-1, keepdims=True) + EPSILON) * gain_row
    )


def plain_norm(values):
    return values * lax.rsqrt(jnp.mean(values * values, axis=-1, keepdims=True) + EPSILON)


def smooth_gate(values):
    return jax.nn.gelu(values, approximate=True)


def rotate(values, angles):
    half_width = values.shape[-1] // 2
    leading = values[..., :half_width]
    trailing = values[..., half_width:]
    cosine = jnp.cos(angles)
    sine_part = jnp.sin(angles)
    return jnp.concatenate(
        [leading * cosine - trailing * sine_part, trailing * cosine + leading * sine_part], axis=-1
    )


def matmul_last(first_array, second_array):
    return lax.dot_general(
        first_array,
        second_array,
        (((first_array.ndim - 1,), (0,)), ((), ())),
        preferred_element_type=jnp.float32,
    )


def matmul_back(first_array, second_array):
    return lax.dot_general(
        first_array,
        second_array,
        (((first_array.ndim - 1,), (1,)), ((), ())),
        preferred_element_type=jnp.float32,
    )


def outer_sum(first_array, second_array):
    return lax.dot_general(
        first_array, second_array, (((0, 1), (0, 1)), ((), ())), preferred_element_type=jnp.float32
    )


def input_norm(residual, gain_rows):
    return root_norm(residual, gain_rows[0])


def middle(residual, out_proj, low_rank, normed, gain_rows):
    merged = (
        residual + root_norm(out_proj, gain_rows[1]) + normed + root_norm(low_rank, gain_rows[4])
    ) * HALF_ROOT
    return (merged, root_norm(merged, gain_rows[2]))


def feed_join(merged, summed, gain_rows):
    return merged + root_norm(summed, gain_rows[3])


def final_join(merged, projected, gain_rows):
    return merged + root_norm(projected, gain_rows[5])


def gated_product(first_array, second_array):
    return smooth_gate(first_array) * second_array


def partners():
    c = lax.axis_index("col")
    sib = c + 1 - 2 * (c % 2)
    xn = c + 2 - 4 * ((c // 2) % 2)
    yn = c + 4 - 8 * (c // 4)
    return c, sib, xn, yn

def greet(devs):
    barrier = pltpu.get_barrier_semaphore()
    for d in devs:
        pl.semaphore_signal(barrier, inc=1, device_id={"col": d}, device_id_type=MESH)
    pl.semaphore_wait(barrier, len(devs))

def spread_kernel(rows, x_ref, o_ref, local_sem, send, recv):
    c, sib, xn, yn = partners()
    def slot(half, who):
        return o_ref.at[half, pl.ds(pl.multiple_of(who * rows, rows), rows), :]
    def both(who):
        return o_ref.at[:, pl.ds(pl.multiple_of(who * rows, rows), rows), :]
    def push(i, src, dst, dev):
        return pltpu.make_async_remote_copy(src_ref=src, dst_ref=dst, send_sem=send.at[i], recv_sem=recv.at[i], device_id={"col": dev}, device_id_type=MESH)
    mine = pltpu.make_async_copy(x_ref, both(c), local_sem)
    mine.start()
    greet((sib, xn, yn))
    x0 = push(0, x_ref.at[0], slot(0, c), xn)
    y1 = push(1, x_ref.at[1], slot(1, c), yn)
    x1 = push(2, x_ref.at[1], slot(1, c), xn)
    y0 = push(3, x_ref.at[0], slot(0, c), yn)
    s = push(4, x_ref, both(c), sib)
    x0.start(); y1.start(); x1.start(); y0.start(); s.start()
    diag = yn + (xn - c)
    x0.wait_recv()
    fy = push(5, slot(0, xn), slot(0, xn), yn)
    fy.start()
    sx0 = push(6, slot(0, xn), slot(0, xn), sib)
    sx0.start()
    y1.wait_recv()
    fx = push(7, slot(1, yn), slot(1, yn), xn)
    fx.start()
    sy1 = push(8, slot(1, yn), slot(1, yn), sib)
    sy1.start()
    x1.wait_recv()
    sx1 = push(9, slot(1, xn), slot(1, xn), sib)
    sx1.start()
    y0.wait_recv()
    sy0 = push(10, slot(0, yn), slot(0, yn), sib)
    sy0.start()
    fy.wait_recv()
    sd0 = push(11, slot(0, diag), slot(0, diag), sib)
    sd0.start()
    fx.wait_recv()
    sd1 = push(12, slot(1, diag), slot(1, diag), sib)
    sd1.start()
    for cp in (s, sx0, sy1, sx1, sy0, sd0, sd1):
        cp.wait_recv()
    for cp in (x0, y1, x1, y0, s, fy, sx0, fx, sy1, sx1, sy0, sd0, sd1):
        cp.wait_send()
    mine.wait()

def spread(x, cid=0):
    h, rows, d = x.shape
    return pl.pallas_call(
        functools.partial(spread_kernel, rows),
        out_shape=jax.ShapeDtypeStruct((h, 8 * rows, d), x.dtype),
        in_specs=[pl.BlockSpec(memory_space=pl.ANY)],
        out_specs=pl.BlockSpec(memory_space=pl.ANY),
        scratch_shapes=[pltpu.SemaphoreType.DMA, pltpu.SemaphoreType.DMA((13,)), pltpu.SemaphoreType.DMA((13,))],
        compiler_params=pltpu.CompilerParams(collective_id=cid, has_side_effects=True),
        cost_estimate=pl.CostEstimate(flops=0, bytes_accessed=120_000_000, transcendentals=0),
        name="spread",
    )(x)

def fold_steps(rows, p_ref, own, sibs, dx, dy, rx, ry, local_sem, send, recv):
    c, sib, xn, yn = partners()
    diag = yn + (xn - c)
    wide = jnp.float32
    tall = 32 if rows % 32 == 0 else 8

    def blk(who):
        return p_ref.at[:, pl.ds(pl.multiple_of(who * rows, rows), rows), :]

    def push(i, src, dst, dev):
        return pltpu.make_async_remote_copy(
            src_ref=src,
            dst_ref=dst,
            send_sem=send.at[i],
            recv_sem=recv.at[i],
            device_id={"col": dev},
            device_id_type=MESH,
        )

    def add(dst, src):
        @pl.loop(0, rows // tall)
        def _(i):
            r = pl.ds(pl.multiple_of(i * tall, tall), tall)
            dst[r, :] = (dst[r, :].astype(wide) + src[r, :].astype(wide)).astype(dst.dtype)

    def pair(j):
        add(own.at[j, 0], sibs.at[j, 0])
        add(own.at[j, 1], sibs.at[j, 1])

    dests = (diag, xn, yn, c)
    loads = [pltpu.make_async_copy(blk(d), own.at[j], local_sem.at[j]) for j, d in enumerate(dests)]
    for load in loads:
        load.start()
    yield None
    sides = [push(j, blk(d + (sib - c)), sibs.at[j], sib) for j, d in enumerate(dests)]
    for side in sides:
        side.start()
    yield None
    loads[0].wait()
    sides[0].wait_recv()
    pair(0)
    a = push(4, own.at[0, 0], dx, xn)
    b = push(5, own.at[0, 1], dy, yn)
    a.start()
    b.start()
    yield None
    loads[1].wait()
    sides[1].wait_recv()
    pair(1)
    x0 = push(6, own.at[1, 0], rx.at[0], xn)
    x0.start()
    yield None
    loads[2].wait()
    sides[2].wait_recv()
    pair(2)
    y1 = push(7, own.at[2, 1], ry.at[1], yn)
    y1.start()
    yield None
    a.wait_recv()
    add(own.at[2, 0], dx)
    y0 = push(8, own.at[2, 0], ry.at[0], yn)
    y0.start()
    yield None
    b.wait_recv()
    add(own.at[1, 1], dy)
    x1 = push(9, own.at[1, 1], rx.at[1], xn)
    x1.start()
    yield None
    loads[3].wait()
    sides[3].wait_recv()
    pair(3)
    yield None
    waits = ((x0, y0), (x1, y1))
    yield tall, waits, (*sides, a, b, x0, y1, y0, x1)


def fold_finish(rows, o_ref, own, rx, ry, tall, waits, sent):
    wide = jnp.float32
    for h in range(2):
        for copy in waits[h]:
            copy.wait_recv()

        @pl.loop(0, rows // tall)
        def _(i):
            r = pl.ds(pl.multiple_of(i * tall, tall), tall)
            o_ref[h, r, :] = (
                own[3, h, r, :].astype(wide) + rx[h, r, :].astype(wide) + ry[h, r, :].astype(wide)
            )

    for copy in sent:
        copy.wait_send()


def fold_scratch(h, rows, d, kind):
    return [
        pltpu.VMEM((4, h, rows, d), kind),
        pltpu.VMEM((4, h, rows, d), kind),
        pltpu.VMEM((rows, d), kind),
        pltpu.VMEM((rows, d), kind),
        pltpu.VMEM((h, rows, d), kind),
        pltpu.VMEM((h, rows, d), kind),
        pltpu.SemaphoreType.DMA((4,)),
        pltpu.SemaphoreType.DMA((10,)),
        pltpu.SemaphoreType.DMA((10,)),
    ]


def product_kernel(
    rows, flip, a_ref, w_ref, o_ref, a_buf, w_buf, stage, own, sibs, dx, dy, rx, ry,
    local_sem, send, recv,
):
    c, sib, xn, yn = partners()
    diag = yn + (xn - c)
    wide = jnp.float32
    d = o_ref.shape[-1]
    tile = 512
    tall = 32

    def push(i, src, dst, dev):
        return pltpu.make_async_remote_copy(
            src_ref=src,
            dst_ref=dst,
            send_sem=send.at[i],
            recv_sem=recv.at[i],
            device_id={"col": dev},
            device_id_type=MESH,
        )

    dests = (diag, xn, yn, c)
    step = sib - c
    weights = pltpu.make_async_copy(w_ref, w_buf, local_sem.at[8])
    weights.start()

    def load(i, who):
        return pltpu.make_async_copy(
            a_ref.at[:, pl.ds(pl.multiple_of(who * rows, rows), rows), :],
            a_buf.at[i],
            local_sem.at[i],
        )

    far = [load(j, dests[j] + step) for j in range(4)]
    near = [load(4 + j, dests[j]) for j in range(4)]
    for first, second in zip(far, near):
        first.start()
        second.start()
    greet((sib, xn, yn))
    weights.wait()

    def product(i, put):
        left = a_buf[i].reshape(2 * rows, a_buf.shape[-1])

        @pl.loop(0, d // tile)
        def _(n):
            cut = pl.ds(pl.multiple_of(n * tile, tile), tile)
            right = w_buf[cut, :] if flip else w_buf[:, cut]
            dims = (((1,), (1,)), ((), ())) if flip else (((1,), (0,)), ((), ()))
            value = lax.dot_general(left, right, dims, preferred_element_type=wide)
            put(cut, value.reshape(2, rows, tile))

    sides = [push(j, stage.at[j], sibs.at[j], sib) for j in range(4)]

    def for_sibling(j):
        far[j].wait()

        def put(cut, value):
            stage[j, :, :, cut] = value.astype(stage.dtype)

        product(j, put)
        sides[j].start()

    def for_chip(j):
        near[j].wait()
        sides[j].wait_recv()

        def put(cut, value):
            own[j, :, :, cut] = (value + sibs[j, :, :, cut].astype(wide)).astype(own.dtype)

        product(4 + j, put)

    def add(dst, src):
        @pl.loop(0, rows // tall)
        def _(i):
            r = pl.ds(pl.multiple_of(i * tall, tall), tall)
            dst[r, :] = (dst[r, :].astype(wide) + src[r, :].astype(wide)).astype(dst.dtype)

    for_sibling(0)
    for_sibling(1)
    for_chip(0)
    a = push(4, own.at[0, 0], dx, xn)
    b = push(5, own.at[0, 1], dy, yn)
    a.start()
    b.start()
    for_sibling(2)
    for_chip(1)
    x0 = push(6, own.at[1, 0], rx.at[0], xn)
    x0.start()
    for_sibling(3)
    for_chip(2)
    y1 = push(7, own.at[2, 1], ry.at[1], yn)
    y1.start()
    a.wait_recv()
    add(own.at[2, 0], dx)
    y0 = push(8, own.at[2, 0], ry.at[0], yn)
    y0.start()
    b.wait_recv()
    add(own.at[1, 1], dy)
    x1 = push(9, own.at[1, 1], rx.at[1], xn)
    x1.start()
    near[3].wait()
    sides[3].wait_recv()

    def put(cut, value):
        o_ref[:, :, cut] = value + sibs[3, :, :, cut].astype(wide)

    product(7, put)
    for h, waits in enumerate(((x0, y0), (x1, y1))):
        for copy in waits:
            copy.wait_recv()

        @pl.loop(0, rows // tall)
        def _(i):
            r = pl.ds(pl.multiple_of(i * tall, tall), tall)
            o_ref[h, r, :] = o_ref[h, r, :] + rx[h, r, :].astype(wide) + ry[h, r, :].astype(wide)

    for copy in (*sides, a, b, x0, y1, y0, x1):
        copy.wait_send()


def product_sum(left, right, flip, cid):
    h, total, depth = left.shape
    rows = total // 8
    d = right.shape[0] if flip else right.shape[1]
    low = left.dtype
    return pl.pallas_call(
        functools.partial(product_kernel, rows, flip),
        out_shape=jax.ShapeDtypeStruct((h, rows, d), jnp.float32),
        in_specs=[pl.BlockSpec(memory_space=pl.ANY)] * 2,
        out_specs=pl.BlockSpec(memory_space=pltpu.VMEM),
        scratch_shapes=[
            pltpu.VMEM((8, h, rows, depth), low),
            pltpu.VMEM(right.shape, low),
            pltpu.VMEM((4, h, rows, d), low),
            pltpu.VMEM((3, h, rows, d), low),
            pltpu.VMEM((4, h, rows, d), low),
            pltpu.VMEM((rows, d), low),
            pltpu.VMEM((rows, d), low),
            pltpu.VMEM((h, rows, d), low),
            pltpu.VMEM((h, rows, d), low),
            pltpu.SemaphoreType.DMA((9,)),
            pltpu.SemaphoreType.DMA((10,)),
            pltpu.SemaphoreType.DMA((10,)),
        ],
        compiler_params=pltpu.CompilerParams(
            collective_id=cid, has_side_effects=True, vmem_limit_bytes=44 << 20
        ),
        cost_estimate=pl.CostEstimate(
            flops=2 * h * total * depth * d, bytes_accessed=130_000_000, transcendentals=0
        ),
        name="product_sum",
    )(left, right)


def fold_small_kernel(
    rows, p_ref, g_ref, o_ref, k_ref, own, sibs, dx, dy, rx, ry, local_sem, send, recv,
    gown, gsibs, grx, glocal, gsend, grecv,
):
    c, sib, xn, yn = partners()
    m = c % 4
    m_sib = m + 1 - 2 * (m % 2)
    m_x = m + 2 - 4 * (m // 2)
    m_diag = m_sib + (m_x - m)
    wide = jnp.float32

    def push(i, src, dst, dev):
        return pltpu.make_async_remote_copy(
            src_ref=src,
            dst_ref=dst,
            send_sem=gsend.at[i],
            recv_sem=grecv.at[i],
            device_id={"col": dev},
            device_id_type=MESH,
        )

    steps = fold_steps(rows, p_ref, own, sibs, dx, dy, rx, ry, local_sem, send, recv)
    next(steps)
    loads = [
        pltpu.make_async_copy(g_ref.at[d], gown.at[j], glocal.at[j])
        for j, d in enumerate((m_x, m))
    ]
    for load in loads:
        load.start()
    greet((sib, xn, yn))
    sides = [push(j, g_ref.at[d], gsibs.at[j], sib) for j, d in enumerate((m_diag, m_sib))]
    sides[0].start()
    next(steps)
    sides[1].start()
    tall = k_ref.shape[0] // 4
    loads[0].wait()
    sides[0].wait_recv()

    @pl.loop(0, 4)
    def _(i):
        r = pl.ds(pl.multiple_of(i * tall, tall), tall)
        gown[0, r, :] = (gown[0, r, :].astype(wide) + gsibs[0, r, :].astype(wide)).astype(
            gown.dtype
        )

    over = push(2, gown.at[0], grx, xn)
    over.start()
    last = None
    for step in steps:
        last = step if step is not None else last
    fold_finish(rows, o_ref, own, rx, ry, *last)
    loads[1].wait()
    sides[1].wait_recv()
    over.wait_recv()

    @pl.loop(0, 4)
    def _(i):
        r = pl.ds(pl.multiple_of(i * tall, tall), tall)
        k_ref[r, :] = (
            gown[1, r, :].astype(wide) + gsibs[1, r, :].astype(wide) + grx[r, :].astype(wide)
        )

    for copy in (*sides, over):
        copy.wait_send()


def fold_small(p, g, cid):
    h, total, d = p.shape
    rows = total // 8
    share, tall, _ = g.shape
    return pl.pallas_call(
        functools.partial(fold_small_kernel, rows),
        out_shape=(
            jax.ShapeDtypeStruct((h, rows, d), jnp.float32),
            jax.ShapeDtypeStruct((tall, d), jnp.float32),
        ),
        in_specs=[pl.BlockSpec(memory_space=pl.ANY)] * 2,
        out_specs=[pl.BlockSpec(memory_space=pltpu.VMEM)] * 2,
        scratch_shapes=fold_scratch(h, rows, d, p.dtype)
        + [
            pltpu.VMEM((2, tall, d), g.dtype),
            pltpu.VMEM((2, tall, d), g.dtype),
            pltpu.VMEM((tall, d), g.dtype),
            pltpu.SemaphoreType.DMA((2,)),
            pltpu.SemaphoreType.DMA((3,)),
            pltpu.SemaphoreType.DMA((3,)),
        ],
        compiler_params=pltpu.CompilerParams(
            collective_id=cid, has_side_effects=True, vmem_limit_bytes=40 << 20
        ),
        cost_estimate=pl.CostEstimate(flops=0, bytes_accessed=60_000_000, transcendentals=0),
        name="fold_small",
    )(p, g)


def open_kernel(
    rows, x_ref, s_ref, q_ref, w_ref, o_ref, sa_ref, qa_ref, wa_ref, local_sem, send, recv
):
    c, sib, xn, yn = partners()
    diag = yn + (xn - c)
    r = lax.axis_index("row")
    tiers = lax.axis_size("row")

    def slot(half, who):
        return o_ref.at[half, pl.ds(pl.multiple_of(who * rows, rows), rows), :]

    def both(who):
        return o_ref.at[:, pl.ds(pl.multiple_of(who * rows, rows), rows), :]

    started = []

    def push(src, dst, **dev):
        i = len(started)
        copy = pltpu.make_async_remote_copy(
            src_ref=src,
            dst_ref=dst,
            send_sem=send.at[i],
            recv_sem=recv.at[i],
            device_id=dev,
            device_id_type=MESH,
        )
        copy.start()
        started.append(copy)
        return copy

    local = [
        pltpu.make_async_copy(x_ref, both(c), local_sem.at[0]),
        pltpu.make_async_copy(s_ref, sa_ref.at[r], local_sem.at[1]),
        pltpu.make_async_copy(q_ref, qa_ref.at[r], local_sem.at[2]),
        pltpu.make_async_copy(w_ref, wa_ref.at[r], local_sem.at[3]),
    ]
    for copy in local:
        copy.start()
    others = [lax.rem(r + k, tiers) for k in range(1, tiers)]
    barrier = pltpu.get_barrier_semaphore()
    for d in (sib, xn, yn):
        pl.semaphore_signal(barrier, inc=1, device_id={"col": d}, device_id_type=MESH)
    for d in others:
        pl.semaphore_signal(barrier, inc=1, device_id={"row": d}, device_id_type=MESH)
    pl.semaphore_wait(barrier, 3 + len(others))
    for src, dst in ((s_ref, sa_ref), (q_ref, qa_ref), (w_ref, wa_ref)):
        for d in others:
            push(src, dst.at[r], row=d)
    x0 = push(x_ref.at[0], slot(0, c), col=xn)
    y1 = push(x_ref.at[1], slot(1, c), col=yn)
    x1 = push(x_ref.at[1], slot(1, c), col=xn)
    y0 = push(x_ref.at[0], slot(0, c), col=yn)
    push(x_ref, both(c), col=sib)
    x0.wait_recv()
    fy = push(slot(0, xn), slot(0, xn), col=yn)
    push(slot(0, xn), slot(0, xn), col=sib)
    y1.wait_recv()
    fx = push(slot(1, yn), slot(1, yn), col=xn)
    push(slot(1, yn), slot(1, yn), col=sib)
    x1.wait_recv()
    push(slot(1, xn), slot(1, xn), col=sib)
    y0.wait_recv()
    push(slot(0, yn), slot(0, yn), col=sib)
    fy.wait_recv()
    push(slot(0, diag), slot(0, diag), col=sib)
    fx.wait_recv()
    push(slot(1, diag), slot(1, diag), col=sib)
    for copy in started:
        if not any(copy is other for other in (x0, y1, x1, y0, fy, fx)):
            copy.wait_recv()
    for copy in started:
        copy.wait_send()
    for copy in local:
        copy.wait()


def open_all(x, small, query, output, tiers, cid):
    h, rows, d = x.shape
    low = x.dtype
    copies = 13 + 3 * (tiers - 1)
    return pl.pallas_call(
        functools.partial(open_kernel, rows),
        out_shape=(
            jax.ShapeDtypeStruct((h, 8 * rows, d), low),
            jax.ShapeDtypeStruct((tiers, *small.shape), low),
            jax.ShapeDtypeStruct((tiers, *query.shape), low),
            jax.ShapeDtypeStruct((tiers, *output.shape), low),
        ),
        in_specs=[pl.BlockSpec(memory_space=pl.ANY)] * 4,
        out_specs=[pl.BlockSpec(memory_space=pl.ANY)] * 4,
        scratch_shapes=[
            pltpu.SemaphoreType.DMA((4,)),
            pltpu.SemaphoreType.DMA((copies,)),
            pltpu.SemaphoreType.DMA((copies,)),
        ],
        compiler_params=pltpu.CompilerParams(collective_id=cid, has_side_effects=True),
        cost_estimate=pl.CostEstimate(flops=0, bytes_accessed=200_000_000, transcendentals=0),
        name="open_all",
    )(x, small, query, output)


def share_kernel(near, s_ref, sa_ref, local_sem, send, recv):
    c, sib, xn, yn = partners()
    diag = yn + (xn - c)
    height = s_ref.shape[1]
    started = []

    def part(ref, first):
        return ref.at[:, pl.ds(0, near) if first else pl.ds(near, height - near), :]

    def push(who, first, dev, own=False):
        i = len(started)
        dst = part(sa_ref.at[who], first)
        copy = pltpu.make_async_remote_copy(
            src_ref=part(s_ref, first) if own else dst,
            dst_ref=dst,
            send_sem=send.at[i],
            recv_sem=recv.at[i],
            device_id={"col": dev},
            device_id_type=MESH,
        )
        copy.start()
        started.append(copy)
        return copy

    mine = pltpu.make_async_copy(s_ref, sa_ref.at[c], local_sem)
    mine.start()
    greet((sib, xn, yn))
    kx = push(c, True, xn, own=True)
    ry = push(c, False, yn, own=True)
    rx = push(c, False, xn, own=True)
    push(c, True, sib, own=True)
    push(c, False, sib, own=True)
    ry.wait_recv()
    push(yn, False, sib)
    kx.wait_recv()
    push(xn, True, sib)
    rx.wait_recv()
    fd = push(xn, False, yn)
    push(xn, False, sib)
    fd.wait_recv()
    push(diag, False, sib)
    for copy in started:
        if not any(copy is other for other in (kx, rx, ry, fd)):
            copy.wait_recv()
    for copy in started:
        copy.wait_send()
    mine.wait()


def share_small(small, near, cid):
    return pl.pallas_call(
        functools.partial(share_kernel, near),
        out_shape=jax.ShapeDtypeStruct((8, *small.shape), small.dtype),
        in_specs=[pl.BlockSpec(memory_space=pl.ANY)],
        out_specs=pl.BlockSpec(memory_space=pl.ANY),
        scratch_shapes=[
            pltpu.SemaphoreType.DMA,
            pltpu.SemaphoreType.DMA((10,)),
            pltpu.SemaphoreType.DMA((10,)),
        ],
        compiler_params=pltpu.CompilerParams(collective_id=cid, has_side_effects=True),
        cost_estimate=pl.CostEstimate(flops=0, bytes_accessed=60_000_000, transcendentals=0),
        name="share_small",
    )(small)


def rounds_of(rows, x_ref, held, local_sem, send, recv, consume):
    c, sib, xn, yn = partners()
    diag = yn + (xn - c)
    step = sib - c

    def place(t, j, n=1):
        return held.at[t, pl.ds(j * rows, n * rows), :]

    started = []

    def push(src, dst, dev):
        i = len(started)
        copy = pltpu.make_async_remote_copy(
            src_ref=src,
            dst_ref=dst,
            send_sem=send.at[i],
            recv_sem=recv.at[i],
            device_id={"col": dev},
            device_id_type=MESH,
        )
        copy.start()
        started.append(copy)
        return copy

    mine = [pltpu.make_async_copy(x_ref.at[h], place(0, h), local_sem.at[h]) for h in range(2)]
    for copy in mine:
        copy.start()
    greet((sib, xn, yn))
    x0 = push(x_ref.at[0], place(1, 0), xn)
    y1 = push(x_ref.at[1], place(1, 1), yn)
    x1 = push(x_ref.at[1], place(2, 0), xn)
    y0 = push(x_ref.at[0], place(2, 1), yn)
    s0 = push(x_ref.at[0], place(0, 2), sib)
    s1 = push(x_ref.at[1], place(0, 3), sib)
    for copy in mine:
        copy.wait()
    s0.wait_recv()
    s1.wait_recv()
    consume(0, ((0, c), (1, c), (0, sib), (1, sib)))
    x0.wait_recv()
    fy = push(place(1, 0), place(3, 0), yn)
    y1.wait_recv()
    fx = push(place(1, 1), place(3, 1), xn)
    t1 = push(place(1, 0, 2), place(1, 2, 2), sib)
    t1.wait_recv()
    consume(1, ((0, xn), (1, yn), (0, xn + step), (1, yn + step)))
    x1.wait_recv()
    y0.wait_recv()
    t2 = push(place(2, 0, 2), place(2, 2, 2), sib)
    t2.wait_recv()
    consume(2, ((1, xn), (0, yn), (1, xn + step), (0, yn + step)))
    fy.wait_recv()
    fx.wait_recv()
    t3 = push(place(3, 0, 2), place(3, 2, 2), sib)
    t3.wait_recv()
    consume(3, ((0, diag), (1, diag), (0, diag + step), (1, diag + step)))
    for copy in started:
        copy.wait_send()


def piece_at(ref, rows, piece):
    half, who = piece
    return ref.at[half, pl.ds(pl.multiple_of(who * rows, rows), rows), :]


def units_back_kernel(
    rows, x_ref, w_ref, u_ref, g_ref, v_ref, p_ref, d_ref,
    held, weights, units, gates, ups, grads, total_ref,
    weight_sem, load_sem, store_sem, local_sem, send, recv,
):
    c, sib, xn, yn = partners()
    diag = yn + (xn - c)
    step = sib - c
    wide = jnp.float32
    width = w_ref.shape[0]
    d = w_ref.shape[1]
    plan = (
        ((0, c), (1, c), (0, sib), (1, sib)),
        ((0, xn), (1, yn), (0, xn + step), (1, yn + step)),
        ((1, xn), (0, yn), (1, xn + step), (0, yn + step)),
        ((0, diag), (1, diag), (0, diag + step), (1, diag + step)),
    )
    fetch = pltpu.make_async_copy(w_ref, weights, weight_sem)
    fetch.start()

    def loads(t):
        copies = []
        for j, piece in enumerate(plan[t]):
            for k, (src, dst) in enumerate(((u_ref, units), (g_ref, gates), (v_ref, ups))):
                copies.append(
                    pltpu.make_async_copy(
                        piece_at(src, rows, piece),
                        dst.at[t % 2, pl.ds(j * rows, rows), :],
                        load_sem.at[t % 2, j, k],
                    )
                )
        return copies

    def stores(t):
        return [
            pltpu.make_async_copy(
                grads.at[t % 2, pl.ds(j * rows, rows), :],
                piece_at(p_ref, rows, piece),
                store_sem.at[t % 2, j],
            )
            for j, piece in enumerate(plan[t])
        ]

    for copy in loads(0):
        copy.start()

    def consume(t, pieces):
        if t == 0:
            fetch.wait()
        if t < 3:
            for copy in loads(t + 1):
                copy.start()
        for copy in loads(t):
            copy.wait()
        if t >= 2:
            for copy in stores(t - 2):
                copy.wait()
        tile = 256

        @pl.loop(0, width // tile)
        def _(n):
            cut = pl.ds(pl.multiple_of(n * tile, tile), tile)
            grad = lax.dot_general(
                held[t], weights[cut, :], (((1,), (1,)), ((), ())), preferred_element_type=wide
            )
            gate = gates[t % 2, :, cut]
            up = ups[t % 2, :, cut]
            inner = CURVE * (gate + BEND * gate * gate * gate)
            bent = jnp.tanh(inner)
            gelu = 0.5 * gate * (1.0 + bent)
            slope = 0.5 * (1.0 + bent) + 0.5 * gate * (1.0 - bent * bent) * CURVE * (
                1.0 + 3.0 * BEND * gate * gate
            )
            grads[t % 2, :, cut] = (grad * up * slope).astype(grads.dtype)
            cut_up = pl.ds(pl.multiple_of(width + n * tile, tile), tile)
            grads[t % 2, :, cut_up] = (grad * gelu).astype(grads.dtype)

        for copy in stores(t):
            copy.start()

        @pl.loop(0, width // tile)
        def _(m):
            cut = pl.ds(pl.multiple_of(m * tile, tile), tile)
            turned = units[t % 2, :, cut].T

            @pl.loop(0, d // 512)
            def _(n):
                wide_cut = pl.ds(pl.multiple_of(n * 512, 512), 512)
                value = jnp.dot(turned, held[t, :, wide_cut], preferred_element_type=wide)
                if t > 0:
                    value = value + total_ref[cut, wide_cut]
                if t < 3:
                    total_ref[cut, wide_cut] = value
                else:
                    d_ref[cut, wide_cut] = value.astype(d_ref.dtype)

    rounds_of(rows, x_ref, held, local_sem, send, recv, consume)
    for copy in (*stores(2), *stores(3)):
        copy.wait()


def units_back(x, down, units, gate, up, cid):
    h, rows, d = x.shape
    width = down.shape[0]
    low = x.dtype
    return pl.pallas_call(
        functools.partial(units_back_kernel, rows),
        out_shape=(
            jax.ShapeDtypeStruct((h, 8 * rows, 2 * width), low),
            jax.ShapeDtypeStruct((width, d), low),
        ),
        in_specs=[pl.BlockSpec(memory_space=pl.ANY)] * 5,
        out_specs=[
            pl.BlockSpec(memory_space=pl.ANY),
            pl.BlockSpec(memory_space=pltpu.VMEM),
        ],
        scratch_shapes=[
            pltpu.VMEM((4, 4 * rows, d), low),
            pltpu.VMEM((width, d), low),
            pltpu.VMEM((2, 4 * rows, width), low),
            pltpu.VMEM((2, 4 * rows, width), jnp.float32),
            pltpu.VMEM((2, 4 * rows, width), jnp.float32),
            pltpu.VMEM((2, 4 * rows, 2 * width), low),
            pltpu.VMEM((width, d), jnp.float32),
            pltpu.SemaphoreType.DMA,
            pltpu.SemaphoreType.DMA((2, 4, 3)),
            pltpu.SemaphoreType.DMA((2, 4)),
            pltpu.SemaphoreType.DMA((2,)),
            pltpu.SemaphoreType.DMA((11,)),
            pltpu.SemaphoreType.DMA((11,)),
        ],
        compiler_params=pltpu.CompilerParams(
            collective_id=cid, has_side_effects=True, vmem_limit_bytes=52 << 20
        ),
        cost_estimate=pl.CostEstimate(
            flops=64 * h * rows * width * d, bytes_accessed=130_000_000, transcendentals=0
        ),
        name="units_back",
    )(x, down, units, gate, up)


def total_kernel(x_ref, o_ref, sums, got, tier_sums, send, recv):
    c, sib, xn, yn = partners()
    r = lax.axis_index("row")
    tiers = lax.axis_size("row")
    others = [lax.rem(r + k, tiers) for k in range(1, tiers)]
    barrier = pltpu.get_barrier_semaphore()
    for d in (sib, xn, yn):
        pl.semaphore_signal(barrier, inc=1, device_id={"col": d}, device_id_type=MESH)
    for d in others:
        pl.semaphore_signal(barrier, inc=1, device_id={"row": d}, device_id_type=MESH)
    pl.semaphore_wait(barrier, 3 + len(others))
    sums[0] = x_ref[...]
    for i, dev in enumerate((sib, xn, yn)):
        copy = pltpu.make_async_remote_copy(
            src_ref=sums.at[i],
            dst_ref=got.at[i],
            send_sem=send.at[i],
            recv_sem=recv.at[i],
            device_id={"col": dev},
            device_id_type=MESH,
        )
        copy.start()
        copy.wait()
        sums[i + 1] = sums[i] + got[i]
    tier_sums[r] = sums[3]
    copies = []
    for k, d in enumerate(others):
        copy = pltpu.make_async_remote_copy(
            src_ref=sums.at[3],
            dst_ref=tier_sums.at[r],
            send_sem=send.at[3 + k],
            recv_sem=recv.at[3 + k],
            device_id={"row": d},
            device_id_type=MESH,
        )
        copy.start()
        copies.append(copy)
    for copy in copies:
        copy.wait()
    result = tier_sums[0]
    for k in range(1, tiers):
        result = result + tier_sums[k]
    o_ref[...] = result


def total(x, tiers, cid):
    return pl.pallas_call(
        total_kernel,
        out_shape=jax.ShapeDtypeStruct(x.shape, x.dtype),
        in_specs=[pl.BlockSpec(memory_space=pltpu.VMEM)],
        out_specs=pl.BlockSpec(memory_space=pltpu.VMEM),
        scratch_shapes=[
            pltpu.VMEM((4, *x.shape), x.dtype),
            pltpu.VMEM((3, *x.shape), x.dtype),
            pltpu.VMEM((tiers, *x.shape), x.dtype),
            pltpu.SemaphoreType.DMA((2 + tiers,)),
            pltpu.SemaphoreType.DMA((2 + tiers,)),
        ],
        compiler_params=pltpu.CompilerParams(collective_id=cid, has_side_effects=True),
        cost_estimate=pl.CostEstimate(flops=0, bytes_accessed=40_000_000, transcendentals=0),
        name="total",
    )(x)


def after(value, *earlier):
    return lax.optimization_barrier((value, *earlier))[0]


def general_body(
    hidden,
    per_layer,
    lengths,
    block_ids,
    out_grad,
    query_weight,
    key_weight,
    value_weight,
    output_weight,
    gate_weight,
    up_weight,
    down_weight,
    laurel_left,
    laurel_right,
    layer_gate,
    layer_proj,
    norm_gains,
    head_gains,
):
    local_rows = hidden.shape[0]
    seq_groups = hidden.shape[1]
    col_index = lax.axis_index("col")
    row_index = lax.axis_index("row")
    all_lengths = lengths
    lengths = lax.dynamic_slice_in_dim(all_lengths, row_index * seq_groups, seq_groups, 0)
    (
        query_cols,
        key_cols,
        value_cols,
        output_rows,
        gate_cols,
        up_cols,
        down_rows,
        left_cols,
        right_rows,
        gate_layer_cols,
        proj_layer_rows,
    ) = (
        lax.all_gather(query_weight, "row", axis=0, tiled=True),
        lax.all_gather(key_weight, "row", axis=0, tiled=True),
        lax.all_gather(value_weight, "row", axis=0, tiled=True),
        lax.all_gather(output_weight, "row", axis=1, tiled=True),
        lax.all_gather(gate_weight, "row", axis=0, tiled=True),
        lax.all_gather(up_weight, "row", axis=0, tiled=True),
        lax.all_gather(down_weight, "row", axis=1, tiled=True),
        lax.all_gather(laurel_left, "row", axis=0, tiled=True),
        lax.all_gather(laurel_right, "row", axis=1, tiled=True),
        lax.all_gather(layer_gate, "row", axis=0, tiled=True),
        lax.all_gather(layer_proj, "row", axis=1, tiled=True),
    )
    (
        query_full,
        key_full,
        value_full,
        output_full,
        left_full,
        right_full,
        gate_layer_full,
        proj_layer_full,
    ) = (
        lax.all_gather(query_cols, "col", axis=1, tiled=True),
        lax.all_gather(key_cols, "col", axis=1, tiled=True),
        lax.all_gather(value_cols, "col", axis=1, tiled=True),
        lax.all_gather(output_rows, "col", axis=0, tiled=True),
        lax.all_gather(left_cols, "col", axis=1, tiled=True),
        lax.all_gather(right_rows, "col", axis=0, tiled=True),
        lax.all_gather(gate_layer_cols, "col", axis=1, tiled=True),
        lax.all_gather(proj_layer_rows, "col", axis=0, tiled=True),
    )
    paired = jnp.concatenate([gate_cols, up_cols], axis=1)
    unit_width = gate_cols.shape[1]
    first_position = col_index * local_rows
    positions = first_position + jnp.arange(local_rows, dtype=jnp.int32)
    live_mask = positions[:, None] < lengths[None, :]
    keep_mask = live_mask.astype(jnp.float32)[:, :, None]
    reach_back = (WINDOW + local_rows - 2) // local_rows
    reach_ahead = (BLOCK + local_rows - 2) // local_rows
    key_span = (reach_back + 1 + reach_ahead) * local_rows
    key_position = first_position - reach_back * local_rows + jnp.arange(key_span, dtype=jnp.int32)
    filler_low = jnp.full((seq_groups, reach_back * local_rows), FAR_BLOCK, jnp.int32)
    filler_high = jnp.full((seq_groups, reach_ahead * local_rows), FAR_BLOCK, jnp.int32)
    padded_blocks = jnp.concatenate([filler_low, block_ids, filler_high], axis=1)
    key_blocks = lax.dynamic_slice_in_dim(padded_blocks, first_position, key_span, 1)
    query_blocks = lax.dynamic_slice_in_dim(block_ids, first_position, local_rows, 1)
    key_live = (key_position[None, :] >= 0) & (key_position[None, :] < lengths[:, None])
    query_live = positions[None, :] < lengths[:, None]
    distance = positions[:, None] - key_position[None, :]
    nearby = (query_blocks[:, :, None] >= key_blocks[:, None, :]) & (distance < WINDOW)[None]
    nearby = nearby & query_live[:, :, None] & key_live[:, None, :]
    visible = (nearby | (distance == 0)[None])[:, None, None]
    residual = hidden.astype(jnp.float32)
    normed_value, input_back = jax.vjp(input_norm, residual, norm_gains)
    normed_low = normed_value.astype(jnp.bfloat16)
    half_width = HD // 2
    frequency = jnp.exp(jnp.arange(half_width, dtype=jnp.float32) * (-2.0 * math.log(10000.0) / HD))
    angles = (positions.astype(jnp.float32)[:, None] * frequency[None, :])[:, None, None, :]

    def prepare(query_in, key_in, value_in, gain_rows):
        return (
            rotate(root_norm(query_in, gain_rows[0]), angles),
            rotate(root_norm(key_in, gain_rows[1]), angles),
            plain_norm(value_in),
        )

    query_raw = matmul_last(normed_low, query_full).reshape(local_rows, seq_groups, H, HD)
    key_raw = matmul_last(normed_low, key_full).reshape(local_rows, seq_groups, KV, HD)
    value_raw = matmul_last(normed_low, value_full).reshape(local_rows, seq_groups, KV, HD)
    (query_value, key_value, value_value), head_back = jax.vjp(
        prepare, query_raw, key_raw, value_raw, head_gains
    )
    query_low = query_value.astype(jnp.bfloat16).reshape(local_rows, seq_groups, KV, H // KV, HD)
    key_low = key_value.astype(jnp.bfloat16)
    value_low = value_value.astype(jnp.bfloat16)
    offsets = list(range(reach_back, -reach_ahead - 1, -1))
    key_parts = []
    value_parts = []
    for offset in offsets:
        if offset == 0:
            key_parts.append(key_low)
            value_parts.append(value_low)
        else:
            moved_key, moved_value = passed_along((key_low, value_low), "col", offset)
            key_parts.append(moved_key)
            value_parts.append(moved_value)
    near_keys = jnp.concatenate(key_parts, axis=0)
    near_values = jnp.concatenate(value_parts, axis=0)
    score_scale = HD ** (-0.5)

    def score_all():
        raw_scores = (
            jnp.einsum(
                "psjgd,esjd->sjgpe", query_low, near_keys, preferred_element_type=jnp.float32
            )
            * score_scale
        )
        return jnp.where(visible, raw_scores, NEGATIVE)

    scores = score_all()
    row_max = jnp.max(scores, axis=-1, keepdims=True)
    exponent = jnp.exp(scores - row_max)
    row_total = jnp.sum(exponent, axis=-1, keepdims=True)
    attn_prob = exponent / row_total
    log_total = row_max + jnp.log(row_total)
    mixed_heads = jnp.einsum(
        "sjgpe,esjd->psjgd",
        attn_prob.astype(jnp.bfloat16),
        near_values,
        preferred_element_type=jnp.float32,
    )
    mixed_low = mixed_heads.reshape(local_rows, seq_groups, H * HD).astype(jnp.bfloat16)
    out_proj = matmul_last(mixed_low, output_full)
    laurel_mid = matmul_last(normed_low, left_full).astype(jnp.bfloat16)
    low_rank = matmul_last(laurel_mid, right_full)
    (after_attention, feed_normed), middle_back = jax.vjp(
        middle, residual, out_proj, low_rank, normed_low.astype(jnp.float32), norm_gains
    )
    feed_low = feed_normed.astype(jnp.bfloat16)
    gate_up = matmul_last(lax.all_gather(feed_low, "col", axis=0, tiled=True), paired)
    unit_value, gate_back = jax.vjp(
        gated_product, gate_up[..., :unit_width], gate_up[..., unit_width:]
    )
    units_low = unit_value.astype(jnp.bfloat16)
    summed = lax.psum_scatter(
        matmul_last(units_low, down_rows), "col", scatter_dimension=0, tiled=True
    )
    after_feed, feed_back = jax.vjp(feed_join, after_attention, summed, norm_gains)
    feed_round = after_feed.astype(jnp.bfloat16)
    layer_pre = matmul_last(feed_round, gate_layer_full)
    layer_input = per_layer.astype(jnp.float32)
    layer_value, layer_back = jax.vjp(gated_product, layer_pre, layer_input)
    layer_low = layer_value.astype(jnp.bfloat16)
    projected = matmul_last(layer_low, proj_layer_full)
    out_value, final_back = jax.vjp(final_join, after_feed, projected, norm_gains)
    square_sums = jnp.stack(
        [
            jnp.sum(keep_mask * residual * residual),
            jnp.sum(keep_mask * after_attention * after_attention),
            jnp.sum(keep_mask * after_feed * after_feed),
            jnp.sum(keep_mask * out_value * out_value),
        ]
    )
    valid_count = jnp.sum(all_lengths).astype(jnp.float32)
    cotangent = out_grad.astype(jnp.float32) * keep_mask
    grad_feed_out, grad_projected, gains_final = final_back(cotangent)
    projected_low = grad_projected.astype(jnp.bfloat16)
    grad_proj_layer = outer_sum(layer_low, projected_low)
    grad_layer_pre, grad_layer_input = layer_back(matmul_back(projected_low, proj_layer_full))
    layer_pre_low = grad_layer_pre.astype(jnp.bfloat16)
    grad_gate_layer = outer_sum(feed_round, layer_pre_low)
    grad_after_feed = grad_feed_out + matmul_back(layer_pre_low, gate_layer_full)
    grad_after_attention_a, grad_summed, gains_feed = feed_back(grad_after_feed)
    summed_low = grad_summed.astype(jnp.bfloat16)
    block_rows = lax.all_gather(summed_low, "col", axis=0, tiled=True)
    grad_down = outer_sum(units_low, block_rows)
    grad_units = matmul_back(block_rows, down_rows)
    grad_down, grad_units = (grad_down, grad_units)
    grad_gate_value, grad_up_value = gate_back(grad_units)
    grad_paired = jnp.concatenate([grad_gate_value, grad_up_value], axis=-1).astype(jnp.bfloat16)
    grad_weights_paired = outer_sum(
        lax.all_gather(feed_low, "col", axis=0, tiled=True), grad_paired
    )
    grad_feed = lax.psum_scatter(
        matmul_back(grad_paired, paired).astype(jnp.bfloat16),
        "col",
        scatter_dimension=0,
        tiled=True,
    ).astype(jnp.float32)
    grad_residual_mid, grad_out_proj, grad_low_rank, grad_normed_mid, gains_middle = middle_back(
        (grad_after_attention_a, grad_feed)
    )
    out_proj_low = grad_out_proj.astype(jnp.bfloat16)
    grad_output = outer_sum(mixed_low, out_proj_low)
    grad_mixed = matmul_back(out_proj_low, output_full).astype(jnp.bfloat16)
    grad_mixed = grad_mixed.reshape(local_rows, seq_groups, KV, H // KV, HD)
    low_rank_grad = grad_low_rank.astype(jnp.bfloat16)
    grad_right = outer_sum(laurel_mid, low_rank_grad)
    grad_laurel_mid = matmul_back(low_rank_grad, right_full).astype(jnp.bfloat16)
    grad_left = outer_sum(normed_low, grad_laurel_mid)
    scores = score_all()
    attn_prob = jnp.exp(scores - log_total)
    grad_prob = jnp.einsum(
        "psjgd,esjd->sjgpe", grad_mixed, near_values, preferred_element_type=jnp.float32
    )
    grad_scores = (
        attn_prob * (grad_prob - jnp.sum(attn_prob * grad_prob, axis=-1, keepdims=True))
    ).astype(jnp.bfloat16)
    grad_queries = (
        jnp.einsum("sjgpe,esjd->psjgd", grad_scores, near_keys, preferred_element_type=jnp.float32)
        * score_scale
    )
    grad_near_keys = (
        jnp.einsum("sjgpe,psjgd->esjd", grad_scores, query_low, preferred_element_type=jnp.float32)
        * score_scale
    )
    grad_near_values = jnp.einsum(
        "sjgpe,psjgd->esjd",
        attn_prob.astype(jnp.bfloat16),
        grad_mixed,
        preferred_element_type=jnp.float32,
    )
    grad_key_total = grad_near_keys[reach_back * local_rows : (reach_back + 1) * local_rows]
    grad_value_total = grad_near_values[reach_back * local_rows : (reach_back + 1) * local_rows]
    for slot_index, offset in enumerate(offsets):
        if offset != 0:
            piece_keys = grad_near_keys[slot_index * local_rows : (slot_index + 1) * local_rows]
            piece_values = grad_near_values[slot_index * local_rows : (slot_index + 1) * local_rows]
            back_keys, back_values = (
                passed_along(piece_keys.astype(jnp.bfloat16), "col", -offset).astype(
                    piece_keys.dtype
                ),
                passed_along(piece_values.astype(jnp.bfloat16), "col", -offset).astype(
                    piece_values.dtype
                ),
            )
            grad_key_total = grad_key_total + back_keys
            grad_value_total = grad_value_total + back_values
    grad_query_raw, grad_key_raw, grad_value_raw, grad_heads = head_back(
        (grad_queries.reshape(local_rows, seq_groups, H, HD), grad_key_total, grad_value_total)
    )
    query_grad_low = grad_query_raw.reshape(local_rows, seq_groups, H * HD).astype(jnp.bfloat16)
    key_grad_low = grad_key_raw.reshape(local_rows, seq_groups, KV * HD).astype(jnp.bfloat16)
    value_grad_low = grad_value_raw.reshape(local_rows, seq_groups, KV * HD).astype(jnp.bfloat16)
    grad_query = outer_sum(normed_low, query_grad_low)
    grad_key = outer_sum(normed_low, key_grad_low)
    grad_value = outer_sum(normed_low, value_grad_low)
    grad_normed = (
        grad_normed_mid
        + matmul_back(grad_laurel_mid, left_full)
        + matmul_back(query_grad_low, query_full)
        + matmul_back(key_grad_low, key_full)
        + matmul_back(value_grad_low, value_full)
    )
    grad_residual_in, gains_input = input_back(grad_normed)
    d_hidden = (grad_residual_mid + grad_residual_in).astype(jnp.bfloat16)
    d_per_layer = grad_layer_input.astype(jnp.bfloat16)
    grad_gains = gains_final + gains_feed + gains_middle + gains_input
    grad_gate = grad_weights_paired[:, :unit_width]
    grad_up = grad_weights_paired[:, unit_width:]
    (
        query_part,
        key_part,
        value_part,
        output_part,
        left_part,
        right_part,
        gate_layer_part,
        proj_layer_part,
    ) = (
        lax.psum_scatter(
            grad_query.astype(jnp.bfloat16), "col", scatter_dimension=1, tiled=True
        ).astype(jnp.float32),
        lax.psum_scatter(
            grad_key.astype(jnp.bfloat16), "col", scatter_dimension=1, tiled=True
        ).astype(jnp.float32),
        lax.psum_scatter(
            grad_value.astype(jnp.bfloat16), "col", scatter_dimension=1, tiled=True
        ).astype(jnp.float32),
        lax.psum_scatter(
            grad_output.astype(jnp.bfloat16), "col", scatter_dimension=0, tiled=True
        ).astype(jnp.float32),
        lax.psum_scatter(
            grad_left.astype(jnp.bfloat16), "col", scatter_dimension=1, tiled=True
        ).astype(jnp.float32),
        lax.psum_scatter(
            grad_right.astype(jnp.bfloat16), "col", scatter_dimension=0, tiled=True
        ).astype(jnp.float32),
        lax.psum_scatter(
            grad_gate_layer.astype(jnp.bfloat16), "col", scatter_dimension=1, tiled=True
        ).astype(jnp.float32),
        lax.psum_scatter(
            grad_proj_layer.astype(jnp.bfloat16), "col", scatter_dimension=0, tiled=True
        ).astype(jnp.float32),
    )
    (
        d_query_weight,
        d_key_weight,
        d_value_weight,
        d_output_weight,
        d_gate_weight,
        d_up_weight,
        d_down_weight,
        d_laurel_left,
        d_laurel_right,
        d_layer_gate,
        d_layer_proj,
    ) = (
        lax.psum_scatter(
            query_part.astype(jnp.bfloat16), "row", scatter_dimension=0, tiled=True
        ).astype(jnp.float32),
        lax.psum_scatter(
            key_part.astype(jnp.bfloat16), "row", scatter_dimension=0, tiled=True
        ).astype(jnp.float32),
        lax.psum_scatter(
            value_part.astype(jnp.bfloat16), "row", scatter_dimension=0, tiled=True
        ).astype(jnp.float32),
        lax.psum_scatter(
            output_part.astype(jnp.bfloat16), "row", scatter_dimension=1, tiled=True
        ).astype(jnp.float32),
        lax.psum_scatter(
            grad_gate.astype(jnp.bfloat16), "row", scatter_dimension=0, tiled=True
        ).astype(jnp.float32),
        lax.psum_scatter(
            grad_up.astype(jnp.bfloat16), "row", scatter_dimension=0, tiled=True
        ).astype(jnp.float32),
        lax.psum_scatter(
            grad_down.astype(jnp.bfloat16), "row", scatter_dimension=1, tiled=True
        ).astype(jnp.float32),
        lax.psum_scatter(
            left_part.astype(jnp.bfloat16), "row", scatter_dimension=0, tiled=True
        ).astype(jnp.float32),
        lax.psum_scatter(
            right_part.astype(jnp.bfloat16), "row", scatter_dimension=1, tiled=True
        ).astype(jnp.float32),
        lax.psum_scatter(
            gate_layer_part.astype(jnp.bfloat16), "row", scatter_dimension=0, tiled=True
        ).astype(jnp.float32),
        lax.psum_scatter(
            proj_layer_part.astype(jnp.bfloat16), "row", scatter_dimension=1, tiled=True
        ).astype(jnp.float32),
    )
    d_norm_gains, d_head_gains, total_squares = lax.psum(
        (grad_gains, grad_heads, square_sums), ("row", "col")
    )
    stats = jnp.sqrt(total_squares / (valid_count * D))
    output = out_value.astype(jnp.bfloat16)
    return (
        output,
        stats,
        d_hidden,
        d_per_layer,
        d_query_weight,
        d_key_weight,
        d_value_weight,
        d_output_weight,
        d_gate_weight,
        d_up_weight,
        d_down_weight,
        d_laurel_left,
        d_laurel_right,
        d_layer_gate,
        d_layer_proj,
        d_norm_gains,
        d_head_gains,
    )


def swap(array):
    return jnp.swapaxes(array, 0, 1)


def heads_body(
    hidden,
    per_layer,
    lengths,
    block_ids,
    out_grad,
    query_weight,
    key_weight,
    value_weight,
    output_weight,
    gate_weight,
    up_weight,
    down_weight,
    laurel_left,
    laurel_right,
    layer_gate,
    layer_proj,
    norm_gains,
    head_gains,
):
    low = jnp.bfloat16
    rows = hidden.shape[0]
    groups = hidden.shape[1]
    cols = lax.axis_size("col")
    seq = rows * cols
    share = cols // KV
    col_index = lax.axis_index("col")
    row_index = lax.axis_index("row")
    all_lengths = lengths
    lengths = lax.dynamic_slice_in_dim(all_lengths, row_index * groups, groups, 0)

    small = jnp.concatenate(
        [key_weight.T, value_weight.T, laurel_left.T, layer_gate.T, laurel_right, layer_proj],
        axis=0,
    )
    heights = [key_weight.shape[1], value_weight.shape[1], laurel_left.shape[1]]
    heights += [layer_gate.shape[1], laurel_right.shape[0], layer_proj.shape[0]]
    edges = [sum(heights[:i]) for i in range(len(heights) + 1)]
    unit_width = gate_weight.shape[1]
    residual = swap(hidden).astype(jnp.float32)
    normed_value, input_back = jax.vjp(input_norm, residual, norm_gains)
    normed_low = normed_value.astype(low)
    tiers = lax.axis_size("row")
    normed_all, small_row, query_full, output_full = open_all(
        normed_low, small, query_weight, output_weight, tiers, 1
    )
    small_all = share_small(small_row, heights[0] + heights[1], 8)
    both_weights = jnp.concatenate([gate_weight, up_weight], axis=1)
    paired = lax.all_gather(after(both_weights, normed_all), "row", axis=0, tiled=True)
    down_full = lax.all_gather(after(down_weight, normed_all), "row", axis=1, tiled=True)
    query_full = query_full.reshape(D, HD).T
    output_full = jnp.swapaxes(output_full, 0, 1).reshape(HD, D)
    pieces = [small_all[:, :, a:b] for a, b in zip(edges[:-1], edges[1:])]
    group_start = (col_index // share) * share

    def joined(piece):
        return jnp.swapaxes(piece, 1, 2).reshape(-1, D)

    key_full, value_full = (
        joined(lax.dynamic_slice_in_dim(piece, group_start, share, 0)) for piece in pieces[:2]
    )
    left_full, gate_layer_full, right_full, proj_layer_full = (
        joined(piece) for piece in pieces[2:]
    )
    head_weights = jnp.concatenate([query_full, key_full, value_full], axis=0)

    positions = jnp.arange(seq, dtype=jnp.int32)
    mine = col_index * rows + jnp.arange(rows, dtype=jnp.int32)
    keep_mask = (mine[None, :] < lengths[:, None]).astype(jnp.float32)[:, :, None]
    live = positions[None, :] < lengths[:, None]
    distance = positions[:, None] - positions[None, :]
    nearby = (block_ids[:, :, None] >= block_ids[:, None, :]) & (distance < WINDOW)[None]
    nearby = nearby & live[:, :, None] & live[:, None, :]
    visible = nearby | (distance == 0)[None]

    half_width = HD // 2
    frequency = jnp.exp(jnp.arange(half_width, dtype=jnp.float32) * (-2.0 * math.log(10000.0) / HD))
    angles = (positions.astype(jnp.float32)[:, None] * frequency[None, :])[None]

    def prepare(query_in, key_in, value_in, gain_rows):
        return (
            rotate(root_norm(query_in, gain_rows[0]), angles),
            rotate(root_norm(key_in, gain_rows[1]), angles),
            plain_norm(value_in),
        )

    head_raw = matmul_back(normed_all, head_weights)
    query_raw, key_raw, value_raw = jnp.split(head_raw, 3, axis=-1)
    (query_value, key_value, value_value), head_back = jax.vjp(
        prepare, query_raw, key_raw, value_raw, head_gains
    )
    query_low = query_value.astype(low)
    key_low = key_value.astype(low)
    value_low = value_value.astype(low)
    score_scale = HD ** (-0.5)

    def score_all():
        raw_scores = (
            jnp.einsum("spd,sed->spe", query_low, key_low, preferred_element_type=jnp.float32)
            * score_scale
        )
        return jnp.where(visible, raw_scores, NEGATIVE)

    scores = score_all()
    row_max = jnp.max(scores, axis=-1, keepdims=True)
    exponent = jnp.exp(scores - row_max)
    row_total = jnp.sum(exponent, axis=-1, keepdims=True)
    attn_prob = exponent / row_total
    log_total = row_max + jnp.log(row_total)
    mixed_low = jnp.einsum(
        "spe,sed->spd", attn_prob.astype(low), value_low, preferred_element_type=jnp.float32
    ).astype(low)
    out_proj = product_sum(mixed_low, output_full, False, 2)
    laurel_mid = matmul_back(normed_low, left_full).astype(low)
    low_rank = matmul_last(laurel_mid, right_full)
    (after_attention, feed_normed), middle_back = jax.vjp(
        middle, residual, out_proj, low_rank, normed_low.astype(jnp.float32), norm_gains
    )
    feed_all = spread(feed_normed.astype(low), 0)
    gate_value = matmul_last(feed_all, paired[:, :unit_width])
    up_value = matmul_last(feed_all, paired[:, unit_width:])
    units_low = gated_product(gate_value, up_value).astype(low)
    summed = product_sum(units_low, down_full, False, 5)
    after_feed, feed_back = jax.vjp(feed_join, after_attention, summed, norm_gains)
    feed_round = after_feed.astype(low)
    layer_pre = matmul_back(feed_round, gate_layer_full)
    layer_input = swap(per_layer).astype(jnp.float32)
    layer_value, layer_back = jax.vjp(gated_product, layer_pre, layer_input)
    layer_low = layer_value.astype(low)
    projected = matmul_last(layer_low, proj_layer_full)
    out_value, final_back = jax.vjp(final_join, after_feed, projected, norm_gains)
    square_sums = jnp.stack(
        [
            jnp.sum(keep_mask * residual * residual),
            jnp.sum(keep_mask * after_attention * after_attention),
            jnp.sum(keep_mask * after_feed * after_feed),
            jnp.sum(keep_mask * out_value * out_value),
        ]
    )
    valid_count = jnp.sum(all_lengths).astype(jnp.float32)

    cotangent = swap(out_grad).astype(jnp.float32) * keep_mask
    grad_feed_out, grad_projected, gains_final = final_back(cotangent)
    projected_low = grad_projected.astype(low)
    grad_proj_layer = outer_sum(layer_low, projected_low)
    grad_layer_pre, grad_layer_input = layer_back(matmul_back(projected_low, proj_layer_full))
    layer_pre_low = grad_layer_pre.astype(low)
    grad_gate_layer = outer_sum(layer_pre_low, feed_round)
    grad_after_feed = grad_feed_out + matmul_last(layer_pre_low, gate_layer_full)
    grad_after_attention_a, grad_summed, gains_feed = feed_back(grad_after_feed)
    grad_paired, grad_down = units_back(
        grad_summed.astype(low), down_full, units_low, gate_value, up_value, 9
    )
    d_down_weight = lax.psum_scatter(
        grad_down, "row", scatter_dimension=1, tiled=True
    ).astype(jnp.float32)
    grad_gate = outer_sum(feed_all, grad_paired[..., :unit_width]).astype(low)
    d_gate_weight = lax.psum_scatter(
        grad_gate, "row", scatter_dimension=0, tiled=True
    ).astype(jnp.float32)
    grad_feed = product_sum(after(grad_paired, grad_gate), paired, True, 6)
    grad_up = outer_sum(feed_all, after(grad_paired, grad_feed)[..., unit_width:]).astype(low)
    d_up_weight = lax.psum_scatter(
        grad_up, "row", scatter_dimension=0, tiled=True
    ).astype(jnp.float32)
    grad_feed = after(grad_feed, grad_up)
    grad_residual_mid, grad_out_proj, grad_low_rank, grad_normed_mid, gains_middle = middle_back(
        (grad_after_attention_a, grad_feed)
    )
    out_proj_all = spread(after(grad_out_proj.astype(low), d_down_weight), 0)
    grad_mixed = matmul_back(out_proj_all, output_full).astype(low)
    low_rank_grad = grad_low_rank.astype(low)
    grad_right = outer_sum(laurel_mid, low_rank_grad)
    grad_laurel_mid = matmul_back(low_rank_grad, right_full).astype(low)
    grad_left = outer_sum(grad_laurel_mid, normed_low)
    attn_prob = jnp.exp(score_all() - log_total)
    grad_prob = jnp.einsum(
        "spd,sed->spe", grad_mixed, value_low, preferred_element_type=jnp.float32
    )
    grad_scores = (
        attn_prob * (grad_prob - jnp.sum(attn_prob * grad_prob, axis=-1, keepdims=True))
    ).astype(low)
    grad_queries = (
        jnp.einsum("spe,sed->spd", grad_scores, key_low, preferred_element_type=jnp.float32)
        * score_scale
    )
    grad_keys = (
        jnp.einsum("spe,spd->sed", grad_scores, query_low, preferred_element_type=jnp.float32)
        * score_scale
    )
    grad_values = jnp.einsum(
        "spe,spd->sed", attn_prob.astype(low), grad_mixed, preferred_element_type=jnp.float32
    )
    grad_query_raw, grad_key_raw, grad_value_raw, grad_heads = head_back(
        (grad_queries, grad_keys, grad_values)
    )
    head_grads = jnp.concatenate([grad_query_raw, grad_key_raw, grad_value_raw], axis=-1)
    head_grads = head_grads.astype(low)
    grad_head_weights = outer_sum(head_grads, normed_all).astype(low)
    grad_query, grad_key, grad_value = jnp.split(grad_head_weights, 3, axis=0)
    grad_output = outer_sum(mixed_low, after(out_proj_all, head_grads)).astype(low)
    grad_group = jnp.concatenate(
        [grad_key.reshape(share, -1, D), grad_value.reshape(share, -1, D)], axis=1
    )
    grad_rest = jnp.concatenate(
        [
            piece.astype(low).reshape(cols, -1, D)
            for piece in (grad_left, grad_gate_layer, grad_right, grad_proj_layer)
        ],
        axis=1,
    )
    half = grad_rest.shape[1] // 2
    grad_rest = jnp.swapaxes(grad_rest.reshape(cols, 2, half, D), 0, 1)
    grad_group = after(grad_group, d_gate_weight)
    rest_part, group_part = fold_small(grad_rest.reshape(2, cols * half, D), grad_group, 3)
    parts = jnp.concatenate(
        [grad_output, grad_query, group_part.astype(low), rest_part.astype(low).reshape(-1, D)],
        axis=0,
    )
    parts_out = lax.psum_scatter(parts, "row", scatter_dimension=1, tiled=True).astype(jnp.float32)
    d_output_weight = parts_out[:HD]
    d_query_weight = parts_out[HD : 2 * HD].T
    small_out = parts_out[2 * HD :]
    small_parts = [small_out[a:b] for a, b in zip(edges[:-1], edges[1:])]
    grad_normed = product_sum(after(head_grads, parts, d_up_weight), head_weights, False, 7)
    grad_normed = grad_normed + grad_normed_mid + matmul_last(grad_laurel_mid, left_full)
    grad_residual_in, gains_input = input_back(grad_normed)
    d_hidden = swap((grad_residual_mid + grad_residual_in).astype(low))
    d_per_layer = swap(grad_layer_input.astype(low))
    grad_gains = gains_final + gains_feed + gains_middle + gains_input
    extra = jnp.concatenate([grad_heads.reshape(-1), square_sums])
    extra = jnp.pad(extra, (0, 2 * D - extra.shape[0])).reshape(2, D)
    totals = total(jnp.concatenate([grad_gains, extra], axis=0), tiers, 4)
    d_norm_gains = totals[:6]
    d_head_gains = totals[6, : 2 * HD].reshape(2, HD)
    total_squares = totals[6, 2 * HD : 2 * HD + 4]
    stats = jnp.sqrt(total_squares / (valid_count * D))
    output = swap(out_value.astype(low))
    return (
        output,
        stats,
        d_hidden,
        d_per_layer,
        d_query_weight,
        small_parts[0].T,
        small_parts[1].T,
        d_output_weight,
        d_gate_weight,
        d_up_weight,
        d_down_weight,
        small_parts[2].T,
        small_parts[4],
        small_parts[3].T,
        small_parts[5],
        d_norm_gains,
        d_head_gains,
    )


def solution(mesh):
    body = heads_body if mesh.shape["col"] == H else general_body
    in_specs = (
        P("col", "row", None),
        P("col", "row", None),
        P(),
        P("row", None),
        P("col", "row", None),
        P("row", "col"),
        P("row", "col"),
        P("row", "col"),
        P("col", "row"),
        P("row", "col"),
        P("row", "col"),
        P("col", "row"),
        P("row", "col"),
        P("col", "row"),
        P("row", "col"),
        P("col", "row"),
        P(),
        P(),
    )
    out_specs = (
        P("col", "row", None),
        P(),
        P("col", "row", None),
        P("col", "row", None),
        P("row", "col"),
        P("row", "col"),
        P("row", "col"),
        P("col", "row"),
        P("row", "col"),
        P("row", "col"),
        P("col", "row"),
        P("row", "col"),
        P("col", "row"),
        P("row", "col"),
        P("col", "row"),
        P(),
        P(),
    )
    return jax.shard_map(body, mesh=mesh, in_specs=in_specs, out_specs=out_specs, check_vma=False)
```

```python
import functools
import math

import jax
import jax.numpy as jnp
from jax import lax
from jax.experimental import pallas as pl
from jax.experimental.pallas import tpu as pltpu
from jax.sharding import PartitionSpec as P

D = 2048
H = 8
KV = 2
HD = 256
WINDOW = 512
BLOCK = 256


EPSILON = 1e-06
FAR_BLOCK = 1 << 30
NEGATIVE = -1e30
HALF_ROOT = 1.0 / math.sqrt(2.0)
CURVE = math.sqrt(2.0 / math.pi)
BEND = 0.044715


MESH = pl.DeviceIdType.MESH


def passed_along(value, axis, steps):
    count = lax.axis_size(axis)
    initial, last = (max(0, -steps), min(count, count - steps))
    return lax.ppermute(value, axis, [(source, source + steps) for source in range(initial, last)])


def root_norm(values, gain_row):
    return (
        values * lax.rsqrt(jnp.mean(values * values, axis=-1, keepdims=True) + EPSILON) * gain_row
    )


def plain_norm(values):
    return values * lax.rsqrt(jnp.mean(values * values, axis=-1, keepdims=True) + EPSILON)


def smooth_gate(values):
    return jax.nn.gelu(values, approximate=True)


def rotate(values, angles):
    half_width = values.shape[-1] // 2
    leading = values[..., :half_width]
    trailing = values[..., half_width:]
    cosine = jnp.cos(angles)
    sine_part = jnp.sin(angles)
    return jnp.concatenate(
        [leading * cosine - trailing * sine_part, trailing * cosine + leading * sine_part], axis=-1
    )


def matmul_last(first_array, second_array):
    return lax.dot_general(
        first_array,
        second_array,
        (((first_array.ndim - 1,), (0,)), ((), ())),
        preferred_element_type=jnp.float32,
    )


def matmul_back(first_array, second_array):
    return lax.dot_general(
        first_array,
        second_array,
        (((first_array.ndim - 1,), (1,)), ((), ())),
        preferred_element_type=jnp.float32,
    )


def outer_sum(first_array, second_array):
    return lax.dot_general(
        first_array, second_array, (((0, 1), (0, 1)), ((), ())), preferred_element_type=jnp.float32
    )


def input_norm(residual, gain_rows):
    return root_norm(residual, gain_rows[0])


def middle(residual, out_proj, low_rank, normed, gain_rows):
    merged = (
        residual + root_norm(out_proj, gain_rows[1]) + normed + root_norm(low_rank, gain_rows[4])
    ) * HALF_ROOT
    return (merged, root_norm(merged, gain_rows[2]))


def feed_join(merged, summed, gain_rows):
    return merged + root_norm(summed, gain_rows[3])


def final_join(merged, projected, gain_rows):
    return merged + root_norm(projected, gain_rows[5])


def gated_product(first_array, second_array):
    return smooth_gate(first_array) * second_array


def partners():
    c = lax.axis_index("col")
    sib = c + 1 - 2 * (c % 2)
    xn = c + 2 - 4 * ((c // 2) % 2)
    yn = c + 4 - 8 * (c // 4)
    return c, sib, xn, yn

def greet(devs):
    barrier = pltpu.get_barrier_semaphore()
    for d in devs:
        pl.semaphore_signal(barrier, inc=1, device_id={"col": d}, device_id_type=MESH)
    pl.semaphore_wait(barrier, len(devs))

def spread_kernel(rows, x_ref, o_ref, local_sem, send, recv):
    c, sib, xn, yn = partners()
    def slot(half, who):
        return o_ref.at[half, pl.ds(pl.multiple_of(who * rows, rows), rows), :]
    def both(who):
        return o_ref.at[:, pl.ds(pl.multiple_of(who * rows, rows), rows), :]
    def push(i, src, dst, dev):
        return pltpu.make_async_remote_copy(src_ref=src, dst_ref=dst, send_sem=send.at[i], recv_sem=recv.at[i], device_id={"col": dev}, device_id_type=MESH)
    mine = pltpu.make_async_copy(x_ref, both(c), local_sem)
    mine.start()
    greet((sib, xn, yn))
    x0 = push(0, x_ref.at[0], slot(0, c), xn)
    y1 = push(1, x_ref.at[1], slot(1, c), yn)
    x1 = push(2, x_ref.at[1], slot(1, c), xn)
    y0 = push(3, x_ref.at[0], slot(0, c), yn)
    s = push(4, x_ref, both(c), sib)
    x0.start(); y1.start(); x1.start(); y0.start(); s.start()
    diag = yn + (xn - c)
    x0.wait_recv()
    fy = push(5, slot(0, xn), slot(0, xn), yn)
    fy.start()
    sx0 = push(6, slot(0, xn), slot(0, xn), sib)
    sx0.start()
    y1.wait_recv()
    fx = push(7, slot(1, yn), slot(1, yn), xn)
    fx.start()
    sy1 = push(8, slot(1, yn), slot(1, yn), sib)
    sy1.start()
    x1.wait_recv()
    sx1 = push(9, slot(1, xn), slot(1, xn), sib)
    sx1.start()
    y0.wait_recv()
    sy0 = push(10, slot(0, yn), slot(0, yn), sib)
    sy0.start()
    fy.wait_recv()
    sd0 = push(11, slot(0, diag), slot(0, diag), sib)
    sd0.start()
    fx.wait_recv()
    sd1 = push(12, slot(1, diag), slot(1, diag), sib)
    sd1.start()
    for cp in (s, sx0, sy1, sx1, sy0, sd0, sd1):
        cp.wait_recv()
    for cp in (x0, y1, x1, y0, s, fy, sx0, fx, sy1, sx1, sy0, sd0, sd1):
        cp.wait_send()
    mine.wait()

def spread(x, cid=0):
    h, rows, d = x.shape
    return pl.pallas_call(
        functools.partial(spread_kernel, rows),
        out_shape=jax.ShapeDtypeStruct((h, 8 * rows, d), x.dtype),
        in_specs=[pl.BlockSpec(memory_space=pl.ANY)],
        out_specs=pl.BlockSpec(memory_space=pl.ANY),
        scratch_shapes=[pltpu.SemaphoreType.DMA, pltpu.SemaphoreType.DMA((13,)), pltpu.SemaphoreType.DMA((13,))],
        compiler_params=pltpu.CompilerParams(collective_id=cid, has_side_effects=True),
        cost_estimate=pl.CostEstimate(flops=0, bytes_accessed=120_000_000, transcendentals=0),
        name="spread",
    )(x)

def fold_steps(rows, p_ref, own, sibs, dx, dy, rx, ry, local_sem, send, recv):
    c, sib, xn, yn = partners()
    diag = yn + (xn - c)
    wide = jnp.float32
    tall = 32 if rows % 32 == 0 else 8

    def blk(who):
        return p_ref.at[:, pl.ds(pl.multiple_of(who * rows, rows), rows), :]

    def push(i, src, dst, dev):
        return pltpu.make_async_remote_copy(
            src_ref=src,
            dst_ref=dst,
            send_sem=send.at[i],
            recv_sem=recv.at[i],
            device_id={"col": dev},
            device_id_type=MESH,
        )

    def add(dst, src):
        @pl.loop(0, rows // tall)
        def _(i):
            r = pl.ds(pl.multiple_of(i * tall, tall), tall)
            dst[r, :] = (dst[r, :].astype(wide) + src[r, :].astype(wide)).astype(dst.dtype)

    def pair(j):
        add(own.at[j, 0], sibs.at[j, 0])
        add(own.at[j, 1], sibs.at[j, 1])

    dests = (diag, xn, yn, c)
    loads = [pltpu.make_async_copy(blk(d), own.at[j], local_sem.at[j]) for j, d in enumerate(dests)]
    for load in loads:
        load.start()
    yield None
    sides = [push(j, blk(d + (sib - c)), sibs.at[j], sib) for j, d in enumerate(dests)]
    for side in sides:
        side.start()
    yield None
    loads[0].wait()
    sides[0].wait_recv()
    pair(0)
    a = push(4, own.at[0, 0], dx, xn)
    b = push(5, own.at[0, 1], dy, yn)
    a.start()
    b.start()
    yield None
    loads[1].wait()
    sides[1].wait_recv()
    pair(1)
    x0 = push(6, own.at[1, 0], rx.at[0], xn)
    x0.start()
    yield None
    loads[2].wait()
    sides[2].wait_recv()
    pair(2)
    y1 = push(7, own.at[2, 1], ry.at[1], yn)
    y1.start()
    yield None
    a.wait_recv()
    add(own.at[2, 0], dx)
    y0 = push(8, own.at[2, 0], ry.at[0], yn)
    y0.start()
    yield None
    b.wait_recv()
    add(own.at[1, 1], dy)
    x1 = push(9, own.at[1, 1], rx.at[1], xn)
    x1.start()
    yield None
    loads[3].wait()
    sides[3].wait_recv()
    pair(3)
    yield None
    waits = ((x0, y0), (x1, y1))
    yield tall, waits, (*sides, a, b, x0, y1, y0, x1)


def fold_finish(rows, o_ref, own, rx, ry, tall, waits, sent):
    wide = jnp.float32
    for h in range(2):
        for copy in waits[h]:
            copy.wait_recv()

        @pl.loop(0, rows // tall)
        def _(i):
            r = pl.ds(pl.multiple_of(i * tall, tall), tall)
            o_ref[h, r, :] = (
                own[3, h, r, :].astype(wide) + rx[h, r, :].astype(wide) + ry[h, r, :].astype(wide)
            )

    for copy in sent:
        copy.wait_send()


def fold_scratch(h, rows, d, kind):
    return [
        pltpu.VMEM((4, h, rows, d), kind),
        pltpu.VMEM((4, h, rows, d), kind),
        pltpu.VMEM((rows, d), kind),
        pltpu.VMEM((rows, d), kind),
        pltpu.VMEM((h, rows, d), kind),
        pltpu.VMEM((h, rows, d), kind),
        pltpu.SemaphoreType.DMA((4,)),
        pltpu.SemaphoreType.DMA((10,)),
        pltpu.SemaphoreType.DMA((10,)),
    ]


def product_kernel(
    rows, flip, a_ref, w_ref, o_ref, a_buf, w_buf, stage, own, sibs, dx, dy, rx, ry,
    local_sem, send, recv,
):
    c, sib, xn, yn = partners()
    diag = yn + (xn - c)
    wide = jnp.float32
    d = o_ref.shape[-1]
    tile = 512
    tall = 32

    def push(i, src, dst, dev):
        return pltpu.make_async_remote_copy(
            src_ref=src,
            dst_ref=dst,
            send_sem=send.at[i],
            recv_sem=recv.at[i],
            device_id={"col": dev},
            device_id_type=MESH,
        )

    dests = (diag, xn, yn, c)
    step = sib - c
    weights = pltpu.make_async_copy(w_ref, w_buf, local_sem.at[8])
    weights.start()

    def load(i, who):
        return pltpu.make_async_copy(
            a_ref.at[:, pl.ds(pl.multiple_of(who * rows, rows), rows), :],
            a_buf.at[i],
            local_sem.at[i],
        )

    far = [load(j, dests[j] + step) for j in range(4)]
    near = [load(4 + j, dests[j]) for j in range(4)]
    for first, second in zip(far, near):
        first.start()
        second.start()
    greet((sib, xn, yn))
    weights.wait()

    def product(i, put):
        left = a_buf[i].reshape(2 * rows, a_buf.shape[-1])

        @pl.loop(0, d // tile)
        def _(n):
            cut = pl.ds(pl.multiple_of(n * tile, tile), tile)
            right = w_buf[cut, :] if flip else w_buf[:, cut]
            dims = (((1,), (1,)), ((), ())) if flip else (((1,), (0,)), ((), ()))
            value = lax.dot_general(left, right, dims, preferred_element_type=wide)
            put(cut, value.reshape(2, rows, tile))

    sides = [push(j, stage.at[j], sibs.at[j], sib) for j in range(4)]

    def for_sibling(j):
        far[j].wait()

        def put(cut, value):
            stage[j, :, :, cut] = value.astype(stage.dtype)

        product(j, put)
        sides[j].start()

    def for_chip(j):
        near[j].wait()
        sides[j].wait_recv()

        def put(cut, value):
            own[j, :, :, cut] = (value + sibs[j, :, :, cut].astype(wide)).astype(own.dtype)

        product(4 + j, put)

    def add(dst, src):
        @pl.loop(0, rows // tall)
        def _(i):
            r = pl.ds(pl.multiple_of(i * tall, tall), tall)
            dst[r, :] = (dst[r, :].astype(wide) + src[r, :].astype(wide)).astype(dst.dtype)

    for_sibling(0)
    for_sibling(1)
    for_chip(0)
    a = push(4, own.at[0, 0], dx, xn)
    b = push(5, own.at[0, 1], dy, yn)
    a.start()
    b.start()
    for_sibling(2)
    for_chip(1)
    x0 = push(6, own.at[1, 0], rx.at[0], xn)
    x0.start()
    for_sibling(3)
    for_chip(2)
    y1 = push(7, own.at[2, 1], ry.at[1], yn)
    y1.start()
    a.wait_recv()
    add(own.at[2, 0], dx)
    y0 = push(8, own.at[2, 0], ry.at[0], yn)
    y0.start()
    b.wait_recv()
    add(own.at[1, 1], dy)
    x1 = push(9, own.at[1, 1], rx.at[1], xn)
    x1.start()
    near[3].wait()
    sides[3].wait_recv()

    def put(cut, value):
        o_ref[:, :, cut] = value + sibs[3, :, :, cut].astype(wide)

    product(7, put)
    for h, waits in enumerate(((x0, y0), (x1, y1))):
        for copy in waits:
            copy.wait_recv()

        @pl.loop(0, rows // tall)
        def _(i):
            r = pl.ds(pl.multiple_of(i * tall, tall), tall)
            o_ref[h, r, :] = o_ref[h, r, :] + rx[h, r, :].astype(wide) + ry[h, r, :].astype(wide)

    for copy in (*sides, a, b, x0, y1, y0, x1):
        copy.wait_send()


def product_sum(left, right, flip, cid):
    h, total, depth = left.shape
    rows = total // 8
    d = right.shape[0] if flip else right.shape[1]
    low = left.dtype
    return pl.pallas_call(
        functools.partial(product_kernel, rows, flip),
        out_shape=jax.ShapeDtypeStruct((h, rows, d), jnp.float32),
        in_specs=[pl.BlockSpec(memory_space=pl.ANY)] * 2,
        out_specs=pl.BlockSpec(memory_space=pltpu.VMEM),
        scratch_shapes=[
            pltpu.VMEM((8, h, rows, depth), low),
            pltpu.VMEM(right.shape, low),
            pltpu.VMEM((4, h, rows, d), low),
            pltpu.VMEM((3, h, rows, d), low),
            pltpu.VMEM((4, h, rows, d), low),
            pltpu.VMEM((rows, d), low),
            pltpu.VMEM((rows, d), low),
            pltpu.VMEM((h, rows, d), low),
            pltpu.VMEM((h, rows, d), low),
            pltpu.SemaphoreType.DMA((9,)),
            pltpu.SemaphoreType.DMA((10,)),
            pltpu.SemaphoreType.DMA((10,)),
        ],
        compiler_params=pltpu.CompilerParams(
            collective_id=cid, has_side_effects=True, vmem_limit_bytes=44 << 20
        ),
        cost_estimate=pl.CostEstimate(
            flops=2 * h * total * depth * d, bytes_accessed=130_000_000, transcendentals=0
        ),
        name="product_sum",
    )(left, right)


def fold_small_kernel(
    rows, p_ref, g_ref, o_ref, k_ref, own, sibs, dx, dy, rx, ry, local_sem, send, recv,
    gown, gsibs, grx, glocal, gsend, grecv,
):
    c, sib, xn, yn = partners()
    m = c % 4
    m_sib = m + 1 - 2 * (m % 2)
    m_x = m + 2 - 4 * (m // 2)
    m_diag = m_sib + (m_x - m)
    wide = jnp.float32

    def push(i, src, dst, dev):
        return pltpu.make_async_remote_copy(
            src_ref=src,
            dst_ref=dst,
            send_sem=gsend.at[i],
            recv_sem=grecv.at[i],
            device_id={"col": dev},
            device_id_type=MESH,
        )

    steps = fold_steps(rows, p_ref, own, sibs, dx, dy, rx, ry, local_sem, send, recv)
    next(steps)
    loads = [
        pltpu.make_async_copy(g_ref.at[d], gown.at[j], glocal.at[j])
        for j, d in enumerate((m_x, m))
    ]
    for load in loads:
        load.start()
    greet((sib, xn, yn))
    sides = [push(j, g_ref.at[d], gsibs.at[j], sib) for j, d in enumerate((m_diag, m_sib))]
    sides[0].start()
    next(steps)
    sides[1].start()
    tall = k_ref.shape[0] // 4
    loads[0].wait()
    sides[0].wait_recv()

    @pl.loop(0, 4)
    def _(i):
        r = pl.ds(pl.multiple_of(i * tall, tall), tall)
        gown[0, r, :] = (gown[0, r, :].astype(wide) + gsibs[0, r, :].astype(wide)).astype(
            gown.dtype
        )

    over = push(2, gown.at[0], grx, xn)
    over.start()
    last = None
    for step in steps:
        last = step if step is not None else last
    fold_finish(rows, o_ref, own, rx, ry, *last)
    loads[1].wait()
    sides[1].wait_recv()
    over.wait_recv()

    @pl.loop(0, 4)
    def _(i):
        r = pl.ds(pl.multiple_of(i * tall, tall), tall)
        k_ref[r, :] = (
            gown[1, r, :].astype(wide) + gsibs[1, r, :].astype(wide) + grx[r, :].astype(wide)
        )

    for copy in (*sides, over):
        copy.wait_send()


def fold_small(p, g, cid):
    h, total, d = p.shape
    rows = total // 8
    share, tall, _ = g.shape
    return pl.pallas_call(
        functools.partial(fold_small_kernel, rows),
        out_shape=(
            jax.ShapeDtypeStruct((h, rows, d), jnp.float32),
            jax.ShapeDtypeStruct((tall, d), jnp.float32),
        ),
        in_specs=[pl.BlockSpec(memory_space=pl.ANY)] * 2,
        out_specs=[pl.BlockSpec(memory_space=pltpu.VMEM)] * 2,
        scratch_shapes=fold_scratch(h, rows, d, p.dtype)
        + [
            pltpu.VMEM((2, tall, d), g.dtype),
            pltpu.VMEM((2, tall, d), g.dtype),
            pltpu.VMEM((tall, d), g.dtype),
            pltpu.SemaphoreType.DMA((2,)),
            pltpu.SemaphoreType.DMA((3,)),
            pltpu.SemaphoreType.DMA((3,)),
        ],
        compiler_params=pltpu.CompilerParams(
            collective_id=cid, has_side_effects=True, vmem_limit_bytes=40 << 20
        ),
        cost_estimate=pl.CostEstimate(flops=0, bytes_accessed=60_000_000, transcendentals=0),
        name="fold_small",
    )(p, g)


def open_kernel(
    rows, x_ref, s_ref, q_ref, w_ref, o_ref, sa_ref, qa_ref, wa_ref, local_sem, send, recv
):
    c, sib, xn, yn = partners()
    diag = yn + (xn - c)
    r = lax.axis_index("row")
    tiers = lax.axis_size("row")

    def slot(half, who):
        return o_ref.at[half, pl.ds(pl.multiple_of(who * rows, rows), rows), :]

    def both(who):
        return o_ref.at[:, pl.ds(pl.multiple_of(who * rows, rows), rows), :]

    started = []

    def push(src, dst, **dev):
        i = len(started)
        copy = pltpu.make_async_remote_copy(
            src_ref=src,
            dst_ref=dst,
            send_sem=send.at[i],
            recv_sem=recv.at[i],
            device_id=dev,
            device_id_type=MESH,
        )
        copy.start()
        started.append(copy)
        return copy

    local = [
        pltpu.make_async_copy(x_ref, both(c), local_sem.at[0]),
        pltpu.make_async_copy(s_ref, sa_ref.at[r], local_sem.at[1]),
        pltpu.make_async_copy(q_ref, qa_ref.at[r], local_sem.at[2]),
        pltpu.make_async_copy(w_ref, wa_ref.at[r], local_sem.at[3]),
    ]
    for copy in local:
        copy.start()
    others = [lax.rem(r + k, tiers) for k in range(1, tiers)]
    barrier = pltpu.get_barrier_semaphore()
    for d in (sib, xn, yn):
        pl.semaphore_signal(barrier, inc=1, device_id={"col": d}, device_id_type=MESH)
    for d in others:
        pl.semaphore_signal(barrier, inc=1, device_id={"row": d}, device_id_type=MESH)
    pl.semaphore_wait(barrier, 3 + len(others))
    x0 = push(x_ref.at[0], slot(0, c), col=xn)
    y1 = push(x_ref.at[1], slot(1, c), col=yn)
    for d in others:
        push(s_ref, sa_ref.at[r], row=d)
    x1 = push(x_ref.at[1], slot(1, c), col=xn)
    y0 = push(x_ref.at[0], slot(0, c), col=yn)
    for src, dst in ((q_ref, qa_ref), (w_ref, wa_ref)):
        for d in others:
            push(src, dst.at[r], row=d)
    push(x_ref, both(c), col=sib)
    x0.wait_recv()
    fy = push(slot(0, xn), slot(0, xn), col=yn)
    push(slot(0, xn), slot(0, xn), col=sib)
    y1.wait_recv()
    fx = push(slot(1, yn), slot(1, yn), col=xn)
    push(slot(1, yn), slot(1, yn), col=sib)
    x1.wait_recv()
    push(slot(1, xn), slot(1, xn), col=sib)
    y0.wait_recv()
    push(slot(0, yn), slot(0, yn), col=sib)
    fy.wait_recv()
    push(slot(0, diag), slot(0, diag), col=sib)
    fx.wait_recv()
    push(slot(1, diag), slot(1, diag), col=sib)
    for copy in started:
        if not any(copy is other for other in (x0, y1, x1, y0, fy, fx)):
            copy.wait_recv()
    for copy in started:
        copy.wait_send()
    for copy in local:
        copy.wait()


def open_all(x, small, query, output, tiers, cid):
    h, rows, d = x.shape
    low = x.dtype
    copies = 13 + 3 * (tiers - 1)
    return pl.pallas_call(
        functools.partial(open_kernel, rows),
        out_shape=(
            jax.ShapeDtypeStruct((h, 8 * rows, d), low),
            jax.ShapeDtypeStruct((tiers, *small.shape), low),
            jax.ShapeDtypeStruct((tiers, *query.shape), low),
            jax.ShapeDtypeStruct((tiers, *output.shape), low),
        ),
        in_specs=[pl.BlockSpec(memory_space=pl.ANY)] * 4,
        out_specs=[pl.BlockSpec(memory_space=pl.ANY)] * 4,
        scratch_shapes=[
            pltpu.SemaphoreType.DMA((4,)),
            pltpu.SemaphoreType.DMA((copies,)),
            pltpu.SemaphoreType.DMA((copies,)),
        ],
        compiler_params=pltpu.CompilerParams(collective_id=cid, has_side_effects=True),
        cost_estimate=pl.CostEstimate(flops=0, bytes_accessed=200_000_000, transcendentals=0),
        name="open_all",
    )(x, small, query, output)


def share_kernel(near, s_ref, sa_ref, local_sem, send, recv):
    c, sib, xn, yn = partners()
    diag = yn + (xn - c)
    height = s_ref.shape[1]
    started = []

    def part(ref, first):
        return ref.at[:, pl.ds(0, near) if first else pl.ds(near, height - near), :]

    def push(who, first, dev, own=False):
        i = len(started)
        dst = part(sa_ref.at[who], first)
        copy = pltpu.make_async_remote_copy(
            src_ref=part(s_ref, first) if own else dst,
            dst_ref=dst,
            send_sem=send.at[i],
            recv_sem=recv.at[i],
            device_id={"col": dev},
            device_id_type=MESH,
        )
        copy.start()
        started.append(copy)
        return copy

    mine = pltpu.make_async_copy(s_ref, sa_ref.at[c], local_sem)
    mine.start()
    greet((sib, xn, yn))
    rx = push(c, False, xn, own=True)
    ry = push(c, False, yn, own=True)
    kx = push(c, True, xn, own=True)
    push(c, True, sib, own=True)
    push(c, False, sib, own=True)
    rx.wait_recv()
    fd = push(xn, False, yn)
    push(xn, False, sib)
    ry.wait_recv()
    push(yn, False, sib)
    fd.wait_recv()
    push(diag, False, sib)
    kx.wait_recv()
    push(xn, True, sib)
    for copy in started:
        if not any(copy is other for other in (kx, rx, ry, fd)):
            copy.wait_recv()
    for copy in started:
        copy.wait_send()
    mine.wait()


def share_small(small, near, cid):
    return pl.pallas_call(
        functools.partial(share_kernel, near),
        out_shape=jax.ShapeDtypeStruct((8, *small.shape), small.dtype),
        in_specs=[pl.BlockSpec(memory_space=pl.ANY)],
        out_specs=pl.BlockSpec(memory_space=pl.ANY),
        scratch_shapes=[
            pltpu.SemaphoreType.DMA,
            pltpu.SemaphoreType.DMA((10,)),
            pltpu.SemaphoreType.DMA((10,)),
        ],
        compiler_params=pltpu.CompilerParams(collective_id=cid, has_side_effects=True),
        cost_estimate=pl.CostEstimate(flops=0, bytes_accessed=60_000_000, transcendentals=0),
        name="share_small",
    )(small)


def rounds_of(rows, x_ref, held, local_sem, send, recv, consume, prepare):
    c, sib, xn, yn = partners()
    diag = yn + (xn - c)
    step = sib - c

    def place(t, j, n=1):
        return held.at[t, pl.ds(j * rows, n * rows), :]

    started = []

    def push(src, dst, dev):
        i = len(started)
        copy = pltpu.make_async_remote_copy(
            src_ref=src,
            dst_ref=dst,
            send_sem=send.at[i],
            recv_sem=recv.at[i],
            device_id={"col": dev},
            device_id_type=MESH,
        )
        copy.start()
        started.append(copy)
        return copy

    mine = [pltpu.make_async_copy(x_ref.at[h], place(0, h), local_sem.at[h]) for h in range(2)]
    for copy in mine:
        copy.start()
    greet((sib, xn, yn))
    x0 = push(x_ref.at[0], place(1, 0), xn)
    y1 = push(x_ref.at[1], place(1, 1), yn)
    x1 = push(x_ref.at[1], place(2, 0), xn)
    y0 = push(x_ref.at[0], place(2, 1), yn)
    s0 = push(x_ref.at[0], place(0, 2), sib)
    s1 = push(x_ref.at[1], place(0, 3), sib)
    prepare(0)
    for copy in mine:
        copy.wait()
    s0.wait_recv()
    s1.wait_recv()
    consume(0, ((0, c), (1, c), (0, sib), (1, sib)))
    x0.wait_recv()
    fy = push(place(1, 0), place(3, 0), yn)
    y1.wait_recv()
    fx = push(place(1, 1), place(3, 1), xn)
    prepare(1)
    t1 = push(place(1, 0, 2), place(1, 2, 2), sib)
    t1.wait_recv()
    consume(1, ((0, xn), (1, yn), (0, xn + step), (1, yn + step)))
    prepare(2)
    x1.wait_recv()
    y0.wait_recv()
    t2 = push(place(2, 0, 2), place(2, 2, 2), sib)
    t2.wait_recv()
    consume(2, ((1, xn), (0, yn), (1, xn + step), (0, yn + step)))
    prepare(3)
    fy.wait_recv()
    fx.wait_recv()
    t3 = push(place(3, 0, 2), place(3, 2, 2), sib)
    t3.wait_recv()
    consume(3, ((0, diag), (1, diag), (0, diag + step), (1, diag + step)))
    for copy in started:
        copy.wait_send()


def piece_at(ref, rows, piece):
    half, who = piece
    return ref.at[half, pl.ds(pl.multiple_of(who * rows, rows), rows), :]


def units_back_kernel(
    rows, x_ref, w_ref, u_ref, g_ref, v_ref, p_ref, d_ref,
    held, weights, units, gates, ups, grads, total_ref,
    weight_sem, load_sem, store_sem, local_sem, send, recv,
):
    c, sib, xn, yn = partners()
    diag = yn + (xn - c)
    step = sib - c
    wide = jnp.float32
    width = w_ref.shape[0]
    d = w_ref.shape[1]
    plan = (
        ((0, c), (1, c), (0, sib), (1, sib)),
        ((0, xn), (1, yn), (0, xn + step), (1, yn + step)),
        ((1, xn), (0, yn), (1, xn + step), (0, yn + step)),
        ((0, diag), (1, diag), (0, diag + step), (1, diag + step)),
    )
    fetch = pltpu.make_async_copy(w_ref, weights, weight_sem)
    fetch.start()

    def loads(t):
        copies = []
        for j, piece in enumerate(plan[t]):
            for k, (src, dst) in enumerate(((u_ref, units), (g_ref, gates), (v_ref, ups))):
                copies.append(
                    pltpu.make_async_copy(
                        piece_at(src, rows, piece),
                        dst.at[t % 2, pl.ds(j * rows, rows), :],
                        load_sem.at[t % 2, j, k],
                    )
                )
        return copies

    def stores(t):
        return [
            pltpu.make_async_copy(
                grads.at[t % 2, pl.ds(j * rows, rows), :],
                piece_at(p_ref, rows, piece),
                store_sem.at[t % 2, j],
            )
            for j, piece in enumerate(plan[t])
        ]

    for copy in loads(0):
        copy.start()

    tile = 256

    def prepare(t):
        if t == 0:
            fetch.wait()
        if t < 3:
            for copy in loads(t + 1):
                copy.start()
        for copy in loads(t):
            copy.wait()

        @pl.loop(0, width // tile)
        def _(n):
            cut = pl.ds(pl.multiple_of(n * tile, tile), tile)
            gate = gates[t % 2, :, cut]
            square = gate * gate
            bent = jnp.tanh(CURVE * (gate + BEND * gate * square))
            rise = 0.5 * (1.0 + bent)
            slope = rise + (0.5 * CURVE) * gate * (1.0 - bent * bent) * (1.0 + 3.0 * BEND * square)
            gates[t % 2, :, cut] = ups[t % 2, :, cut] * slope
            ups[t % 2, :, cut] = gate * rise

    def consume(t, pieces):
        if t >= 2:
            for copy in stores(t - 2):
                copy.wait()

        @pl.loop(0, width // tile)
        def _(n):
            cut = pl.ds(pl.multiple_of(n * tile, tile), tile)
            grad = lax.dot_general(
                held[t], weights[cut, :], (((1,), (1,)), ((), ())), preferred_element_type=wide
            )
            grads[t % 2, :, cut] = (grad * gates[t % 2, :, cut]).astype(grads.dtype)
            cut_up = pl.ds(pl.multiple_of(width + n * tile, tile), tile)
            grads[t % 2, :, cut_up] = (grad * ups[t % 2, :, cut]).astype(grads.dtype)

        for copy in stores(t):
            copy.start()

        @pl.loop(0, width // tile)
        def _(m):
            cut = pl.ds(pl.multiple_of(m * tile, tile), tile)
            turned = units[t % 2, :, cut].T

            @pl.loop(0, d // 512)
            def _(n):
                wide_cut = pl.ds(pl.multiple_of(n * 512, 512), 512)
                value = jnp.dot(turned, held[t, :, wide_cut], preferred_element_type=wide)
                if t > 0:
                    value = value + total_ref[cut, wide_cut]
                if t < 3:
                    total_ref[cut, wide_cut] = value
                else:
                    d_ref[cut, wide_cut] = value.astype(d_ref.dtype)

    rounds_of(rows, x_ref, held, local_sem, send, recv, consume, prepare)
    for copy in (*stores(2), *stores(3)):
        copy.wait()


def units_back(x, down, units, gate, up, cid):
    h, rows, d = x.shape
    width = down.shape[0]
    low = x.dtype
    return pl.pallas_call(
        functools.partial(units_back_kernel, rows),
        out_shape=(
            jax.ShapeDtypeStruct((h, 8 * rows, 2 * width), low),
            jax.ShapeDtypeStruct((width, d), low),
        ),
        in_specs=[pl.BlockSpec(memory_space=pl.ANY)] * 5,
        out_specs=[
            pl.BlockSpec(memory_space=pl.ANY),
            pl.BlockSpec(memory_space=pltpu.VMEM),
        ],
        scratch_shapes=[
            pltpu.VMEM((4, 4 * rows, d), low),
            pltpu.VMEM((width, d), low),
            pltpu.VMEM((2, 4 * rows, width), low),
            pltpu.VMEM((2, 4 * rows, width), jnp.float32),
            pltpu.VMEM((2, 4 * rows, width), jnp.float32),
            pltpu.VMEM((2, 4 * rows, 2 * width), low),
            pltpu.VMEM((width, d), jnp.float32),
            pltpu.SemaphoreType.DMA,
            pltpu.SemaphoreType.DMA((2, 4, 3)),
            pltpu.SemaphoreType.DMA((2, 4)),
            pltpu.SemaphoreType.DMA((2,)),
            pltpu.SemaphoreType.DMA((11,)),
            pltpu.SemaphoreType.DMA((11,)),
        ],
        compiler_params=pltpu.CompilerParams(
            collective_id=cid, has_side_effects=True, vmem_limit_bytes=52 << 20
        ),
        cost_estimate=pl.CostEstimate(
            flops=64 * h * rows * width * d, bytes_accessed=130_000_000, transcendentals=0
        ),
        name="units_back",
    )(x, down, units, gate, up)


def heads_back_kernel(
    rows, scale, x_ref, w_ref, m_ref, q_ref, k_ref, v_ref, s_ref, gq_ref, gk_ref, gv_ref, d_ref,
    held, weights, mixed, queries, keys, values, seen, total_ref, load_sem, local_sem, send, recv,
):
    wide = jnp.float32
    d = w_ref.shape[1]
    low = weights.dtype
    pairs = (
        (w_ref, weights), (q_ref, queries), (k_ref, keys), (v_ref, values), (s_ref, seen),
        (m_ref, mixed),
    )
    loads = [
        pltpu.make_async_copy(src, dst, load_sem.at[i]) for i, (src, dst) in enumerate(pairs)
    ]
    for copy in loads:
        copy.start()
    back = (((1,), (1,)), ((), ()))

    def prepare(t):
        if t == 0:
            for copy in loads:
                copy.wait()
            gk_ref[...] = jnp.zeros_like(gk_ref)
            gv_ref[...] = jnp.zeros_like(gv_ref)

    def consume(t, pieces):
        grad_mixed = lax.dot_general(held[t], weights[...], back, preferred_element_type=wide)
        grad_mixed = grad_mixed.astype(low)
        spans = []
        for j, (half, who) in enumerate(pieces):
            span = pl.ds(pl.multiple_of(who * rows, rows), rows)
            spans.append(mixed[half, span, :])
            query = queries[half, span, :]
            grad = grad_mixed[j * rows : (j + 1) * rows]
            score = lax.dot_general(query, keys[half], back, preferred_element_type=wide) * scale
            score = jnp.where(seen[half, span, :] > 0, score, NEGATIVE)
            power = jnp.exp(score - jnp.max(score, axis=-1, keepdims=True))
            prob = power / jnp.sum(power, axis=-1, keepdims=True)
            slope = lax.dot_general(grad, values[half], back, preferred_element_type=wide)
            mean = jnp.sum(prob * slope, axis=-1, keepdims=True)
            flow = (prob * (slope - mean)).astype(low)
            gq_ref[half, span, :] = jnp.dot(flow, keys[half], preferred_element_type=wide) * scale
            gk_ref[half] += jnp.dot(flow.T, query, preferred_element_type=wide) * scale
            gv_ref[half] += jnp.dot(prob.astype(low).T, grad, preferred_element_type=wide)
        turned = jnp.concatenate(spans, axis=0).T

        @pl.loop(0, d // 512)
        def _(n):
            cut = pl.ds(pl.multiple_of(n * 512, 512), 512)
            value = jnp.dot(turned, held[t, :, cut], preferred_element_type=wide)
            if t > 0:
                value = value + total_ref[:, cut]
            if t < 3:
                total_ref[:, cut] = value
            else:
                d_ref[:, cut] = value.astype(d_ref.dtype)

    rounds_of(rows, x_ref, held, local_sem, send, recv, consume, prepare)


def heads_back(x, output, mixed, query, key, value, visible, scale, cid):
    h, rows, d = x.shape
    low = x.dtype
    grad = jax.ShapeDtypeStruct(query.shape, jnp.float32)
    return pl.pallas_call(
        functools.partial(heads_back_kernel, rows, scale),
        out_shape=(grad, grad, grad, jax.ShapeDtypeStruct(output.shape, low)),
        in_specs=[pl.BlockSpec(memory_space=pl.ANY)] * 7,
        out_specs=[pl.BlockSpec(memory_space=pltpu.VMEM)] * 4,
        scratch_shapes=[
            pltpu.VMEM((4, 4 * rows, d), low),
            pltpu.VMEM(output.shape, low),
            pltpu.VMEM(mixed.shape, low),
            pltpu.VMEM(query.shape, low),
            pltpu.VMEM(query.shape, low),
            pltpu.VMEM(query.shape, low),
            pltpu.VMEM(visible.shape, visible.dtype),
            pltpu.VMEM(output.shape, jnp.float32),
            pltpu.SemaphoreType.DMA((6,)),
            pltpu.SemaphoreType.DMA((2,)),
            pltpu.SemaphoreType.DMA((11,)),
            pltpu.SemaphoreType.DMA((11,)),
        ],
        compiler_params=pltpu.CompilerParams(
            collective_id=cid, has_side_effects=True, vmem_limit_bytes=48 << 20
        ),
        cost_estimate=pl.CostEstimate(
            flops=20_000_000_000, bytes_accessed=130_000_000, transcendentals=0
        ),
        name="heads_back",
    )(x, output, mixed, query, key, value, visible)


def total_kernel(x_ref, o_ref, sums, got, tier_sums, send, recv):
    c, sib, xn, yn = partners()
    r = lax.axis_index("row")
    tiers = lax.axis_size("row")
    others = [lax.rem(r + k, tiers) for k in range(1, tiers)]
    barrier = pltpu.get_barrier_semaphore()
    for d in (sib, xn, yn):
        pl.semaphore_signal(barrier, inc=1, device_id={"col": d}, device_id_type=MESH)
    for d in others:
        pl.semaphore_signal(barrier, inc=1, device_id={"row": d}, device_id_type=MESH)
    pl.semaphore_wait(barrier, 3 + len(others))
    sums[0] = x_ref[...]
    for i, dev in enumerate((sib, xn, yn)):
        copy = pltpu.make_async_remote_copy(
            src_ref=sums.at[i],
            dst_ref=got.at[i],
            send_sem=send.at[i],
            recv_sem=recv.at[i],
            device_id={"col": dev},
            device_id_type=MESH,
        )
        copy.start()
        copy.wait()
        sums[i + 1] = sums[i] + got[i]
    tier_sums[r] = sums[3]
    copies = []
    for k, d in enumerate(others):
        copy = pltpu.make_async_remote_copy(
            src_ref=sums.at[3],
            dst_ref=tier_sums.at[r],
            send_sem=send.at[3 + k],
            recv_sem=recv.at[3 + k],
            device_id={"row": d},
            device_id_type=MESH,
        )
        copy.start()
        copies.append(copy)
    for copy in copies:
        copy.wait()
    result = tier_sums[0]
    for k in range(1, tiers):
        result = result + tier_sums[k]
    o_ref[...] = result


def total(x, tiers, cid):
    return pl.pallas_call(
        total_kernel,
        out_shape=jax.ShapeDtypeStruct(x.shape, x.dtype),
        in_specs=[pl.BlockSpec(memory_space=pltpu.VMEM)],
        out_specs=pl.BlockSpec(memory_space=pltpu.VMEM),
        scratch_shapes=[
            pltpu.VMEM((4, *x.shape), x.dtype),
            pltpu.VMEM((3, *x.shape), x.dtype),
            pltpu.VMEM((tiers, *x.shape), x.dtype),
            pltpu.SemaphoreType.DMA((2 + tiers,)),
            pltpu.SemaphoreType.DMA((2 + tiers,)),
        ],
        compiler_params=pltpu.CompilerParams(collective_id=cid, has_side_effects=True),
        cost_estimate=pl.CostEstimate(flops=0, bytes_accessed=40_000_000, transcendentals=0),
        name="total",
    )(x)


def after(value, *earlier):
    return lax.optimization_barrier((value, *earlier))[0]


def general_body(
    hidden,
    per_layer,
    lengths,
    block_ids,
    out_grad,
    query_weight,
    key_weight,
    value_weight,
    output_weight,
    gate_weight,
    up_weight,
    down_weight,
    laurel_left,
    laurel_right,
    layer_gate,
    layer_proj,
    norm_gains,
    head_gains,
):
    local_rows = hidden.shape[0]
    seq_groups = hidden.shape[1]
    col_index = lax.axis_index("col")
    row_index = lax.axis_index("row")
    all_lengths = lengths
    lengths = lax.dynamic_slice_in_dim(all_lengths, row_index * seq_groups, seq_groups, 0)
    (
        query_cols,
        key_cols,
        value_cols,
        output_rows,
        gate_cols,
        up_cols,
        down_rows,
        left_cols,
        right_rows,
        gate_layer_cols,
        proj_layer_rows,
    ) = (
        lax.all_gather(query_weight, "row", axis=0, tiled=True),
        lax.all_gather(key_weight, "row", axis=0, tiled=True),
        lax.all_gather(value_weight, "row", axis=0, tiled=True),
        lax.all_gather(output_weight, "row", axis=1, tiled=True),
        lax.all_gather(gate_weight, "row", axis=0, tiled=True),
        lax.all_gather(up_weight, "row", axis=0, tiled=True),
        lax.all_gather(down_weight, "row", axis=1, tiled=True),
        lax.all_gather(laurel_left, "row", axis=0, tiled=True),
        lax.all_gather(laurel_right, "row", axis=1, tiled=True),
        lax.all_gather(layer_gate, "row", axis=0, tiled=True),
        lax.all_gather(layer_proj, "row", axis=1, tiled=True),
    )
    (
        query_full,
        key_full,
        value_full,
        output_full,
        left_full,
        right_full,
        gate_layer_full,
        proj_layer_full,
    ) = (
        lax.all_gather(query_cols, "col", axis=1, tiled=True),
        lax.all_gather(key_cols, "col", axis=1, tiled=True),
        lax.all_gather(value_cols, "col", axis=1, tiled=True),
        lax.all_gather(output_rows, "col", axis=0, tiled=True),
        lax.all_gather(left_cols, "col", axis=1, tiled=True),
        lax.all_gather(right_rows, "col", axis=0, tiled=True),
        lax.all_gather(gate_layer_cols, "col", axis=1, tiled=True),
        lax.all_gather(proj_layer_rows, "col", axis=0, tiled=True),
    )
    paired = jnp.concatenate([gate_cols, up_cols], axis=1)
    unit_width = gate_cols.shape[1]
    first_position = col_index * local_rows
    positions = first_position + jnp.arange(local_rows, dtype=jnp.int32)
    live_mask = positions[:, None] < lengths[None, :]
    keep_mask = live_mask.astype(jnp.float32)[:, :, None]
    reach_back = (WINDOW + local_rows - 2) // local_rows
    reach_ahead = (BLOCK + local_rows - 2) // local_rows
    key_span = (reach_back + 1 + reach_ahead) * local_rows
    key_position = first_position - reach_back * local_rows + jnp.arange(key_span, dtype=jnp.int32)
    filler_low = jnp.full((seq_groups, reach_back * local_rows), FAR_BLOCK, jnp.int32)
    filler_high = jnp.full((seq_groups, reach_ahead * local_rows), FAR_BLOCK, jnp.int32)
    padded_blocks = jnp.concatenate([filler_low, block_ids, filler_high], axis=1)
    key_blocks = lax.dynamic_slice_in_dim(padded_blocks, first_position, key_span, 1)
    query_blocks = lax.dynamic_slice_in_dim(block_ids, first_position, local_rows, 1)
    key_live = (key_position[None, :] >= 0) & (key_position[None, :] < lengths[:, None])
    query_live = positions[None, :] < lengths[:, None]
    distance = positions[:, None] - key_position[None, :]
    nearby = (query_blocks[:, :, None] >= key_blocks[:, None, :]) & (distance < WINDOW)[None]
    nearby = nearby & query_live[:, :, None] & key_live[:, None, :]
    visible = (nearby | (distance == 0)[None])[:, None, None]
    residual = hidden.astype(jnp.float32)
    normed_value, input_back = jax.vjp(input_norm, residual, norm_gains)
    normed_low = normed_value.astype(jnp.bfloat16)
    half_width = HD // 2
    frequency = jnp.exp(jnp.arange(half_width, dtype=jnp.float32) * (-2.0 * math.log(10000.0) / HD))
    angles = (positions.astype(jnp.float32)[:, None] * frequency[None, :])[:, None, None, :]

    def prepare(query_in, key_in, value_in, gain_rows):
        return (
            rotate(root_norm(query_in, gain_rows[0]), angles),
            rotate(root_norm(key_in, gain_rows[1]), angles),
            plain_norm(value_in),
        )

    query_raw = matmul_last(normed_low, query_full).reshape(local_rows, seq_groups, H, HD)
    key_raw = matmul_last(normed_low, key_full).reshape(local_rows, seq_groups, KV, HD)
    value_raw = matmul_last(normed_low, value_full).reshape(local_rows, seq_groups, KV, HD)
    (query_value, key_value, value_value), head_back = jax.vjp(
        prepare, query_raw, key_raw, value_raw, head_gains
    )
    query_low = query_value.astype(jnp.bfloat16).reshape(local_rows, seq_groups, KV, H // KV, HD)
    key_low = key_value.astype(jnp.bfloat16)
    value_low = value_value.astype(jnp.bfloat16)
    offsets = list(range(reach_back, -reach_ahead - 1, -1))
    key_parts = []
    value_parts = []
    for offset in offsets:
        if offset == 0:
            key_parts.append(key_low)
            value_parts.append(value_low)
        else:
            moved_key, moved_value = passed_along((key_low, value_low), "col", offset)
            key_parts.append(moved_key)
            value_parts.append(moved_value)
    near_keys = jnp.concatenate(key_parts, axis=0)
    near_values = jnp.concatenate(value_parts, axis=0)
    score_scale = HD ** (-0.5)

    def score_all():
        raw_scores = (
            jnp.einsum(
                "psjgd,esjd->sjgpe", query_low, near_keys, preferred_element_type=jnp.float32
            )
            * score_scale
        )
        return jnp.where(visible, raw_scores, NEGATIVE)

    scores = score_all()
    row_max = jnp.max(scores, axis=-1, keepdims=True)
    exponent = jnp.exp(scores - row_max)
    row_total = jnp.sum(exponent, axis=-1, keepdims=True)
    attn_prob = exponent / row_total
    log_total = row_max + jnp.log(row_total)
    mixed_heads = jnp.einsum(
        "sjgpe,esjd->psjgd",
        attn_prob.astype(jnp.bfloat16),
        near_values,
        preferred_element_type=jnp.float32,
    )
    mixed_low = mixed_heads.reshape(local_rows, seq_groups, H * HD).astype(jnp.bfloat16)
    out_proj = matmul_last(mixed_low, output_full)
    laurel_mid = matmul_last(normed_low, left_full).astype(jnp.bfloat16)
    low_rank = matmul_last(laurel_mid, right_full)
    (after_attention, feed_normed), middle_back = jax.vjp(
        middle, residual, out_proj, low_rank, normed_low.astype(jnp.float32), norm_gains
    )
    feed_low = feed_normed.astype(jnp.bfloat16)
    gate_up = matmul_last(lax.all_gather(feed_low, "col", axis=0, tiled=True), paired)
    unit_value, gate_back = jax.vjp(
        gated_product, gate_up[..., :unit_width], gate_up[..., unit_width:]
    )
    units_low = unit_value.astype(jnp.bfloat16)
    summed = lax.psum_scatter(
        matmul_last(units_low, down_rows), "col", scatter_dimension=0, tiled=True
    )
    after_feed, feed_back = jax.vjp(feed_join, after_attention, summed, norm_gains)
    feed_round = after_feed.astype(jnp.bfloat16)
    layer_pre = matmul_last(feed_round, gate_layer_full)
    layer_input = per_layer.astype(jnp.float32)
    layer_value, layer_back = jax.vjp(gated_product, layer_pre, layer_input)
    layer_low = layer_value.astype(jnp.bfloat16)
    projected = matmul_last(layer_low, proj_layer_full)
    out_value, final_back = jax.vjp(final_join, after_feed, projected, norm_gains)
    square_sums = jnp.stack(
        [
            jnp.sum(keep_mask * residual * residual),
            jnp.sum(keep_mask * after_attention * after_attention),
            jnp.sum(keep_mask * after_feed * after_feed),
            jnp.sum(keep_mask * out_value * out_value),
        ]
    )
    valid_count = jnp.sum(all_lengths).astype(jnp.float32)
    cotangent = out_grad.astype(jnp.float32) * keep_mask
    grad_feed_out, grad_projected, gains_final = final_back(cotangent)
    projected_low = grad_projected.astype(jnp.bfloat16)
    grad_proj_layer = outer_sum(layer_low, projected_low)
    grad_layer_pre, grad_layer_input = layer_back(matmul_back(projected_low, proj_layer_full))
    layer_pre_low = grad_layer_pre.astype(jnp.bfloat16)
    grad_gate_layer = outer_sum(feed_round, layer_pre_low)
    grad_after_feed = grad_feed_out + matmul_back(layer_pre_low, gate_layer_full)
    grad_after_attention_a, grad_summed, gains_feed = feed_back(grad_after_feed)
    summed_low = grad_summed.astype(jnp.bfloat16)
    block_rows = lax.all_gather(summed_low, "col", axis=0, tiled=True)
    grad_down = outer_sum(units_low, block_rows)
    grad_units = matmul_back(block_rows, down_rows)
    grad_down, grad_units = (grad_down, grad_units)
    grad_gate_value, grad_up_value = gate_back(grad_units)
    grad_paired = jnp.concatenate([grad_gate_value, grad_up_value], axis=-1).astype(jnp.bfloat16)
    grad_weights_paired = outer_sum(
        lax.all_gather(feed_low, "col", axis=0, tiled=True), grad_paired
    )
    grad_feed = lax.psum_scatter(
        matmul_back(grad_paired, paired).astype(jnp.bfloat16),
        "col",
        scatter_dimension=0,
        tiled=True,
    ).astype(jnp.float32)
    grad_residual_mid, grad_out_proj, grad_low_rank, grad_normed_mid, gains_middle = middle_back(
        (grad_after_attention_a, grad_feed)
    )
    out_proj_low = grad_out_proj.astype(jnp.bfloat16)
    grad_output = outer_sum(mixed_low, out_proj_low)
    grad_mixed = matmul_back(out_proj_low, output_full).astype(jnp.bfloat16)
    grad_mixed = grad_mixed.reshape(local_rows, seq_groups, KV, H // KV, HD)
    low_rank_grad = grad_low_rank.astype(jnp.bfloat16)
    grad_right = outer_sum(laurel_mid, low_rank_grad)
    grad_laurel_mid = matmul_back(low_rank_grad, right_full).astype(jnp.bfloat16)
    grad_left = outer_sum(normed_low, grad_laurel_mid)
    scores = score_all()
    attn_prob = jnp.exp(scores - log_total)
    grad_prob = jnp.einsum(
        "psjgd,esjd->sjgpe", grad_mixed, near_values, preferred_element_type=jnp.float32
    )
    grad_scores = (
        attn_prob * (grad_prob - jnp.sum(attn_prob * grad_prob, axis=-1, keepdims=True))
    ).astype(jnp.bfloat16)
    grad_queries = (
        jnp.einsum("sjgpe,esjd->psjgd", grad_scores, near_keys, preferred_element_type=jnp.float32)
        * score_scale
    )
    grad_near_keys = (
        jnp.einsum("sjgpe,psjgd->esjd", grad_scores, query_low, preferred_element_type=jnp.float32)
        * score_scale
    )
    grad_near_values = jnp.einsum(
        "sjgpe,psjgd->esjd",
        attn_prob.astype(jnp.bfloat16),
        grad_mixed,
        preferred_element_type=jnp.float32,
    )
    grad_key_total = grad_near_keys[reach_back * local_rows : (reach_back + 1) * local_rows]
    grad_value_total = grad_near_values[reach_back * local_rows : (reach_back + 1) * local_rows]
    for slot_index, offset in enumerate(offsets):
        if offset != 0:
            piece_keys = grad_near_keys[slot_index * local_rows : (slot_index + 1) * local_rows]
            piece_values = grad_near_values[slot_index * local_rows : (slot_index + 1) * local_rows]
            back_keys, back_values = (
                passed_along(piece_keys.astype(jnp.bfloat16), "col", -offset).astype(
                    piece_keys.dtype
                ),
                passed_along(piece_values.astype(jnp.bfloat16), "col", -offset).astype(
                    piece_values.dtype
                ),
            )
            grad_key_total = grad_key_total + back_keys
            grad_value_total = grad_value_total + back_values
    grad_query_raw, grad_key_raw, grad_value_raw, grad_heads = head_back(
        (grad_queries.reshape(local_rows, seq_groups, H, HD), grad_key_total, grad_value_total)
    )
    query_grad_low = grad_query_raw.reshape(local_rows, seq_groups, H * HD).astype(jnp.bfloat16)
    key_grad_low = grad_key_raw.reshape(local_rows, seq_groups, KV * HD).astype(jnp.bfloat16)
    value_grad_low = grad_value_raw.reshape(local_rows, seq_groups, KV * HD).astype(jnp.bfloat16)
    grad_query = outer_sum(normed_low, query_grad_low)
    grad_key = outer_sum(normed_low, key_grad_low)
    grad_value = outer_sum(normed_low, value_grad_low)
    grad_normed = (
        grad_normed_mid
        + matmul_back(grad_laurel_mid, left_full)
        + matmul_back(query_grad_low, query_full)
        + matmul_back(key_grad_low, key_full)
        + matmul_back(value_grad_low, value_full)
    )
    grad_residual_in, gains_input = input_back(grad_normed)
    d_hidden = (grad_residual_mid + grad_residual_in).astype(jnp.bfloat16)
    d_per_layer = grad_layer_input.astype(jnp.bfloat16)
    grad_gains = gains_final + gains_feed + gains_middle + gains_input
    grad_gate = grad_weights_paired[:, :unit_width]
    grad_up = grad_weights_paired[:, unit_width:]
    (
        query_part,
        key_part,
        value_part,
        output_part,
        left_part,
        right_part,
        gate_layer_part,
        proj_layer_part,
    ) = (
        lax.psum_scatter(
            grad_query.astype(jnp.bfloat16), "col", scatter_dimension=1, tiled=True
        ).astype(jnp.float32),
        lax.psum_scatter(
            grad_key.astype(jnp.bfloat16), "col", scatter_dimension=1, tiled=True
        ).astype(jnp.float32),
        lax.psum_scatter(
            grad_value.astype(jnp.bfloat16), "col", scatter_dimension=1, tiled=True
        ).astype(jnp.float32),
        lax.psum_scatter(
            grad_output.astype(jnp.bfloat16), "col", scatter_dimension=0, tiled=True
        ).astype(jnp.float32),
        lax.psum_scatter(
            grad_left.astype(jnp.bfloat16), "col", scatter_dimension=1, tiled=True
        ).astype(jnp.float32),
        lax.psum_scatter(
            grad_right.astype(jnp.bfloat16), "col", scatter_dimension=0, tiled=True
        ).astype(jnp.float32),
        lax.psum_scatter(
            grad_gate_layer.astype(jnp.bfloat16), "col", scatter_dimension=1, tiled=True
        ).astype(jnp.float32),
        lax.psum_scatter(
            grad_proj_layer.astype(jnp.bfloat16), "col", scatter_dimension=0, tiled=True
        ).astype(jnp.float32),
    )
    (
        d_query_weight,
        d_key_weight,
        d_value_weight,
        d_output_weight,
        d_gate_weight,
        d_up_weight,
        d_down_weight,
        d_laurel_left,
        d_laurel_right,
        d_layer_gate,
        d_layer_proj,
    ) = (
        lax.psum_scatter(
            query_part.astype(jnp.bfloat16), "row", scatter_dimension=0, tiled=True
        ).astype(jnp.float32),
        lax.psum_scatter(
            key_part.astype(jnp.bfloat16), "row", scatter_dimension=0, tiled=True
        ).astype(jnp.float32),
        lax.psum_scatter(
            value_part.astype(jnp.bfloat16), "row", scatter_dimension=0, tiled=True
        ).astype(jnp.float32),
        lax.psum_scatter(
            output_part.astype(jnp.bfloat16), "row", scatter_dimension=1, tiled=True
        ).astype(jnp.float32),
        lax.psum_scatter(
            grad_gate.astype(jnp.bfloat16), "row", scatter_dimension=0, tiled=True
        ).astype(jnp.float32),
        lax.psum_scatter(
            grad_up.astype(jnp.bfloat16), "row", scatter_dimension=0, tiled=True
        ).astype(jnp.float32),
        lax.psum_scatter(
            grad_down.astype(jnp.bfloat16), "row", scatter_dimension=1, tiled=True
        ).astype(jnp.float32),
        lax.psum_scatter(
            left_part.astype(jnp.bfloat16), "row", scatter_dimension=0, tiled=True
        ).astype(jnp.float32),
        lax.psum_scatter(
            right_part.astype(jnp.bfloat16), "row", scatter_dimension=1, tiled=True
        ).astype(jnp.float32),
        lax.psum_scatter(
            gate_layer_part.astype(jnp.bfloat16), "row", scatter_dimension=0, tiled=True
        ).astype(jnp.float32),
        lax.psum_scatter(
            proj_layer_part.astype(jnp.bfloat16), "row", scatter_dimension=1, tiled=True
        ).astype(jnp.float32),
    )
    d_norm_gains, d_head_gains, total_squares = lax.psum(
        (grad_gains, grad_heads, square_sums), ("row", "col")
    )
    stats = jnp.sqrt(total_squares / (valid_count * D))
    output = out_value.astype(jnp.bfloat16)
    return (
        output,
        stats,
        d_hidden,
        d_per_layer,
        d_query_weight,
        d_key_weight,
        d_value_weight,
        d_output_weight,
        d_gate_weight,
        d_up_weight,
        d_down_weight,
        d_laurel_left,
        d_laurel_right,
        d_layer_gate,
        d_layer_proj,
        d_norm_gains,
        d_head_gains,
    )


def swap(array):
    return jnp.swapaxes(array, 0, 1)


def heads_body(
    hidden,
    per_layer,
    lengths,
    block_ids,
    out_grad,
    query_weight,
    key_weight,
    value_weight,
    output_weight,
    gate_weight,
    up_weight,
    down_weight,
    laurel_left,
    laurel_right,
    layer_gate,
    layer_proj,
    norm_gains,
    head_gains,
):
    low = jnp.bfloat16
    rows = hidden.shape[0]
    groups = hidden.shape[1]
    cols = lax.axis_size("col")
    seq = rows * cols
    share = cols // KV
    col_index = lax.axis_index("col")
    row_index = lax.axis_index("row")
    all_lengths = lengths
    lengths = lax.dynamic_slice_in_dim(all_lengths, row_index * groups, groups, 0)

    small = jnp.concatenate(
        [key_weight.T, value_weight.T, laurel_left.T, layer_gate.T, laurel_right, layer_proj],
        axis=0,
    )
    heights = [key_weight.shape[1], value_weight.shape[1], laurel_left.shape[1]]
    heights += [layer_gate.shape[1], laurel_right.shape[0], layer_proj.shape[0]]
    edges = [sum(heights[:i]) for i in range(len(heights) + 1)]
    unit_width = gate_weight.shape[1]
    residual = swap(hidden).astype(jnp.float32)
    normed_value, input_back = jax.vjp(input_norm, residual, norm_gains)
    normed_low = normed_value.astype(low)
    tiers = lax.axis_size("row")
    normed_all, small_row, query_full, output_full = open_all(
        normed_low, small, query_weight, output_weight, tiers, 1
    )
    small_all = share_small(small_row, heights[0] + heights[1], 8)
    both_weights = jnp.concatenate([gate_weight, up_weight], axis=1)
    paired = lax.all_gather(after(both_weights, normed_all), "row", axis=0, tiled=True)
    down_full = lax.all_gather(after(down_weight, normed_all), "row", axis=1, tiled=True)
    query_full = query_full.reshape(D, HD).T
    output_full = jnp.swapaxes(output_full, 0, 1).reshape(HD, D)
    pieces = [small_all[:, :, a:b] for a, b in zip(edges[:-1], edges[1:])]
    group_start = (col_index // share) * share

    def joined(piece):
        return jnp.swapaxes(piece, 1, 2).reshape(-1, D)

    key_full, value_full = (
        joined(lax.dynamic_slice_in_dim(piece, group_start, share, 0)) for piece in pieces[:2]
    )
    left_full, gate_layer_full, right_full, proj_layer_full = (
        joined(piece) for piece in pieces[2:]
    )
    head_weights = jnp.concatenate([query_full, key_full, value_full], axis=0)

    positions = jnp.arange(seq, dtype=jnp.int32)
    mine = col_index * rows + jnp.arange(rows, dtype=jnp.int32)
    keep_mask = (mine[None, :] < lengths[:, None]).astype(jnp.float32)[:, :, None]
    live = positions[None, :] < lengths[:, None]
    distance = positions[:, None] - positions[None, :]
    nearby = (block_ids[:, :, None] >= block_ids[:, None, :]) & (distance < WINDOW)[None]
    nearby = nearby & live[:, :, None] & live[:, None, :]
    visible = nearby | (distance == 0)[None]

    half_width = HD // 2
    frequency = jnp.exp(jnp.arange(half_width, dtype=jnp.float32) * (-2.0 * math.log(10000.0) / HD))
    angles = (positions.astype(jnp.float32)[:, None] * frequency[None, :])[None]

    def prepare(query_in, key_in, value_in, gain_rows):
        return (
            rotate(root_norm(query_in, gain_rows[0]), angles),
            rotate(root_norm(key_in, gain_rows[1]), angles),
            plain_norm(value_in),
        )

    head_raw = matmul_back(normed_all, head_weights)
    query_raw, key_raw, value_raw = jnp.split(head_raw, 3, axis=-1)
    (query_value, key_value, value_value), head_back = jax.vjp(
        prepare, query_raw, key_raw, value_raw, head_gains
    )
    query_low = query_value.astype(low)
    key_low = key_value.astype(low)
    value_low = value_value.astype(low)
    score_scale = HD ** (-0.5)

    def score_all():
        raw_scores = (
            jnp.einsum("spd,sed->spe", query_low, key_low, preferred_element_type=jnp.float32)
            * score_scale
        )
        return jnp.where(visible, raw_scores, NEGATIVE)

    scores = score_all()
    row_max = jnp.max(scores, axis=-1, keepdims=True)
    exponent = jnp.exp(scores - row_max)
    row_total = jnp.sum(exponent, axis=-1, keepdims=True)
    attn_prob = exponent / row_total
    mixed_low = jnp.einsum(
        "spe,sed->spd", attn_prob.astype(low), value_low, preferred_element_type=jnp.float32
    ).astype(low)
    out_proj = product_sum(mixed_low, output_full, False, 2)
    laurel_mid = matmul_back(normed_low, left_full).astype(low)
    low_rank = matmul_last(laurel_mid, right_full)
    (after_attention, feed_normed), middle_back = jax.vjp(
        middle, residual, out_proj, low_rank, normed_low.astype(jnp.float32), norm_gains
    )
    feed_all = spread(feed_normed.astype(low), 0)
    gate_value = matmul_last(feed_all, paired[:, :unit_width])
    up_value = matmul_last(feed_all, paired[:, unit_width:])
    units_low = gated_product(gate_value, up_value).astype(low)
    summed = product_sum(units_low, down_full, False, 5)
    after_feed, feed_back = jax.vjp(feed_join, after_attention, summed, norm_gains)
    feed_round = after_feed.astype(low)
    layer_pre = matmul_back(feed_round, gate_layer_full)
    layer_input = swap(per_layer).astype(jnp.float32)
    layer_value, layer_back = jax.vjp(gated_product, layer_pre, layer_input)
    layer_low = layer_value.astype(low)
    projected = matmul_last(layer_low, proj_layer_full)
    out_value, final_back = jax.vjp(final_join, after_feed, projected, norm_gains)
    square_sums = jnp.stack(
        [
            jnp.sum(keep_mask * residual * residual),
            jnp.sum(keep_mask * after_attention * after_attention),
            jnp.sum(keep_mask * after_feed * after_feed),
            jnp.sum(keep_mask * out_value * out_value),
        ]
    )
    valid_count = jnp.sum(all_lengths).astype(jnp.float32)

    cotangent = swap(out_grad).astype(jnp.float32) * keep_mask
    grad_feed_out, grad_projected, gains_final = final_back(cotangent)
    projected_low = grad_projected.astype(low)
    grad_proj_layer = outer_sum(layer_low, projected_low)
    grad_layer_pre, grad_layer_input = layer_back(matmul_back(projected_low, proj_layer_full))
    layer_pre_low = grad_layer_pre.astype(low)
    grad_gate_layer = outer_sum(layer_pre_low, feed_round)
    grad_after_feed = grad_feed_out + matmul_last(layer_pre_low, gate_layer_full)
    grad_after_attention_a, grad_summed, gains_feed = feed_back(grad_after_feed)
    grad_paired, grad_down = units_back(
        grad_summed.astype(low), down_full, units_low, gate_value, up_value, 9
    )
    d_down_weight = lax.psum_scatter(
        grad_down, "row", scatter_dimension=1, tiled=True
    ).astype(jnp.float32)
    grad_gate = outer_sum(feed_all, grad_paired[..., :unit_width]).astype(low)
    d_gate_weight = lax.psum_scatter(
        grad_gate, "row", scatter_dimension=0, tiled=True
    ).astype(jnp.float32)
    grad_feed = product_sum(after(grad_paired, grad_gate), paired, True, 6)
    grad_up = outer_sum(feed_all, after(grad_paired, grad_feed)[..., unit_width:]).astype(low)
    d_up_weight = lax.psum_scatter(
        grad_up, "row", scatter_dimension=0, tiled=True
    ).astype(jnp.float32)
    grad_feed = after(grad_feed, grad_up)
    grad_residual_mid, grad_out_proj, grad_low_rank, grad_normed_mid, gains_middle = middle_back(
        (grad_after_attention_a, grad_feed)
    )
    grad_queries, grad_keys, grad_values, grad_output = heads_back(
        after(grad_out_proj.astype(low), d_down_weight),
        output_full,
        mixed_low,
        query_low,
        key_low,
        value_low,
        visible.astype(jnp.float32),
        score_scale,
        10,
    )
    low_rank_grad = grad_low_rank.astype(low)
    grad_right = outer_sum(laurel_mid, low_rank_grad)
    grad_laurel_mid = matmul_back(low_rank_grad, right_full).astype(low)
    grad_left = outer_sum(grad_laurel_mid, normed_low)
    grad_query_raw, grad_key_raw, grad_value_raw, grad_heads = head_back(
        (grad_queries, grad_keys, grad_values)
    )
    head_grads = jnp.concatenate([grad_query_raw, grad_key_raw, grad_value_raw], axis=-1)
    head_grads = head_grads.astype(low)
    grad_head_weights = outer_sum(head_grads, normed_all).astype(low)
    grad_query, grad_key, grad_value = jnp.split(grad_head_weights, 3, axis=0)
    grad_group = jnp.concatenate(
        [grad_key.reshape(share, -1, D), grad_value.reshape(share, -1, D)], axis=1
    )
    grad_rest = jnp.concatenate(
        [
            piece.astype(low).reshape(cols, -1, D)
            for piece in (grad_left, grad_gate_layer, grad_right, grad_proj_layer)
        ],
        axis=1,
    )
    half = grad_rest.shape[1] // 2
    grad_rest = jnp.swapaxes(grad_rest.reshape(cols, 2, half, D), 0, 1)
    rest_part, group_part = fold_small(grad_rest.reshape(2, cols * half, D), grad_group, 3)
    parts = jnp.concatenate(
        [grad_output, grad_query, group_part.astype(low), rest_part.astype(low).reshape(-1, D)],
        axis=0,
    )
    parts_out = lax.psum_scatter(parts, "row", scatter_dimension=1, tiled=True).astype(jnp.float32)
    d_output_weight = parts_out[:HD]
    d_query_weight = parts_out[HD : 2 * HD].T
    small_out = parts_out[2 * HD :]
    small_parts = [small_out[a:b] for a, b in zip(edges[:-1], edges[1:])]
    grad_normed = product_sum(
        after(head_grads, parts, d_gate_weight, d_up_weight), head_weights, False, 7
    )
    grad_normed = grad_normed + grad_normed_mid + matmul_last(grad_laurel_mid, left_full)
    grad_residual_in, gains_input = input_back(grad_normed)
    d_hidden = swap((grad_residual_mid + grad_residual_in).astype(low))
    d_per_layer = swap(grad_layer_input.astype(low))
    grad_gains = gains_final + gains_feed + gains_middle + gains_input
    extra = jnp.concatenate([grad_heads.reshape(-1), square_sums])
    extra = jnp.pad(extra, (0, 2 * D - extra.shape[0])).reshape(2, D)
    totals = total(jnp.concatenate([grad_gains, extra], axis=0), tiers, 4)
    d_norm_gains = totals[:6]
    d_head_gains = totals[6, : 2 * HD].reshape(2, HD)
    total_squares = totals[6, 2 * HD : 2 * HD + 4]
    stats = jnp.sqrt(total_squares / (valid_count * D))
    output = swap(out_value.astype(low))
    return (
        output,
        stats,
        d_hidden,
        d_per_layer,
        d_query_weight,
        small_parts[0].T,
        small_parts[1].T,
        d_output_weight,
        d_gate_weight,
        d_up_weight,
        d_down_weight,
        small_parts[2].T,
        small_parts[4],
        small_parts[3].T,
        small_parts[5],
        d_norm_gains,
        d_head_gains,
    )


def solution(mesh):
    body = heads_body if mesh.shape["col"] == H else general_body
    in_specs = (
        P("col", "row", None),
        P("col", "row", None),
        P(),
        P("row", None),
        P("col", "row", None),
        P("row", "col"),
        P("row", "col"),
        P("row", "col"),
        P("col", "row"),
        P("row", "col"),
        P("row", "col"),
        P("col", "row"),
        P("row", "col"),
        P("col", "row"),
        P("row", "col"),
        P("col", "row"),
        P(),
        P(),
    )
    out_specs = (
        P("col", "row", None),
        P(),
        P("col", "row", None),
        P("col", "row", None),
        P("row", "col"),
        P("row", "col"),
        P("row", "col"),
        P("col", "row"),
        P("row", "col"),
        P("row", "col"),
        P("col", "row"),
        P("row", "col"),
        P("col", "row"),
        P("row", "col"),
        P("col", "row"),
        P(),
        P(),
    )
    return jax.shard_map(body, mesh=mesh, in_specs=in_specs, out_specs=out_specs, check_vma=False)
```

```python
import functools
import math

import jax
import jax.numpy as jnp
from jax import lax
from jax.experimental import pallas as pl
from jax.experimental.pallas import tpu as pltpu
from jax.sharding import PartitionSpec as P

D = 2048
H = 8
KV = 2
HD = 256
WINDOW = 512
BLOCK = 256


EPSILON = 1e-06
FAR_BLOCK = 1 << 30
NEGATIVE = -1e30
HALF_ROOT = 1.0 / math.sqrt(2.0)
CURVE = math.sqrt(2.0 / math.pi)
BEND = 0.044715


MESH = pl.DeviceIdType.MESH


def passed_along(value, axis, steps):
    count = lax.axis_size(axis)
    initial, last = (max(0, -steps), min(count, count - steps))
    return lax.ppermute(value, axis, [(source, source + steps) for source in range(initial, last)])


def root_norm(values, gain_row):
    return (
        values * lax.rsqrt(jnp.mean(values * values, axis=-1, keepdims=True) + EPSILON) * gain_row
    )


def plain_norm(values):
    return values * lax.rsqrt(jnp.mean(values * values, axis=-1, keepdims=True) + EPSILON)


def smooth_gate(values):
    return jax.nn.gelu(values, approximate=True)


def rotate(values, angles):
    half_width = values.shape[-1] // 2
    leading = values[..., :half_width]
    trailing = values[..., half_width:]
    cosine = jnp.cos(angles)
    sine_part = jnp.sin(angles)
    return jnp.concatenate(
        [leading * cosine - trailing * sine_part, trailing * cosine + leading * sine_part], axis=-1
    )


def matmul_last(first_array, second_array):
    return lax.dot_general(
        first_array,
        second_array,
        (((first_array.ndim - 1,), (0,)), ((), ())),
        preferred_element_type=jnp.float32,
    )


def matmul_back(first_array, second_array):
    return lax.dot_general(
        first_array,
        second_array,
        (((first_array.ndim - 1,), (1,)), ((), ())),
        preferred_element_type=jnp.float32,
    )


def outer_sum(first_array, second_array):
    return lax.dot_general(
        first_array, second_array, (((0, 1), (0, 1)), ((), ())), preferred_element_type=jnp.float32
    )


def input_norm(residual, gain_rows):
    return root_norm(residual, gain_rows[0])


def middle(residual, out_proj, low_rank, normed, gain_rows):
    merged = (
        residual + root_norm(out_proj, gain_rows[1]) + normed + root_norm(low_rank, gain_rows[4])
    ) * HALF_ROOT
    return (merged, root_norm(merged, gain_rows[2]))


def feed_join(merged, summed, gain_rows):
    return merged + root_norm(summed, gain_rows[3])


def final_join(merged, projected, gain_rows):
    return merged + root_norm(projected, gain_rows[5])


def gated_product(first_array, second_array):
    return smooth_gate(first_array) * second_array


def partners():
    c = lax.axis_index("col")
    sib = c + 1 - 2 * (c % 2)
    xn = c + 2 - 4 * ((c // 2) % 2)
    yn = c + 4 - 8 * (c // 4)
    return c, sib, xn, yn

def greet(devs):
    barrier = pltpu.get_barrier_semaphore()
    for d in devs:
        pl.semaphore_signal(barrier, inc=1, device_id={"col": d}, device_id_type=MESH)
    pl.semaphore_wait(barrier, len(devs))

def spread_kernel(rows, x_ref, o_ref, local_sem, send, recv):
    c, sib, xn, yn = partners()
    def slot(half, who):
        return o_ref.at[half, pl.ds(pl.multiple_of(who * rows, rows), rows), :]
    def both(who):
        return o_ref.at[:, pl.ds(pl.multiple_of(who * rows, rows), rows), :]
    def push(i, src, dst, dev):
        return pltpu.make_async_remote_copy(src_ref=src, dst_ref=dst, send_sem=send.at[i], recv_sem=recv.at[i], device_id={"col": dev}, device_id_type=MESH)
    mine = pltpu.make_async_copy(x_ref, both(c), local_sem)
    mine.start()
    greet((sib, xn, yn))
    x0 = push(0, x_ref.at[0], slot(0, c), xn)
    y1 = push(1, x_ref.at[1], slot(1, c), yn)
    x1 = push(2, x_ref.at[1], slot(1, c), xn)
    y0 = push(3, x_ref.at[0], slot(0, c), yn)
    s = push(4, x_ref, both(c), sib)
    x0.start(); y1.start(); x1.start(); y0.start(); s.start()
    diag = yn + (xn - c)
    x0.wait_recv()
    fy = push(5, slot(0, xn), slot(0, xn), yn)
    fy.start()
    sx0 = push(6, slot(0, xn), slot(0, xn), sib)
    sx0.start()
    y1.wait_recv()
    fx = push(7, slot(1, yn), slot(1, yn), xn)
    fx.start()
    sy1 = push(8, slot(1, yn), slot(1, yn), sib)
    sy1.start()
    x1.wait_recv()
    sx1 = push(9, slot(1, xn), slot(1, xn), sib)
    sx1.start()
    y0.wait_recv()
    sy0 = push(10, slot(0, yn), slot(0, yn), sib)
    sy0.start()
    fy.wait_recv()
    sd0 = push(11, slot(0, diag), slot(0, diag), sib)
    sd0.start()
    fx.wait_recv()
    sd1 = push(12, slot(1, diag), slot(1, diag), sib)
    sd1.start()
    for cp in (s, sx0, sy1, sx1, sy0, sd0, sd1):
        cp.wait_recv()
    for cp in (x0, y1, x1, y0, s, fy, sx0, fx, sy1, sx1, sy0, sd0, sd1):
        cp.wait_send()
    mine.wait()

def spread(x, cid=0):
    h, rows, d = x.shape
    return pl.pallas_call(
        functools.partial(spread_kernel, rows),
        out_shape=jax.ShapeDtypeStruct((h, 8 * rows, d), x.dtype),
        in_specs=[pl.BlockSpec(memory_space=pl.ANY)],
        out_specs=pl.BlockSpec(memory_space=pl.ANY),
        scratch_shapes=[pltpu.SemaphoreType.DMA, pltpu.SemaphoreType.DMA((13,)), pltpu.SemaphoreType.DMA((13,))],
        compiler_params=pltpu.CompilerParams(collective_id=cid, has_side_effects=True),
        cost_estimate=pl.CostEstimate(flops=0, bytes_accessed=120_000_000, transcendentals=0),
        name="spread",
    )(x)

def fold_steps(rows, p_ref, own, sibs, dx, dy, rx, ry, local_sem, send, recv):
    c, sib, xn, yn = partners()
    diag = yn + (xn - c)
    wide = jnp.float32
    tall = 32 if rows % 32 == 0 else 8

    def blk(who):
        return p_ref.at[:, pl.ds(pl.multiple_of(who * rows, rows), rows), :]

    def push(i, src, dst, dev):
        return pltpu.make_async_remote_copy(
            src_ref=src,
            dst_ref=dst,
            send_sem=send.at[i],
            recv_sem=recv.at[i],
            device_id={"col": dev},
            device_id_type=MESH,
        )

    def add(dst, src):
        @pl.loop(0, rows // tall)
        def _(i):
            r = pl.ds(pl.multiple_of(i * tall, tall), tall)
            dst[r, :] = (dst[r, :].astype(wide) + src[r, :].astype(wide)).astype(dst.dtype)

    def pair(j):
        add(own.at[j, 0], sibs.at[j, 0])
        add(own.at[j, 1], sibs.at[j, 1])

    dests = (diag, xn, yn, c)
    loads = [pltpu.make_async_copy(blk(d), own.at[j], local_sem.at[j]) for j, d in enumerate(dests)]
    for load in loads:
        load.start()
    yield None
    sides = [push(j, blk(d + (sib - c)), sibs.at[j], sib) for j, d in enumerate(dests)]
    for side in sides:
        side.start()
    yield None
    loads[0].wait()
    sides[0].wait_recv()
    pair(0)
    a = push(4, own.at[0, 0], dx, xn)
    b = push(5, own.at[0, 1], dy, yn)
    a.start()
    b.start()
    yield None
    loads[1].wait()
    sides[1].wait_recv()
    pair(1)
    x0 = push(6, own.at[1, 0], rx.at[0], xn)
    x0.start()
    yield None
    loads[2].wait()
    sides[2].wait_recv()
    pair(2)
    y1 = push(7, own.at[2, 1], ry.at[1], yn)
    y1.start()
    yield None
    a.wait_recv()
    add(own.at[2, 0], dx)
    y0 = push(8, own.at[2, 0], ry.at[0], yn)
    y0.start()
    yield None
    b.wait_recv()
    add(own.at[1, 1], dy)
    x1 = push(9, own.at[1, 1], rx.at[1], xn)
    x1.start()
    yield None
    loads[3].wait()
    sides[3].wait_recv()
    pair(3)
    yield None
    waits = ((x0, y0), (x1, y1))
    yield tall, waits, (*sides, a, b, x0, y1, y0, x1)


def fold_finish(rows, o_ref, own, rx, ry, tall, waits, sent):
    wide = jnp.float32
    for h in range(2):
        for copy in waits[h]:
            copy.wait_recv()

        @pl.loop(0, rows // tall)
        def _(i):
            r = pl.ds(pl.multiple_of(i * tall, tall), tall)
            o_ref[h, r, :] = (
                own[3, h, r, :].astype(wide) + rx[h, r, :].astype(wide) + ry[h, r, :].astype(wide)
            )

    for copy in sent:
        copy.wait_send()


def fold_scratch(h, rows, d, kind):
    return [
        pltpu.VMEM((4, h, rows, d), kind),
        pltpu.VMEM((4, h, rows, d), kind),
        pltpu.VMEM((rows, d), kind),
        pltpu.VMEM((rows, d), kind),
        pltpu.VMEM((h, rows, d), kind),
        pltpu.VMEM((h, rows, d), kind),
        pltpu.SemaphoreType.DMA((4,)),
        pltpu.SemaphoreType.DMA((10,)),
        pltpu.SemaphoreType.DMA((10,)),
    ]


def product_kernel(
    rows, flip, a_ref, w_ref, o_ref, a_buf, w_buf, stage, own, sibs, dx, dy, rx, ry,
    local_sem, send, recv,
):
    c, sib, xn, yn = partners()
    diag = yn + (xn - c)
    wide = jnp.float32
    d = o_ref.shape[-1]
    tile = 512
    tall = 32

    def push(i, src, dst, dev):
        return pltpu.make_async_remote_copy(
            src_ref=src,
            dst_ref=dst,
            send_sem=send.at[i],
            recv_sem=recv.at[i],
            device_id={"col": dev},
            device_id_type=MESH,
        )

    dests = (diag, xn, yn, c)
    step = sib - c
    weights = pltpu.make_async_copy(w_ref, w_buf, local_sem.at[8])
    weights.start()

    def load(i, who):
        return pltpu.make_async_copy(
            a_ref.at[:, pl.ds(pl.multiple_of(who * rows, rows), rows), :],
            a_buf.at[i],
            local_sem.at[i],
        )

    far = [load(j, dests[j] + step) for j in range(4)]
    near = [load(4 + j, dests[j]) for j in range(4)]
    for first, second in zip(far, near):
        first.start()
        second.start()
    greet((sib, xn, yn))
    weights.wait()

    def product(i, put):
        left = a_buf[i].reshape(2 * rows, a_buf.shape[-1])

        @pl.loop(0, d // tile)
        def _(n):
            cut = pl.ds(pl.multiple_of(n * tile, tile), tile)
            right = w_buf[cut, :] if flip else w_buf[:, cut]
            dims = (((1,), (1,)), ((), ())) if flip else (((1,), (0,)), ((), ()))
            value = lax.dot_general(left, right, dims, preferred_element_type=wide)
            put(cut, value.reshape(2, rows, tile))

    sides = [push(j, stage.at[j], sibs.at[j], sib) for j in range(4)]

    def for_sibling(j):
        far[j].wait()

        def put(cut, value):
            stage[j, :, :, cut] = value.astype(stage.dtype)

        product(j, put)
        sides[j].start()

    def for_chip(j):
        near[j].wait()
        sides[j].wait_recv()

        def put(cut, value):
            own[j, :, :, cut] = (value + sibs[j, :, :, cut].astype(wide)).astype(own.dtype)

        product(4 + j, put)

    def add(dst, src):
        @pl.loop(0, rows // tall)
        def _(i):
            r = pl.ds(pl.multiple_of(i * tall, tall), tall)
            dst[r, :] = (dst[r, :].astype(wide) + src[r, :].astype(wide)).astype(dst.dtype)

    for_sibling(0)
    near[0].wait()

    def hold(cut, value):
        o_ref[:, :, cut] = value

    product(4, hold)
    sides[0].wait_recv()
    for h in range(2):

        @pl.loop(0, rows // tall)
        def _(i):
            r = pl.ds(pl.multiple_of(i * tall, tall), tall)
            own[0, h, r, :] = (o_ref[h, r, :] + sibs[0, h, r, :].astype(wide)).astype(own.dtype)

    a = push(4, own.at[0, 0], dx, xn)
    b = push(5, own.at[0, 1], dy, yn)
    a.start()
    b.start()
    for_sibling(1)
    for_sibling(2)
    for_chip(1)
    x0 = push(6, own.at[1, 0], rx.at[0], xn)
    x0.start()
    for_sibling(3)
    for_chip(2)
    y1 = push(7, own.at[2, 1], ry.at[1], yn)
    y1.start()
    a.wait_recv()
    add(own.at[2, 0], dx)
    y0 = push(8, own.at[2, 0], ry.at[0], yn)
    y0.start()
    b.wait_recv()
    add(own.at[1, 1], dy)
    x1 = push(9, own.at[1, 1], rx.at[1], xn)
    x1.start()
    near[3].wait()
    sides[3].wait_recv()

    def put(cut, value):
        o_ref[:, :, cut] = value + sibs[3, :, :, cut].astype(wide)

    product(7, put)
    for h, waits in enumerate(((x0, y0), (x1, y1))):
        for copy in waits:
            copy.wait_recv()

        @pl.loop(0, rows // tall)
        def _(i):
            r = pl.ds(pl.multiple_of(i * tall, tall), tall)
            o_ref[h, r, :] = o_ref[h, r, :] + rx[h, r, :].astype(wide) + ry[h, r, :].astype(wide)

    for copy in (*sides, a, b, x0, y1, y0, x1):
        copy.wait_send()


def product_sum(left, right, flip, cid):
    h, total, depth = left.shape
    rows = total // 8
    d = right.shape[0] if flip else right.shape[1]
    low = left.dtype
    return pl.pallas_call(
        functools.partial(product_kernel, rows, flip),
        out_shape=jax.ShapeDtypeStruct((h, rows, d), jnp.float32),
        in_specs=[pl.BlockSpec(memory_space=pl.ANY)] * 2,
        out_specs=pl.BlockSpec(memory_space=pltpu.VMEM),
        scratch_shapes=[
            pltpu.VMEM((8, h, rows, depth), low),
            pltpu.VMEM(right.shape, low),
            pltpu.VMEM((4, h, rows, d), low),
            pltpu.VMEM((3, h, rows, d), low),
            pltpu.VMEM((4, h, rows, d), low),
            pltpu.VMEM((rows, d), low),
            pltpu.VMEM((rows, d), low),
            pltpu.VMEM((h, rows, d), low),
            pltpu.VMEM((h, rows, d), low),
            pltpu.SemaphoreType.DMA((9,)),
            pltpu.SemaphoreType.DMA((10,)),
            pltpu.SemaphoreType.DMA((10,)),
        ],
        compiler_params=pltpu.CompilerParams(
            collective_id=cid, has_side_effects=True, vmem_limit_bytes=44 << 20
        ),
        cost_estimate=pl.CostEstimate(
            flops=2 * h * total * depth * d, bytes_accessed=130_000_000, transcendentals=0
        ),
        name="product_sum",
    )(left, right)


def fold_small_kernel(
    rows, p_ref, g_ref, o_ref, k_ref, own, sibs, dx, dy, rx, ry, local_sem, send, recv,
    gown, gsibs, grx, glocal, gsend, grecv,
):
    c, sib, xn, yn = partners()
    m = c % 4
    m_sib = m + 1 - 2 * (m % 2)
    m_x = m + 2 - 4 * (m // 2)
    m_diag = m_sib + (m_x - m)
    wide = jnp.float32

    def push(i, src, dst, dev):
        return pltpu.make_async_remote_copy(
            src_ref=src,
            dst_ref=dst,
            send_sem=gsend.at[i],
            recv_sem=grecv.at[i],
            device_id={"col": dev},
            device_id_type=MESH,
        )

    steps = fold_steps(rows, p_ref, own, sibs, dx, dy, rx, ry, local_sem, send, recv)
    next(steps)
    loads = [
        pltpu.make_async_copy(g_ref.at[d], gown.at[j], glocal.at[j])
        for j, d in enumerate((m_x, m))
    ]
    for load in loads:
        load.start()
    greet((sib, xn, yn))
    sides = [push(j, g_ref.at[d], gsibs.at[j], sib) for j, d in enumerate((m_diag, m_sib))]
    sides[0].start()
    next(steps)
    sides[1].start()
    tall = k_ref.shape[0] // 4
    loads[0].wait()
    sides[0].wait_recv()

    @pl.loop(0, 4)
    def _(i):
        r = pl.ds(pl.multiple_of(i * tall, tall), tall)
        gown[0, r, :] = (gown[0, r, :].astype(wide) + gsibs[0, r, :].astype(wide)).astype(
            gown.dtype
        )

    over = push(2, gown.at[0], grx, xn)
    over.start()
    last = None
    for step in steps:
        last = step if step is not None else last
    fold_finish(rows, o_ref, own, rx, ry, *last)
    loads[1].wait()
    sides[1].wait_recv()
    over.wait_recv()

    @pl.loop(0, 4)
    def _(i):
        r = pl.ds(pl.multiple_of(i * tall, tall), tall)
        k_ref[r, :] = (
            gown[1, r, :].astype(wide) + gsibs[1, r, :].astype(wide) + grx[r, :].astype(wide)
        )

    for copy in (*sides, over):
        copy.wait_send()


def fold_small(p, g, cid):
    h, total, d = p.shape
    rows = total // 8
    share, tall, _ = g.shape
    return pl.pallas_call(
        functools.partial(fold_small_kernel, rows),
        out_shape=(
            jax.ShapeDtypeStruct((h, rows, d), jnp.float32),
            jax.ShapeDtypeStruct((tall, d), jnp.float32),
        ),
        in_specs=[pl.BlockSpec(memory_space=pl.ANY)] * 2,
        out_specs=[pl.BlockSpec(memory_space=pltpu.VMEM)] * 2,
        scratch_shapes=fold_scratch(h, rows, d, p.dtype)
        + [
            pltpu.VMEM((2, tall, d), g.dtype),
            pltpu.VMEM((2, tall, d), g.dtype),
            pltpu.VMEM((tall, d), g.dtype),
            pltpu.SemaphoreType.DMA((2,)),
            pltpu.SemaphoreType.DMA((3,)),
            pltpu.SemaphoreType.DMA((3,)),
        ],
        compiler_params=pltpu.CompilerParams(
            collective_id=cid, has_side_effects=True, vmem_limit_bytes=40 << 20
        ),
        cost_estimate=pl.CostEstimate(flops=0, bytes_accessed=60_000_000, transcendentals=0),
        name="fold_small",
    )(p, g)


def open_kernel(
    rows, tiers, x_ref, s_ref, q_ref, w_ref, o_ref, sa_ref, qa_ref, wa_ref,
    local_sem, send, recv, line_send, line_recv,
):
    c, sib, xn, yn = partners()
    diag = yn + (xn - c)
    r = lax.axis_index("row")
    last = tiers - 1
    weights = ((s_ref, sa_ref), (q_ref, qa_ref), (w_ref, wa_ref))

    def slot(half, who):
        return o_ref.at[half, pl.ds(pl.multiple_of(who * rows, rows), rows), :]

    def both(who):
        return o_ref.at[:, pl.ds(pl.multiple_of(who * rows, rows), rows), :]

    started = []

    def push(src, dst, **dev):
        i = len(started)
        copy = pltpu.make_async_remote_copy(
            src_ref=src,
            dst_ref=dst,
            send_sem=send.at[i],
            recv_sem=recv.at[i],
            device_id=dev,
            device_id_type=MESH,
        )
        copy.start()
        started.append(copy)
        return copy

    local = [
        pltpu.make_async_copy(x_ref, both(c), local_sem.at[0]),
        pltpu.make_async_copy(s_ref, sa_ref.at[r], local_sem.at[1]),
        pltpu.make_async_copy(q_ref, qa_ref.at[r], local_sem.at[2]),
        pltpu.make_async_copy(w_ref, wa_ref.at[r], local_sem.at[3]),
    ]
    for copy in local:
        copy.start()
    barrier = pltpu.get_barrier_semaphore()
    for d in (sib, xn, yn):
        pl.semaphore_signal(barrier, inc=1, device_id={"col": d}, device_id_type=MESH)

    @pl.when(r < last)
    def _():
        pl.semaphore_signal(barrier, inc=1, device_id={"row": r + 1}, device_id_type=MESH)

    @pl.when(r > 0)
    def _():
        pl.semaphore_signal(barrier, inc=1, device_id={"row": r - 1}, device_id_type=MESH)

    @pl.when((r > 0) & (r < last))
    def _():
        pl.semaphore_wait(barrier, 5)

    @pl.when((r == 0) | (r == last))
    def _():
        pl.semaphore_wait(barrier, 4)

    def passing(way, hop, j):
        src, dst = weights[j]
        whose = r - hop if way == 0 else r + hop
        return pltpu.make_async_remote_copy(
            src_ref=src if hop == 0 else dst.at[whose],
            dst_ref=dst.at[whose],
            send_sem=line_send.at[way, hop, j],
            recv_sem=line_recv.at[way, hop, j],
            device_id={"row": r + 1 if way == 0 else r - 1},
            device_id_type=MESH,
        )

    def going(way, hop):
        return (r < last) & (r >= hop) if way == 0 else (r > 0) & (r + hop <= last)

    def coming(way, hop):
        return r > hop if way == 0 else r + hop < last

    def forward(hop, j):
        for way in range(2):
            if hop > 0:

                @pl.when(coming(way, hop - 1))
                def _():
                    passing(way, hop - 1, j).wait_recv()

            @pl.when(going(way, hop))
            def _():
                passing(way, hop, j).start()

    x0 = push(x_ref.at[0], slot(0, c), col=xn)
    y1 = push(x_ref.at[1], slot(1, c), col=yn)
    for j in range(3):
        forward(0, j)
    x1 = push(x_ref.at[1], slot(1, c), col=xn)
    y0 = push(x_ref.at[0], slot(0, c), col=yn)
    push(x_ref, both(c), col=sib)
    forward(1, 0)
    x0.wait_recv()
    fy = push(slot(0, xn), slot(0, xn), col=yn)
    push(slot(0, xn), slot(0, xn), col=sib)
    y1.wait_recv()
    fx = push(slot(1, yn), slot(1, yn), col=xn)
    push(slot(1, yn), slot(1, yn), col=sib)
    forward(1, 1)
    forward(1, 2)
    x1.wait_recv()
    push(slot(1, xn), slot(1, xn), col=sib)
    y0.wait_recv()
    push(slot(0, yn), slot(0, yn), col=sib)
    for hop in range(2, last):
        for j in range(3):
            forward(hop, j)
    fy.wait_recv()
    push(slot(0, diag), slot(0, diag), col=sib)
    fx.wait_recv()
    push(slot(1, diag), slot(1, diag), col=sib)
    for copy in started:
        if not any(copy is other for other in (x0, y1, x1, y0, fy, fx)):
            copy.wait_recv()
    for j in range(3):
        for way in range(2):

            @pl.when(coming(way, last - 1))
            def _():
                passing(way, last - 1, j).wait_recv()

            for hop in range(last):

                @pl.when(going(way, hop))
                def _():
                    passing(way, hop, j).wait_send()

    for copy in started:
        copy.wait_send()
    for copy in local:
        copy.wait()


def open_all(x, small, query, output, tiers, cid):
    h, rows, d = x.shape
    low = x.dtype
    copies = 13
    return pl.pallas_call(
        functools.partial(open_kernel, rows, tiers),
        out_shape=(
            jax.ShapeDtypeStruct((h, 8 * rows, d), low),
            jax.ShapeDtypeStruct((tiers, *small.shape), low),
            jax.ShapeDtypeStruct((tiers, *query.shape), low),
            jax.ShapeDtypeStruct((tiers, *output.shape), low),
        ),
        in_specs=[pl.BlockSpec(memory_space=pl.ANY)] * 4,
        out_specs=[pl.BlockSpec(memory_space=pl.ANY)] * 4,
        scratch_shapes=[
            pltpu.SemaphoreType.DMA((4,)),
            pltpu.SemaphoreType.DMA((copies,)),
            pltpu.SemaphoreType.DMA((copies,)),
            pltpu.SemaphoreType.DMA((2, tiers - 1, 3)),
            pltpu.SemaphoreType.DMA((2, tiers - 1, 3)),
        ],
        compiler_params=pltpu.CompilerParams(collective_id=cid, has_side_effects=True),
        cost_estimate=pl.CostEstimate(flops=0, bytes_accessed=200_000_000, transcendentals=0),
        name="open_all",
    )(x, small, query, output)


def share_kernel(near, s_ref, sa_ref, local_sem, send, recv):
    c, sib, xn, yn = partners()
    diag = yn + (xn - c)
    height = s_ref.shape[1]
    started = []

    def part(ref, first):
        return ref.at[:, pl.ds(0, near) if first else pl.ds(near, height - near), :]

    def push(who, first, dev, own=False):
        i = len(started)
        dst = part(sa_ref.at[who], first)
        copy = pltpu.make_async_remote_copy(
            src_ref=part(s_ref, first) if own else dst,
            dst_ref=dst,
            send_sem=send.at[i],
            recv_sem=recv.at[i],
            device_id={"col": dev},
            device_id_type=MESH,
        )
        copy.start()
        started.append(copy)
        return copy

    mine = pltpu.make_async_copy(s_ref, sa_ref.at[c], local_sem)
    mine.start()
    greet((sib, xn, yn))
    rx = push(c, False, xn, own=True)
    ry = push(c, False, yn, own=True)
    kx = push(c, True, xn, own=True)
    push(c, True, sib, own=True)
    push(c, False, sib, own=True)
    rx.wait_recv()
    fd = push(xn, False, yn)
    push(xn, False, sib)
    ry.wait_recv()
    push(yn, False, sib)
    fd.wait_recv()
    push(diag, False, sib)
    kx.wait_recv()
    push(xn, True, sib)
    for copy in started:
        if not any(copy is other for other in (kx, rx, ry, fd)):
            copy.wait_recv()
    for copy in started:
        copy.wait_send()
    mine.wait()


def share_small(small, near, cid):
    return pl.pallas_call(
        functools.partial(share_kernel, near),
        out_shape=jax.ShapeDtypeStruct((8, *small.shape), small.dtype),
        in_specs=[pl.BlockSpec(memory_space=pl.ANY)],
        out_specs=pl.BlockSpec(memory_space=pl.ANY),
        scratch_shapes=[
            pltpu.SemaphoreType.DMA,
            pltpu.SemaphoreType.DMA((10,)),
            pltpu.SemaphoreType.DMA((10,)),
        ],
        compiler_params=pltpu.CompilerParams(collective_id=cid, has_side_effects=True),
        cost_estimate=pl.CostEstimate(flops=0, bytes_accessed=60_000_000, transcendentals=0),
        name="share_small",
    )(small)


def rounds_of(rows, x_ref, held, local_sem, send, recv, consume, prepare):
    c, sib, xn, yn = partners()
    diag = yn + (xn - c)
    step = sib - c

    def place(t, j, n=1):
        return held.at[t, pl.ds(j * rows, n * rows), :]

    started = []

    def push(src, dst, dev):
        i = len(started)
        copy = pltpu.make_async_remote_copy(
            src_ref=src,
            dst_ref=dst,
            send_sem=send.at[i],
            recv_sem=recv.at[i],
            device_id={"col": dev},
            device_id_type=MESH,
        )
        copy.start()
        started.append(copy)
        return copy

    mine = [pltpu.make_async_copy(x_ref.at[h], place(0, h), local_sem.at[h]) for h in range(2)]
    for copy in mine:
        copy.start()
    greet((sib, xn, yn))
    x0 = push(x_ref.at[0], place(1, 0), xn)
    y1 = push(x_ref.at[1], place(1, 1), yn)
    x1 = push(x_ref.at[1], place(2, 0), xn)
    y0 = push(x_ref.at[0], place(2, 1), yn)
    s0 = push(x_ref.at[0], place(0, 2), sib)
    s1 = push(x_ref.at[1], place(0, 3), sib)
    prepare(0)
    for copy in mine:
        copy.wait()
    s0.wait_recv()
    s1.wait_recv()
    consume(0, ((0, c), (1, c), (0, sib), (1, sib)))
    x0.wait_recv()
    fy = push(place(1, 0), place(3, 0), yn)
    y1.wait_recv()
    fx = push(place(1, 1), place(3, 1), xn)
    prepare(1)
    t1 = push(place(1, 0, 2), place(1, 2, 2), sib)
    t1.wait_recv()
    consume(1, ((0, xn), (1, yn), (0, xn + step), (1, yn + step)))
    prepare(2)
    x1.wait_recv()
    y0.wait_recv()
    t2 = push(place(2, 0, 2), place(2, 2, 2), sib)
    t2.wait_recv()
    consume(2, ((1, xn), (0, yn), (1, xn + step), (0, yn + step)))
    prepare(3)
    fy.wait_recv()
    fx.wait_recv()
    t3 = push(place(3, 0, 2), place(3, 2, 2), sib)
    t3.wait_recv()
    consume(3, ((0, diag), (1, diag), (0, diag + step), (1, diag + step)))
    for copy in started:
        copy.wait_send()


def piece_at(ref, rows, piece):
    half, who = piece
    return ref.at[half, pl.ds(pl.multiple_of(who * rows, rows), rows), :]


def units_back_kernel(
    rows, x_ref, w_ref, u_ref, g_ref, v_ref, p_ref, d_ref,
    held, weights, units, turned, gates, ups, grads, total_ref,
    weight_sem, load_sem, store_sem, local_sem, send, recv,
):
    c, sib, xn, yn = partners()
    diag = yn + (xn - c)
    step = sib - c
    wide = jnp.float32
    width = w_ref.shape[0]
    d = w_ref.shape[1]
    plan = (
        ((0, c), (1, c), (0, sib), (1, sib)),
        ((0, xn), (1, yn), (0, xn + step), (1, yn + step)),
        ((1, xn), (0, yn), (1, xn + step), (0, yn + step)),
        ((0, diag), (1, diag), (0, diag + step), (1, diag + step)),
    )
    fetch = pltpu.make_async_copy(w_ref, weights, weight_sem)
    fetch.start()

    def loads(t):
        copies = []
        for j, piece in enumerate(plan[t]):
            for k, (src, dst) in enumerate(((u_ref, units), (g_ref, gates), (v_ref, ups))):
                copies.append(
                    pltpu.make_async_copy(
                        piece_at(src, rows, piece),
                        dst.at[t % 2, pl.ds(j * rows, rows), :],
                        load_sem.at[t % 2, j, k],
                    )
                )
        return copies

    def stores(t):
        return [
            pltpu.make_async_copy(
                grads.at[t % 2, pl.ds(j * rows, rows), :],
                piece_at(p_ref, rows, piece),
                store_sem.at[t % 2, j],
            )
            for j, piece in enumerate(plan[t])
        ]

    for copy in loads(0):
        copy.start()

    tile = 256

    def prepare(t):
        if t == 0:
            fetch.wait()
        if t < 3:
            for copy in loads(t + 1):
                copy.start()
        for copy in loads(t):
            copy.wait()

        @pl.loop(0, width // tile)
        def _(n):
            cut = pl.ds(pl.multiple_of(n * tile, tile), tile)
            gate = gates[t % 2, :, cut]
            square = gate * gate
            bent = jnp.tanh(CURVE * (gate + BEND * gate * square))
            rise = 0.5 * (1.0 + bent)
            slope = rise + (0.5 * CURVE) * gate * (1.0 - bent * bent) * (1.0 + 3.0 * BEND * square)
            gates[t % 2, :, cut] = ups[t % 2, :, cut] * slope
            ups[t % 2, :, cut] = gate * rise
            turned[cut, :] = units[t % 2, :, cut].T

    def consume(t, pieces):
        if t >= 2:
            for copy in stores(t - 2):
                copy.wait()

        @pl.loop(0, width // tile)
        def _(n):
            cut = pl.ds(pl.multiple_of(n * tile, tile), tile)
            grad = lax.dot_general(
                held[t], weights[cut, :], (((1,), (1,)), ((), ())), preferred_element_type=wide
            )
            grads[t % 2, :, cut] = (grad * gates[t % 2, :, cut]).astype(grads.dtype)
            cut_up = pl.ds(pl.multiple_of(width + n * tile, tile), tile)
            grads[t % 2, :, cut_up] = (grad * ups[t % 2, :, cut]).astype(grads.dtype)

        for copy in stores(t):
            copy.start()

        @pl.loop(0, d // tile)
        def _(n):
            cut = pl.ds(pl.multiple_of(n * tile, tile), tile)
            value = jnp.dot(turned[...], held[t, :, cut], preferred_element_type=wide)
            if t > 0:
                value = value + total_ref[:, cut]
            if t < 3:
                total_ref[:, cut] = value
            else:
                d_ref[:, cut] = value.astype(d_ref.dtype)

    rounds_of(rows, x_ref, held, local_sem, send, recv, consume, prepare)
    for copy in (*stores(2), *stores(3)):
        copy.wait()


def units_back(x, down, units, gate, up, cid):
    h, rows, d = x.shape
    width = down.shape[0]
    low = x.dtype
    return pl.pallas_call(
        functools.partial(units_back_kernel, rows),
        out_shape=(
            jax.ShapeDtypeStruct((h, 8 * rows, 2 * width), low),
            jax.ShapeDtypeStruct((width, d), low),
        ),
        in_specs=[pl.BlockSpec(memory_space=pl.ANY)] * 5,
        out_specs=[
            pl.BlockSpec(memory_space=pl.ANY),
            pl.BlockSpec(memory_space=pltpu.VMEM),
        ],
        scratch_shapes=[
            pltpu.VMEM((4, 4 * rows, d), low),
            pltpu.VMEM((width, d), low),
            pltpu.VMEM((2, 4 * rows, width), low),
            pltpu.VMEM((width, 4 * rows), low),
            pltpu.VMEM((2, 4 * rows, width), jnp.float32),
            pltpu.VMEM((2, 4 * rows, width), jnp.float32),
            pltpu.VMEM((2, 4 * rows, 2 * width), low),
            pltpu.VMEM((width, d), jnp.float32),
            pltpu.SemaphoreType.DMA,
            pltpu.SemaphoreType.DMA((2, 4, 3)),
            pltpu.SemaphoreType.DMA((2, 4)),
            pltpu.SemaphoreType.DMA((2,)),
            pltpu.SemaphoreType.DMA((11,)),
            pltpu.SemaphoreType.DMA((11,)),
        ],
        compiler_params=pltpu.CompilerParams(
            collective_id=cid, has_side_effects=True, vmem_limit_bytes=52 << 20
        ),
        cost_estimate=pl.CostEstimate(
            flops=64 * h * rows * width * d, bytes_accessed=130_000_000, transcendentals=0
        ),
        name="units_back",
    )(x, down, units, gate, up)


def heads_back_kernel(
    rows, scale, x_ref, w_ref, m_ref, q_ref, k_ref, v_ref, s_ref, gq_ref, gk_ref, gv_ref, d_ref,
    held, weights, mixed, queries, keys, values, seen, total_ref, load_sem, local_sem, send, recv,
):
    wide = jnp.float32
    d = w_ref.shape[1]
    low = weights.dtype
    pairs = (
        (w_ref, weights), (q_ref, queries), (k_ref, keys), (v_ref, values), (s_ref, seen),
        (m_ref, mixed),
    )
    loads = [
        pltpu.make_async_copy(src, dst, load_sem.at[i]) for i, (src, dst) in enumerate(pairs)
    ]
    for copy in loads:
        copy.start()
    back = (((1,), (1,)), ((), ()))

    def prepare(t):
        if t == 0:
            for copy in loads:
                copy.wait()
            gk_ref[...] = jnp.zeros_like(gk_ref)
            gv_ref[...] = jnp.zeros_like(gv_ref)

    def consume(t, pieces):
        grad_mixed = lax.dot_general(held[t], weights[...], back, preferred_element_type=wide)
        grad_mixed = grad_mixed.astype(low)
        spans = []
        for j, (half, who) in enumerate(pieces):
            span = pl.ds(pl.multiple_of(who * rows, rows), rows)
            spans.append(mixed[half, span, :])
            query = queries[half, span, :]
            grad = grad_mixed[j * rows : (j + 1) * rows]
            score = lax.dot_general(query, keys[half], back, preferred_element_type=wide) * scale
            score = jnp.where(seen[half, span, :] > 0, score, NEGATIVE)
            power = jnp.exp(score - jnp.max(score, axis=-1, keepdims=True))
            prob = power / jnp.sum(power, axis=-1, keepdims=True)
            slope = lax.dot_general(grad, values[half], back, preferred_element_type=wide)
            mean = jnp.sum(prob * slope, axis=-1, keepdims=True)
            flow = (prob * (slope - mean)).astype(low)
            gq_ref[half, span, :] = jnp.dot(flow, keys[half], preferred_element_type=wide) * scale
            gk_ref[half] += jnp.dot(flow.T, query, preferred_element_type=wide) * scale
            gv_ref[half] += jnp.dot(prob.astype(low).T, grad, preferred_element_type=wide)
        turned = jnp.concatenate(spans, axis=0).T

        @pl.loop(0, d // 512)
        def _(n):
            cut = pl.ds(pl.multiple_of(n * 512, 512), 512)
            value = jnp.dot(turned, held[t, :, cut], preferred_element_type=wide)
            if t > 0:
                value = value + total_ref[:, cut]
            if t < 3:
                total_ref[:, cut] = value
            else:
                d_ref[:, cut] = value.astype(d_ref.dtype)

    rounds_of(rows, x_ref, held, local_sem, send, recv, consume, prepare)


def heads_back(x, output, mixed, query, key, value, visible, scale, cid):
    h, rows, d = x.shape
    low = x.dtype
    grad = jax.ShapeDtypeStruct(query.shape, jnp.float32)
    return pl.pallas_call(
        functools.partial(heads_back_kernel, rows, scale),
        out_shape=(grad, grad, grad, jax.ShapeDtypeStruct(output.shape, low)),
        in_specs=[pl.BlockSpec(memory_space=pl.ANY)] * 7,
        out_specs=[pl.BlockSpec(memory_space=pltpu.VMEM)] * 4,
        scratch_shapes=[
            pltpu.VMEM((4, 4 * rows, d), low),
            pltpu.VMEM(output.shape, low),
            pltpu.VMEM(mixed.shape, low),
            pltpu.VMEM(query.shape, low),
            pltpu.VMEM(query.shape, low),
            pltpu.VMEM(query.shape, low),
            pltpu.VMEM(visible.shape, visible.dtype),
            pltpu.VMEM(output.shape, jnp.float32),
            pltpu.SemaphoreType.DMA((6,)),
            pltpu.SemaphoreType.DMA((2,)),
            pltpu.SemaphoreType.DMA((11,)),
            pltpu.SemaphoreType.DMA((11,)),
        ],
        compiler_params=pltpu.CompilerParams(
            collective_id=cid, has_side_effects=True, vmem_limit_bytes=48 << 20
        ),
        cost_estimate=pl.CostEstimate(
            flops=20_000_000_000, bytes_accessed=130_000_000, transcendentals=0
        ),
        name="heads_back",
    )(x, output, mixed, query, key, value, visible)


def total_kernel(x_ref, o_ref, sums, got, tier_sums, send, recv):
    c, sib, xn, yn = partners()
    r = lax.axis_index("row")
    tiers = lax.axis_size("row")
    others = [lax.rem(r + k, tiers) for k in range(1, tiers)]
    barrier = pltpu.get_barrier_semaphore()
    for d in (sib, xn, yn):
        pl.semaphore_signal(barrier, inc=1, device_id={"col": d}, device_id_type=MESH)
    for d in others:
        pl.semaphore_signal(barrier, inc=1, device_id={"row": d}, device_id_type=MESH)
    pl.semaphore_wait(barrier, 3 + len(others))
    sums[0] = x_ref[...]
    for i, dev in enumerate((sib, xn, yn)):
        copy = pltpu.make_async_remote_copy(
            src_ref=sums.at[i],
            dst_ref=got.at[i],
            send_sem=send.at[i],
            recv_sem=recv.at[i],
            device_id={"col": dev},
            device_id_type=MESH,
        )
        copy.start()
        copy.wait()
        sums[i + 1] = sums[i] + got[i]
    tier_sums[r] = sums[3]
    copies = []
    for k, d in enumerate(others):
        copy = pltpu.make_async_remote_copy(
            src_ref=sums.at[3],
            dst_ref=tier_sums.at[r],
            send_sem=send.at[3 + k],
            recv_sem=recv.at[3 + k],
            device_id={"row": d},
            device_id_type=MESH,
        )
        copy.start()
        copies.append(copy)
    for copy in copies:
        copy.wait()
    result = tier_sums[0]
    for k in range(1, tiers):
        result = result + tier_sums[k]
    o_ref[...] = result


def total(x, tiers, cid):
    return pl.pallas_call(
        total_kernel,
        out_shape=jax.ShapeDtypeStruct(x.shape, x.dtype),
        in_specs=[pl.BlockSpec(memory_space=pltpu.VMEM)],
        out_specs=pl.BlockSpec(memory_space=pltpu.VMEM),
        scratch_shapes=[
            pltpu.VMEM((4, *x.shape), x.dtype),
            pltpu.VMEM((3, *x.shape), x.dtype),
            pltpu.VMEM((tiers, *x.shape), x.dtype),
            pltpu.SemaphoreType.DMA((2 + tiers,)),
            pltpu.SemaphoreType.DMA((2 + tiers,)),
        ],
        compiler_params=pltpu.CompilerParams(collective_id=cid, has_side_effects=True),
        cost_estimate=pl.CostEstimate(flops=0, bytes_accessed=40_000_000, transcendentals=0),
        name="total",
    )(x)


def after(value, *earlier):
    return lax.optimization_barrier((value, *earlier))[0]


def general_body(
    hidden,
    per_layer,
    lengths,
    block_ids,
    out_grad,
    query_weight,
    key_weight,
    value_weight,
    output_weight,
    gate_weight,
    up_weight,
    down_weight,
    laurel_left,
    laurel_right,
    layer_gate,
    layer_proj,
    norm_gains,
    head_gains,
):
    local_rows = hidden.shape[0]
    seq_groups = hidden.shape[1]
    col_index = lax.axis_index("col")
    row_index = lax.axis_index("row")
    all_lengths = lengths
    lengths = lax.dynamic_slice_in_dim(all_lengths, row_index * seq_groups, seq_groups, 0)
    (
        query_cols,
        key_cols,
        value_cols,
        output_rows,
        gate_cols,
        up_cols,
        down_rows,
        left_cols,
        right_rows,
        gate_layer_cols,
        proj_layer_rows,
    ) = (
        lax.all_gather(query_weight, "row", axis=0, tiled=True),
        lax.all_gather(key_weight, "row", axis=0, tiled=True),
        lax.all_gather(value_weight, "row", axis=0, tiled=True),
        lax.all_gather(output_weight, "row", axis=1, tiled=True),
        lax.all_gather(gate_weight, "row", axis=0, tiled=True),
        lax.all_gather(up_weight, "row", axis=0, tiled=True),
        lax.all_gather(down_weight, "row", axis=1, tiled=True),
        lax.all_gather(laurel_left, "row", axis=0, tiled=True),
        lax.all_gather(laurel_right, "row", axis=1, tiled=True),
        lax.all_gather(layer_gate, "row", axis=0, tiled=True),
        lax.all_gather(layer_proj, "row", axis=1, tiled=True),
    )
    (
        query_full,
        key_full,
        value_full,
        output_full,
        left_full,
        right_full,
        gate_layer_full,
        proj_layer_full,
    ) = (
        lax.all_gather(query_cols, "col", axis=1, tiled=True),
        lax.all_gather(key_cols, "col", axis=1, tiled=True),
        lax.all_gather(value_cols, "col", axis=1, tiled=True),
        lax.all_gather(output_rows, "col", axis=0, tiled=True),
        lax.all_gather(left_cols, "col", axis=1, tiled=True),
        lax.all_gather(right_rows, "col", axis=0, tiled=True),
        lax.all_gather(gate_layer_cols, "col", axis=1, tiled=True),
        lax.all_gather(proj_layer_rows, "col", axis=0, tiled=True),
    )
    paired = jnp.concatenate([gate_cols, up_cols], axis=1)
    unit_width = gate_cols.shape[1]
    first_position = col_index * local_rows
    positions = first_position + jnp.arange(local_rows, dtype=jnp.int32)
    live_mask = positions[:, None] < lengths[None, :]
    keep_mask = live_mask.astype(jnp.float32)[:, :, None]
    reach_back = (WINDOW + local_rows - 2) // local_rows
    reach_ahead = (BLOCK + local_rows - 2) // local_rows
    key_span = (reach_back + 1 + reach_ahead) * local_rows
    key_position = first_position - reach_back * local_rows + jnp.arange(key_span, dtype=jnp.int32)
    filler_low = jnp.full((seq_groups, reach_back * local_rows), FAR_BLOCK, jnp.int32)
    filler_high = jnp.full((seq_groups, reach_ahead * local_rows), FAR_BLOCK, jnp.int32)
    padded_blocks = jnp.concatenate([filler_low, block_ids, filler_high], axis=1)
    key_blocks = lax.dynamic_slice_in_dim(padded_blocks, first_position, key_span, 1)
    query_blocks = lax.dynamic_slice_in_dim(block_ids, first_position, local_rows, 1)
    key_live = (key_position[None, :] >= 0) & (key_position[None, :] < lengths[:, None])
    query_live = positions[None, :] < lengths[:, None]
    distance = positions[:, None] - key_position[None, :]
    nearby = (query_blocks[:, :, None] >= key_blocks[:, None, :]) & (distance < WINDOW)[None]
    nearby = nearby & query_live[:, :, None] & key_live[:, None, :]
    visible = (nearby | (distance == 0)[None])[:, None, None]
    residual = hidden.astype(jnp.float32)
    normed_value, input_back = jax.vjp(input_norm, residual, norm_gains)
    normed_low = normed_value.astype(jnp.bfloat16)
    half_width = HD // 2
    frequency = jnp.exp(jnp.arange(half_width, dtype=jnp.float32) * (-2.0 * math.log(10000.0) / HD))
    angles = (positions.astype(jnp.float32)[:, None] * frequency[None, :])[:, None, None, :]

    def prepare(query_in, key_in, value_in, gain_rows):
        return (
            rotate(root_norm(query_in, gain_rows[0]), angles),
            rotate(root_norm(key_in, gain_rows[1]), angles),
            plain_norm(value_in),
        )

    query_raw = matmul_last(normed_low, query_full).reshape(local_rows, seq_groups, H, HD)
    key_raw = matmul_last(normed_low, key_full).reshape(local_rows, seq_groups, KV, HD)
    value_raw = matmul_last(normed_low, value_full).reshape(local_rows, seq_groups, KV, HD)
    (query_value, key_value, value_value), head_back = jax.vjp(
        prepare, query_raw, key_raw, value_raw, head_gains
    )
    query_low = query_value.astype(jnp.bfloat16).reshape(local_rows, seq_groups, KV, H // KV, HD)
    key_low = key_value.astype(jnp.bfloat16)
    value_low = value_value.astype(jnp.bfloat16)
    offsets = list(range(reach_back, -reach_ahead - 1, -1))
    key_parts = []
    value_parts = []
    for offset in offsets:
        if offset == 0:
            key_parts.append(key_low)
            value_parts.append(value_low)
        else:
            moved_key, moved_value = passed_along((key_low, value_low), "col", offset)
            key_parts.append(moved_key)
            value_parts.append(moved_value)
    near_keys = jnp.concatenate(key_parts, axis=0)
    near_values = jnp.concatenate(value_parts, axis=0)
    score_scale = HD ** (-0.5)

    def score_all():
        raw_scores = (
            jnp.einsum(
                "psjgd,esjd->sjgpe", query_low, near_keys, preferred_element_type=jnp.float32
            )
            * score_scale
        )
        return jnp.where(visible, raw_scores, NEGATIVE)

    scores = score_all()
    row_max = jnp.max(scores, axis=-1, keepdims=True)
    exponent = jnp.exp(scores - row_max)
    row_total = jnp.sum(exponent, axis=-1, keepdims=True)
    attn_prob = exponent / row_total
    log_total = row_max + jnp.log(row_total)
    mixed_heads = jnp.einsum(
        "sjgpe,esjd->psjgd",
        attn_prob.astype(jnp.bfloat16),
        near_values,
        preferred_element_type=jnp.float32,
    )
    mixed_low = mixed_heads.reshape(local_rows, seq_groups, H * HD).astype(jnp.bfloat16)
    out_proj = matmul_last(mixed_low, output_full)
    laurel_mid = matmul_last(normed_low, left_full).astype(jnp.bfloat16)
    low_rank = matmul_last(laurel_mid, right_full)
    (after_attention, feed_normed), middle_back = jax.vjp(
        middle, residual, out_proj, low_rank, normed_low.astype(jnp.float32), norm_gains
    )
    feed_low = feed_normed.astype(jnp.bfloat16)
    gate_up = matmul_last(lax.all_gather(feed_low, "col", axis=0, tiled=True), paired)
    unit_value, gate_back = jax.vjp(
        gated_product, gate_up[..., :unit_width], gate_up[..., unit_width:]
    )
    units_low = unit_value.astype(jnp.bfloat16)
    summed = lax.psum_scatter(
        matmul_last(units_low, down_rows), "col", scatter_dimension=0, tiled=True
    )
    after_feed, feed_back = jax.vjp(feed_join, after_attention, summed, norm_gains)
    feed_round = after_feed.astype(jnp.bfloat16)
    layer_pre = matmul_last(feed_round, gate_layer_full)
    layer_input = per_layer.astype(jnp.float32)
    layer_value, layer_back = jax.vjp(gated_product, layer_pre, layer_input)
    layer_low = layer_value.astype(jnp.bfloat16)
    projected = matmul_last(layer_low, proj_layer_full)
    out_value, final_back = jax.vjp(final_join, after_feed, projected, norm_gains)
    square_sums = jnp.stack(
        [
            jnp.sum(keep_mask * residual * residual),
            jnp.sum(keep_mask * after_attention * after_attention),
            jnp.sum(keep_mask * after_feed * after_feed),
            jnp.sum(keep_mask * out_value * out_value),
        ]
    )
    valid_count = jnp.sum(all_lengths).astype(jnp.float32)
    cotangent = out_grad.astype(jnp.float32) * keep_mask
    grad_feed_out, grad_projected, gains_final = final_back(cotangent)
    projected_low = grad_projected.astype(jnp.bfloat16)
    grad_proj_layer = outer_sum(layer_low, projected_low)
    grad_layer_pre, grad_layer_input = layer_back(matmul_back(projected_low, proj_layer_full))
    layer_pre_low = grad_layer_pre.astype(jnp.bfloat16)
    grad_gate_layer = outer_sum(feed_round, layer_pre_low)
    grad_after_feed = grad_feed_out + matmul_back(layer_pre_low, gate_layer_full)
    grad_after_attention_a, grad_summed, gains_feed = feed_back(grad_after_feed)
    summed_low = grad_summed.astype(jnp.bfloat16)
    block_rows = lax.all_gather(summed_low, "col", axis=0, tiled=True)
    grad_down = outer_sum(units_low, block_rows)
    grad_units = matmul_back(block_rows, down_rows)
    grad_down, grad_units = (grad_down, grad_units)
    grad_gate_value, grad_up_value = gate_back(grad_units)
    grad_paired = jnp.concatenate([grad_gate_value, grad_up_value], axis=-1).astype(jnp.bfloat16)
    grad_weights_paired = outer_sum(
        lax.all_gather(feed_low, "col", axis=0, tiled=True), grad_paired
    )
    grad_feed = lax.psum_scatter(
        matmul_back(grad_paired, paired).astype(jnp.bfloat16),
        "col",
        scatter_dimension=0,
        tiled=True,
    ).astype(jnp.float32)
    grad_residual_mid, grad_out_proj, grad_low_rank, grad_normed_mid, gains_middle = middle_back(
        (grad_after_attention_a, grad_feed)
    )
    out_proj_low = grad_out_proj.astype(jnp.bfloat16)
    grad_output = outer_sum(mixed_low, out_proj_low)
    grad_mixed = matmul_back(out_proj_low, output_full).astype(jnp.bfloat16)
    grad_mixed = grad_mixed.reshape(local_rows, seq_groups, KV, H // KV, HD)
    low_rank_grad = grad_low_rank.astype(jnp.bfloat16)
    grad_right = outer_sum(laurel_mid, low_rank_grad)
    grad_laurel_mid = matmul_back(low_rank_grad, right_full).astype(jnp.bfloat16)
    grad_left = outer_sum(normed_low, grad_laurel_mid)
    scores = score_all()
    attn_prob = jnp.exp(scores - log_total)
    grad_prob = jnp.einsum(
        "psjgd,esjd->sjgpe", grad_mixed, near_values, preferred_element_type=jnp.float32
    )
    grad_scores = (
        attn_prob * (grad_prob - jnp.sum(attn_prob * grad_prob, axis=-1, keepdims=True))
    ).astype(jnp.bfloat16)
    grad_queries = (
        jnp.einsum("sjgpe,esjd->psjgd", grad_scores, near_keys, preferred_element_type=jnp.float32)
        * score_scale
    )
    grad_near_keys = (
        jnp.einsum("sjgpe,psjgd->esjd", grad_scores, query_low, preferred_element_type=jnp.float32)
        * score_scale
    )
    grad_near_values = jnp.einsum(
        "sjgpe,psjgd->esjd",
        attn_prob.astype(jnp.bfloat16),
        grad_mixed,
        preferred_element_type=jnp.float32,
    )
    grad_key_total = grad_near_keys[reach_back * local_rows : (reach_back + 1) * local_rows]
    grad_value_total = grad_near_values[reach_back * local_rows : (reach_back + 1) * local_rows]
    for slot_index, offset in enumerate(offsets):
        if offset != 0:
            piece_keys = grad_near_keys[slot_index * local_rows : (slot_index + 1) * local_rows]
            piece_values = grad_near_values[slot_index * local_rows : (slot_index + 1) * local_rows]
            back_keys, back_values = (
                passed_along(piece_keys.astype(jnp.bfloat16), "col", -offset).astype(
                    piece_keys.dtype
                ),
                passed_along(piece_values.astype(jnp.bfloat16), "col", -offset).astype(
                    piece_values.dtype
                ),
            )
            grad_key_total = grad_key_total + back_keys
            grad_value_total = grad_value_total + back_values
    grad_query_raw, grad_key_raw, grad_value_raw, grad_heads = head_back(
        (grad_queries.reshape(local_rows, seq_groups, H, HD), grad_key_total, grad_value_total)
    )
    query_grad_low = grad_query_raw.reshape(local_rows, seq_groups, H * HD).astype(jnp.bfloat16)
    key_grad_low = grad_key_raw.reshape(local_rows, seq_groups, KV * HD).astype(jnp.bfloat16)
    value_grad_low = grad_value_raw.reshape(local_rows, seq_groups, KV * HD).astype(jnp.bfloat16)
    grad_query = outer_sum(normed_low, query_grad_low)
    grad_key = outer_sum(normed_low, key_grad_low)
    grad_value = outer_sum(normed_low, value_grad_low)
    grad_normed = (
        grad_normed_mid
        + matmul_back(grad_laurel_mid, left_full)
        + matmul_back(query_grad_low, query_full)
        + matmul_back(key_grad_low, key_full)
        + matmul_back(value_grad_low, value_full)
    )
    grad_residual_in, gains_input = input_back(grad_normed)
    d_hidden = (grad_residual_mid + grad_residual_in).astype(jnp.bfloat16)
    d_per_layer = grad_layer_input.astype(jnp.bfloat16)
    grad_gains = gains_final + gains_feed + gains_middle + gains_input
    grad_gate = grad_weights_paired[:, :unit_width]
    grad_up = grad_weights_paired[:, unit_width:]
    (
        query_part,
        key_part,
        value_part,
        output_part,
        left_part,
        right_part,
        gate_layer_part,
        proj_layer_part,
    ) = (
        lax.psum_scatter(
            grad_query.astype(jnp.bfloat16), "col", scatter_dimension=1, tiled=True
        ).astype(jnp.float32),
        lax.psum_scatter(
            grad_key.astype(jnp.bfloat16), "col", scatter_dimension=1, tiled=True
        ).astype(jnp.float32),
        lax.psum_scatter(
            grad_value.astype(jnp.bfloat16), "col", scatter_dimension=1, tiled=True
        ).astype(jnp.float32),
        lax.psum_scatter(
            grad_output.astype(jnp.bfloat16), "col", scatter_dimension=0, tiled=True
        ).astype(jnp.float32),
        lax.psum_scatter(
            grad_left.astype(jnp.bfloat16), "col", scatter_dimension=1, tiled=True
        ).astype(jnp.float32),
        lax.psum_scatter(
            grad_right.astype(jnp.bfloat16), "col", scatter_dimension=0, tiled=True
        ).astype(jnp.float32),
        lax.psum_scatter(
            grad_gate_layer.astype(jnp.bfloat16), "col", scatter_dimension=1, tiled=True
        ).astype(jnp.float32),
        lax.psum_scatter(
            grad_proj_layer.astype(jnp.bfloat16), "col", scatter_dimension=0, tiled=True
        ).astype(jnp.float32),
    )
    (
        d_query_weight,
        d_key_weight,
        d_value_weight,
        d_output_weight,
        d_gate_weight,
        d_up_weight,
        d_down_weight,
        d_laurel_left,
        d_laurel_right,
        d_layer_gate,
        d_layer_proj,
    ) = (
        lax.psum_scatter(
            query_part.astype(jnp.bfloat16), "row", scatter_dimension=0, tiled=True
        ).astype(jnp.float32),
        lax.psum_scatter(
            key_part.astype(jnp.bfloat16), "row", scatter_dimension=0, tiled=True
        ).astype(jnp.float32),
        lax.psum_scatter(
            value_part.astype(jnp.bfloat16), "row", scatter_dimension=0, tiled=True
        ).astype(jnp.float32),
        lax.psum_scatter(
            output_part.astype(jnp.bfloat16), "row", scatter_dimension=1, tiled=True
        ).astype(jnp.float32),
        lax.psum_scatter(
            grad_gate.astype(jnp.bfloat16), "row", scatter_dimension=0, tiled=True
        ).astype(jnp.float32),
        lax.psum_scatter(
            grad_up.astype(jnp.bfloat16), "row", scatter_dimension=0, tiled=True
        ).astype(jnp.float32),
        lax.psum_scatter(
            grad_down.astype(jnp.bfloat16), "row", scatter_dimension=1, tiled=True
        ).astype(jnp.float32),
        lax.psum_scatter(
            left_part.astype(jnp.bfloat16), "row", scatter_dimension=0, tiled=True
        ).astype(jnp.float32),
        lax.psum_scatter(
            right_part.astype(jnp.bfloat16), "row", scatter_dimension=1, tiled=True
        ).astype(jnp.float32),
        lax.psum_scatter(
            gate_layer_part.astype(jnp.bfloat16), "row", scatter_dimension=0, tiled=True
        ).astype(jnp.float32),
        lax.psum_scatter(
            proj_layer_part.astype(jnp.bfloat16), "row", scatter_dimension=1, tiled=True
        ).astype(jnp.float32),
    )
    d_norm_gains, d_head_gains, total_squares = lax.psum(
        (grad_gains, grad_heads, square_sums), ("row", "col")
    )
    stats = jnp.sqrt(total_squares / (valid_count * D))
    output = out_value.astype(jnp.bfloat16)
    return (
        output,
        stats,
        d_hidden,
        d_per_layer,
        d_query_weight,
        d_key_weight,
        d_value_weight,
        d_output_weight,
        d_gate_weight,
        d_up_weight,
        d_down_weight,
        d_laurel_left,
        d_laurel_right,
        d_layer_gate,
        d_layer_proj,
        d_norm_gains,
        d_head_gains,
    )


def swap(array):
    return jnp.swapaxes(array, 0, 1)


def heads_body(
    hidden,
    per_layer,
    lengths,
    block_ids,
    out_grad,
    query_weight,
    key_weight,
    value_weight,
    output_weight,
    gate_weight,
    up_weight,
    down_weight,
    laurel_left,
    laurel_right,
    layer_gate,
    layer_proj,
    norm_gains,
    head_gains,
):
    low = jnp.bfloat16
    rows = hidden.shape[0]
    groups = hidden.shape[1]
    cols = lax.axis_size("col")
    seq = rows * cols
    share = cols // KV
    col_index = lax.axis_index("col")
    row_index = lax.axis_index("row")
    all_lengths = lengths
    lengths = lax.dynamic_slice_in_dim(all_lengths, row_index * groups, groups, 0)

    small = jnp.concatenate(
        [key_weight.T, value_weight.T, laurel_left.T, layer_gate.T, laurel_right, layer_proj],
        axis=0,
    )
    heights = [key_weight.shape[1], value_weight.shape[1], laurel_left.shape[1]]
    heights += [layer_gate.shape[1], laurel_right.shape[0], layer_proj.shape[0]]
    edges = [sum(heights[:i]) for i in range(len(heights) + 1)]
    unit_width = gate_weight.shape[1]
    residual = swap(hidden).astype(jnp.float32)
    normed_value, input_back = jax.vjp(input_norm, residual, norm_gains)
    normed_low = normed_value.astype(low)
    tiers = lax.axis_size("row")
    normed_all, small_row, query_full, output_full = open_all(
        normed_low, small, query_weight, output_weight, tiers, 1
    )
    small_all = share_small(small_row, heights[0] + heights[1], 8)
    both_weights = jnp.concatenate([gate_weight, up_weight], axis=1)
    paired = lax.all_gather(after(both_weights, normed_all), "row", axis=0, tiled=True)
    down_full = lax.all_gather(after(down_weight, normed_all), "row", axis=1, tiled=True)
    query_full = query_full.reshape(D, HD).T
    output_full = jnp.swapaxes(output_full, 0, 1).reshape(HD, D)
    pieces = [small_all[:, :, a:b] for a, b in zip(edges[:-1], edges[1:])]
    group_start = (col_index // share) * share

    def joined(piece):
        return jnp.swapaxes(piece, 1, 2).reshape(-1, D)

    key_full, value_full = (
        joined(lax.dynamic_slice_in_dim(piece, group_start, share, 0)) for piece in pieces[:2]
    )
    left_full, gate_layer_full, right_full, proj_layer_full = (
        joined(piece) for piece in pieces[2:]
    )
    head_weights = jnp.concatenate([query_full, key_full, value_full], axis=0)

    positions = jnp.arange(seq, dtype=jnp.int32)
    mine = col_index * rows + jnp.arange(rows, dtype=jnp.int32)
    keep_mask = (mine[None, :] < lengths[:, None]).astype(jnp.float32)[:, :, None]
    live = positions[None, :] < lengths[:, None]
    distance = positions[:, None] - positions[None, :]
    nearby = (block_ids[:, :, None] >= block_ids[:, None, :]) & (distance < WINDOW)[None]
    nearby = nearby & live[:, :, None] & live[:, None, :]
    visible = nearby | (distance == 0)[None]

    half_width = HD // 2
    frequency = jnp.exp(jnp.arange(half_width, dtype=jnp.float32) * (-2.0 * math.log(10000.0) / HD))
    angles = (positions.astype(jnp.float32)[:, None] * frequency[None, :])[None]

    def prepare(query_in, key_in, value_in, gain_rows):
        return (
            rotate(root_norm(query_in, gain_rows[0]), angles),
            rotate(root_norm(key_in, gain_rows[1]), angles),
            plain_norm(value_in),
        )

    head_raw = matmul_back(normed_all, head_weights)
    query_raw, key_raw, value_raw = jnp.split(head_raw, 3, axis=-1)
    (query_value, key_value, value_value), head_back = jax.vjp(
        prepare, query_raw, key_raw, value_raw, head_gains
    )
    query_low = query_value.astype(low)
    key_low = key_value.astype(low)
    value_low = value_value.astype(low)
    score_scale = HD ** (-0.5)

    def score_all():
        raw_scores = (
            jnp.einsum("spd,sed->spe", query_low, key_low, preferred_element_type=jnp.float32)
            * score_scale
        )
        return jnp.where(visible, raw_scores, NEGATIVE)

    scores = score_all()
    row_max = jnp.max(scores, axis=-1, keepdims=True)
    exponent = jnp.exp(scores - row_max)
    row_total = jnp.sum(exponent, axis=-1, keepdims=True)
    attn_prob = exponent / row_total
    mixed_low = jnp.einsum(
        "spe,sed->spd", attn_prob.astype(low), value_low, preferred_element_type=jnp.float32
    ).astype(low)
    out_proj = product_sum(mixed_low, output_full, False, 2)
    laurel_mid = matmul_back(normed_low, left_full).astype(low)
    low_rank = matmul_last(laurel_mid, right_full)
    (after_attention, feed_normed), middle_back = jax.vjp(
        middle, residual, out_proj, low_rank, normed_low.astype(jnp.float32), norm_gains
    )
    feed_all = spread(feed_normed.astype(low), 0)
    gate_value = matmul_last(feed_all, paired[:, :unit_width])
    up_value = matmul_last(feed_all, paired[:, unit_width:])
    units_low = gated_product(gate_value, up_value).astype(low)
    summed = product_sum(units_low, down_full, False, 5)
    after_feed, feed_back = jax.vjp(feed_join, after_attention, summed, norm_gains)
    feed_round = after_feed.astype(low)
    layer_pre = matmul_back(feed_round, gate_layer_full)
    layer_input = swap(per_layer).astype(jnp.float32)
    layer_value, layer_back = jax.vjp(gated_product, layer_pre, layer_input)
    layer_low = layer_value.astype(low)
    projected = matmul_last(layer_low, proj_layer_full)
    out_value, final_back = jax.vjp(final_join, after_feed, projected, norm_gains)
    square_sums = jnp.stack(
        [
            jnp.sum(keep_mask * residual * residual),
            jnp.sum(keep_mask * after_attention * after_attention),
            jnp.sum(keep_mask * after_feed * after_feed),
            jnp.sum(keep_mask * out_value * out_value),
        ]
    )
    valid_count = jnp.sum(all_lengths).astype(jnp.float32)

    cotangent = swap(out_grad).astype(jnp.float32) * keep_mask
    grad_feed_out, grad_projected, gains_final = final_back(cotangent)
    projected_low = grad_projected.astype(low)
    grad_proj_layer = outer_sum(layer_low, projected_low)
    grad_layer_pre, grad_layer_input = layer_back(matmul_back(projected_low, proj_layer_full))
    layer_pre_low = grad_layer_pre.astype(low)
    grad_gate_layer = outer_sum(layer_pre_low, feed_round)
    grad_after_feed = grad_feed_out + matmul_last(layer_pre_low, gate_layer_full)
    grad_after_attention_a, grad_summed, gains_feed = feed_back(grad_after_feed)
    grad_paired, grad_down = units_back(
        grad_summed.astype(low), down_full, units_low, gate_value, up_value, 9
    )
    d_down_weight = lax.psum_scatter(
        grad_down, "row", scatter_dimension=1, tiled=True
    ).astype(jnp.float32)
    grad_gate = outer_sum(feed_all, grad_paired[..., :unit_width]).astype(low)
    d_gate_weight = lax.psum_scatter(
        grad_gate, "row", scatter_dimension=0, tiled=True
    ).astype(jnp.float32)
    grad_feed = product_sum(after(grad_paired, grad_gate), paired, True, 6)
    grad_up = outer_sum(feed_all, after(grad_paired, grad_feed)[..., unit_width:]).astype(low)
    d_up_weight = lax.psum_scatter(
        grad_up, "row", scatter_dimension=0, tiled=True
    ).astype(jnp.float32)
    grad_feed = after(grad_feed, grad_up)
    grad_residual_mid, grad_out_proj, grad_low_rank, grad_normed_mid, gains_middle = middle_back(
        (grad_after_attention_a, grad_feed)
    )
    grad_queries, grad_keys, grad_values, grad_output = heads_back(
        after(grad_out_proj.astype(low), d_down_weight),
        output_full,
        mixed_low,
        query_low,
        key_low,
        value_low,
        visible.astype(jnp.float32),
        score_scale,
        10,
    )
    low_rank_grad = grad_low_rank.astype(low)
    grad_right = outer_sum(laurel_mid, low_rank_grad)
    grad_laurel_mid = matmul_back(low_rank_grad, right_full).astype(low)
    grad_left = outer_sum(grad_laurel_mid, normed_low)
    grad_query_raw, grad_key_raw, grad_value_raw, grad_heads = head_back(
        (grad_queries, grad_keys, grad_values)
    )
    head_grads = jnp.concatenate([grad_query_raw, grad_key_raw, grad_value_raw], axis=-1)
    head_grads = head_grads.astype(low)
    grad_head_weights = outer_sum(head_grads, normed_all).astype(low)
    grad_query, grad_key, grad_value = jnp.split(grad_head_weights, 3, axis=0)
    grad_group = jnp.concatenate(
        [grad_key.reshape(share, -1, D), grad_value.reshape(share, -1, D)], axis=1
    )
    grad_rest = jnp.concatenate(
        [
            piece.astype(low).reshape(cols, -1, D)
            for piece in (grad_left, grad_gate_layer, grad_right, grad_proj_layer)
        ],
        axis=1,
    )
    half = grad_rest.shape[1] // 2
    grad_rest = jnp.swapaxes(grad_rest.reshape(cols, 2, half, D), 0, 1)
    rest_part, group_part = fold_small(grad_rest.reshape(2, cols * half, D), grad_group, 3)
    parts = jnp.concatenate(
        [grad_output, grad_query, group_part.astype(low), rest_part.astype(low).reshape(-1, D)],
        axis=0,
    )
    parts_out = lax.psum_scatter(parts, "row", scatter_dimension=1, tiled=True).astype(jnp.float32)
    d_output_weight = parts_out[:HD]
    d_query_weight = parts_out[HD : 2 * HD].T
    small_out = parts_out[2 * HD :]
    small_parts = [small_out[a:b] for a, b in zip(edges[:-1], edges[1:])]
    grad_normed = product_sum(
        after(head_grads, parts, d_gate_weight), head_weights, False, 7
    )
    grad_normed = grad_normed + grad_normed_mid + matmul_last(grad_laurel_mid, left_full)
    grad_residual_in, gains_input = input_back(grad_normed)
    d_hidden = swap((grad_residual_mid + grad_residual_in).astype(low))
    d_per_layer = swap(grad_layer_input.astype(low))
    grad_gains = gains_final + gains_feed + gains_middle + gains_input
    extra = jnp.concatenate([grad_heads.reshape(-1), square_sums])
    extra = jnp.pad(extra, (0, 2 * D - extra.shape[0])).reshape(2, D)
    all_sums = jnp.concatenate([grad_gains, extra], axis=0)
    totals = total(after(all_sums, d_up_weight), tiers, 4)
    d_norm_gains = totals[:6]
    d_head_gains = totals[6, : 2 * HD].reshape(2, HD)
    total_squares = totals[6, 2 * HD : 2 * HD + 4]
    stats = jnp.sqrt(total_squares / (valid_count * D))
    output = swap(out_value.astype(low))
    return (
        output,
        stats,
        d_hidden,
        d_per_layer,
        d_query_weight,
        small_parts[0].T,
        small_parts[1].T,
        d_output_weight,
        d_gate_weight,
        d_up_weight,
        d_down_weight,
        small_parts[2].T,
        small_parts[4],
        small_parts[3].T,
        small_parts[5],
        d_norm_gains,
        d_head_gains,
    )


def solution(mesh):
    body = heads_body if mesh.shape["col"] == H else general_body
    in_specs = (
        P("col", "row", None),
        P("col", "row", None),
        P(),
        P("row", None),
        P("col", "row", None),
        P("row", "col"),
        P("row", "col"),
        P("row", "col"),
        P("col", "row"),
        P("row", "col"),
        P("row", "col"),
        P("col", "row"),
        P("row", "col"),
        P("col", "row"),
        P("row", "col"),
        P("col", "row"),
        P(),
        P(),
    )
    out_specs = (
        P("col", "row", None),
        P(),
        P("col", "row", None),
        P("col", "row", None),
        P("row", "col"),
        P("row", "col"),
        P("row", "col"),
        P("col", "row"),
        P("row", "col"),
        P("row", "col"),
        P("col", "row"),
        P("row", "col"),
        P("col", "row"),
        P("row", "col"),
        P("col", "row"),
        P(),
        P(),
    )
    return jax.shard_map(body, mesh=mesh, in_specs=in_specs, out_specs=out_specs, check_vma=False)
```

```python
import functools
import math

import jax
import jax.numpy as jnp
from jax import lax
from jax.experimental import pallas as pl
from jax.experimental.pallas import tpu as pltpu
from jax.sharding import PartitionSpec as P

D = 2048
H = 8
KV = 2
HD = 256
WINDOW = 512
BLOCK = 256


EPSILON = 1e-06
FAR_BLOCK = 1 << 30
NEGATIVE = -1e30
HALF_ROOT = 1.0 / math.sqrt(2.0)
CURVE = math.sqrt(2.0 / math.pi)
BEND = 0.044715


MESH = pl.DeviceIdType.MESH


def passed_along(value, axis, steps):
    count = lax.axis_size(axis)
    initial, last = (max(0, -steps), min(count, count - steps))
    return lax.ppermute(value, axis, [(source, source + steps) for source in range(initial, last)])


def root_norm(values, gain_row):
    return (
        values * lax.rsqrt(jnp.mean(values * values, axis=-1, keepdims=True) + EPSILON) * gain_row
    )


def plain_norm(values):
    return values * lax.rsqrt(jnp.mean(values * values, axis=-1, keepdims=True) + EPSILON)


def smooth_gate(values):
    return jax.nn.gelu(values, approximate=True)


def rotate(values, angles):
    half_width = values.shape[-1] // 2
    leading = values[..., :half_width]
    trailing = values[..., half_width:]
    cosine = jnp.cos(angles)
    sine_part = jnp.sin(angles)
    return jnp.concatenate(
        [leading * cosine - trailing * sine_part, trailing * cosine + leading * sine_part], axis=-1
    )


def matmul_last(first_array, second_array):
    return lax.dot_general(
        first_array,
        second_array,
        (((first_array.ndim - 1,), (0,)), ((), ())),
        preferred_element_type=jnp.float32,
    )


def matmul_back(first_array, second_array):
    return lax.dot_general(
        first_array,
        second_array,
        (((first_array.ndim - 1,), (1,)), ((), ())),
        preferred_element_type=jnp.float32,
    )


def outer_sum(first_array, second_array):
    return lax.dot_general(
        first_array, second_array, (((0, 1), (0, 1)), ((), ())), preferred_element_type=jnp.float32
    )


def input_norm(residual, gain_rows):
    return root_norm(residual, gain_rows[0])


def middle(residual, out_proj, low_rank, normed, gain_rows):
    merged = (
        residual + root_norm(out_proj, gain_rows[1]) + normed + root_norm(low_rank, gain_rows[4])
    ) * HALF_ROOT
    return (merged, root_norm(merged, gain_rows[2]))


def feed_join(merged, summed, gain_rows):
    return merged + root_norm(summed, gain_rows[3])


def final_join(merged, projected, gain_rows):
    return merged + root_norm(projected, gain_rows[5])


def gated_product(first_array, second_array):
    return smooth_gate(first_array) * second_array


def partners():
    c = lax.axis_index("col")
    sib = c + 1 - 2 * (c % 2)
    xn = c + 2 - 4 * ((c // 2) % 2)
    yn = c + 4 - 8 * (c // 4)
    return c, sib, xn, yn

def greet(devs):
    barrier = pltpu.get_barrier_semaphore()
    for d in devs:
        pl.semaphore_signal(barrier, inc=1, device_id={"col": d}, device_id_type=MESH)
    pl.semaphore_wait(barrier, len(devs))

def spread_kernel(rows, x_ref, o_ref, local_sem, send, recv):
    c, sib, xn, yn = partners()
    def slot(half, who):
        return o_ref.at[half, pl.ds(pl.multiple_of(who * rows, rows), rows), :]
    def both(who):
        return o_ref.at[:, pl.ds(pl.multiple_of(who * rows, rows), rows), :]
    def push(i, src, dst, dev):
        return pltpu.make_async_remote_copy(src_ref=src, dst_ref=dst, send_sem=send.at[i], recv_sem=recv.at[i], device_id={"col": dev}, device_id_type=MESH)
    mine = pltpu.make_async_copy(x_ref, both(c), local_sem)
    mine.start()
    greet((sib, xn, yn))
    x0 = push(0, x_ref.at[0], slot(0, c), xn)
    y1 = push(1, x_ref.at[1], slot(1, c), yn)
    x1 = push(2, x_ref.at[1], slot(1, c), xn)
    y0 = push(3, x_ref.at[0], slot(0, c), yn)
    s = push(4, x_ref, both(c), sib)
    x0.start(); y1.start(); x1.start(); y0.start(); s.start()
    diag = yn + (xn - c)
    x0.wait_recv()
    fy = push(5, slot(0, xn), slot(0, xn), yn)
    fy.start()
    sx0 = push(6, slot(0, xn), slot(0, xn), sib)
    sx0.start()
    y1.wait_recv()
    fx = push(7, slot(1, yn), slot(1, yn), xn)
    fx.start()
    sy1 = push(8, slot(1, yn), slot(1, yn), sib)
    sy1.start()
    x1.wait_recv()
    sx1 = push(9, slot(1, xn), slot(1, xn), sib)
    sx1.start()
    y0.wait_recv()
    sy0 = push(10, slot(0, yn), slot(0, yn), sib)
    sy0.start()
    fy.wait_recv()
    sd0 = push(11, slot(0, diag), slot(0, diag), sib)
    sd0.start()
    fx.wait_recv()
    sd1 = push(12, slot(1, diag), slot(1, diag), sib)
    sd1.start()
    for cp in (s, sx0, sy1, sx1, sy0, sd0, sd1):
        cp.wait_recv()
    for cp in (x0, y1, x1, y0, s, fy, sx0, fx, sy1, sx1, sy0, sd0, sd1):
        cp.wait_send()
    mine.wait()

def spread(x, cid=0):
    h, rows, d = x.shape
    return pl.pallas_call(
        functools.partial(spread_kernel, rows),
        out_shape=jax.ShapeDtypeStruct((h, 8 * rows, d), x.dtype),
        in_specs=[pl.BlockSpec(memory_space=pl.ANY)],
        out_specs=pl.BlockSpec(memory_space=pl.ANY),
        scratch_shapes=[pltpu.SemaphoreType.DMA, pltpu.SemaphoreType.DMA((13,)), pltpu.SemaphoreType.DMA((13,))],
        compiler_params=pltpu.CompilerParams(collective_id=cid, has_side_effects=True),
        cost_estimate=pl.CostEstimate(flops=0, bytes_accessed=120_000_000, transcendentals=0),
        name="spread",
    )(x)

def fold_steps(rows, p_ref, own, sibs, dx, dy, rx, ry, local_sem, send, recv):
    c, sib, xn, yn = partners()
    diag = yn + (xn - c)
    wide = jnp.float32
    tall = 32 if rows % 32 == 0 else 8

    def blk(who):
        return p_ref.at[:, pl.ds(pl.multiple_of(who * rows, rows), rows), :]

    def push(i, src, dst, dev):
        return pltpu.make_async_remote_copy(
            src_ref=src,
            dst_ref=dst,
            send_sem=send.at[i],
            recv_sem=recv.at[i],
            device_id={"col": dev},
            device_id_type=MESH,
        )

    def add(dst, src):
        @pl.loop(0, rows // tall)
        def _(i):
            r = pl.ds(pl.multiple_of(i * tall, tall), tall)
            dst[r, :] = (dst[r, :].astype(wide) + src[r, :].astype(wide)).astype(dst.dtype)

    def pair(j):
        add(own.at[j, 0], sibs.at[j, 0])
        add(own.at[j, 1], sibs.at[j, 1])

    dests = (diag, xn, yn, c)
    loads = [pltpu.make_async_copy(blk(d), own.at[j], local_sem.at[j]) for j, d in enumerate(dests)]
    for load in loads:
        load.start()
    yield None
    sides = [push(j, blk(d + (sib - c)), sibs.at[j], sib) for j, d in enumerate(dests)]
    for side in sides:
        side.start()
    yield None
    loads[0].wait()
    sides[0].wait_recv()
    pair(0)
    a = push(4, own.at[0, 0], dx, xn)
    b = push(5, own.at[0, 1], dy, yn)
    a.start()
    b.start()
    yield None
    loads[1].wait()
    sides[1].wait_recv()
    pair(1)
    x0 = push(6, own.at[1, 0], rx.at[0], xn)
    x0.start()
    yield None
    loads[2].wait()
    sides[2].wait_recv()
    pair(2)
    y1 = push(7, own.at[2, 1], ry.at[1], yn)
    y1.start()
    yield None
    a.wait_recv()
    add(own.at[2, 0], dx)
    y0 = push(8, own.at[2, 0], ry.at[0], yn)
    y0.start()
    yield None
    b.wait_recv()
    add(own.at[1, 1], dy)
    x1 = push(9, own.at[1, 1], rx.at[1], xn)
    x1.start()
    yield None
    loads[3].wait()
    sides[3].wait_recv()
    pair(3)
    yield None
    waits = ((x0, y0), (x1, y1))
    yield tall, waits, (*sides, a, b, x0, y1, y0, x1)


def fold_finish(rows, o_ref, own, rx, ry, tall, waits, sent):
    wide = jnp.float32
    for h in range(2):
        for copy in waits[h]:
            copy.wait_recv()

        @pl.loop(0, rows // tall)
        def _(i):
            r = pl.ds(pl.multiple_of(i * tall, tall), tall)
            o_ref[h, r, :] = (
                own[3, h, r, :].astype(wide) + rx[h, r, :].astype(wide) + ry[h, r, :].astype(wide)
            )

    for copy in sent:
        copy.wait_send()


def fold_scratch(h, rows, d, kind):
    return [
        pltpu.VMEM((4, h, rows, d), kind),
        pltpu.VMEM((4, h, rows, d), kind),
        pltpu.VMEM((rows, d), kind),
        pltpu.VMEM((rows, d), kind),
        pltpu.VMEM((h, rows, d), kind),
        pltpu.VMEM((h, rows, d), kind),
        pltpu.SemaphoreType.DMA((4,)),
        pltpu.SemaphoreType.DMA((10,)),
        pltpu.SemaphoreType.DMA((10,)),
    ]


def product_kernel(rows, flip, outer, *refs):
    if outer:
        a_ref, w_ref, f_ref, o_ref, g_ref = refs[:5]
        f_buf, g_buf, turned, f_sem, g_sem = refs[-5:]
        refs = refs[5:-5]
    else:
        a_ref, w_ref, o_ref = refs[:3]
        refs = refs[3:]
    a_buf, w_buf, stage, own, sibs, dx, dy, rx, ry, local_sem, send, recv = refs
    c, sib, xn, yn = partners()
    diag = yn + (xn - c)
    wide = jnp.float32
    d = o_ref.shape[-1]
    tile = 512
    tall = 32

    def push(i, src, dst, dev):
        return pltpu.make_async_remote_copy(
            src_ref=src,
            dst_ref=dst,
            send_sem=send.at[i],
            recv_sem=recv.at[i],
            device_id={"col": dev},
            device_id_type=MESH,
        )

    dests = (diag, xn, yn, c)
    step = sib - c
    weights = pltpu.make_async_copy(w_ref, w_buf, local_sem.at[8])
    weights.start()

    def load(i, who):
        return pltpu.make_async_copy(
            a_ref.at[:, pl.ds(pl.multiple_of(who * rows, rows), rows), :],
            a_buf.at[i],
            local_sem.at[i],
        )

    far = [load(j, dests[j] + step) for j in range(4)]
    near = [load(4 + j, dests[j]) for j in range(4)]
    for first, second in zip(far, near):
        first.start()
        second.start()
    owners = [d + step for d in dests] + list(dests)
    strip = 256

    def strips(n):
        cut = pl.ds(pl.multiple_of(n * strip, strip), strip)
        return [
            pltpu.make_async_copy(
                f_ref.at[:, pl.ds(pl.multiple_of(who * rows, rows), rows), cut],
                f_buf.at[lax.rem(n, 2), i],
                f_sem.at[lax.rem(n, 2), i],
            )
            for i, who in enumerate(owners)
        ]

    def strip_out(n):
        cut = pl.ds(pl.multiple_of(n * strip, strip), strip)
        slot = lax.rem(n, 2)
        return pltpu.make_async_copy(g_buf.at[slot], g_ref.at[cut, :], g_sem.at[slot])

    def outer_product():
        count = g_ref.shape[0] // strip
        depth = a_buf.shape[-1]

        @pl.loop(0, count)
        def _(n):
            slot = lax.rem(n, 2)
            for copy in strips(n):
                copy.wait()

            @pl.when(n + 1 < count)
            def _():
                for copy in strips(n + 1):
                    copy.start()

            @pl.when(n >= 2)
            def _():
                strip_out(n - 2).wait()

            turned[...] = f_buf[slot].reshape(16 * rows, strip).T

            @pl.loop(0, depth // tile)
            def _(m):
                cut = pl.ds(pl.multiple_of(m * tile, tile), tile)
                right = a_buf[:, :, :, cut].reshape(16 * rows, tile)
                value = jnp.dot(turned[...], right, preferred_element_type=wide)
                g_buf[slot, :, cut] = value.astype(g_buf.dtype)

            strip_out(n).start()

        strip_out(count - 2).wait()
        strip_out(count - 1).wait()

    if outer:
        for copy in strips(0):
            copy.start()
    greet((sib, xn, yn))
    weights.wait()

    def product(i, put):
        left = a_buf[i].reshape(2 * rows, a_buf.shape[-1])

        @pl.loop(0, d // tile)
        def _(n):
            cut = pl.ds(pl.multiple_of(n * tile, tile), tile)
            right = w_buf[cut, :] if flip else w_buf[:, cut]
            dims = (((1,), (1,)), ((), ())) if flip else (((1,), (0,)), ((), ()))
            value = lax.dot_general(left, right, dims, preferred_element_type=wide)
            put(cut, value.reshape(2, rows, tile))

    sides = [push(j, stage.at[j], sibs.at[j], sib) for j in range(4)]

    def for_sibling(j):
        far[j].wait()

        def put(cut, value):
            stage[j, :, :, cut] = value.astype(stage.dtype)

        product(j, put)
        sides[j].start()

    def for_chip(j):
        near[j].wait()
        sides[j].wait_recv()

        def put(cut, value):
            own[j, :, :, cut] = (value + sibs[j, :, :, cut].astype(wide)).astype(own.dtype)

        product(4 + j, put)

    def add(dst, src):
        @pl.loop(0, rows // tall)
        def _(i):
            r = pl.ds(pl.multiple_of(i * tall, tall), tall)
            dst[r, :] = (dst[r, :].astype(wide) + src[r, :].astype(wide)).astype(dst.dtype)

    for_sibling(0)
    near[0].wait()

    def hold(cut, value):
        o_ref[:, :, cut] = value

    product(4, hold)
    sides[0].wait_recv()
    for h in range(2):

        @pl.loop(0, rows // tall)
        def _(i):
            r = pl.ds(pl.multiple_of(i * tall, tall), tall)
            own[0, h, r, :] = (o_ref[h, r, :] + sibs[0, h, r, :].astype(wide)).astype(own.dtype)

    a = push(4, own.at[0, 0], dx, xn)
    b = push(5, own.at[0, 1], dy, yn)
    a.start()
    b.start()
    for_sibling(1)
    for_sibling(2)
    for_chip(1)
    x0 = push(6, own.at[1, 0], rx.at[0], xn)
    x0.start()
    for_sibling(3)
    for_chip(2)
    y1 = push(7, own.at[2, 1], ry.at[1], yn)
    y1.start()
    a.wait_recv()
    add(own.at[2, 0], dx)
    y0 = push(8, own.at[2, 0], ry.at[0], yn)
    y0.start()
    b.wait_recv()
    add(own.at[1, 1], dy)
    x1 = push(9, own.at[1, 1], rx.at[1], xn)
    x1.start()
    near[3].wait()
    sides[3].wait_recv()

    def put(cut, value):
        o_ref[:, :, cut] = value + sibs[3, :, :, cut].astype(wide)

    product(7, put)
    if outer:
        outer_product()
    for h, waits in enumerate(((x0, y0), (x1, y1))):
        for copy in waits:
            copy.wait_recv()

        @pl.loop(0, rows // tall)
        def _(i):
            r = pl.ds(pl.multiple_of(i * tall, tall), tall)
            o_ref[h, r, :] = o_ref[h, r, :] + rx[h, r, :].astype(wide) + ry[h, r, :].astype(wide)

    for copy in (*sides, a, b, x0, y1, y0, x1):
        copy.wait_send()


def product_sum(left, right, flip, cid, feed=None):
    h, total, depth = left.shape
    rows = total // 8
    d = right.shape[0] if flip else right.shape[1]
    low = left.dtype
    outer = feed is not None
    out_shape = [jax.ShapeDtypeStruct((h, rows, d), jnp.float32)]
    out_specs = [pl.BlockSpec(memory_space=pltpu.VMEM)]
    scratch = [
        pltpu.VMEM((8, h, rows, depth), low),
        pltpu.VMEM(right.shape, low),
        pltpu.VMEM((4, h, rows, d), low),
        pltpu.VMEM((3, h, rows, d), low),
        pltpu.VMEM((4, h, rows, d), low),
        pltpu.VMEM((rows, d), low),
        pltpu.VMEM((rows, d), low),
        pltpu.VMEM((h, rows, d), low),
        pltpu.VMEM((h, rows, d), low),
        pltpu.SemaphoreType.DMA((9,)),
        pltpu.SemaphoreType.DMA((10,)),
        pltpu.SemaphoreType.DMA((10,)),
    ]
    flops = 2 * h * total * depth * d
    if outer:
        width = feed.shape[-1]
        flops += 2 * h * total * depth * width
        out_shape.append(jax.ShapeDtypeStruct((width, depth), low))
        out_specs.append(pl.BlockSpec(memory_space=pl.ANY))
        scratch += [
            pltpu.VMEM((2, 8, h, rows, 256), low),
            pltpu.VMEM((2, 256, depth), low),
            pltpu.VMEM((256, h * total), low),
            pltpu.SemaphoreType.DMA((2, 8)),
            pltpu.SemaphoreType.DMA((2,)),
        ]
    result = pl.pallas_call(
        functools.partial(product_kernel, rows, flip, outer),
        out_shape=out_shape,
        in_specs=[pl.BlockSpec(memory_space=pl.ANY)] * (3 if outer else 2),
        out_specs=out_specs,
        scratch_shapes=scratch,
        compiler_params=pltpu.CompilerParams(
            collective_id=cid,
            has_side_effects=True,
            vmem_limit_bytes=(52 if outer else 44) << 20,
        ),
        cost_estimate=pl.CostEstimate(
            flops=flops, bytes_accessed=130_000_000, transcendentals=0
        ),
        name="product_sum",
    )(*((left, right, feed) if outer else (left, right)))
    return result if outer else result[0]


def fold_small_kernel(
    rows, p_ref, g_ref, o_ref, k_ref, own, sibs, dx, dy, rx, ry, local_sem, send, recv,
    gown, gsibs, grx, glocal, gsend, grecv,
):
    c, sib, xn, yn = partners()
    m = c % 4
    m_sib = m + 1 - 2 * (m % 2)
    m_x = m + 2 - 4 * (m // 2)
    m_diag = m_sib + (m_x - m)
    wide = jnp.float32

    def push(i, src, dst, dev):
        return pltpu.make_async_remote_copy(
            src_ref=src,
            dst_ref=dst,
            send_sem=gsend.at[i],
            recv_sem=grecv.at[i],
            device_id={"col": dev},
            device_id_type=MESH,
        )

    steps = fold_steps(rows, p_ref, own, sibs, dx, dy, rx, ry, local_sem, send, recv)
    next(steps)
    loads = [
        pltpu.make_async_copy(g_ref.at[d], gown.at[j], glocal.at[j])
        for j, d in enumerate((m_x, m))
    ]
    for load in loads:
        load.start()
    greet((sib, xn, yn))
    sides = [push(j, g_ref.at[d], gsibs.at[j], sib) for j, d in enumerate((m_diag, m_sib))]
    sides[0].start()
    next(steps)
    sides[1].start()
    tall = k_ref.shape[0] // 4
    loads[0].wait()
    sides[0].wait_recv()

    @pl.loop(0, 4)
    def _(i):
        r = pl.ds(pl.multiple_of(i * tall, tall), tall)
        gown[0, r, :] = (gown[0, r, :].astype(wide) + gsibs[0, r, :].astype(wide)).astype(
            gown.dtype
        )

    over = push(2, gown.at[0], grx, xn)
    over.start()
    last = None
    for step in steps:
        last = step if step is not None else last
    fold_finish(rows, o_ref, own, rx, ry, *last)
    loads[1].wait()
    sides[1].wait_recv()
    over.wait_recv()

    @pl.loop(0, 4)
    def _(i):
        r = pl.ds(pl.multiple_of(i * tall, tall), tall)
        k_ref[r, :] = (
            gown[1, r, :].astype(wide) + gsibs[1, r, :].astype(wide) + grx[r, :].astype(wide)
        )

    for copy in (*sides, over):
        copy.wait_send()


def fold_small(p, g, cid):
    h, total, d = p.shape
    rows = total // 8
    share, tall, _ = g.shape
    return pl.pallas_call(
        functools.partial(fold_small_kernel, rows),
        out_shape=(
            jax.ShapeDtypeStruct((h, rows, d), jnp.float32),
            jax.ShapeDtypeStruct((tall, d), jnp.float32),
        ),
        in_specs=[pl.BlockSpec(memory_space=pl.ANY)] * 2,
        out_specs=[pl.BlockSpec(memory_space=pltpu.VMEM)] * 2,
        scratch_shapes=fold_scratch(h, rows, d, p.dtype)
        + [
            pltpu.VMEM((2, tall, d), g.dtype),
            pltpu.VMEM((2, tall, d), g.dtype),
            pltpu.VMEM((tall, d), g.dtype),
            pltpu.SemaphoreType.DMA((2,)),
            pltpu.SemaphoreType.DMA((3,)),
            pltpu.SemaphoreType.DMA((3,)),
        ],
        compiler_params=pltpu.CompilerParams(
            collective_id=cid, has_side_effects=True, vmem_limit_bytes=40 << 20
        ),
        cost_estimate=pl.CostEstimate(flops=0, bytes_accessed=60_000_000, transcendentals=0),
        name="fold_small",
    )(p, g)


def open_kernel(
    rows, tiers, x_ref, s_ref, q_ref, w_ref, o_ref, sa_ref, qa_ref, wa_ref,
    local_sem, send, recv, line_send, line_recv,
):
    c, sib, xn, yn = partners()
    diag = yn + (xn - c)
    r = lax.axis_index("row")
    last = tiers - 1
    weights = ((s_ref, sa_ref), (q_ref, qa_ref), (w_ref, wa_ref))

    def slot(half, who):
        return o_ref.at[half, pl.ds(pl.multiple_of(who * rows, rows), rows), :]

    def both(who):
        return o_ref.at[:, pl.ds(pl.multiple_of(who * rows, rows), rows), :]

    started = []

    def push(src, dst, **dev):
        i = len(started)
        copy = pltpu.make_async_remote_copy(
            src_ref=src,
            dst_ref=dst,
            send_sem=send.at[i],
            recv_sem=recv.at[i],
            device_id=dev,
            device_id_type=MESH,
        )
        copy.start()
        started.append(copy)
        return copy

    local = [
        pltpu.make_async_copy(x_ref, both(c), local_sem.at[0]),
        pltpu.make_async_copy(s_ref, sa_ref.at[r], local_sem.at[1]),
        pltpu.make_async_copy(q_ref, qa_ref.at[r], local_sem.at[2]),
        pltpu.make_async_copy(w_ref, wa_ref.at[r], local_sem.at[3]),
    ]
    for copy in local:
        copy.start()
    barrier = pltpu.get_barrier_semaphore()
    for d in (sib, xn, yn):
        pl.semaphore_signal(barrier, inc=1, device_id={"col": d}, device_id_type=MESH)

    @pl.when(r < last)
    def _():
        pl.semaphore_signal(barrier, inc=1, device_id={"row": r + 1}, device_id_type=MESH)

    @pl.when(r > 0)
    def _():
        pl.semaphore_signal(barrier, inc=1, device_id={"row": r - 1}, device_id_type=MESH)

    @pl.when((r > 0) & (r < last))
    def _():
        pl.semaphore_wait(barrier, 5)

    @pl.when((r == 0) | (r == last))
    def _():
        pl.semaphore_wait(barrier, 4)

    def passing(way, hop, j):
        src, dst = weights[j]
        whose = r - hop if way == 0 else r + hop
        return pltpu.make_async_remote_copy(
            src_ref=src if hop == 0 else dst.at[whose],
            dst_ref=dst.at[whose],
            send_sem=line_send.at[way, hop, j],
            recv_sem=line_recv.at[way, hop, j],
            device_id={"row": r + 1 if way == 0 else r - 1},
            device_id_type=MESH,
        )

    def going(way, hop):
        return (r < last) & (r >= hop) if way == 0 else (r > 0) & (r + hop <= last)

    def coming(way, hop):
        return r > hop if way == 0 else r + hop < last

    def forward(hop, j):
        for way in range(2):
            if hop > 0:

                @pl.when(coming(way, hop - 1))
                def _():
                    passing(way, hop - 1, j).wait_recv()

            @pl.when(going(way, hop))
            def _():
                passing(way, hop, j).start()

    x0 = push(x_ref.at[0], slot(0, c), col=xn)
    y1 = push(x_ref.at[1], slot(1, c), col=yn)
    for j in range(3):
        forward(0, j)
    x1 = push(x_ref.at[1], slot(1, c), col=xn)
    y0 = push(x_ref.at[0], slot(0, c), col=yn)
    push(x_ref, both(c), col=sib)
    forward(1, 0)
    x0.wait_recv()
    fy = push(slot(0, xn), slot(0, xn), col=yn)
    push(slot(0, xn), slot(0, xn), col=sib)
    y1.wait_recv()
    fx = push(slot(1, yn), slot(1, yn), col=xn)
    push(slot(1, yn), slot(1, yn), col=sib)
    forward(1, 1)
    forward(1, 2)
    x1.wait_recv()
    push(slot(1, xn), slot(1, xn), col=sib)
    y0.wait_recv()
    push(slot(0, yn), slot(0, yn), col=sib)
    for hop in range(2, last):
        for j in range(3):
            forward(hop, j)
    fy.wait_recv()
    push(slot(0, diag), slot(0, diag), col=sib)
    fx.wait_recv()
    push(slot(1, diag), slot(1, diag), col=sib)
    for copy in started:
        if not any(copy is other for other in (x0, y1, x1, y0, fy, fx)):
            copy.wait_recv()
    for j in range(3):
        for way in range(2):

            @pl.when(coming(way, last - 1))
            def _():
                passing(way, last - 1, j).wait_recv()

            for hop in range(last):

                @pl.when(going(way, hop))
                def _():
                    passing(way, hop, j).wait_send()

    for copy in started:
        copy.wait_send()
    for copy in local:
        copy.wait()


def open_all(x, small, query, output, tiers, cid):
    h, rows, d = x.shape
    low = x.dtype
    copies = 13
    return pl.pallas_call(
        functools.partial(open_kernel, rows, tiers),
        out_shape=(
            jax.ShapeDtypeStruct((h, 8 * rows, d), low),
            jax.ShapeDtypeStruct((tiers, *small.shape), low),
            jax.ShapeDtypeStruct((tiers, *query.shape), low),
            jax.ShapeDtypeStruct((tiers, *output.shape), low),
        ),
        in_specs=[pl.BlockSpec(memory_space=pl.ANY)] * 4,
        out_specs=[pl.BlockSpec(memory_space=pl.ANY)] * 4,
        scratch_shapes=[
            pltpu.SemaphoreType.DMA((4,)),
            pltpu.SemaphoreType.DMA((copies,)),
            pltpu.SemaphoreType.DMA((copies,)),
            pltpu.SemaphoreType.DMA((2, tiers - 1, 3)),
            pltpu.SemaphoreType.DMA((2, tiers - 1, 3)),
        ],
        compiler_params=pltpu.CompilerParams(collective_id=cid, has_side_effects=True),
        cost_estimate=pl.CostEstimate(flops=0, bytes_accessed=200_000_000, transcendentals=0),
        name="open_all",
    )(x, small, query, output)


def share_kernel(near, s_ref, sa_ref, local_sem, send, recv):
    c, sib, xn, yn = partners()
    diag = yn + (xn - c)
    height = s_ref.shape[1]
    started = []

    def part(ref, first):
        return ref.at[:, pl.ds(0, near) if first else pl.ds(near, height - near), :]

    def push(who, first, dev, own=False):
        i = len(started)
        dst = part(sa_ref.at[who], first)
        copy = pltpu.make_async_remote_copy(
            src_ref=part(s_ref, first) if own else dst,
            dst_ref=dst,
            send_sem=send.at[i],
            recv_sem=recv.at[i],
            device_id={"col": dev},
            device_id_type=MESH,
        )
        copy.start()
        started.append(copy)
        return copy

    mine = pltpu.make_async_copy(s_ref, sa_ref.at[c], local_sem)
    mine.start()
    greet((sib, xn, yn))
    rx = push(c, False, xn, own=True)
    ry = push(c, False, yn, own=True)
    kx = push(c, True, xn, own=True)
    push(c, True, sib, own=True)
    push(c, False, sib, own=True)
    rx.wait_recv()
    fd = push(xn, False, yn)
    push(xn, False, sib)
    ry.wait_recv()
    push(yn, False, sib)
    fd.wait_recv()
    push(diag, False, sib)
    kx.wait_recv()
    push(xn, True, sib)
    for copy in started:
        if not any(copy is other for other in (kx, rx, ry, fd)):
            copy.wait_recv()
    for copy in started:
        copy.wait_send()
    mine.wait()


def share_small(small, near, cid):
    return pl.pallas_call(
        functools.partial(share_kernel, near),
        out_shape=jax.ShapeDtypeStruct((8, *small.shape), small.dtype),
        in_specs=[pl.BlockSpec(memory_space=pl.ANY)],
        out_specs=pl.BlockSpec(memory_space=pl.ANY),
        scratch_shapes=[
            pltpu.SemaphoreType.DMA,
            pltpu.SemaphoreType.DMA((10,)),
            pltpu.SemaphoreType.DMA((10,)),
        ],
        compiler_params=pltpu.CompilerParams(collective_id=cid, has_side_effects=True),
        cost_estimate=pl.CostEstimate(flops=0, bytes_accessed=60_000_000, transcendentals=0),
        name="share_small",
    )(small)


def rounds_of(rows, x_ref, held, local_sem, send, recv, consume, prepare):
    c, sib, xn, yn = partners()
    diag = yn + (xn - c)
    step = sib - c

    def place(t, j, n=1):
        return held.at[t, pl.ds(j * rows, n * rows), :]

    started = []

    def push(src, dst, dev):
        i = len(started)
        copy = pltpu.make_async_remote_copy(
            src_ref=src,
            dst_ref=dst,
            send_sem=send.at[i],
            recv_sem=recv.at[i],
            device_id={"col": dev},
            device_id_type=MESH,
        )
        copy.start()
        started.append(copy)
        return copy

    mine = [pltpu.make_async_copy(x_ref.at[h], place(0, h), local_sem.at[h]) for h in range(2)]
    for copy in mine:
        copy.start()
    greet((sib, xn, yn))
    x0 = push(x_ref.at[0], place(1, 0), xn)
    y1 = push(x_ref.at[1], place(1, 1), yn)
    x1 = push(x_ref.at[1], place(2, 0), xn)
    y0 = push(x_ref.at[0], place(2, 1), yn)
    s0 = push(x_ref.at[0], place(0, 2), sib)
    s1 = push(x_ref.at[1], place(0, 3), sib)
    prepare(0)
    for copy in mine:
        copy.wait()
    s0.wait_recv()
    s1.wait_recv()
    consume(0, 0, ((0, c), (1, c), (0, sib), (1, sib)))
    x0.wait_recv()
    fy = push(place(1, 0), place(3, 0), yn)
    y1.wait_recv()
    fx = push(place(1, 1), place(3, 1), xn)
    prepare(1)
    t1 = push(place(1, 0, 2), place(1, 2, 2), sib)
    t1.wait_recv()
    consume(1, 0, ((0, xn), (1, yn), (0, xn + step), (1, yn + step)))
    prepare(2)
    x1.wait_recv()
    y0.wait_recv()
    t2 = push(place(2, 0, 2), place(2, 2, 2), sib)
    t2.wait_recv()
    consume(2, 0, ((1, xn), (0, yn), (1, xn + step), (0, yn + step)))
    prepare(3)
    fy.wait_recv()
    fx.wait_recv()
    t3 = push(place(3, 0, 2), place(3, 2, 2), sib)
    consume(3, 0, ((0, diag), (1, diag)))
    t3.wait_recv()
    consume(3, 2, ((0, diag + step), (1, diag + step)))
    for copy in started:
        copy.wait_send()


def piece_at(ref, rows, piece):
    half, who = piece
    return ref.at[half, pl.ds(pl.multiple_of(who * rows, rows), rows), :]


def units_back_kernel(
    rows, x_ref, w_ref, u_ref, g_ref, v_ref, p_ref, d_ref,
    held, weights, units, turned, gates, ups, grads, total_ref,
    weight_sem, load_sem, store_sem, local_sem, send, recv,
):
    c, sib, xn, yn = partners()
    diag = yn + (xn - c)
    step = sib - c
    wide = jnp.float32
    width = w_ref.shape[0]
    d = w_ref.shape[1]
    plan = (
        ((0, c), (1, c), (0, sib), (1, sib)),
        ((0, xn), (1, yn), (0, xn + step), (1, yn + step)),
        ((1, xn), (0, yn), (1, xn + step), (0, yn + step)),
        ((0, diag), (1, diag), (0, diag + step), (1, diag + step)),
    )
    fetch = pltpu.make_async_copy(w_ref, weights, weight_sem)
    fetch.start()

    def loads(t):
        copies = []
        for j, piece in enumerate(plan[t]):
            for k, (src, dst) in enumerate(((u_ref, units), (g_ref, gates), (v_ref, ups))):
                copies.append(
                    pltpu.make_async_copy(
                        piece_at(src, rows, piece),
                        dst.at[t % 2, pl.ds(j * rows, rows), :],
                        load_sem.at[t % 2, j, k],
                    )
                )
        return copies

    def stores(t, first=0, count=4):
        return [
            pltpu.make_async_copy(
                grads.at[t % 2, pl.ds(j * rows, rows), :],
                piece_at(p_ref, rows, plan[t][j]),
                store_sem.at[t % 2, j],
            )
            for j in range(first, first + count)
        ]

    for copy in loads(0):
        copy.start()

    tile = 256

    def prepare(t):
        if t == 0:
            fetch.wait()
        if t < 3:
            for copy in loads(t + 1):
                copy.start()
        for copy in loads(t):
            copy.wait()

        @pl.loop(0, width // tile)
        def _(n):
            cut = pl.ds(pl.multiple_of(n * tile, tile), tile)
            gate = gates[t % 2, :, cut]
            square = gate * gate
            bent = jnp.tanh(CURVE * (gate + BEND * gate * square))
            rise = 0.5 * (1.0 + bent)
            slope = rise + (0.5 * CURVE) * gate * (1.0 - bent * bent) * (1.0 + 3.0 * BEND * square)
            gates[t % 2, :, cut] = ups[t % 2, :, cut] * slope
            ups[t % 2, :, cut] = gate * rise
            turned[cut, :] = units[t % 2, :, cut].T

    def consume(t, first, pieces):
        if t >= 2 and first == 0:
            for copy in stores(t - 2):
                copy.wait()
        span = slice(first * rows, (first + len(pieces)) * rows)

        @pl.loop(0, width // 512)
        def _(n):
            cut = pl.ds(pl.multiple_of(n * 512, 512), 512)
            grad = lax.dot_general(
                held[t, span, :],
                weights[cut, :],
                (((1,), (1,)), ((), ())),
                preferred_element_type=wide,
            )
            grads[t % 2, span, cut] = (grad * gates[t % 2, span, cut]).astype(grads.dtype)
            cut_up = pl.ds(pl.multiple_of(width + n * 512, 512), 512)
            grads[t % 2, span, cut_up] = (grad * ups[t % 2, span, cut]).astype(grads.dtype)

        for copy in stores(t, first, len(pieces)):
            copy.start()

        @pl.loop(0, d // 512)
        def _(n):
            cut = pl.ds(pl.multiple_of(n * 512, 512), 512)
            value = jnp.dot(turned[:, span], held[t, span, cut], preferred_element_type=wide)
            if t > 0:
                value = value + total_ref[:, cut]
            if first == 0:
                total_ref[:, cut] = value
            else:
                d_ref[:, cut] = value.astype(d_ref.dtype)

    rounds_of(rows, x_ref, held, local_sem, send, recv, consume, prepare)
    for copy in (*stores(2), *stores(3)):
        copy.wait()


def units_back(x, down, units, gate, up, cid):
    h, rows, d = x.shape
    width = down.shape[0]
    low = x.dtype
    return pl.pallas_call(
        functools.partial(units_back_kernel, rows),
        out_shape=(
            jax.ShapeDtypeStruct((h, 8 * rows, 2 * width), low),
            jax.ShapeDtypeStruct((width, d), low),
        ),
        in_specs=[pl.BlockSpec(memory_space=pl.ANY)] * 5,
        out_specs=[
            pl.BlockSpec(memory_space=pl.ANY),
            pl.BlockSpec(memory_space=pltpu.VMEM),
        ],
        scratch_shapes=[
            pltpu.VMEM((4, 4 * rows, d), low),
            pltpu.VMEM((width, d), low),
            pltpu.VMEM((2, 4 * rows, width), low),
            pltpu.VMEM((width, 4 * rows), low),
            pltpu.VMEM((2, 4 * rows, width), jnp.float32),
            pltpu.VMEM((2, 4 * rows, width), jnp.float32),
            pltpu.VMEM((2, 4 * rows, 2 * width), low),
            pltpu.VMEM((width, d), jnp.float32),
            pltpu.SemaphoreType.DMA,
            pltpu.SemaphoreType.DMA((2, 4, 3)),
            pltpu.SemaphoreType.DMA((2, 4)),
            pltpu.SemaphoreType.DMA((2,)),
            pltpu.SemaphoreType.DMA((11,)),
            pltpu.SemaphoreType.DMA((11,)),
        ],
        compiler_params=pltpu.CompilerParams(
            collective_id=cid, has_side_effects=True, vmem_limit_bytes=52 << 20
        ),
        cost_estimate=pl.CostEstimate(
            flops=64 * h * rows * width * d, bytes_accessed=130_000_000, transcendentals=0
        ),
        name="units_back",
    )(x, down, units, gate, up)


def heads_back_kernel(
    rows, scale, x_ref, w_ref, m_ref, q_ref, k_ref, v_ref, s_ref, gq_ref, gk_ref, gv_ref, d_ref,
    held, weights, mixed, queries, keys, values, seen, total_ref, load_sem, local_sem, send, recv,
):
    wide = jnp.float32
    d = w_ref.shape[1]
    low = weights.dtype
    pairs = (
        (w_ref, weights), (q_ref, queries), (k_ref, keys), (v_ref, values), (s_ref, seen),
        (m_ref, mixed),
    )
    loads = [
        pltpu.make_async_copy(src, dst, load_sem.at[i]) for i, (src, dst) in enumerate(pairs)
    ]
    for copy in loads:
        copy.start()
    back = (((1,), (1,)), ((), ()))

    def prepare(t):
        if t == 0:
            for copy in loads:
                copy.wait()
            gk_ref[...] = jnp.zeros_like(gk_ref)
            gv_ref[...] = jnp.zeros_like(gv_ref)

    def consume(t, first, pieces):
        part = slice(first * rows, (first + len(pieces)) * rows)
        grad_mixed = lax.dot_general(
            held[t, part, :], weights[...], back, preferred_element_type=wide
        )
        grad_mixed = grad_mixed.astype(low)
        spans = []
        for j, (half, who) in enumerate(pieces):
            span = pl.ds(pl.multiple_of(who * rows, rows), rows)
            spans.append(mixed[half, span, :])
            query = queries[half, span, :]
            grad = grad_mixed[j * rows : (j + 1) * rows]
            score = lax.dot_general(query, keys[half], back, preferred_element_type=wide) * scale
            score = jnp.where(seen[half, span, :] > 0, score, NEGATIVE)
            power = jnp.exp(score - jnp.max(score, axis=-1, keepdims=True))
            prob = power / jnp.sum(power, axis=-1, keepdims=True)
            slope = lax.dot_general(grad, values[half], back, preferred_element_type=wide)
            mean = jnp.sum(prob * slope, axis=-1, keepdims=True)
            flow = (prob * (slope - mean)).astype(low)
            gq_ref[half, span, :] = jnp.dot(flow, keys[half], preferred_element_type=wide) * scale
            gk_ref[half] += jnp.dot(flow.T, query, preferred_element_type=wide) * scale
            gv_ref[half] += jnp.dot(prob.astype(low).T, grad, preferred_element_type=wide)
        turned = jnp.concatenate(spans, axis=0).T

        @pl.loop(0, d // 512)
        def _(n):
            cut = pl.ds(pl.multiple_of(n * 512, 512), 512)
            value = jnp.dot(turned, held[t, part, cut], preferred_element_type=wide)
            if t > 0:
                value = value + total_ref[:, cut]
            if first == 0:
                total_ref[:, cut] = value
            else:
                d_ref[:, cut] = value.astype(d_ref.dtype)

    rounds_of(rows, x_ref, held, local_sem, send, recv, consume, prepare)


def heads_back(x, output, mixed, query, key, value, visible, scale, cid):
    h, rows, d = x.shape
    low = x.dtype
    grad = jax.ShapeDtypeStruct(query.shape, jnp.float32)
    return pl.pallas_call(
        functools.partial(heads_back_kernel, rows, scale),
        out_shape=(grad, grad, grad, jax.ShapeDtypeStruct(output.shape, low)),
        in_specs=[pl.BlockSpec(memory_space=pl.ANY)] * 7,
        out_specs=[pl.BlockSpec(memory_space=pltpu.VMEM)] * 4,
        scratch_shapes=[
            pltpu.VMEM((4, 4 * rows, d), low),
            pltpu.VMEM(output.shape, low),
            pltpu.VMEM(mixed.shape, low),
            pltpu.VMEM(query.shape, low),
            pltpu.VMEM(query.shape, low),
            pltpu.VMEM(query.shape, low),
            pltpu.VMEM(visible.shape, visible.dtype),
            pltpu.VMEM(output.shape, jnp.float32),
            pltpu.SemaphoreType.DMA((6,)),
            pltpu.SemaphoreType.DMA((2,)),
            pltpu.SemaphoreType.DMA((11,)),
            pltpu.SemaphoreType.DMA((11,)),
        ],
        compiler_params=pltpu.CompilerParams(
            collective_id=cid, has_side_effects=True, vmem_limit_bytes=48 << 20
        ),
        cost_estimate=pl.CostEstimate(
            flops=20_000_000_000, bytes_accessed=130_000_000, transcendentals=0
        ),
        name="heads_back",
    )(x, output, mixed, query, key, value, visible)


def total_kernel(x_ref, o_ref, sums, got, tier_sums, send, recv):
    c, sib, xn, yn = partners()
    r = lax.axis_index("row")
    tiers = lax.axis_size("row")
    others = [lax.rem(r + k, tiers) for k in range(1, tiers)]
    barrier = pltpu.get_barrier_semaphore()
    for d in (sib, xn, yn):
        pl.semaphore_signal(barrier, inc=1, device_id={"col": d}, device_id_type=MESH)
    for d in others:
        pl.semaphore_signal(barrier, inc=1, device_id={"row": d}, device_id_type=MESH)
    pl.semaphore_wait(barrier, 3 + len(others))
    sums[0] = x_ref[...]
    for i, dev in enumerate((sib, xn, yn)):
        copy = pltpu.make_async_remote_copy(
            src_ref=sums.at[i],
            dst_ref=got.at[i],
            send_sem=send.at[i],
            recv_sem=recv.at[i],
            device_id={"col": dev},
            device_id_type=MESH,
        )
        copy.start()
        copy.wait()
        sums[i + 1] = sums[i] + got[i]
    tier_sums[r] = sums[3]
    copies = []
    for k, d in enumerate(others):
        copy = pltpu.make_async_remote_copy(
            src_ref=sums.at[3],
            dst_ref=tier_sums.at[r],
            send_sem=send.at[3 + k],
            recv_sem=recv.at[3 + k],
            device_id={"row": d},
            device_id_type=MESH,
        )
        copy.start()
        copies.append(copy)
    for copy in copies:
        copy.wait()
    result = tier_sums[0]
    for k in range(1, tiers):
        result = result + tier_sums[k]
    o_ref[...] = result


def total(x, tiers, cid):
    return pl.pallas_call(
        total_kernel,
        out_shape=jax.ShapeDtypeStruct(x.shape, x.dtype),
        in_specs=[pl.BlockSpec(memory_space=pltpu.VMEM)],
        out_specs=pl.BlockSpec(memory_space=pltpu.VMEM),
        scratch_shapes=[
            pltpu.VMEM((4, *x.shape), x.dtype),
            pltpu.VMEM((3, *x.shape), x.dtype),
            pltpu.VMEM((tiers, *x.shape), x.dtype),
            pltpu.SemaphoreType.DMA((2 + tiers,)),
            pltpu.SemaphoreType.DMA((2 + tiers,)),
        ],
        compiler_params=pltpu.CompilerParams(collective_id=cid, has_side_effects=True),
        cost_estimate=pl.CostEstimate(flops=0, bytes_accessed=40_000_000, transcendentals=0),
        name="total",
    )(x)


def after(value, *earlier):
    return lax.optimization_barrier((value, *earlier))[0]


def general_body(
    hidden,
    per_layer,
    lengths,
    block_ids,
    out_grad,
    query_weight,
    key_weight,
    value_weight,
    output_weight,
    gate_weight,
    up_weight,
    down_weight,
    laurel_left,
    laurel_right,
    layer_gate,
    layer_proj,
    norm_gains,
    head_gains,
):
    local_rows = hidden.shape[0]
    seq_groups = hidden.shape[1]
    col_index = lax.axis_index("col")
    row_index = lax.axis_index("row")
    all_lengths = lengths
    lengths = lax.dynamic_slice_in_dim(all_lengths, row_index * seq_groups, seq_groups, 0)
    (
        query_cols,
        key_cols,
        value_cols,
        output_rows,
        gate_cols,
        up_cols,
        down_rows,
        left_cols,
        right_rows,
        gate_layer_cols,
        proj_layer_rows,
    ) = (
        lax.all_gather(query_weight, "row", axis=0, tiled=True),
        lax.all_gather(key_weight, "row", axis=0, tiled=True),
        lax.all_gather(value_weight, "row", axis=0, tiled=True),
        lax.all_gather(output_weight, "row", axis=1, tiled=True),
        lax.all_gather(gate_weight, "row", axis=0, tiled=True),
        lax.all_gather(up_weight, "row", axis=0, tiled=True),
        lax.all_gather(down_weight, "row", axis=1, tiled=True),
        lax.all_gather(laurel_left, "row", axis=0, tiled=True),
        lax.all_gather(laurel_right, "row", axis=1, tiled=True),
        lax.all_gather(layer_gate, "row", axis=0, tiled=True),
        lax.all_gather(layer_proj, "row", axis=1, tiled=True),
    )
    (
        query_full,
        key_full,
        value_full,
        output_full,
        left_full,
        right_full,
        gate_layer_full,
        proj_layer_full,
    ) = (
        lax.all_gather(query_cols, "col", axis=1, tiled=True),
        lax.all_gather(key_cols, "col", axis=1, tiled=True),
        lax.all_gather(value_cols, "col", axis=1, tiled=True),
        lax.all_gather(output_rows, "col", axis=0, tiled=True),
        lax.all_gather(left_cols, "col", axis=1, tiled=True),
        lax.all_gather(right_rows, "col", axis=0, tiled=True),
        lax.all_gather(gate_layer_cols, "col", axis=1, tiled=True),
        lax.all_gather(proj_layer_rows, "col", axis=0, tiled=True),
    )
    paired = jnp.concatenate([gate_cols, up_cols], axis=1)
    unit_width = gate_cols.shape[1]
    first_position = col_index * local_rows
    positions = first_position + jnp.arange(local_rows, dtype=jnp.int32)
    live_mask = positions[:, None] < lengths[None, :]
    keep_mask = live_mask.astype(jnp.float32)[:, :, None]
    reach_back = (WINDOW + local_rows - 2) // local_rows
    reach_ahead = (BLOCK + local_rows - 2) // local_rows
    key_span = (reach_back + 1 + reach_ahead) * local_rows
    key_position = first_position - reach_back * local_rows + jnp.arange(key_span, dtype=jnp.int32)
    filler_low = jnp.full((seq_groups, reach_back * local_rows), FAR_BLOCK, jnp.int32)
    filler_high = jnp.full((seq_groups, reach_ahead * local_rows), FAR_BLOCK, jnp.int32)
    padded_blocks = jnp.concatenate([filler_low, block_ids, filler_high], axis=1)
    key_blocks = lax.dynamic_slice_in_dim(padded_blocks, first_position, key_span, 1)
    query_blocks = lax.dynamic_slice_in_dim(block_ids, first_position, local_rows, 1)
    key_live = (key_position[None, :] >= 0) & (key_position[None, :] < lengths[:, None])
    query_live = positions[None, :] < lengths[:, None]
    distance = positions[:, None] - key_position[None, :]
    nearby = (query_blocks[:, :, None] >= key_blocks[:, None, :]) & (distance < WINDOW)[None]
    nearby = nearby & query_live[:, :, None] & key_live[:, None, :]
    visible = (nearby | (distance == 0)[None])[:, None, None]
    residual = hidden.astype(jnp.float32)
    normed_value, input_back = jax.vjp(input_norm, residual, norm_gains)
    normed_low = normed_value.astype(jnp.bfloat16)
    half_width = HD // 2
    frequency = jnp.exp(jnp.arange(half_width, dtype=jnp.float32) * (-2.0 * math.log(10000.0) / HD))
    angles = (positions.astype(jnp.float32)[:, None] * frequency[None, :])[:, None, None, :]

    def prepare(query_in, key_in, value_in, gain_rows):
        return (
            rotate(root_norm(query_in, gain_rows[0]), angles),
            rotate(root_norm(key_in, gain_rows[1]), angles),
            plain_norm(value_in),
        )

    query_raw = matmul_last(normed_low, query_full).reshape(local_rows, seq_groups, H, HD)
    key_raw = matmul_last(normed_low, key_full).reshape(local_rows, seq_groups, KV, HD)
    value_raw = matmul_last(normed_low, value_full).reshape(local_rows, seq_groups, KV, HD)
    (query_value, key_value, value_value), head_back = jax.vjp(
        prepare, query_raw, key_raw, value_raw, head_gains
    )
    query_low = query_value.astype(jnp.bfloat16).reshape(local_rows, seq_groups, KV, H // KV, HD)
    key_low = key_value.astype(jnp.bfloat16)
    value_low = value_value.astype(jnp.bfloat16)
    offsets = list(range(reach_back, -reach_ahead - 1, -1))
    key_parts = []
    value_parts = []
    for offset in offsets:
        if offset == 0:
            key_parts.append(key_low)
            value_parts.append(value_low)
        else:
            moved_key, moved_value = passed_along((key_low, value_low), "col", offset)
            key_parts.append(moved_key)
            value_parts.append(moved_value)
    near_keys = jnp.concatenate(key_parts, axis=0)
    near_values = jnp.concatenate(value_parts, axis=0)
    score_scale = HD ** (-0.5)

    def score_all():
        raw_scores = (
            jnp.einsum(
                "psjgd,esjd->sjgpe", query_low, near_keys, preferred_element_type=jnp.float32
            )
            * score_scale
        )
        return jnp.where(visible, raw_scores, NEGATIVE)

    scores = score_all()
    row_max = jnp.max(scores, axis=-1, keepdims=True)
    exponent = jnp.exp(scores - row_max)
    row_total = jnp.sum(exponent, axis=-1, keepdims=True)
    attn_prob = exponent / row_total
    log_total = row_max + jnp.log(row_total)
    mixed_heads = jnp.einsum(
        "sjgpe,esjd->psjgd",
        attn_prob.astype(jnp.bfloat16),
        near_values,
        preferred_element_type=jnp.float32,
    )
    mixed_low = mixed_heads.reshape(local_rows, seq_groups, H * HD).astype(jnp.bfloat16)
    out_proj = matmul_last(mixed_low, output_full)
    laurel_mid = matmul_last(normed_low, left_full).astype(jnp.bfloat16)
    low_rank = matmul_last(laurel_mid, right_full)
    (after_attention, feed_normed), middle_back = jax.vjp(
        middle, residual, out_proj, low_rank, normed_low.astype(jnp.float32), norm_gains
    )
    feed_low = feed_normed.astype(jnp.bfloat16)
    gate_up = matmul_last(lax.all_gather(feed_low, "col", axis=0, tiled=True), paired)
    unit_value, gate_back = jax.vjp(
        gated_product, gate_up[..., :unit_width], gate_up[..., unit_width:]
    )
    units_low = unit_value.astype(jnp.bfloat16)
    summed = lax.psum_scatter(
        matmul_last(units_low, down_rows), "col", scatter_dimension=0, tiled=True
    )
    after_feed, feed_back = jax.vjp(feed_join, after_attention, summed, norm_gains)
    feed_round = after_feed.astype(jnp.bfloat16)
    layer_pre = matmul_last(feed_round, gate_layer_full)
    layer_input = per_layer.astype(jnp.float32)
    layer_value, layer_back = jax.vjp(gated_product, layer_pre, layer_input)
    layer_low = layer_value.astype(jnp.bfloat16)
    projected = matmul_last(layer_low, proj_layer_full)
    out_value, final_back = jax.vjp(final_join, after_feed, projected, norm_gains)
    square_sums = jnp.stack(
        [
            jnp.sum(keep_mask * residual * residual),
            jnp.sum(keep_mask * after_attention * after_attention),
            jnp.sum(keep_mask * after_feed * after_feed),
            jnp.sum(keep_mask * out_value * out_value),
        ]
    )
    valid_count = jnp.sum(all_lengths).astype(jnp.float32)
    cotangent = out_grad.astype(jnp.float32) * keep_mask
    grad_feed_out, grad_projected, gains_final = final_back(cotangent)
    projected_low = grad_projected.astype(jnp.bfloat16)
    grad_proj_layer = outer_sum(layer_low, projected_low)
    grad_layer_pre, grad_layer_input = layer_back(matmul_back(projected_low, proj_layer_full))
    layer_pre_low = grad_layer_pre.astype(jnp.bfloat16)
    grad_gate_layer = outer_sum(feed_round, layer_pre_low)
    grad_after_feed = grad_feed_out + matmul_back(layer_pre_low, gate_layer_full)
    grad_after_attention_a, grad_summed, gains_feed = feed_back(grad_after_feed)
    summed_low = grad_summed.astype(jnp.bfloat16)
    block_rows = lax.all_gather(summed_low, "col", axis=0, tiled=True)
    grad_down = outer_sum(units_low, block_rows)
    grad_units = matmul_back(block_rows, down_rows)
    grad_down, grad_units = (grad_down, grad_units)
    grad_gate_value, grad_up_value = gate_back(grad_units)
    grad_paired = jnp.concatenate([grad_gate_value, grad_up_value], axis=-1).astype(jnp.bfloat16)
    grad_weights_paired = outer_sum(
        lax.all_gather(feed_low, "col", axis=0, tiled=True), grad_paired
    )
    grad_feed = lax.psum_scatter(
        matmul_back(grad_paired, paired).astype(jnp.bfloat16),
        "col",
        scatter_dimension=0,
        tiled=True,
    ).astype(jnp.float32)
    grad_residual_mid, grad_out_proj, grad_low_rank, grad_normed_mid, gains_middle = middle_back(
        (grad_after_attention_a, grad_feed)
    )
    out_proj_low = grad_out_proj.astype(jnp.bfloat16)
    grad_output = outer_sum(mixed_low, out_proj_low)
    grad_mixed = matmul_back(out_proj_low, output_full).astype(jnp.bfloat16)
    grad_mixed = grad_mixed.reshape(local_rows, seq_groups, KV, H // KV, HD)
    low_rank_grad = grad_low_rank.astype(jnp.bfloat16)
    grad_right = outer_sum(laurel_mid, low_rank_grad)
    grad_laurel_mid = matmul_back(low_rank_grad, right_full).astype(jnp.bfloat16)
    grad_left = outer_sum(normed_low, grad_laurel_mid)
    scores = score_all()
    attn_prob = jnp.exp(scores - log_total)
    grad_prob = jnp.einsum(
        "psjgd,esjd->sjgpe", grad_mixed, near_values, preferred_element_type=jnp.float32
    )
    grad_scores = (
        attn_prob * (grad_prob - jnp.sum(attn_prob * grad_prob, axis=-1, keepdims=True))
    ).astype(jnp.bfloat16)
    grad_queries = (
        jnp.einsum("sjgpe,esjd->psjgd", grad_scores, near_keys, preferred_element_type=jnp.float32)
        * score_scale
    )
    grad_near_keys = (
        jnp.einsum("sjgpe,psjgd->esjd", grad_scores, query_low, preferred_element_type=jnp.float32)
        * score_scale
    )
    grad_near_values = jnp.einsum(
        "sjgpe,psjgd->esjd",
        attn_prob.astype(jnp.bfloat16),
        grad_mixed,
        preferred_element_type=jnp.float32,
    )
    grad_key_total = grad_near_keys[reach_back * local_rows : (reach_back + 1) * local_rows]
    grad_value_total = grad_near_values[reach_back * local_rows : (reach_back + 1) * local_rows]
    for slot_index, offset in enumerate(offsets):
        if offset != 0:
            piece_keys = grad_near_keys[slot_index * local_rows : (slot_index + 1) * local_rows]
            piece_values = grad_near_values[slot_index * local_rows : (slot_index + 1) * local_rows]
            back_keys, back_values = (
                passed_along(piece_keys.astype(jnp.bfloat16), "col", -offset).astype(
                    piece_keys.dtype
                ),
                passed_along(piece_values.astype(jnp.bfloat16), "col", -offset).astype(
                    piece_values.dtype
                ),
            )
            grad_key_total = grad_key_total + back_keys
            grad_value_total = grad_value_total + back_values
    grad_query_raw, grad_key_raw, grad_value_raw, grad_heads = head_back(
        (grad_queries.reshape(local_rows, seq_groups, H, HD), grad_key_total, grad_value_total)
    )
    query_grad_low = grad_query_raw.reshape(local_rows, seq_groups, H * HD).astype(jnp.bfloat16)
    key_grad_low = grad_key_raw.reshape(local_rows, seq_groups, KV * HD).astype(jnp.bfloat16)
    value_grad_low = grad_value_raw.reshape(local_rows, seq_groups, KV * HD).astype(jnp.bfloat16)
    grad_query = outer_sum(normed_low, query_grad_low)
    grad_key = outer_sum(normed_low, key_grad_low)
    grad_value = outer_sum(normed_low, value_grad_low)
    grad_normed = (
        grad_normed_mid
        + matmul_back(grad_laurel_mid, left_full)
        + matmul_back(query_grad_low, query_full)
        + matmul_back(key_grad_low, key_full)
        + matmul_back(value_grad_low, value_full)
    )
    grad_residual_in, gains_input = input_back(grad_normed)
    d_hidden = (grad_residual_mid + grad_residual_in).astype(jnp.bfloat16)
    d_per_layer = grad_layer_input.astype(jnp.bfloat16)
    grad_gains = gains_final + gains_feed + gains_middle + gains_input
    grad_gate = grad_weights_paired[:, :unit_width]
    grad_up = grad_weights_paired[:, unit_width:]
    (
        query_part,
        key_part,
        value_part,
        output_part,
        left_part,
        right_part,
        gate_layer_part,
        proj_layer_part,
    ) = (
        lax.psum_scatter(
            grad_query.astype(jnp.bfloat16), "col", scatter_dimension=1, tiled=True
        ).astype(jnp.float32),
        lax.psum_scatter(
            grad_key.astype(jnp.bfloat16), "col", scatter_dimension=1, tiled=True
        ).astype(jnp.float32),
        lax.psum_scatter(
            grad_value.astype(jnp.bfloat16), "col", scatter_dimension=1, tiled=True
        ).astype(jnp.float32),
        lax.psum_scatter(
            grad_output.astype(jnp.bfloat16), "col", scatter_dimension=0, tiled=True
        ).astype(jnp.float32),
        lax.psum_scatter(
            grad_left.astype(jnp.bfloat16), "col", scatter_dimension=1, tiled=True
        ).astype(jnp.float32),
        lax.psum_scatter(
            grad_right.astype(jnp.bfloat16), "col", scatter_dimension=0, tiled=True
        ).astype(jnp.float32),
        lax.psum_scatter(
            grad_gate_layer.astype(jnp.bfloat16), "col", scatter_dimension=1, tiled=True
        ).astype(jnp.float32),
        lax.psum_scatter(
            grad_proj_layer.astype(jnp.bfloat16), "col", scatter_dimension=0, tiled=True
        ).astype(jnp.float32),
    )
    (
        d_query_weight,
        d_key_weight,
        d_value_weight,
        d_output_weight,
        d_gate_weight,
        d_up_weight,
        d_down_weight,
        d_laurel_left,
        d_laurel_right,
        d_layer_gate,
        d_layer_proj,
    ) = (
        lax.psum_scatter(
            query_part.astype(jnp.bfloat16), "row", scatter_dimension=0, tiled=True
        ).astype(jnp.float32),
        lax.psum_scatter(
            key_part.astype(jnp.bfloat16), "row", scatter_dimension=0, tiled=True
        ).astype(jnp.float32),
        lax.psum_scatter(
            value_part.astype(jnp.bfloat16), "row", scatter_dimension=0, tiled=True
        ).astype(jnp.float32),
        lax.psum_scatter(
            output_part.astype(jnp.bfloat16), "row", scatter_dimension=1, tiled=True
        ).astype(jnp.float32),
        lax.psum_scatter(
            grad_gate.astype(jnp.bfloat16), "row", scatter_dimension=0, tiled=True
        ).astype(jnp.float32),
        lax.psum_scatter(
            grad_up.astype(jnp.bfloat16), "row", scatter_dimension=0, tiled=True
        ).astype(jnp.float32),
        lax.psum_scatter(
            grad_down.astype(jnp.bfloat16), "row", scatter_dimension=1, tiled=True
        ).astype(jnp.float32),
        lax.psum_scatter(
            left_part.astype(jnp.bfloat16), "row", scatter_dimension=0, tiled=True
        ).astype(jnp.float32),
        lax.psum_scatter(
            right_part.astype(jnp.bfloat16), "row", scatter_dimension=1, tiled=True
        ).astype(jnp.float32),
        lax.psum_scatter(
            gate_layer_part.astype(jnp.bfloat16), "row", scatter_dimension=0, tiled=True
        ).astype(jnp.float32),
        lax.psum_scatter(
            proj_layer_part.astype(jnp.bfloat16), "row", scatter_dimension=1, tiled=True
        ).astype(jnp.float32),
    )
    d_norm_gains, d_head_gains, total_squares = lax.psum(
        (grad_gains, grad_heads, square_sums), ("row", "col")
    )
    stats = jnp.sqrt(total_squares / (valid_count * D))
    output = out_value.astype(jnp.bfloat16)
    return (
        output,
        stats,
        d_hidden,
        d_per_layer,
        d_query_weight,
        d_key_weight,
        d_value_weight,
        d_output_weight,
        d_gate_weight,
        d_up_weight,
        d_down_weight,
        d_laurel_left,
        d_laurel_right,
        d_layer_gate,
        d_layer_proj,
        d_norm_gains,
        d_head_gains,
    )


def swap(array):
    return jnp.swapaxes(array, 0, 1)


def heads_body(
    hidden,
    per_layer,
    lengths,
    block_ids,
    out_grad,
    query_weight,
    key_weight,
    value_weight,
    output_weight,
    gate_weight,
    up_weight,
    down_weight,
    laurel_left,
    laurel_right,
    layer_gate,
    layer_proj,
    norm_gains,
    head_gains,
):
    low = jnp.bfloat16
    rows = hidden.shape[0]
    groups = hidden.shape[1]
    cols = lax.axis_size("col")
    seq = rows * cols
    share = cols // KV
    col_index = lax.axis_index("col")
    row_index = lax.axis_index("row")
    all_lengths = lengths
    lengths = lax.dynamic_slice_in_dim(all_lengths, row_index * groups, groups, 0)

    small = jnp.concatenate(
        [key_weight.T, value_weight.T, laurel_left.T, layer_gate.T, laurel_right, layer_proj],
        axis=0,
    )
    heights = [key_weight.shape[1], value_weight.shape[1], laurel_left.shape[1]]
    heights += [layer_gate.shape[1], laurel_right.shape[0], layer_proj.shape[0]]
    edges = [sum(heights[:i]) for i in range(len(heights) + 1)]
    unit_width = gate_weight.shape[1]
    residual = swap(hidden).astype(jnp.float32)
    normed_value, input_back = jax.vjp(input_norm, residual, norm_gains)
    normed_low = normed_value.astype(low)
    tiers = lax.axis_size("row")
    normed_all, small_row, query_full, output_full = open_all(
        normed_low, small, query_weight, output_weight, tiers, 1
    )
    small_all = share_small(small_row, heights[0] + heights[1], 8)
    both_weights = jnp.concatenate([gate_weight, up_weight], axis=1)
    paired = lax.all_gather(after(both_weights, normed_all), "row", axis=0, tiled=True)
    down_full = lax.all_gather(after(down_weight, normed_all), "row", axis=1, tiled=True)
    query_full = query_full.reshape(D, HD).T
    output_full = jnp.swapaxes(output_full, 0, 1).reshape(HD, D)
    pieces = [small_all[:, :, a:b] for a, b in zip(edges[:-1], edges[1:])]
    group_start = (col_index // share) * share

    def joined(piece):
        return jnp.swapaxes(piece, 1, 2).reshape(-1, D)

    key_full, value_full = (
        joined(lax.dynamic_slice_in_dim(piece, group_start, share, 0)) for piece in pieces[:2]
    )
    left_full, gate_layer_full, right_full, proj_layer_full = (
        joined(piece) for piece in pieces[2:]
    )
    head_weights = jnp.concatenate([query_full, key_full, value_full], axis=0)

    positions = jnp.arange(seq, dtype=jnp.int32)
    mine = col_index * rows + jnp.arange(rows, dtype=jnp.int32)
    keep_mask = (mine[None, :] < lengths[:, None]).astype(jnp.float32)[:, :, None]
    live = positions[None, :] < lengths[:, None]
    distance = positions[:, None] - positions[None, :]
    nearby = (block_ids[:, :, None] >= block_ids[:, None, :]) & (distance < WINDOW)[None]
    nearby = nearby & live[:, :, None] & live[:, None, :]
    visible = nearby | (distance == 0)[None]

    half_width = HD // 2
    frequency = jnp.exp(jnp.arange(half_width, dtype=jnp.float32) * (-2.0 * math.log(10000.0) / HD))
    angles = (positions.astype(jnp.float32)[:, None] * frequency[None, :])[None]

    def prepare(query_in, key_in, value_in, gain_rows):
        return (
            rotate(root_norm(query_in, gain_rows[0]), angles),
            rotate(root_norm(key_in, gain_rows[1]), angles),
            plain_norm(value_in),
        )

    head_raw = matmul_back(normed_all, head_weights)
    query_raw, key_raw, value_raw = jnp.split(head_raw, 3, axis=-1)
    (query_value, key_value, value_value), head_back = jax.vjp(
        prepare, query_raw, key_raw, value_raw, head_gains
    )
    query_low = query_value.astype(low)
    key_low = key_value.astype(low)
    value_low = value_value.astype(low)
    score_scale = HD ** (-0.5)

    def score_all():
        raw_scores = (
            jnp.einsum("spd,sed->spe", query_low, key_low, preferred_element_type=jnp.float32)
            * score_scale
        )
        return jnp.where(visible, raw_scores, NEGATIVE)

    scores = score_all()
    row_max = jnp.max(scores, axis=-1, keepdims=True)
    exponent = jnp.exp(scores - row_max)
    row_total = jnp.sum(exponent, axis=-1, keepdims=True)
    attn_prob = exponent / row_total
    mixed_low = jnp.einsum(
        "spe,sed->spd", attn_prob.astype(low), value_low, preferred_element_type=jnp.float32
    ).astype(low)
    out_proj = product_sum(mixed_low, output_full, False, 2)
    laurel_mid = matmul_back(normed_low, left_full).astype(low)
    low_rank = matmul_last(laurel_mid, right_full)
    (after_attention, feed_normed), middle_back = jax.vjp(
        middle, residual, out_proj, low_rank, normed_low.astype(jnp.float32), norm_gains
    )
    feed_all = spread(feed_normed.astype(low), 0)
    gate_value = matmul_last(feed_all, paired[:, :unit_width])
    up_value = matmul_last(feed_all, paired[:, unit_width:])
    units_low = gated_product(gate_value, up_value).astype(low)
    summed = product_sum(units_low, down_full, False, 5)
    after_feed, feed_back = jax.vjp(feed_join, after_attention, summed, norm_gains)
    feed_round = after_feed.astype(low)
    layer_pre = matmul_back(feed_round, gate_layer_full)
    layer_input = swap(per_layer).astype(jnp.float32)
    layer_value, layer_back = jax.vjp(gated_product, layer_pre, layer_input)
    layer_low = layer_value.astype(low)
    projected = matmul_last(layer_low, proj_layer_full)
    out_value, final_back = jax.vjp(final_join, after_feed, projected, norm_gains)
    square_sums = jnp.stack(
        [
            jnp.sum(keep_mask * residual * residual),
            jnp.sum(keep_mask * after_attention * after_attention),
            jnp.sum(keep_mask * after_feed * after_feed),
            jnp.sum(keep_mask * out_value * out_value),
        ]
    )
    valid_count = jnp.sum(all_lengths).astype(jnp.float32)

    cotangent = swap(out_grad).astype(jnp.float32) * keep_mask
    grad_feed_out, grad_projected, gains_final = final_back(cotangent)
    projected_low = grad_projected.astype(low)
    grad_proj_layer = outer_sum(layer_low, projected_low)
    grad_layer_pre, grad_layer_input = layer_back(matmul_back(projected_low, proj_layer_full))
    layer_pre_low = grad_layer_pre.astype(low)
    grad_gate_layer = outer_sum(layer_pre_low, feed_round)
    grad_after_feed = grad_feed_out + matmul_last(layer_pre_low, gate_layer_full)
    grad_after_attention_a, grad_summed, gains_feed = feed_back(grad_after_feed)
    grad_paired, grad_down = units_back(
        grad_summed.astype(low), down_full, units_low, gate_value, up_value, 9
    )
    d_down_weight = lax.psum_scatter(
        grad_down, "row", scatter_dimension=1, tiled=True
    ).astype(jnp.float32)
    grad_feed, grad_both = product_sum(grad_paired, paired, True, 6, feed_all)
    d_both = lax.psum_scatter(grad_both, "row", scatter_dimension=0, tiled=True).astype(
        jnp.float32
    )
    d_gate_weight = d_both[:, :unit_width]
    d_up_weight = d_both[:, unit_width:]
    grad_residual_mid, grad_out_proj, grad_low_rank, grad_normed_mid, gains_middle = middle_back(
        (grad_after_attention_a, grad_feed)
    )
    grad_queries, grad_keys, grad_values, grad_output = heads_back(
        after(grad_out_proj.astype(low), d_down_weight),
        output_full,
        mixed_low,
        query_low,
        key_low,
        value_low,
        visible.astype(jnp.float32),
        score_scale,
        10,
    )
    low_rank_grad = grad_low_rank.astype(low)
    grad_right = outer_sum(laurel_mid, low_rank_grad)
    grad_laurel_mid = matmul_back(low_rank_grad, right_full).astype(low)
    grad_left = outer_sum(grad_laurel_mid, normed_low)
    grad_query_raw, grad_key_raw, grad_value_raw, grad_heads = head_back(
        (grad_queries, grad_keys, grad_values)
    )
    head_grads = jnp.concatenate([grad_query_raw, grad_key_raw, grad_value_raw], axis=-1)
    head_grads = head_grads.astype(low)
    grad_head_weights = outer_sum(head_grads, normed_all).astype(low)
    grad_query, grad_key, grad_value = jnp.split(grad_head_weights, 3, axis=0)
    grad_group = jnp.concatenate(
        [grad_key.reshape(share, -1, D), grad_value.reshape(share, -1, D)], axis=1
    )
    grad_rest = jnp.concatenate(
        [
            piece.astype(low).reshape(cols, -1, D)
            for piece in (grad_left, grad_gate_layer, grad_right, grad_proj_layer)
        ],
        axis=1,
    )
    half = grad_rest.shape[1] // 2
    grad_rest = jnp.swapaxes(grad_rest.reshape(cols, 2, half, D), 0, 1)
    rest_part, group_part = fold_small(grad_rest.reshape(2, cols * half, D), grad_group, 3)
    parts = jnp.concatenate(
        [grad_output, grad_query, group_part.astype(low), rest_part.astype(low).reshape(-1, D)],
        axis=0,
    )
    grad_normed = product_sum(after(head_grads, parts), head_weights, False, 7)
    parts = after(parts, d_both, grad_normed)
    parts_out = lax.psum_scatter(parts, "row", scatter_dimension=1, tiled=True).astype(jnp.float32)
    d_output_weight = parts_out[:HD]
    d_query_weight = parts_out[HD : 2 * HD].T
    small_out = parts_out[2 * HD :]
    small_parts = [small_out[a:b] for a, b in zip(edges[:-1], edges[1:])]
    grad_normed = grad_normed + grad_normed_mid + matmul_last(grad_laurel_mid, left_full)
    grad_residual_in, gains_input = input_back(grad_normed)
    d_hidden = swap((grad_residual_mid + grad_residual_in).astype(low))
    d_per_layer = swap(grad_layer_input.astype(low))
    grad_gains = gains_final + gains_feed + gains_middle + gains_input
    extra = jnp.concatenate([grad_heads.reshape(-1), square_sums])
    extra = jnp.pad(extra, (0, 2 * D - extra.shape[0])).reshape(2, D)
    all_sums = jnp.concatenate([grad_gains, extra], axis=0)
    totals = total(after(all_sums, parts), tiers, 4)
    d_norm_gains = totals[:6]
    d_head_gains = totals[6, : 2 * HD].reshape(2, HD)
    total_squares = totals[6, 2 * HD : 2 * HD + 4]
    stats = jnp.sqrt(total_squares / (valid_count * D))
    output = swap(out_value.astype(low))
    return (
        output,
        stats,
        d_hidden,
        d_per_layer,
        d_query_weight,
        small_parts[0].T,
        small_parts[1].T,
        d_output_weight,
        d_gate_weight,
        d_up_weight,
        d_down_weight,
        small_parts[2].T,
        small_parts[4],
        small_parts[3].T,
        small_parts[5],
        d_norm_gains,
        d_head_gains,
    )


def solution(mesh):
    body = heads_body if mesh.shape["col"] == H else general_body
    in_specs = (
        P("col", "row", None),
        P("col", "row", None),
        P(),
        P("row", None),
        P("col", "row", None),
        P("row", "col"),
        P("row", "col"),
        P("row", "col"),
        P("col", "row"),
        P("row", "col"),
        P("row", "col"),
        P("col", "row"),
        P("row", "col"),
        P("col", "row"),
        P("row", "col"),
        P("col", "row"),
        P(),
        P(),
    )
    out_specs = (
        P("col", "row", None),
        P(),
        P("col", "row", None),
        P("col", "row", None),
        P("row", "col"),
        P("row", "col"),
        P("row", "col"),
        P("col", "row"),
        P("row", "col"),
        P("row", "col"),
        P("col", "row"),
        P("row", "col"),
        P("col", "row"),
        P("row", "col"),
        P("col", "row"),
        P(),
        P(),
    )
    return jax.shard_map(body, mesh=mesh, in_specs=in_specs, out_specs=out_specs, check_vma=False)
```

```python
import functools
import math

import jax
import jax.numpy as jnp
from jax import lax
from jax.experimental import pallas as pl
from jax.experimental.pallas import tpu as pltpu
from jax.sharding import PartitionSpec as P

D = 2048
H = 8
KV = 2
HD = 256
WINDOW = 512
BLOCK = 256


EPSILON = 1e-06
FAR_BLOCK = 1 << 30
NEGATIVE = -1e30
HALF_ROOT = 1.0 / math.sqrt(2.0)
CURVE = math.sqrt(2.0 / math.pi)
BEND = 0.044715


MESH = pl.DeviceIdType.MESH


def passed_along(value, axis, steps):
    count = lax.axis_size(axis)
    initial, last = (max(0, -steps), min(count, count - steps))
    return lax.ppermute(value, axis, [(source, source + steps) for source in range(initial, last)])


def root_norm(values, gain_row):
    return (
        values * lax.rsqrt(jnp.mean(values * values, axis=-1, keepdims=True) + EPSILON) * gain_row
    )


def plain_norm(values):
    return values * lax.rsqrt(jnp.mean(values * values, axis=-1, keepdims=True) + EPSILON)


def smooth_gate(values):
    return jax.nn.gelu(values, approximate=True)


def rotate(values, angles):
    half_width = values.shape[-1] // 2
    leading = values[..., :half_width]
    trailing = values[..., half_width:]
    cosine = jnp.cos(angles)
    sine_part = jnp.sin(angles)
    return jnp.concatenate(
        [leading * cosine - trailing * sine_part, trailing * cosine + leading * sine_part], axis=-1
    )


def matmul_last(first_array, second_array):
    return lax.dot_general(
        first_array,
        second_array,
        (((first_array.ndim - 1,), (0,)), ((), ())),
        preferred_element_type=jnp.float32,
    )


def matmul_back(first_array, second_array):
    return lax.dot_general(
        first_array,
        second_array,
        (((first_array.ndim - 1,), (1,)), ((), ())),
        preferred_element_type=jnp.float32,
    )


def outer_sum(first_array, second_array):
    return lax.dot_general(
        first_array, second_array, (((0, 1), (0, 1)), ((), ())), preferred_element_type=jnp.float32
    )


def input_norm(residual, gain_rows):
    return root_norm(residual, gain_rows[0])


def middle(residual, out_proj, low_rank, normed, gain_rows):
    merged = (
        residual + root_norm(out_proj, gain_rows[1]) + normed + root_norm(low_rank, gain_rows[4])
    ) * HALF_ROOT
    return (merged, root_norm(merged, gain_rows[2]))


def feed_join(merged, summed, gain_rows):
    return merged + root_norm(summed, gain_rows[3])


def final_join(merged, projected, gain_rows):
    return merged + root_norm(projected, gain_rows[5])


def gated_product(first_array, second_array):
    return smooth_gate(first_array) * second_array


def partners():
    c = lax.axis_index("col")
    sib = c + 1 - 2 * (c % 2)
    xn = c + 2 - 4 * ((c // 2) % 2)
    yn = c + 4 - 8 * (c // 4)
    return c, sib, xn, yn

def greet(devs):
    barrier = pltpu.get_barrier_semaphore()
    for d in devs:
        pl.semaphore_signal(barrier, inc=1, device_id={"col": d}, device_id_type=MESH)
    pl.semaphore_wait(barrier, len(devs))

def spread_kernel(rows, x_ref, o_ref, local_sem, send, recv):
    c, sib, xn, yn = partners()
    def slot(half, who):
        return o_ref.at[half, pl.ds(pl.multiple_of(who * rows, rows), rows), :]
    def both(who):
        return o_ref.at[:, pl.ds(pl.multiple_of(who * rows, rows), rows), :]
    def push(i, src, dst, dev):
        return pltpu.make_async_remote_copy(src_ref=src, dst_ref=dst, send_sem=send.at[i], recv_sem=recv.at[i], device_id={"col": dev}, device_id_type=MESH)
    mine = pltpu.make_async_copy(x_ref, both(c), local_sem)
    mine.start()
    greet((sib, xn, yn))
    x0 = push(0, x_ref.at[0], slot(0, c), xn)
    y1 = push(1, x_ref.at[1], slot(1, c), yn)
    x1 = push(2, x_ref.at[1], slot(1, c), xn)
    y0 = push(3, x_ref.at[0], slot(0, c), yn)
    s = push(4, x_ref, both(c), sib)
    x0.start(); y1.start(); x1.start(); y0.start(); s.start()
    diag = yn + (xn - c)
    x0.wait_recv()
    fy = push(5, slot(0, xn), slot(0, xn), yn)
    fy.start()
    sx0 = push(6, slot(0, xn), slot(0, xn), sib)
    sx0.start()
    y1.wait_recv()
    fx = push(7, slot(1, yn), slot(1, yn), xn)
    fx.start()
    sy1 = push(8, slot(1, yn), slot(1, yn), sib)
    sy1.start()
    x1.wait_recv()
    sx1 = push(9, slot(1, xn), slot(1, xn), sib)
    sx1.start()
    y0.wait_recv()
    sy0 = push(10, slot(0, yn), slot(0, yn), sib)
    sy0.start()
    fy.wait_recv()
    sd0 = push(11, slot(0, diag), slot(0, diag), sib)
    sd0.start()
    fx.wait_recv()
    sd1 = push(12, slot(1, diag), slot(1, diag), sib)
    sd1.start()
    for cp in (s, sx0, sy1, sx1, sy0, sd0, sd1):
        cp.wait_recv()
    for cp in (x0, y1, x1, y0, s, fy, sx0, fx, sy1, sx1, sy0, sd0, sd1):
        cp.wait_send()
    mine.wait()

def spread(x, cid=0):
    h, rows, d = x.shape
    return pl.pallas_call(
        functools.partial(spread_kernel, rows),
        out_shape=jax.ShapeDtypeStruct((h, 8 * rows, d), x.dtype),
        in_specs=[pl.BlockSpec(memory_space=pl.ANY)],
        out_specs=pl.BlockSpec(memory_space=pl.ANY),
        scratch_shapes=[pltpu.SemaphoreType.DMA, pltpu.SemaphoreType.DMA((13,)), pltpu.SemaphoreType.DMA((13,))],
        compiler_params=pltpu.CompilerParams(collective_id=cid, has_side_effects=True),
        cost_estimate=pl.CostEstimate(flops=0, bytes_accessed=120_000_000, transcendentals=0),
        name="spread",
    )(x)

def fold_steps(rows, p_ref, own, sibs, dx, dy, rx, ry, local_sem, send, recv):
    c, sib, xn, yn = partners()
    diag = yn + (xn - c)
    wide = jnp.float32
    tall = 32 if rows % 32 == 0 else 8

    def blk(who):
        return p_ref.at[:, pl.ds(pl.multiple_of(who * rows, rows), rows), :]

    def push(i, src, dst, dev):
        return pltpu.make_async_remote_copy(
            src_ref=src,
            dst_ref=dst,
            send_sem=send.at[i],
            recv_sem=recv.at[i],
            device_id={"col": dev},
            device_id_type=MESH,
        )

    def add(dst, src):
        @pl.loop(0, rows // tall)
        def _(i):
            r = pl.ds(pl.multiple_of(i * tall, tall), tall)
            dst[r, :] = (dst[r, :].astype(wide) + src[r, :].astype(wide)).astype(dst.dtype)

    def pair(j):
        add(own.at[j, 0], sibs.at[j, 0])
        add(own.at[j, 1], sibs.at[j, 1])

    dests = (diag, xn, yn, c)
    loads = [pltpu.make_async_copy(blk(d), own.at[j], local_sem.at[j]) for j, d in enumerate(dests)]
    for load in loads:
        load.start()
    yield None
    sides = [push(j, blk(d + (sib - c)), sibs.at[j], sib) for j, d in enumerate(dests)]
    for side in sides:
        side.start()
    yield None
    loads[0].wait()
    sides[0].wait_recv()
    pair(0)
    a = push(4, own.at[0, 0], dx, xn)
    b = push(5, own.at[0, 1], dy, yn)
    a.start()
    b.start()
    yield None
    loads[1].wait()
    sides[1].wait_recv()
    pair(1)
    x0 = push(6, own.at[1, 0], rx.at[0], xn)
    x0.start()
    yield None
    loads[2].wait()
    sides[2].wait_recv()
    pair(2)
    y1 = push(7, own.at[2, 1], ry.at[1], yn)
    y1.start()
    yield None
    a.wait_recv()
    add(own.at[2, 0], dx)
    y0 = push(8, own.at[2, 0], ry.at[0], yn)
    y0.start()
    yield None
    b.wait_recv()
    add(own.at[1, 1], dy)
    x1 = push(9, own.at[1, 1], rx.at[1], xn)
    x1.start()
    yield None
    loads[3].wait()
    sides[3].wait_recv()
    pair(3)
    yield None
    waits = ((x0, y0), (x1, y1))
    yield tall, waits, (*sides, a, b, x0, y1, y0, x1)


def fold_finish(rows, o_ref, own, rx, ry, tall, waits, sent):
    wide = jnp.float32
    for h in range(2):
        for copy in waits[h]:
            copy.wait_recv()

        @pl.loop(0, rows // tall)
        def _(i):
            r = pl.ds(pl.multiple_of(i * tall, tall), tall)
            o_ref[h, r, :] = (
                own[3, h, r, :].astype(wide) + rx[h, r, :].astype(wide) + ry[h, r, :].astype(wide)
            )

    for copy in sent:
        copy.wait_send()


def fold_scratch(h, rows, d, kind):
    return [
        pltpu.VMEM((4, h, rows, d), kind),
        pltpu.VMEM((4, h, rows, d), kind),
        pltpu.VMEM((rows, d), kind),
        pltpu.VMEM((rows, d), kind),
        pltpu.VMEM((h, rows, d), kind),
        pltpu.VMEM((h, rows, d), kind),
        pltpu.SemaphoreType.DMA((4,)),
        pltpu.SemaphoreType.DMA((10,)),
        pltpu.SemaphoreType.DMA((10,)),
    ]


def product_kernel(rows, flip, outer, *refs):
    if outer:
        a_ref, w_ref, f_ref, o_ref, g_ref = refs[:5]
        f_buf, g_buf, turned, f_sem, g_sem = refs[-5:]
        refs = refs[5:-5]
    else:
        a_ref, w_ref, o_ref = refs[:3]
        refs = refs[3:]
    a_buf, w_buf, stage, own, sibs, dx, dy, rx, ry, local_sem, send, recv = refs
    c, sib, xn, yn = partners()
    diag = yn + (xn - c)
    wide = jnp.float32
    d = o_ref.shape[-1]
    tile = 512
    tall = 32

    def push(i, src, dst, dev):
        return pltpu.make_async_remote_copy(
            src_ref=src,
            dst_ref=dst,
            send_sem=send.at[i],
            recv_sem=recv.at[i],
            device_id={"col": dev},
            device_id_type=MESH,
        )

    dests = (diag, xn, yn, c)
    step = sib - c
    weights = pltpu.make_async_copy(w_ref, w_buf, local_sem.at[8])
    weights.start()

    def load(i, who):
        return pltpu.make_async_copy(
            a_ref.at[:, pl.ds(pl.multiple_of(who * rows, rows), rows), :],
            a_buf.at[i],
            local_sem.at[i],
        )

    far = [load(j, dests[j] + step) for j in range(4)]
    near = [load(4 + j, dests[j]) for j in range(4)]
    for first, second in zip(far, near):
        first.start()
        second.start()
    owners = [d + step for d in dests] + list(dests)
    strip = 256

    def strips(n):
        cut = pl.ds(pl.multiple_of(n * strip, strip), strip)
        return [
            pltpu.make_async_copy(
                f_ref.at[:, pl.ds(pl.multiple_of(who * rows, rows), rows), cut],
                f_buf.at[lax.rem(n, 2), i],
                f_sem.at[lax.rem(n, 2), i],
            )
            for i, who in enumerate(owners)
        ]

    def strip_out(n):
        cut = pl.ds(pl.multiple_of(n * strip, strip), strip)
        slot = lax.rem(n, 2)
        return pltpu.make_async_copy(g_buf.at[slot], g_ref.at[cut, :], g_sem.at[slot])

    def outer_product():
        count = g_ref.shape[0] // strip
        depth = a_buf.shape[-1]

        @pl.loop(0, count)
        def _(n):
            slot = lax.rem(n, 2)
            for copy in strips(n):
                copy.wait()

            @pl.when(n + 1 < count)
            def _():
                for copy in strips(n + 1):
                    copy.start()

            @pl.when(n >= 2)
            def _():
                strip_out(n - 2).wait()

            turned[...] = f_buf[slot].reshape(16 * rows, strip).T

            @pl.loop(0, depth // tile)
            def _(m):
                cut = pl.ds(pl.multiple_of(m * tile, tile), tile)
                right = a_buf[:, :, :, cut].reshape(16 * rows, tile)
                value = jnp.dot(turned[...], right, preferred_element_type=wide)
                g_buf[slot, :, cut] = value.astype(g_buf.dtype)

            strip_out(n).start()

        strip_out(count - 2).wait()
        strip_out(count - 1).wait()

    if outer:
        for copy in strips(0):
            copy.start()
    greet((sib, xn, yn))
    weights.wait()

    def product(i, put):
        left = a_buf[i].reshape(2 * rows, a_buf.shape[-1])

        @pl.loop(0, d // tile)
        def _(n):
            cut = pl.ds(pl.multiple_of(n * tile, tile), tile)
            right = w_buf[cut, :] if flip else w_buf[:, cut]
            dims = (((1,), (1,)), ((), ())) if flip else (((1,), (0,)), ((), ()))
            value = lax.dot_general(left, right, dims, preferred_element_type=wide)
            put(cut, value.reshape(2, rows, tile))

    sides = [push(j, stage.at[j], sibs.at[j], sib) for j in range(4)]

    def for_sibling(j):
        far[j].wait()

        def put(cut, value):
            stage[j, :, :, cut] = value.astype(stage.dtype)

        product(j, put)
        sides[j].start()

    def for_chip(j):
        near[j].wait()
        sides[j].wait_recv()

        def put(cut, value):
            own[j, :, :, cut] = (value + sibs[j, :, :, cut].astype(wide)).astype(own.dtype)

        product(4 + j, put)

    def add(dst, src):
        @pl.loop(0, rows // tall)
        def _(i):
            r = pl.ds(pl.multiple_of(i * tall, tall), tall)
            dst[r, :] = (dst[r, :].astype(wide) + src[r, :].astype(wide)).astype(dst.dtype)

    for_sibling(0)
    near[0].wait()

    def hold(cut, value):
        o_ref[:, :, cut] = value

    product(4, hold)
    sides[0].wait_recv()
    for h in range(2):

        @pl.loop(0, rows // tall)
        def _(i):
            r = pl.ds(pl.multiple_of(i * tall, tall), tall)
            own[0, h, r, :] = (o_ref[h, r, :] + sibs[0, h, r, :].astype(wide)).astype(own.dtype)

    a = push(4, own.at[0, 0], dx, xn)
    b = push(5, own.at[0, 1], dy, yn)
    a.start()
    b.start()
    for_sibling(1)
    for_sibling(2)
    for_chip(1)
    x0 = push(6, own.at[1, 0], rx.at[0], xn)
    x0.start()
    for_sibling(3)
    for_chip(2)
    y1 = push(7, own.at[2, 1], ry.at[1], yn)
    y1.start()
    a.wait_recv()
    add(own.at[2, 0], dx)
    y0 = push(8, own.at[2, 0], ry.at[0], yn)
    y0.start()
    b.wait_recv()
    add(own.at[1, 1], dy)
    x1 = push(9, own.at[1, 1], rx.at[1], xn)
    x1.start()
    near[3].wait()
    sides[3].wait_recv()

    def put(cut, value):
        o_ref[:, :, cut] = value + sibs[3, :, :, cut].astype(wide)

    product(7, put)
    if outer:
        outer_product()
    for h, waits in enumerate(((x0, y0), (x1, y1))):
        for copy in waits:
            copy.wait_recv()

        @pl.loop(0, rows // tall)
        def _(i):
            r = pl.ds(pl.multiple_of(i * tall, tall), tall)
            o_ref[h, r, :] = o_ref[h, r, :] + rx[h, r, :].astype(wide) + ry[h, r, :].astype(wide)

    for copy in (*sides, a, b, x0, y1, y0, x1):
        copy.wait_send()


def product_sum(left, right, flip, cid, feed=None):
    h, total, depth = left.shape
    rows = total // 8
    d = right.shape[0] if flip else right.shape[1]
    low = left.dtype
    outer = feed is not None
    out_shape = [jax.ShapeDtypeStruct((h, rows, d), jnp.float32)]
    out_specs = [pl.BlockSpec(memory_space=pltpu.VMEM)]
    scratch = [
        pltpu.VMEM((8, h, rows, depth), low),
        pltpu.VMEM(right.shape, low),
        pltpu.VMEM((4, h, rows, d), low),
        pltpu.VMEM((3, h, rows, d), low),
        pltpu.VMEM((4, h, rows, d), low),
        pltpu.VMEM((rows, d), low),
        pltpu.VMEM((rows, d), low),
        pltpu.VMEM((h, rows, d), low),
        pltpu.VMEM((h, rows, d), low),
        pltpu.SemaphoreType.DMA((9,)),
        pltpu.SemaphoreType.DMA((10,)),
        pltpu.SemaphoreType.DMA((10,)),
    ]
    flops = 2 * h * total * depth * d
    if outer:
        width = feed.shape[-1]
        flops += 2 * h * total * depth * width
        out_shape.append(jax.ShapeDtypeStruct((width, depth), low))
        out_specs.append(pl.BlockSpec(memory_space=pl.ANY))
        scratch += [
            pltpu.VMEM((2, 8, h, rows, 256), low),
            pltpu.VMEM((2, 256, depth), low),
            pltpu.VMEM((256, h * total), low),
            pltpu.SemaphoreType.DMA((2, 8)),
            pltpu.SemaphoreType.DMA((2,)),
        ]
    result = pl.pallas_call(
        functools.partial(product_kernel, rows, flip, outer),
        out_shape=out_shape,
        in_specs=[pl.BlockSpec(memory_space=pl.ANY)] * (3 if outer else 2),
        out_specs=out_specs,
        scratch_shapes=scratch,
        compiler_params=pltpu.CompilerParams(
            collective_id=cid,
            has_side_effects=True,
            vmem_limit_bytes=(52 if outer else 44) << 20,
        ),
        cost_estimate=pl.CostEstimate(
            flops=flops, bytes_accessed=130_000_000, transcendentals=0
        ),
        name="product_sum",
    )(*((left, right, feed) if outer else (left, right)))
    return result if outer else result[0]


def fold_small_kernel(
    rows, p_ref, g_ref, o_ref, k_ref, own, sibs, dx, dy, rx, ry, local_sem, send, recv,
    gown, gsibs, grx, glocal, gsend, grecv,
):
    c, sib, xn, yn = partners()
    m = c % 4
    m_sib = m + 1 - 2 * (m % 2)
    m_x = m + 2 - 4 * (m // 2)
    m_diag = m_sib + (m_x - m)
    wide = jnp.float32

    def push(i, src, dst, dev):
        return pltpu.make_async_remote_copy(
            src_ref=src,
            dst_ref=dst,
            send_sem=gsend.at[i],
            recv_sem=grecv.at[i],
            device_id={"col": dev},
            device_id_type=MESH,
        )

    steps = fold_steps(rows, p_ref, own, sibs, dx, dy, rx, ry, local_sem, send, recv)
    next(steps)
    loads = [
        pltpu.make_async_copy(g_ref.at[d], gown.at[j], glocal.at[j])
        for j, d in enumerate((m_x, m))
    ]
    for load in loads:
        load.start()
    greet((sib, xn, yn))
    sides = [push(j, g_ref.at[d], gsibs.at[j], sib) for j, d in enumerate((m_diag, m_sib))]
    sides[0].start()
    next(steps)
    sides[1].start()
    tall = k_ref.shape[0] // 4
    loads[0].wait()
    sides[0].wait_recv()

    @pl.loop(0, 4)
    def _(i):
        r = pl.ds(pl.multiple_of(i * tall, tall), tall)
        gown[0, r, :] = (gown[0, r, :].astype(wide) + gsibs[0, r, :].astype(wide)).astype(
            gown.dtype
        )

    over = push(2, gown.at[0], grx, xn)
    over.start()
    last = None
    for step in steps:
        last = step if step is not None else last
    fold_finish(rows, o_ref, own, rx, ry, *last)
    loads[1].wait()
    sides[1].wait_recv()
    over.wait_recv()

    @pl.loop(0, 4)
    def _(i):
        r = pl.ds(pl.multiple_of(i * tall, tall), tall)
        k_ref[r, :] = (
            gown[1, r, :].astype(wide) + gsibs[1, r, :].astype(wide) + grx[r, :].astype(wide)
        )

    for copy in (*sides, over):
        copy.wait_send()


def fold_small(p, g, cid):
    h, total, d = p.shape
    rows = total // 8
    share, tall, _ = g.shape
    return pl.pallas_call(
        functools.partial(fold_small_kernel, rows),
        out_shape=(
            jax.ShapeDtypeStruct((h, rows, d), jnp.float32),
            jax.ShapeDtypeStruct((tall, d), jnp.float32),
        ),
        in_specs=[pl.BlockSpec(memory_space=pl.ANY)] * 2,
        out_specs=[pl.BlockSpec(memory_space=pltpu.VMEM)] * 2,
        scratch_shapes=fold_scratch(h, rows, d, p.dtype)
        + [
            pltpu.VMEM((2, tall, d), g.dtype),
            pltpu.VMEM((2, tall, d), g.dtype),
            pltpu.VMEM((tall, d), g.dtype),
            pltpu.SemaphoreType.DMA((2,)),
            pltpu.SemaphoreType.DMA((3,)),
            pltpu.SemaphoreType.DMA((3,)),
        ],
        compiler_params=pltpu.CompilerParams(
            collective_id=cid, has_side_effects=True, vmem_limit_bytes=40 << 20
        ),
        cost_estimate=pl.CostEstimate(flops=0, bytes_accessed=60_000_000, transcendentals=0),
        name="fold_small",
    )(p, g)


def open_kernel(
    rows, tiers, x_ref, s_ref, q_ref, w_ref, o_ref, sa_ref, qa_ref, wa_ref,
    local_sem, send, recv, line_send, line_recv,
):
    c, sib, xn, yn = partners()
    diag = yn + (xn - c)
    r = lax.axis_index("row")
    last = tiers - 1
    weights = []
    for src, dst in ((s_ref, sa_ref), (q_ref, qa_ref), (w_ref, wa_ref)):
        cut = src.shape[0] // 2
        weights += [(src, dst, pl.ds(0, cut)), (src, dst, pl.ds(cut, src.shape[0] - cut))]
    pieces = len(weights)

    def slot(half, who):
        return o_ref.at[half, pl.ds(pl.multiple_of(who * rows, rows), rows), :]

    def both(who):
        return o_ref.at[:, pl.ds(pl.multiple_of(who * rows, rows), rows), :]

    started = []

    def push(src, dst, **dev):
        i = len(started)
        copy = pltpu.make_async_remote_copy(
            src_ref=src,
            dst_ref=dst,
            send_sem=send.at[i],
            recv_sem=recv.at[i],
            device_id=dev,
            device_id_type=MESH,
        )
        copy.start()
        started.append(copy)
        return copy

    local = [
        pltpu.make_async_copy(x_ref, both(c), local_sem.at[0]),
        pltpu.make_async_copy(s_ref, sa_ref.at[r], local_sem.at[1]),
        pltpu.make_async_copy(q_ref, qa_ref.at[r], local_sem.at[2]),
        pltpu.make_async_copy(w_ref, wa_ref.at[r], local_sem.at[3]),
    ]
    for copy in local:
        copy.start()
    barrier = pltpu.get_barrier_semaphore()
    for d in (sib, xn, yn):
        pl.semaphore_signal(barrier, inc=1, device_id={"col": d}, device_id_type=MESH)

    @pl.when(r < last)
    def _():
        pl.semaphore_signal(barrier, inc=1, device_id={"row": r + 1}, device_id_type=MESH)

    @pl.when(r > 0)
    def _():
        pl.semaphore_signal(barrier, inc=1, device_id={"row": r - 1}, device_id_type=MESH)

    @pl.when((r > 0) & (r < last))
    def _():
        pl.semaphore_wait(barrier, 5)

    @pl.when((r == 0) | (r == last))
    def _():
        pl.semaphore_wait(barrier, 4)

    def passing(way, hop, j):
        src, dst, cut = weights[j]
        whose = r - hop if way == 0 else r + hop
        return pltpu.make_async_remote_copy(
            src_ref=src.at[cut] if hop == 0 else dst.at[whose, cut],
            dst_ref=dst.at[whose, cut],
            send_sem=line_send.at[way, hop, j],
            recv_sem=line_recv.at[way, hop, j],
            device_id={"row": r + 1 if way == 0 else r - 1},
            device_id_type=MESH,
        )

    def going(way, hop):
        return (r < last) & (r >= hop) if way == 0 else (r > 0) & (r + hop <= last)

    def coming(way, hop):
        return r > hop if way == 0 else r + hop < last

    def forward(hop, j):
        for way in range(2):
            if hop > 0:

                @pl.when(coming(way, hop - 1))
                def _():
                    passing(way, hop - 1, j).wait_recv()

            @pl.when(going(way, hop))
            def _():
                passing(way, hop, j).start()

    x0 = push(x_ref.at[0], slot(0, c), col=xn)
    y1 = push(x_ref.at[1], slot(1, c), col=yn)
    for j in range(pieces):
        forward(0, j)
    x1 = push(x_ref.at[1], slot(1, c), col=xn)
    y0 = push(x_ref.at[0], slot(0, c), col=yn)
    push(x_ref, both(c), col=sib)
    forward(1, 0)
    forward(1, 1)
    x0.wait_recv()
    fy = push(slot(0, xn), slot(0, xn), col=yn)
    push(slot(0, xn), slot(0, xn), col=sib)
    y1.wait_recv()
    fx = push(slot(1, yn), slot(1, yn), col=xn)
    push(slot(1, yn), slot(1, yn), col=sib)
    for j in range(2, pieces):
        forward(1, j)
    x1.wait_recv()
    push(slot(1, xn), slot(1, xn), col=sib)
    y0.wait_recv()
    push(slot(0, yn), slot(0, yn), col=sib)
    for hop in range(2, last):
        for j in range(pieces):
            forward(hop, j)
    fy.wait_recv()
    push(slot(0, diag), slot(0, diag), col=sib)
    fx.wait_recv()
    push(slot(1, diag), slot(1, diag), col=sib)
    for copy in started:
        if not any(copy is other for other in (x0, y1, x1, y0, fy, fx)):
            copy.wait_recv()
    for j in range(pieces):
        for way in range(2):

            @pl.when(coming(way, last - 1))
            def _():
                passing(way, last - 1, j).wait_recv()

            for hop in range(last):

                @pl.when(going(way, hop))
                def _():
                    passing(way, hop, j).wait_send()

    for copy in started:
        copy.wait_send()
    for copy in local:
        copy.wait()


def open_all(x, small, query, output, tiers, cid):
    h, rows, d = x.shape
    low = x.dtype
    copies = 13
    return pl.pallas_call(
        functools.partial(open_kernel, rows, tiers),
        out_shape=(
            jax.ShapeDtypeStruct((h, 8 * rows, d), low),
            jax.ShapeDtypeStruct((tiers, *small.shape), low),
            jax.ShapeDtypeStruct((tiers, *query.shape), low),
            jax.ShapeDtypeStruct((tiers, *output.shape), low),
        ),
        in_specs=[pl.BlockSpec(memory_space=pl.ANY)] * 4,
        out_specs=[pl.BlockSpec(memory_space=pl.ANY)] * 4,
        scratch_shapes=[
            pltpu.SemaphoreType.DMA((4,)),
            pltpu.SemaphoreType.DMA((copies,)),
            pltpu.SemaphoreType.DMA((copies,)),
            pltpu.SemaphoreType.DMA((2, tiers - 1, 6)),
            pltpu.SemaphoreType.DMA((2, tiers - 1, 6)),
        ],
        compiler_params=pltpu.CompilerParams(collective_id=cid, has_side_effects=True),
        cost_estimate=pl.CostEstimate(flops=0, bytes_accessed=200_000_000, transcendentals=0),
        name="open_all",
    )(x, small, query, output)


def share_kernel(near, s_ref, sa_ref, local_sem, send, recv):
    c, sib, xn, yn = partners()
    diag = yn + (xn - c)
    height = s_ref.shape[1]
    started = []

    def part(ref, first):
        return ref.at[:, pl.ds(0, near) if first else pl.ds(near, height - near), :]

    def push(who, first, dev, own=False):
        i = len(started)
        dst = part(sa_ref.at[who], first)
        copy = pltpu.make_async_remote_copy(
            src_ref=part(s_ref, first) if own else dst,
            dst_ref=dst,
            send_sem=send.at[i],
            recv_sem=recv.at[i],
            device_id={"col": dev},
            device_id_type=MESH,
        )
        copy.start()
        started.append(copy)
        return copy

    mine = pltpu.make_async_copy(s_ref, sa_ref.at[c], local_sem)
    mine.start()
    greet((sib, xn, yn))
    rx = push(c, False, xn, own=True)
    ry = push(c, False, yn, own=True)
    kx = push(c, True, xn, own=True)
    push(c, True, sib, own=True)
    push(c, False, sib, own=True)
    rx.wait_recv()
    fd = push(xn, False, yn)
    push(xn, False, sib)
    ry.wait_recv()
    push(yn, False, sib)
    fd.wait_recv()
    push(diag, False, sib)
    kx.wait_recv()
    push(xn, True, sib)
    for copy in started:
        if not any(copy is other for other in (kx, rx, ry, fd)):
            copy.wait_recv()
    for copy in started:
        copy.wait_send()
    mine.wait()


def share_small(small, near, cid):
    return pl.pallas_call(
        functools.partial(share_kernel, near),
        out_shape=jax.ShapeDtypeStruct((8, *small.shape), small.dtype),
        in_specs=[pl.BlockSpec(memory_space=pl.ANY)],
        out_specs=pl.BlockSpec(memory_space=pl.ANY),
        scratch_shapes=[
            pltpu.SemaphoreType.DMA,
            pltpu.SemaphoreType.DMA((10,)),
            pltpu.SemaphoreType.DMA((10,)),
        ],
        compiler_params=pltpu.CompilerParams(collective_id=cid, has_side_effects=True),
        cost_estimate=pl.CostEstimate(flops=0, bytes_accessed=60_000_000, transcendentals=0),
        name="share_small",
    )(small)


def rounds_of(rows, x_ref, held, local_sem, send, recv, consume, prepare):
    c, sib, xn, yn = partners()
    diag = yn + (xn - c)
    step = sib - c

    def place(t, j, n=1):
        return held.at[t, pl.ds(j * rows, n * rows), :]

    started = []

    def push(src, dst, dev):
        i = len(started)
        copy = pltpu.make_async_remote_copy(
            src_ref=src,
            dst_ref=dst,
            send_sem=send.at[i],
            recv_sem=recv.at[i],
            device_id={"col": dev},
            device_id_type=MESH,
        )
        copy.start()
        started.append(copy)
        return copy

    mine = [pltpu.make_async_copy(x_ref.at[h], place(0, h), local_sem.at[h]) for h in range(2)]
    for copy in mine:
        copy.start()
    greet((sib, xn, yn))
    x0 = push(x_ref.at[0], place(1, 0), xn)
    y1 = push(x_ref.at[1], place(1, 1), yn)
    x1 = push(x_ref.at[1], place(2, 0), xn)
    y0 = push(x_ref.at[0], place(2, 1), yn)
    s0 = push(x_ref.at[0], place(0, 2), sib)
    s1 = push(x_ref.at[1], place(0, 3), sib)
    prepare(0)
    for copy in mine:
        copy.wait()
    s0.wait_recv()
    s1.wait_recv()
    consume(0, 0, ((0, c), (1, c), (0, sib), (1, sib)))
    x0.wait_recv()
    fy = push(place(1, 0), place(3, 0), yn)
    y1.wait_recv()
    fx = push(place(1, 1), place(3, 1), xn)
    prepare(1)
    t1 = push(place(1, 0, 2), place(1, 2, 2), sib)
    t1.wait_recv()
    consume(1, 0, ((0, xn), (1, yn), (0, xn + step), (1, yn + step)))
    prepare(2)
    x1.wait_recv()
    y0.wait_recv()
    t2 = push(place(2, 0, 2), place(2, 2, 2), sib)
    t2.wait_recv()
    consume(2, 0, ((1, xn), (0, yn), (1, xn + step), (0, yn + step)))
    prepare(3)
    fy.wait_recv()
    fx.wait_recv()
    t3 = push(place(3, 0, 2), place(3, 2, 2), sib)
    consume(3, 0, ((0, diag), (1, diag)))
    t3.wait_recv()
    consume(3, 2, ((0, diag + step), (1, diag + step)))
    for copy in started:
        copy.wait_send()


def piece_at(ref, rows, piece):
    half, who = piece
    return ref.at[half, pl.ds(pl.multiple_of(who * rows, rows), rows), :]


def units_back_kernel(
    rows, x_ref, w_ref, u_ref, g_ref, v_ref, p_ref, d_ref,
    held, weights, units, turned, gates, ups, grads, total_ref,
    weight_sem, load_sem, store_sem, local_sem, send, recv,
):
    c, sib, xn, yn = partners()
    diag = yn + (xn - c)
    step = sib - c
    wide = jnp.float32
    width = w_ref.shape[0]
    d = w_ref.shape[1]
    plan = (
        ((0, c), (1, c), (0, sib), (1, sib)),
        ((0, xn), (1, yn), (0, xn + step), (1, yn + step)),
        ((1, xn), (0, yn), (1, xn + step), (0, yn + step)),
        ((0, diag), (1, diag), (0, diag + step), (1, diag + step)),
    )
    fetch = pltpu.make_async_copy(w_ref, weights, weight_sem)
    fetch.start()

    def loads(t):
        copies = []
        for j, piece in enumerate(plan[t]):
            for k, (src, dst) in enumerate(((u_ref, units), (g_ref, gates), (v_ref, ups))):
                copies.append(
                    pltpu.make_async_copy(
                        piece_at(src, rows, piece),
                        dst.at[t % 2, pl.ds(j * rows, rows), :],
                        load_sem.at[t % 2, j, k],
                    )
                )
        return copies

    def stores(t, first=0, count=4):
        return [
            pltpu.make_async_copy(
                grads.at[t % 2, pl.ds(j * rows, rows), :],
                piece_at(p_ref, rows, plan[t][j]),
                store_sem.at[t % 2, j],
            )
            for j in range(first, first + count)
        ]

    for copy in loads(0):
        copy.start()

    tile = 256

    def prepare(t):
        if t == 0:
            fetch.wait()
        if t < 3:
            for copy in loads(t + 1):
                copy.start()
        for copy in loads(t):
            copy.wait()

        @pl.loop(0, width // tile)
        def _(n):
            cut = pl.ds(pl.multiple_of(n * tile, tile), tile)
            gate = gates[t % 2, :, cut]
            square = gate * gate
            bent = jnp.tanh(CURVE * (gate + BEND * gate * square))
            rise = 0.5 * (1.0 + bent)
            slope = rise + (0.5 * CURVE) * gate * (1.0 - bent * bent) * (1.0 + 3.0 * BEND * square)
            gates[t % 2, :, cut] = ups[t % 2, :, cut] * slope
            ups[t % 2, :, cut] = gate * rise
            turned[cut, :] = units[t % 2, :, cut].T

    def consume(t, first, pieces):
        if t >= 2 and first == 0:
            for copy in stores(t - 2):
                copy.wait()
        span = slice(first * rows, (first + len(pieces)) * rows)

        @pl.loop(0, width // 512)
        def _(n):
            cut = pl.ds(pl.multiple_of(n * 512, 512), 512)
            grad = lax.dot_general(
                held[t, span, :],
                weights[cut, :],
                (((1,), (1,)), ((), ())),
                preferred_element_type=wide,
            )
            grads[t % 2, span, cut] = (grad * gates[t % 2, span, cut]).astype(grads.dtype)
            cut_up = pl.ds(pl.multiple_of(width + n * 512, 512), 512)
            grads[t % 2, span, cut_up] = (grad * ups[t % 2, span, cut]).astype(grads.dtype)

        for copy in stores(t, first, len(pieces)):
            copy.start()

        @pl.loop(0, d // 512)
        def _(n):
            cut = pl.ds(pl.multiple_of(n * 512, 512), 512)
            value = jnp.dot(turned[:, span], held[t, span, cut], preferred_element_type=wide)
            if t > 0:
                value = value + total_ref[:, cut]
            if first == 0:
                total_ref[:, cut] = value
            else:
                d_ref[:, cut] = value.astype(d_ref.dtype)

    rounds_of(rows, x_ref, held, local_sem, send, recv, consume, prepare)
    for copy in (*stores(2), *stores(3)):
        copy.wait()


def units_back(x, down, units, gate, up, cid):
    h, rows, d = x.shape
    width = down.shape[0]
    low = x.dtype
    return pl.pallas_call(
        functools.partial(units_back_kernel, rows),
        out_shape=(
            jax.ShapeDtypeStruct((h, 8 * rows, 2 * width), low),
            jax.ShapeDtypeStruct((width, d), low),
        ),
        in_specs=[pl.BlockSpec(memory_space=pl.ANY)] * 5,
        out_specs=[
            pl.BlockSpec(memory_space=pl.ANY),
            pl.BlockSpec(memory_space=pltpu.VMEM),
        ],
        scratch_shapes=[
            pltpu.VMEM((4, 4 * rows, d), low),
            pltpu.VMEM((width, d), low),
            pltpu.VMEM((2, 4 * rows, width), low),
            pltpu.VMEM((width, 4 * rows), low),
            pltpu.VMEM((2, 4 * rows, width), jnp.float32),
            pltpu.VMEM((2, 4 * rows, width), jnp.float32),
            pltpu.VMEM((2, 4 * rows, 2 * width), low),
            pltpu.VMEM((width, d), jnp.float32),
            pltpu.SemaphoreType.DMA,
            pltpu.SemaphoreType.DMA((2, 4, 3)),
            pltpu.SemaphoreType.DMA((2, 4)),
            pltpu.SemaphoreType.DMA((2,)),
            pltpu.SemaphoreType.DMA((11,)),
            pltpu.SemaphoreType.DMA((11,)),
        ],
        compiler_params=pltpu.CompilerParams(
            collective_id=cid, has_side_effects=True, vmem_limit_bytes=52 << 20
        ),
        cost_estimate=pl.CostEstimate(
            flops=64 * h * rows * width * d, bytes_accessed=130_000_000, transcendentals=0
        ),
        name="units_back",
    )(x, down, units, gate, up)


def heads_back_kernel(
    rows, scale, x_ref, w_ref, m_ref, q_ref, k_ref, v_ref, s_ref, gq_ref, gk_ref, gv_ref, d_ref,
    held, weights, mixed, queries, keys, values, seen, total_ref, load_sem, local_sem, send, recv,
):
    wide = jnp.float32
    d = w_ref.shape[1]
    low = weights.dtype
    pairs = (
        (w_ref, weights), (q_ref, queries), (k_ref, keys), (v_ref, values), (s_ref, seen),
        (m_ref, mixed),
    )
    loads = [
        pltpu.make_async_copy(src, dst, load_sem.at[i]) for i, (src, dst) in enumerate(pairs)
    ]
    for copy in loads:
        copy.start()
    back = (((1,), (1,)), ((), ()))

    def prepare(t):
        if t == 0:
            for copy in loads:
                copy.wait()
            gk_ref[...] = jnp.zeros_like(gk_ref)
            gv_ref[...] = jnp.zeros_like(gv_ref)

    def consume(t, first, pieces):
        part = slice(first * rows, (first + len(pieces)) * rows)
        grad_mixed = lax.dot_general(
            held[t, part, :], weights[...], back, preferred_element_type=wide
        )
        grad_mixed = grad_mixed.astype(low)
        spans = []
        for j, (half, who) in enumerate(pieces):
            span = pl.ds(pl.multiple_of(who * rows, rows), rows)
            spans.append(mixed[half, span, :])
            query = queries[half, span, :]
            grad = grad_mixed[j * rows : (j + 1) * rows]
            score = lax.dot_general(query, keys[half], back, preferred_element_type=wide) * scale
            score = jnp.where(seen[half, span, :] > 0, score, NEGATIVE)
            power = jnp.exp(score - jnp.max(score, axis=-1, keepdims=True))
            prob = power / jnp.sum(power, axis=-1, keepdims=True)
            slope = lax.dot_general(grad, values[half], back, preferred_element_type=wide)
            mean = jnp.sum(prob * slope, axis=-1, keepdims=True)
            flow = (prob * (slope - mean)).astype(low)
            gq_ref[half, span, :] = jnp.dot(flow, keys[half], preferred_element_type=wide) * scale
            gk_ref[half] += jnp.dot(flow.T, query, preferred_element_type=wide) * scale
            gv_ref[half] += jnp.dot(prob.astype(low).T, grad, preferred_element_type=wide)
        turned = jnp.concatenate(spans, axis=0).T

        @pl.loop(0, d // 512)
        def _(n):
            cut = pl.ds(pl.multiple_of(n * 512, 512), 512)
            value = jnp.dot(turned, held[t, part, cut], preferred_element_type=wide)
            if t > 0:
                value = value + total_ref[:, cut]
            if first == 0:
                total_ref[:, cut] = value
            else:
                d_ref[:, cut] = value.astype(d_ref.dtype)

    rounds_of(rows, x_ref, held, local_sem, send, recv, consume, prepare)


def heads_back(x, output, mixed, query, key, value, visible, scale, cid):
    h, rows, d = x.shape
    low = x.dtype
    grad = jax.ShapeDtypeStruct(query.shape, jnp.float32)
    return pl.pallas_call(
        functools.partial(heads_back_kernel, rows, scale),
        out_shape=(grad, grad, grad, jax.ShapeDtypeStruct(output.shape, low)),
        in_specs=[pl.BlockSpec(memory_space=pl.ANY)] * 7,
        out_specs=[pl.BlockSpec(memory_space=pltpu.VMEM)] * 4,
        scratch_shapes=[
            pltpu.VMEM((4, 4 * rows, d), low),
            pltpu.VMEM(output.shape, low),
            pltpu.VMEM(mixed.shape, low),
            pltpu.VMEM(query.shape, low),
            pltpu.VMEM(query.shape, low),
            pltpu.VMEM(query.shape, low),
            pltpu.VMEM(visible.shape, visible.dtype),
            pltpu.VMEM(output.shape, jnp.float32),
            pltpu.SemaphoreType.DMA((6,)),
            pltpu.SemaphoreType.DMA((2,)),
            pltpu.SemaphoreType.DMA((11,)),
            pltpu.SemaphoreType.DMA((11,)),
        ],
        compiler_params=pltpu.CompilerParams(
            collective_id=cid, has_side_effects=True, vmem_limit_bytes=48 << 20
        ),
        cost_estimate=pl.CostEstimate(
            flops=20_000_000_000, bytes_accessed=130_000_000, transcendentals=0
        ),
        name="heads_back",
    )(x, output, mixed, query, key, value, visible)


def total_kernel(x_ref, o_ref, sums, got, tier_sums, send, recv):
    c, sib, xn, yn = partners()
    r = lax.axis_index("row")
    tiers = lax.axis_size("row")
    others = [lax.rem(r + k, tiers) for k in range(1, tiers)]
    barrier = pltpu.get_barrier_semaphore()
    for d in (sib, xn, yn):
        pl.semaphore_signal(barrier, inc=1, device_id={"col": d}, device_id_type=MESH)
    for d in others:
        pl.semaphore_signal(barrier, inc=1, device_id={"row": d}, device_id_type=MESH)
    pl.semaphore_wait(barrier, 3 + len(others))
    sums[0] = x_ref[...]
    for i, dev in enumerate((sib, xn, yn)):
        copy = pltpu.make_async_remote_copy(
            src_ref=sums.at[i],
            dst_ref=got.at[i],
            send_sem=send.at[i],
            recv_sem=recv.at[i],
            device_id={"col": dev},
            device_id_type=MESH,
        )
        copy.start()
        copy.wait()
        sums[i + 1] = sums[i] + got[i]
    tier_sums[r] = sums[3]
    copies = []
    for k, d in enumerate(others):
        copy = pltpu.make_async_remote_copy(
            src_ref=sums.at[3],
            dst_ref=tier_sums.at[r],
            send_sem=send.at[3 + k],
            recv_sem=recv.at[3 + k],
            device_id={"row": d},
            device_id_type=MESH,
        )
        copy.start()
        copies.append(copy)
    for copy in copies:
        copy.wait()
    result = tier_sums[0]
    for k in range(1, tiers):
        result = result + tier_sums[k]
    o_ref[...] = result


def total(x, tiers, cid):
    return pl.pallas_call(
        total_kernel,
        out_shape=jax.ShapeDtypeStruct(x.shape, x.dtype),
        in_specs=[pl.BlockSpec(memory_space=pltpu.VMEM)],
        out_specs=pl.BlockSpec(memory_space=pltpu.VMEM),
        scratch_shapes=[
            pltpu.VMEM((4, *x.shape), x.dtype),
            pltpu.VMEM((3, *x.shape), x.dtype),
            pltpu.VMEM((tiers, *x.shape), x.dtype),
            pltpu.SemaphoreType.DMA((2 + tiers,)),
            pltpu.SemaphoreType.DMA((2 + tiers,)),
        ],
        compiler_params=pltpu.CompilerParams(collective_id=cid, has_side_effects=True),
        cost_estimate=pl.CostEstimate(flops=0, bytes_accessed=40_000_000, transcendentals=0),
        name="total",
    )(x)


def after(value, *earlier):
    return lax.optimization_barrier((value, *earlier))[0]


def general_body(
    hidden,
    per_layer,
    lengths,
    block_ids,
    out_grad,
    query_weight,
    key_weight,
    value_weight,
    output_weight,
    gate_weight,
    up_weight,
    down_weight,
    laurel_left,
    laurel_right,
    layer_gate,
    layer_proj,
    norm_gains,
    head_gains,
):
    local_rows = hidden.shape[0]
    seq_groups = hidden.shape[1]
    col_index = lax.axis_index("col")
    row_index = lax.axis_index("row")
    all_lengths = lengths
    lengths = lax.dynamic_slice_in_dim(all_lengths, row_index * seq_groups, seq_groups, 0)
    (
        query_cols,
        key_cols,
        value_cols,
        output_rows,
        gate_cols,
        up_cols,
        down_rows,
        left_cols,
        right_rows,
        gate_layer_cols,
        proj_layer_rows,
    ) = (
        lax.all_gather(query_weight, "row", axis=0, tiled=True),
        lax.all_gather(key_weight, "row", axis=0, tiled=True),
        lax.all_gather(value_weight, "row", axis=0, tiled=True),
        lax.all_gather(output_weight, "row", axis=1, tiled=True),
        lax.all_gather(gate_weight, "row", axis=0, tiled=True),
        lax.all_gather(up_weight, "row", axis=0, tiled=True),
        lax.all_gather(down_weight, "row", axis=1, tiled=True),
        lax.all_gather(laurel_left, "row", axis=0, tiled=True),
        lax.all_gather(laurel_right, "row", axis=1, tiled=True),
        lax.all_gather(layer_gate, "row", axis=0, tiled=True),
        lax.all_gather(layer_proj, "row", axis=1, tiled=True),
    )
    (
        query_full,
        key_full,
        value_full,
        output_full,
        left_full,
        right_full,
        gate_layer_full,
        proj_layer_full,
    ) = (
        lax.all_gather(query_cols, "col", axis=1, tiled=True),
        lax.all_gather(key_cols, "col", axis=1, tiled=True),
        lax.all_gather(value_cols, "col", axis=1, tiled=True),
        lax.all_gather(output_rows, "col", axis=0, tiled=True),
        lax.all_gather(left_cols, "col", axis=1, tiled=True),
        lax.all_gather(right_rows, "col", axis=0, tiled=True),
        lax.all_gather(gate_layer_cols, "col", axis=1, tiled=True),
        lax.all_gather(proj_layer_rows, "col", axis=0, tiled=True),
    )
    paired = jnp.concatenate([gate_cols, up_cols], axis=1)
    unit_width = gate_cols.shape[1]
    first_position = col_index * local_rows
    positions = first_position + jnp.arange(local_rows, dtype=jnp.int32)
    live_mask = positions[:, None] < lengths[None, :]
    keep_mask = live_mask.astype(jnp.float32)[:, :, None]
    reach_back = (WINDOW + local_rows - 2) // local_rows
    reach_ahead = (BLOCK + local_rows - 2) // local_rows
    key_span = (reach_back + 1 + reach_ahead) * local_rows
    key_position = first_position - reach_back * local_rows + jnp.arange(key_span, dtype=jnp.int32)
    filler_low = jnp.full((seq_groups, reach_back * local_rows), FAR_BLOCK, jnp.int32)
    filler_high = jnp.full((seq_groups, reach_ahead * local_rows), FAR_BLOCK, jnp.int32)
    padded_blocks = jnp.concatenate([filler_low, block_ids, filler_high], axis=1)
    key_blocks = lax.dynamic_slice_in_dim(padded_blocks, first_position, key_span, 1)
    query_blocks = lax.dynamic_slice_in_dim(block_ids, first_position, local_rows, 1)
    key_live = (key_position[None, :] >= 0) & (key_position[None, :] < lengths[:, None])
    query_live = positions[None, :] < lengths[:, None]
    distance = positions[:, None] - key_position[None, :]
    nearby = (query_blocks[:, :, None] >= key_blocks[:, None, :]) & (distance < WINDOW)[None]
    nearby = nearby & query_live[:, :, None] & key_live[:, None, :]
    visible = (nearby | (distance == 0)[None])[:, None, None]
    residual = hidden.astype(jnp.float32)
    normed_value, input_back = jax.vjp(input_norm, residual, norm_gains)
    normed_low = normed_value.astype(jnp.bfloat16)
    half_width = HD // 2
    frequency = jnp.exp(jnp.arange(half_width, dtype=jnp.float32) * (-2.0 * math.log(10000.0) / HD))
    angles = (positions.astype(jnp.float32)[:, None] * frequency[None, :])[:, None, None, :]

    def prepare(query_in, key_in, value_in, gain_rows):
        return (
            rotate(root_norm(query_in, gain_rows[0]), angles),
            rotate(root_norm(key_in, gain_rows[1]), angles),
            plain_norm(value_in),
        )

    query_raw = matmul_last(normed_low, query_full).reshape(local_rows, seq_groups, H, HD)
    key_raw = matmul_last(normed_low, key_full).reshape(local_rows, seq_groups, KV, HD)
    value_raw = matmul_last(normed_low, value_full).reshape(local_rows, seq_groups, KV, HD)
    (query_value, key_value, value_value), head_back = jax.vjp(
        prepare, query_raw, key_raw, value_raw, head_gains
    )
    query_low = query_value.astype(jnp.bfloat16).reshape(local_rows, seq_groups, KV, H // KV, HD)
    key_low = key_value.astype(jnp.bfloat16)
    value_low = value_value.astype(jnp.bfloat16)
    offsets = list(range(reach_back, -reach_ahead - 1, -1))
    key_parts = []
    value_parts = []
    for offset in offsets:
        if offset == 0:
            key_parts.append(key_low)
            value_parts.append(value_low)
        else:
            moved_key, moved_value = passed_along((key_low, value_low), "col", offset)
            key_parts.append(moved_key)
            value_parts.append(moved_value)
    near_keys = jnp.concatenate(key_parts, axis=0)
    near_values = jnp.concatenate(value_parts, axis=0)
    score_scale = HD ** (-0.5)

    def score_all():
        raw_scores = (
            jnp.einsum(
                "psjgd,esjd->sjgpe", query_low, near_keys, preferred_element_type=jnp.float32
            )
            * score_scale
        )
        return jnp.where(visible, raw_scores, NEGATIVE)

    scores = score_all()
    row_max = jnp.max(scores, axis=-1, keepdims=True)
    exponent = jnp.exp(scores - row_max)
    row_total = jnp.sum(exponent, axis=-1, keepdims=True)
    attn_prob = exponent / row_total
    log_total = row_max + jnp.log(row_total)
    mixed_heads = jnp.einsum(
        "sjgpe,esjd->psjgd",
        attn_prob.astype(jnp.bfloat16),
        near_values,
        preferred_element_type=jnp.float32,
    )
    mixed_low = mixed_heads.reshape(local_rows, seq_groups, H * HD).astype(jnp.bfloat16)
    out_proj = matmul_last(mixed_low, output_full)
    laurel_mid = matmul_last(normed_low, left_full).astype(jnp.bfloat16)
    low_rank = matmul_last(laurel_mid, right_full)
    (after_attention, feed_normed), middle_back = jax.vjp(
        middle, residual, out_proj, low_rank, normed_low.astype(jnp.float32), norm_gains
    )
    feed_low = feed_normed.astype(jnp.bfloat16)
    gate_up = matmul_last(lax.all_gather(feed_low, "col", axis=0, tiled=True), paired)
    unit_value, gate_back = jax.vjp(
        gated_product, gate_up[..., :unit_width], gate_up[..., unit_width:]
    )
    units_low = unit_value.astype(jnp.bfloat16)
    summed = lax.psum_scatter(
        matmul_last(units_low, down_rows), "col", scatter_dimension=0, tiled=True
    )
    after_feed, feed_back = jax.vjp(feed_join, after_attention, summed, norm_gains)
    feed_round = after_feed.astype(jnp.bfloat16)
    layer_pre = matmul_last(feed_round, gate_layer_full)
    layer_input = per_layer.astype(jnp.float32)
    layer_value, layer_back = jax.vjp(gated_product, layer_pre, layer_input)
    layer_low = layer_value.astype(jnp.bfloat16)
    projected = matmul_last(layer_low, proj_layer_full)
    out_value, final_back = jax.vjp(final_join, after_feed, projected, norm_gains)
    square_sums = jnp.stack(
        [
            jnp.sum(keep_mask * residual * residual),
            jnp.sum(keep_mask * after_attention * after_attention),
            jnp.sum(keep_mask * after_feed * after_feed),
            jnp.sum(keep_mask * out_value * out_value),
        ]
    )
    valid_count = jnp.sum(all_lengths).astype(jnp.float32)
    cotangent = out_grad.astype(jnp.float32) * keep_mask
    grad_feed_out, grad_projected, gains_final = final_back(cotangent)
    projected_low = grad_projected.astype(jnp.bfloat16)
    grad_proj_layer = outer_sum(layer_low, projected_low)
    grad_layer_pre, grad_layer_input = layer_back(matmul_back(projected_low, proj_layer_full))
    layer_pre_low = grad_layer_pre.astype(jnp.bfloat16)
    grad_gate_layer = outer_sum(feed_round, layer_pre_low)
    grad_after_feed = grad_feed_out + matmul_back(layer_pre_low, gate_layer_full)
    grad_after_attention_a, grad_summed, gains_feed = feed_back(grad_after_feed)
    summed_low = grad_summed.astype(jnp.bfloat16)
    block_rows = lax.all_gather(summed_low, "col", axis=0, tiled=True)
    grad_down = outer_sum(units_low, block_rows)
    grad_units = matmul_back(block_rows, down_rows)
    grad_down, grad_units = (grad_down, grad_units)
    grad_gate_value, grad_up_value = gate_back(grad_units)
    grad_paired = jnp.concatenate([grad_gate_value, grad_up_value], axis=-1).astype(jnp.bfloat16)
    grad_weights_paired = outer_sum(
        lax.all_gather(feed_low, "col", axis=0, tiled=True), grad_paired
    )
    grad_feed = lax.psum_scatter(
        matmul_back(grad_paired, paired).astype(jnp.bfloat16),
        "col",
        scatter_dimension=0,
        tiled=True,
    ).astype(jnp.float32)
    grad_residual_mid, grad_out_proj, grad_low_rank, grad_normed_mid, gains_middle = middle_back(
        (grad_after_attention_a, grad_feed)
    )
    out_proj_low = grad_out_proj.astype(jnp.bfloat16)
    grad_output = outer_sum(mixed_low, out_proj_low)
    grad_mixed = matmul_back(out_proj_low, output_full).astype(jnp.bfloat16)
    grad_mixed = grad_mixed.reshape(local_rows, seq_groups, KV, H // KV, HD)
    low_rank_grad = grad_low_rank.astype(jnp.bfloat16)
    grad_right = outer_sum(laurel_mid, low_rank_grad)
    grad_laurel_mid = matmul_back(low_rank_grad, right_full).astype(jnp.bfloat16)
    grad_left = outer_sum(normed_low, grad_laurel_mid)
    scores = score_all()
    attn_prob = jnp.exp(scores - log_total)
    grad_prob = jnp.einsum(
        "psjgd,esjd->sjgpe", grad_mixed, near_values, preferred_element_type=jnp.float32
    )
    grad_scores = (
        attn_prob * (grad_prob - jnp.sum(attn_prob * grad_prob, axis=-1, keepdims=True))
    ).astype(jnp.bfloat16)
    grad_queries = (
        jnp.einsum("sjgpe,esjd->psjgd", grad_scores, near_keys, preferred_element_type=jnp.float32)
        * score_scale
    )
    grad_near_keys = (
        jnp.einsum("sjgpe,psjgd->esjd", grad_scores, query_low, preferred_element_type=jnp.float32)
        * score_scale
    )
    grad_near_values = jnp.einsum(
        "sjgpe,psjgd->esjd",
        attn_prob.astype(jnp.bfloat16),
        grad_mixed,
        preferred_element_type=jnp.float32,
    )
    grad_key_total = grad_near_keys[reach_back * local_rows : (reach_back + 1) * local_rows]
    grad_value_total = grad_near_values[reach_back * local_rows : (reach_back + 1) * local_rows]
    for slot_index, offset in enumerate(offsets):
        if offset != 0:
            piece_keys = grad_near_keys[slot_index * local_rows : (slot_index + 1) * local_rows]
            piece_values = grad_near_values[slot_index * local_rows : (slot_index + 1) * local_rows]
            back_keys, back_values = (
                passed_along(piece_keys.astype(jnp.bfloat16), "col", -offset).astype(
                    piece_keys.dtype
                ),
                passed_along(piece_values.astype(jnp.bfloat16), "col", -offset).astype(
                    piece_values.dtype
                ),
            )
            grad_key_total = grad_key_total + back_keys
            grad_value_total = grad_value_total + back_values
    grad_query_raw, grad_key_raw, grad_value_raw, grad_heads = head_back(
        (grad_queries.reshape(local_rows, seq_groups, H, HD), grad_key_total, grad_value_total)
    )
    query_grad_low = grad_query_raw.reshape(local_rows, seq_groups, H * HD).astype(jnp.bfloat16)
    key_grad_low = grad_key_raw.reshape(local_rows, seq_groups, KV * HD).astype(jnp.bfloat16)
    value_grad_low = grad_value_raw.reshape(local_rows, seq_groups, KV * HD).astype(jnp.bfloat16)
    grad_query = outer_sum(normed_low, query_grad_low)
    grad_key = outer_sum(normed_low, key_grad_low)
    grad_value = outer_sum(normed_low, value_grad_low)
    grad_normed = (
        grad_normed_mid
        + matmul_back(grad_laurel_mid, left_full)
        + matmul_back(query_grad_low, query_full)
        + matmul_back(key_grad_low, key_full)
        + matmul_back(value_grad_low, value_full)
    )
    grad_residual_in, gains_input = input_back(grad_normed)
    d_hidden = (grad_residual_mid + grad_residual_in).astype(jnp.bfloat16)
    d_per_layer = grad_layer_input.astype(jnp.bfloat16)
    grad_gains = gains_final + gains_feed + gains_middle + gains_input
    grad_gate = grad_weights_paired[:, :unit_width]
    grad_up = grad_weights_paired[:, unit_width:]
    (
        query_part,
        key_part,
        value_part,
        output_part,
        left_part,
        right_part,
        gate_layer_part,
        proj_layer_part,
    ) = (
        lax.psum_scatter(
            grad_query.astype(jnp.bfloat16), "col", scatter_dimension=1, tiled=True
        ).astype(jnp.float32),
        lax.psum_scatter(
            grad_key.astype(jnp.bfloat16), "col", scatter_dimension=1, tiled=True
        ).astype(jnp.float32),
        lax.psum_scatter(
            grad_value.astype(jnp.bfloat16), "col", scatter_dimension=1, tiled=True
        ).astype(jnp.float32),
        lax.psum_scatter(
            grad_output.astype(jnp.bfloat16), "col", scatter_dimension=0, tiled=True
        ).astype(jnp.float32),
        lax.psum_scatter(
            grad_left.astype(jnp.bfloat16), "col", scatter_dimension=1, tiled=True
        ).astype(jnp.float32),
        lax.psum_scatter(
            grad_right.astype(jnp.bfloat16), "col", scatter_dimension=0, tiled=True
        ).astype(jnp.float32),
        lax.psum_scatter(
            grad_gate_layer.astype(jnp.bfloat16), "col", scatter_dimension=1, tiled=True
        ).astype(jnp.float32),
        lax.psum_scatter(
            grad_proj_layer.astype(jnp.bfloat16), "col", scatter_dimension=0, tiled=True
        ).astype(jnp.float32),
    )
    (
        d_query_weight,
        d_key_weight,
        d_value_weight,
        d_output_weight,
        d_gate_weight,
        d_up_weight,
        d_down_weight,
        d_laurel_left,
        d_laurel_right,
        d_layer_gate,
        d_layer_proj,
    ) = (
        lax.psum_scatter(
            query_part.astype(jnp.bfloat16), "row", scatter_dimension=0, tiled=True
        ).astype(jnp.float32),
        lax.psum_scatter(
            key_part.astype(jnp.bfloat16), "row", scatter_dimension=0, tiled=True
        ).astype(jnp.float32),
        lax.psum_scatter(
            value_part.astype(jnp.bfloat16), "row", scatter_dimension=0, tiled=True
        ).astype(jnp.float32),
        lax.psum_scatter(
            output_part.astype(jnp.bfloat16), "row", scatter_dimension=1, tiled=True
        ).astype(jnp.float32),
        lax.psum_scatter(
            grad_gate.astype(jnp.bfloat16), "row", scatter_dimension=0, tiled=True
        ).astype(jnp.float32),
        lax.psum_scatter(
            grad_up.astype(jnp.bfloat16), "row", scatter_dimension=0, tiled=True
        ).astype(jnp.float32),
        lax.psum_scatter(
            grad_down.astype(jnp.bfloat16), "row", scatter_dimension=1, tiled=True
        ).astype(jnp.float32),
        lax.psum_scatter(
            left_part.astype(jnp.bfloat16), "row", scatter_dimension=0, tiled=True
        ).astype(jnp.float32),
        lax.psum_scatter(
            right_part.astype(jnp.bfloat16), "row", scatter_dimension=1, tiled=True
        ).astype(jnp.float32),
        lax.psum_scatter(
            gate_layer_part.astype(jnp.bfloat16), "row", scatter_dimension=0, tiled=True
        ).astype(jnp.float32),
        lax.psum_scatter(
            proj_layer_part.astype(jnp.bfloat16), "row", scatter_dimension=1, tiled=True
        ).astype(jnp.float32),
    )
    d_norm_gains, d_head_gains, total_squares = lax.psum(
        (grad_gains, grad_heads, square_sums), ("row", "col")
    )
    stats = jnp.sqrt(total_squares / (valid_count * D))
    output = out_value.astype(jnp.bfloat16)
    return (
        output,
        stats,
        d_hidden,
        d_per_layer,
        d_query_weight,
        d_key_weight,
        d_value_weight,
        d_output_weight,
        d_gate_weight,
        d_up_weight,
        d_down_weight,
        d_laurel_left,
        d_laurel_right,
        d_layer_gate,
        d_layer_proj,
        d_norm_gains,
        d_head_gains,
    )


def swap(array):
    return jnp.swapaxes(array, 0, 1)


def heads_body(
    hidden,
    per_layer,
    lengths,
    block_ids,
    out_grad,
    query_weight,
    key_weight,
    value_weight,
    output_weight,
    gate_weight,
    up_weight,
    down_weight,
    laurel_left,
    laurel_right,
    layer_gate,
    layer_proj,
    norm_gains,
    head_gains,
):
    low = jnp.bfloat16
    rows = hidden.shape[0]
    groups = hidden.shape[1]
    cols = lax.axis_size("col")
    seq = rows * cols
    share = cols // KV
    col_index = lax.axis_index("col")
    row_index = lax.axis_index("row")
    all_lengths = lengths
    lengths = lax.dynamic_slice_in_dim(all_lengths, row_index * groups, groups, 0)

    small = jnp.concatenate(
        [key_weight.T, value_weight.T, laurel_left.T, layer_gate.T, laurel_right, layer_proj],
        axis=0,
    )
    heights = [key_weight.shape[1], value_weight.shape[1], laurel_left.shape[1]]
    heights += [layer_gate.shape[1], laurel_right.shape[0], layer_proj.shape[0]]
    edges = [sum(heights[:i]) for i in range(len(heights) + 1)]
    unit_width = gate_weight.shape[1]
    residual = swap(hidden).astype(jnp.float32)
    normed_value, input_back = jax.vjp(input_norm, residual, norm_gains)
    normed_low = normed_value.astype(low)
    tiers = lax.axis_size("row")
    normed_all, small_row, query_full, output_full = open_all(
        normed_low, small, query_weight, output_weight, tiers, 1
    )
    small_all = share_small(small_row, heights[0] + heights[1], 8)
    both_weights = jnp.concatenate([gate_weight, up_weight], axis=1)
    paired = lax.all_gather(after(both_weights, normed_all), "row", axis=0, tiled=True)
    down_full = lax.all_gather(after(down_weight, normed_all), "row", axis=1, tiled=True)
    query_full = query_full.reshape(D, HD).T
    output_full = jnp.swapaxes(output_full, 0, 1).reshape(HD, D)
    pieces = [small_all[:, :, a:b] for a, b in zip(edges[:-1], edges[1:])]
    group_start = (col_index // share) * share

    def joined(piece):
        return jnp.swapaxes(piece, 1, 2).reshape(-1, D)

    key_full, value_full = (
        joined(lax.dynamic_slice_in_dim(piece, group_start, share, 0)) for piece in pieces[:2]
    )
    left_full, gate_layer_full, right_full, proj_layer_full = (
        joined(piece) for piece in pieces[2:]
    )
    head_weights = jnp.concatenate([query_full, key_full, value_full], axis=0)

    positions = jnp.arange(seq, dtype=jnp.int32)
    mine = col_index * rows + jnp.arange(rows, dtype=jnp.int32)
    keep_mask = (mine[None, :] < lengths[:, None]).astype(jnp.float32)[:, :, None]
    live = positions[None, :] < lengths[:, None]
    distance = positions[:, None] - positions[None, :]
    nearby = (block_ids[:, :, None] >= block_ids[:, None, :]) & (distance < WINDOW)[None]
    nearby = nearby & live[:, :, None] & live[:, None, :]
    visible = nearby | (distance == 0)[None]

    half_width = HD // 2
    frequency = jnp.exp(jnp.arange(half_width, dtype=jnp.float32) * (-2.0 * math.log(10000.0) / HD))
    angles = (positions.astype(jnp.float32)[:, None] * frequency[None, :])[None]

    def prepare(query_in, key_in, value_in, gain_rows):
        return (
            rotate(root_norm(query_in, gain_rows[0]), angles),
            rotate(root_norm(key_in, gain_rows[1]), angles),
            plain_norm(value_in),
        )

    head_raw = matmul_back(normed_all, head_weights)
    query_raw, key_raw, value_raw = jnp.split(head_raw, 3, axis=-1)
    (query_value, key_value, value_value), head_back = jax.vjp(
        prepare, query_raw, key_raw, value_raw, head_gains
    )
    query_low = query_value.astype(low)
    key_low = key_value.astype(low)
    value_low = value_value.astype(low)
    score_scale = HD ** (-0.5)

    def score_all():
        raw_scores = (
            jnp.einsum("spd,sed->spe", query_low, key_low, preferred_element_type=jnp.float32)
            * score_scale
        )
        return jnp.where(visible, raw_scores, NEGATIVE)

    scores = score_all()
    row_max = jnp.max(scores, axis=-1, keepdims=True)
    exponent = jnp.exp(scores - row_max)
    row_total = jnp.sum(exponent, axis=-1, keepdims=True)
    attn_prob = exponent / row_total
    mixed_low = jnp.einsum(
        "spe,sed->spd", attn_prob.astype(low), value_low, preferred_element_type=jnp.float32
    ).astype(low)
    out_proj = product_sum(mixed_low, output_full, False, 2)
    laurel_mid = matmul_back(normed_low, left_full).astype(low)
    low_rank = matmul_last(laurel_mid, right_full)
    (after_attention, feed_normed), middle_back = jax.vjp(
        middle, residual, out_proj, low_rank, normed_low.astype(jnp.float32), norm_gains
    )
    feed_all = spread(feed_normed.astype(low), 0)
    gate_value = matmul_last(feed_all, paired[:, :unit_width])
    up_value = matmul_last(feed_all, paired[:, unit_width:])
    units_low = gated_product(gate_value, up_value).astype(low)
    units_low, query_low, key_low, value_low, seen, head_weights = lax.optimization_barrier(
        (units_low, query_low, key_low, value_low, visible.astype(jnp.float32), head_weights)
    )
    summed = product_sum(units_low, down_full, False, 5)
    after_feed, feed_back = jax.vjp(feed_join, after_attention, summed, norm_gains)
    feed_round = after_feed.astype(low)
    layer_pre = matmul_back(feed_round, gate_layer_full)
    layer_input = swap(per_layer).astype(jnp.float32)
    layer_value, layer_back = jax.vjp(gated_product, layer_pre, layer_input)
    layer_low = layer_value.astype(low)
    projected = matmul_last(layer_low, proj_layer_full)
    out_value, final_back = jax.vjp(final_join, after_feed, projected, norm_gains)
    square_sums = jnp.stack(
        [
            jnp.sum(keep_mask * residual * residual),
            jnp.sum(keep_mask * after_attention * after_attention),
            jnp.sum(keep_mask * after_feed * after_feed),
            jnp.sum(keep_mask * out_value * out_value),
        ]
    )
    valid_count = jnp.sum(all_lengths).astype(jnp.float32)

    cotangent = swap(out_grad).astype(jnp.float32) * keep_mask
    grad_feed_out, grad_projected, gains_final = final_back(cotangent)
    projected_low = grad_projected.astype(low)
    grad_proj_layer = outer_sum(layer_low, projected_low)
    grad_layer_pre, grad_layer_input = layer_back(matmul_back(projected_low, proj_layer_full))
    layer_pre_low = grad_layer_pre.astype(low)
    grad_gate_layer = outer_sum(layer_pre_low, feed_round)
    grad_after_feed = grad_feed_out + matmul_last(layer_pre_low, gate_layer_full)
    grad_after_attention_a, grad_summed, gains_feed = feed_back(grad_after_feed)
    grad_paired, grad_down = units_back(
        grad_summed.astype(low), down_full, units_low, gate_value, up_value, 9
    )
    d_down_weight = lax.psum_scatter(grad_down, "row", scatter_dimension=1, tiled=True)
    grad_feed, grad_both = product_sum(grad_paired, paired, True, 6, feed_all)
    d_both = lax.psum_scatter(grad_both, "row", scatter_dimension=0, tiled=True)
    grad_residual_mid, grad_out_proj, grad_low_rank, grad_normed_mid, gains_middle = middle_back(
        (grad_after_attention_a, grad_feed)
    )
    grad_queries, grad_keys, grad_values, grad_output = heads_back(
        after(grad_out_proj.astype(low), d_down_weight),
        output_full,
        mixed_low,
        query_low,
        key_low,
        value_low,
        seen,
        score_scale,
        10,
    )
    low_rank_grad = grad_low_rank.astype(low)
    grad_right = outer_sum(laurel_mid, low_rank_grad)
    grad_laurel_mid = matmul_back(low_rank_grad, right_full).astype(low)
    grad_left = outer_sum(grad_laurel_mid, normed_low)
    grad_query_raw, grad_key_raw, grad_value_raw, grad_heads = head_back(
        (grad_queries, grad_keys, grad_values)
    )
    head_grads = jnp.concatenate([grad_query_raw, grad_key_raw, grad_value_raw], axis=-1)
    head_grads = head_grads.astype(low)
    grad_head_weights = outer_sum(head_grads, normed_all).astype(low)
    grad_query, grad_key, grad_value = jnp.split(grad_head_weights, 3, axis=0)
    grad_group = jnp.concatenate(
        [grad_key.reshape(share, -1, D), grad_value.reshape(share, -1, D)], axis=1
    )
    grad_rest = jnp.concatenate(
        [
            piece.astype(low).reshape(cols, -1, D)
            for piece in (grad_left, grad_gate_layer, grad_right, grad_proj_layer)
        ],
        axis=1,
    )
    half = grad_rest.shape[1] // 2
    grad_rest = jnp.swapaxes(grad_rest.reshape(cols, 2, half, D), 0, 1)
    rest_part, group_part = fold_small(grad_rest.reshape(2, cols * half, D), grad_group, 3)
    parts = jnp.concatenate(
        [grad_output, grad_query, group_part.astype(low), rest_part.astype(low).reshape(-1, D)],
        axis=0,
    )
    grad_normed = product_sum(after(head_grads, parts), head_weights, False, 7)
    parts = after(parts, d_both, grad_normed)
    parts_out = lax.psum_scatter(parts, "row", scatter_dimension=1, tiled=True).astype(jnp.float32)
    d_output_weight = parts_out[:HD]
    d_query_weight = parts_out[HD : 2 * HD].T
    small_out = parts_out[2 * HD :]
    small_parts = [small_out[a:b] for a, b in zip(edges[:-1], edges[1:])]
    grad_normed = grad_normed + grad_normed_mid + matmul_last(grad_laurel_mid, left_full)
    grad_residual_in, gains_input = input_back(grad_normed)
    d_hidden = swap((grad_residual_mid + grad_residual_in).astype(low))
    d_per_layer = swap(grad_layer_input.astype(low))
    grad_gains = gains_final + gains_feed + gains_middle + gains_input
    extra = jnp.concatenate([grad_heads.reshape(-1), square_sums])
    extra = jnp.pad(extra, (0, 2 * D - extra.shape[0])).reshape(2, D)
    all_sums = jnp.concatenate([grad_gains, extra], axis=0)
    totals = total(after(all_sums, parts), tiers, 4)
    d_down_weight = after(d_down_weight, totals).astype(jnp.float32)
    d_both = after(d_both, totals).astype(jnp.float32)
    d_gate_weight = d_both[:, :unit_width]
    d_up_weight = d_both[:, unit_width:]
    d_norm_gains = totals[:6]
    d_head_gains = totals[6, : 2 * HD].reshape(2, HD)
    total_squares = totals[6, 2 * HD : 2 * HD + 4]
    stats = jnp.sqrt(total_squares / (valid_count * D))
    output = swap(out_value.astype(low))
    return (
        output,
        stats,
        d_hidden,
        d_per_layer,
        d_query_weight,
        small_parts[0].T,
        small_parts[1].T,
        d_output_weight,
        d_gate_weight,
        d_up_weight,
        d_down_weight,
        small_parts[2].T,
        small_parts[4],
        small_parts[3].T,
        small_parts[5],
        d_norm_gains,
        d_head_gains,
    )


def solution(mesh):
    body = heads_body if mesh.shape["col"] == H else general_body
    in_specs = (
        P("col", "row", None),
        P("col", "row", None),
        P(),
        P("row", None),
        P("col", "row", None),
        P("row", "col"),
        P("row", "col"),
        P("row", "col"),
        P("col", "row"),
        P("row", "col"),
        P("row", "col"),
        P("col", "row"),
        P("row", "col"),
        P("col", "row"),
        P("row", "col"),
        P("col", "row"),
        P(),
        P(),
    )
    out_specs = (
        P("col", "row", None),
        P(),
        P("col", "row", None),
        P("col", "row", None),
        P("row", "col"),
        P("row", "col"),
        P("row", "col"),
        P("col", "row"),
        P("row", "col"),
        P("row", "col"),
        P("col", "row"),
        P("row", "col"),
        P("col", "row"),
        P("row", "col"),
        P("col", "row"),
        P(),
        P(),
    )
    return jax.shard_map(body, mesh=mesh, in_specs=in_specs, out_specs=out_specs, check_vma=False)
```

```python
import functools
import math

import jax
import jax.numpy as jnp
from jax import lax
from jax.experimental import pallas as pl
from jax.experimental.pallas import tpu as pltpu
from jax.sharding import PartitionSpec as P

D = 2048
H = 8
KV = 2
HD = 256
WINDOW = 512
BLOCK = 256


EPSILON = 1e-06
FAR_BLOCK = 1 << 30
NEGATIVE = -1e30
HALF_ROOT = 1.0 / math.sqrt(2.0)
CURVE = math.sqrt(2.0 / math.pi)
BEND = 0.044715


MESH = pl.DeviceIdType.MESH


def passed_along(value, axis, steps):
    count = lax.axis_size(axis)
    initial, last = (max(0, -steps), min(count, count - steps))
    return lax.ppermute(value, axis, [(source, source + steps) for source in range(initial, last)])


def root_norm(values, gain_row):
    return (
        values * lax.rsqrt(jnp.mean(values * values, axis=-1, keepdims=True) + EPSILON) * gain_row
    )


def plain_norm(values):
    return values * lax.rsqrt(jnp.mean(values * values, axis=-1, keepdims=True) + EPSILON)


def smooth_gate(values):
    return jax.nn.gelu(values, approximate=True)


def rotate(values, angles):
    half_width = values.shape[-1] // 2
    leading = values[..., :half_width]
    trailing = values[..., half_width:]
    cosine = jnp.cos(angles)
    sine_part = jnp.sin(angles)
    return jnp.concatenate(
        [leading * cosine - trailing * sine_part, trailing * cosine + leading * sine_part], axis=-1
    )


def matmul_last(first_array, second_array):
    return lax.dot_general(
        first_array,
        second_array,
        (((first_array.ndim - 1,), (0,)), ((), ())),
        preferred_element_type=jnp.float32,
    )


def matmul_back(first_array, second_array):
    return lax.dot_general(
        first_array,
        second_array,
        (((first_array.ndim - 1,), (1,)), ((), ())),
        preferred_element_type=jnp.float32,
    )


def outer_sum(first_array, second_array):
    return lax.dot_general(
        first_array, second_array, (((0, 1), (0, 1)), ((), ())), preferred_element_type=jnp.float32
    )


def input_norm(residual, gain_rows):
    return root_norm(residual, gain_rows[0])


def middle(residual, out_proj, low_rank, normed, gain_rows):
    merged = (
        residual + root_norm(out_proj, gain_rows[1]) + normed + root_norm(low_rank, gain_rows[4])
    ) * HALF_ROOT
    return (merged, root_norm(merged, gain_rows[2]))


def feed_join(merged, summed, gain_rows):
    return merged + root_norm(summed, gain_rows[3])


def final_join(merged, projected, gain_rows):
    return merged + root_norm(projected, gain_rows[5])


def gated_product(first_array, second_array):
    return smooth_gate(first_array) * second_array


def partners():
    c = lax.axis_index("col")
    sib = c + 1 - 2 * (c % 2)
    xn = c + 2 - 4 * ((c // 2) % 2)
    yn = c + 4 - 8 * (c // 4)
    return c, sib, xn, yn

def greet(devs):
    barrier = pltpu.get_barrier_semaphore()
    for d in devs:
        pl.semaphore_signal(barrier, inc=1, device_id={"col": d}, device_id_type=MESH)
    pl.semaphore_wait(barrier, len(devs))

def spread_kernel(rows, x_ref, o_ref, local_sem, send, recv):
    c, sib, xn, yn = partners()
    def slot(half, who):
        return o_ref.at[half, pl.ds(pl.multiple_of(who * rows, rows), rows), :]
    def both(who):
        return o_ref.at[:, pl.ds(pl.multiple_of(who * rows, rows), rows), :]
    def push(i, src, dst, dev):
        return pltpu.make_async_remote_copy(src_ref=src, dst_ref=dst, send_sem=send.at[i], recv_sem=recv.at[i], device_id={"col": dev}, device_id_type=MESH)
    mine = pltpu.make_async_copy(x_ref, both(c), local_sem)
    mine.start()
    greet((sib, xn, yn))
    x0 = push(0, x_ref.at[0], slot(0, c), xn)
    y1 = push(1, x_ref.at[1], slot(1, c), yn)
    x1 = push(2, x_ref.at[1], slot(1, c), xn)
    y0 = push(3, x_ref.at[0], slot(0, c), yn)
    s = push(4, x_ref, both(c), sib)
    x0.start(); y1.start(); x1.start(); y0.start(); s.start()
    diag = yn + (xn - c)
    x0.wait_recv()
    fy = push(5, slot(0, xn), slot(0, xn), yn)
    fy.start()
    sx0 = push(6, slot(0, xn), slot(0, xn), sib)
    sx0.start()
    y1.wait_recv()
    fx = push(7, slot(1, yn), slot(1, yn), xn)
    fx.start()
    sy1 = push(8, slot(1, yn), slot(1, yn), sib)
    sy1.start()
    x1.wait_recv()
    sx1 = push(9, slot(1, xn), slot(1, xn), sib)
    sx1.start()
    y0.wait_recv()
    sy0 = push(10, slot(0, yn), slot(0, yn), sib)
    sy0.start()
    fy.wait_recv()
    sd0 = push(11, slot(0, diag), slot(0, diag), sib)
    sd0.start()
    fx.wait_recv()
    sd1 = push(12, slot(1, diag), slot(1, diag), sib)
    sd1.start()
    for cp in (s, sx0, sy1, sx1, sy0, sd0, sd1):
        cp.wait_recv()
    for cp in (x0, y1, x1, y0, s, fy, sx0, fx, sy1, sx1, sy0, sd0, sd1):
        cp.wait_send()
    mine.wait()

def spread(x, cid=0):
    h, rows, d = x.shape
    return pl.pallas_call(
        functools.partial(spread_kernel, rows),
        out_shape=jax.ShapeDtypeStruct((h, 8 * rows, d), x.dtype),
        in_specs=[pl.BlockSpec(memory_space=pl.ANY)],
        out_specs=pl.BlockSpec(memory_space=pl.ANY),
        scratch_shapes=[pltpu.SemaphoreType.DMA, pltpu.SemaphoreType.DMA((13,)), pltpu.SemaphoreType.DMA((13,))],
        compiler_params=pltpu.CompilerParams(collective_id=cid, has_side_effects=True),
        cost_estimate=pl.CostEstimate(flops=0, bytes_accessed=120_000_000, transcendentals=0),
        name="spread",
    )(x)

def fold_steps(rows, p_ref, own, sibs, dx, dy, rx, ry, local_sem, send, recv):
    c, sib, xn, yn = partners()
    diag = yn + (xn - c)
    wide = jnp.float32
    tall = 32 if rows % 32 == 0 else 8

    def blk(who):
        return p_ref.at[:, pl.ds(pl.multiple_of(who * rows, rows), rows), :]

    def push(i, src, dst, dev):
        return pltpu.make_async_remote_copy(
            src_ref=src,
            dst_ref=dst,
            send_sem=send.at[i],
            recv_sem=recv.at[i],
            device_id={"col": dev},
            device_id_type=MESH,
        )

    def add(dst, src):
        @pl.loop(0, rows // tall)
        def _(i):
            r = pl.ds(pl.multiple_of(i * tall, tall), tall)
            dst[r, :] = (dst[r, :].astype(wide) + src[r, :].astype(wide)).astype(dst.dtype)

    def pair(j):
        add(own.at[j, 0], sibs.at[j, 0])
        add(own.at[j, 1], sibs.at[j, 1])

    dests = (diag, xn, yn, c)
    loads = [pltpu.make_async_copy(blk(d), own.at[j], local_sem.at[j]) for j, d in enumerate(dests)]
    for load in loads:
        load.start()
    yield None
    sides = [push(j, blk(d + (sib - c)), sibs.at[j], sib) for j, d in enumerate(dests)]
    for side in sides:
        side.start()
    yield None
    loads[0].wait()
    sides[0].wait_recv()
    pair(0)
    a = push(4, own.at[0, 0], dx, xn)
    b = push(5, own.at[0, 1], dy, yn)
    a.start()
    b.start()
    yield None
    loads[1].wait()
    sides[1].wait_recv()
    pair(1)
    x0 = push(6, own.at[1, 0], rx.at[0], xn)
    x0.start()
    yield None
    loads[2].wait()
    sides[2].wait_recv()
    pair(2)
    y1 = push(7, own.at[2, 1], ry.at[1], yn)
    y1.start()
    yield None
    a.wait_recv()
    add(own.at[2, 0], dx)
    y0 = push(8, own.at[2, 0], ry.at[0], yn)
    y0.start()
    yield None
    b.wait_recv()
    add(own.at[1, 1], dy)
    x1 = push(9, own.at[1, 1], rx.at[1], xn)
    x1.start()
    yield None
    loads[3].wait()
    sides[3].wait_recv()
    pair(3)
    yield None
    waits = ((x0, y0), (x1, y1))
    yield tall, waits, (*sides, a, b, x0, y1, y0, x1)


def fold_finish(rows, o_ref, own, rx, ry, tall, waits, sent):
    wide = jnp.float32
    for h in range(2):
        for copy in waits[h]:
            copy.wait_recv()

        @pl.loop(0, rows // tall)
        def _(i):
            r = pl.ds(pl.multiple_of(i * tall, tall), tall)
            o_ref[h, r, :] = (
                own[3, h, r, :].astype(wide) + rx[h, r, :].astype(wide) + ry[h, r, :].astype(wide)
            )

    for copy in sent:
        copy.wait_send()


def fold_scratch(h, rows, d, kind):
    return [
        pltpu.VMEM((4, h, rows, d), kind),
        pltpu.VMEM((4, h, rows, d), kind),
        pltpu.VMEM((rows, d), kind),
        pltpu.VMEM((rows, d), kind),
        pltpu.VMEM((h, rows, d), kind),
        pltpu.VMEM((h, rows, d), kind),
        pltpu.SemaphoreType.DMA((4,)),
        pltpu.SemaphoreType.DMA((10,)),
        pltpu.SemaphoreType.DMA((10,)),
    ]


def product_kernel(rows, flip, outer, *refs):
    if outer:
        a_ref, w_ref, f_ref, o_ref, g_ref = refs[:5]
        f_buf, g_buf, turned, f_sem, g_sem = refs[-5:]
        refs = refs[5:-5]
    else:
        a_ref, w_ref, o_ref = refs[:3]
        refs = refs[3:]
    a_buf, w_buf, stage, own, sibs, dx, dy, rx, ry, local_sem, send, recv = refs
    c, sib, xn, yn = partners()
    diag = yn + (xn - c)
    wide = jnp.float32
    d = o_ref.shape[-1]
    tile = 512
    tall = 32

    def push(i, src, dst, dev):
        return pltpu.make_async_remote_copy(
            src_ref=src,
            dst_ref=dst,
            send_sem=send.at[i],
            recv_sem=recv.at[i],
            device_id={"col": dev},
            device_id_type=MESH,
        )

    dests = (diag, xn, yn, c)
    step = sib - c
    weights = pltpu.make_async_copy(w_ref, w_buf, local_sem.at[8])
    weights.start()

    def load(i, who):
        return pltpu.make_async_copy(
            a_ref.at[:, pl.ds(pl.multiple_of(who * rows, rows), rows), :],
            a_buf.at[i],
            local_sem.at[i],
        )

    far = [load(j, dests[j] + step) for j in range(4)]
    near = [load(4 + j, dests[j]) for j in range(4)]
    for first, second in zip(far, near):
        first.start()
        second.start()
    owners = [d + step for d in dests] + list(dests)
    strip = 256

    def strips(n):
        cut = pl.ds(pl.multiple_of(n * strip, strip), strip)
        return [
            pltpu.make_async_copy(
                f_ref.at[:, pl.ds(pl.multiple_of(who * rows, rows), rows), cut],
                f_buf.at[lax.rem(n, 2), i],
                f_sem.at[lax.rem(n, 2), i],
            )
            for i, who in enumerate(owners)
        ]

    def strip_out(n):
        cut = pl.ds(pl.multiple_of(n * strip, strip), strip)
        slot = lax.rem(n, 2)
        return pltpu.make_async_copy(g_buf.at[slot], g_ref.at[cut, :], g_sem.at[slot])

    def outer_product():
        count = g_ref.shape[0] // strip
        depth = a_buf.shape[-1]

        @pl.loop(0, count)
        def _(n):
            slot = lax.rem(n, 2)
            for copy in strips(n):
                copy.wait()

            @pl.when(n + 1 < count)
            def _():
                for copy in strips(n + 1):
                    copy.start()

            @pl.when(n >= 2)
            def _():
                strip_out(n - 2).wait()

            turned[...] = f_buf[slot].reshape(16 * rows, strip).T

            @pl.loop(0, depth // tile)
            def _(m):
                cut = pl.ds(pl.multiple_of(m * tile, tile), tile)
                right = a_buf[:, :, :, cut].reshape(16 * rows, tile)
                value = jnp.dot(turned[...], right, preferred_element_type=wide)
                g_buf[slot, :, cut] = value.astype(g_buf.dtype)

            strip_out(n).start()

        strip_out(count - 2).wait()
        strip_out(count - 1).wait()

    if outer:
        for copy in strips(0):
            copy.start()
    greet((sib, xn, yn))
    weights.wait()

    def product(i, put):
        left = a_buf[i].reshape(2 * rows, a_buf.shape[-1])

        @pl.loop(0, d // tile)
        def _(n):
            cut = pl.ds(pl.multiple_of(n * tile, tile), tile)
            right = w_buf[cut, :] if flip else w_buf[:, cut]
            dims = (((1,), (1,)), ((), ())) if flip else (((1,), (0,)), ((), ()))
            value = lax.dot_general(left, right, dims, preferred_element_type=wide)
            put(cut, value.reshape(2, rows, tile))

    sides = [push(j, stage.at[j], sibs.at[j], sib) for j in range(4)]

    def for_sibling(j):
        far[j].wait()

        def put(cut, value):
            stage[j, :, :, cut] = value.astype(stage.dtype)

        product(j, put)
        sides[j].start()

    def for_chip(j):
        near[j].wait()
        sides[j].wait_recv()

        def put(cut, value):
            own[j, :, :, cut] = (value + sibs[j, :, :, cut].astype(wide)).astype(own.dtype)

        product(4 + j, put)

    def add(dst, src):
        @pl.loop(0, rows // tall)
        def _(i):
            r = pl.ds(pl.multiple_of(i * tall, tall), tall)
            dst[r, :] = (dst[r, :].astype(wide) + src[r, :].astype(wide)).astype(dst.dtype)

    for_sibling(0)
    near[0].wait()

    def hold(cut, value):
        o_ref[:, :, cut] = value

    product(4, hold)
    sides[0].wait_recv()
    for h in range(2):

        @pl.loop(0, rows // tall)
        def _(i):
            r = pl.ds(pl.multiple_of(i * tall, tall), tall)
            own[0, h, r, :] = (o_ref[h, r, :] + sibs[0, h, r, :].astype(wide)).astype(own.dtype)

    a = push(4, own.at[0, 0], dx, xn)
    b = push(5, own.at[0, 1], dy, yn)
    a.start()
    b.start()
    for_sibling(1)
    for_sibling(2)
    for_chip(1)
    x0 = push(6, own.at[1, 0], rx.at[0], xn)
    x0.start()
    for_sibling(3)
    for_chip(2)
    y1 = push(7, own.at[2, 1], ry.at[1], yn)
    y1.start()
    a.wait_recv()
    add(own.at[2, 0], dx)
    y0 = push(8, own.at[2, 0], ry.at[0], yn)
    y0.start()
    b.wait_recv()
    add(own.at[1, 1], dy)
    x1 = push(9, own.at[1, 1], rx.at[1], xn)
    x1.start()
    near[3].wait()
    sides[3].wait_recv()

    def put(cut, value):
        o_ref[:, :, cut] = value + sibs[3, :, :, cut].astype(wide)

    product(7, put)
    if outer:
        outer_product()
    for h, waits in enumerate(((x0, y0), (x1, y1))):
        for copy in waits:
            copy.wait_recv()

        @pl.loop(0, rows // tall)
        def _(i):
            r = pl.ds(pl.multiple_of(i * tall, tall), tall)
            o_ref[h, r, :] = o_ref[h, r, :] + rx[h, r, :].astype(wide) + ry[h, r, :].astype(wide)

    for copy in (*sides, a, b, x0, y1, y0, x1):
        copy.wait_send()


def product_sum(left, right, flip, cid, feed=None):
    h, total, depth = left.shape
    rows = total // 8
    d = right.shape[0] if flip else right.shape[1]
    low = left.dtype
    outer = feed is not None
    out_shape = [jax.ShapeDtypeStruct((h, rows, d), jnp.float32)]
    out_specs = [pl.BlockSpec(memory_space=pltpu.VMEM)]
    scratch = [
        pltpu.VMEM((8, h, rows, depth), low),
        pltpu.VMEM(right.shape, low),
        pltpu.VMEM((4, h, rows, d), low),
        pltpu.VMEM((3, h, rows, d), low),
        pltpu.VMEM((4, h, rows, d), low),
        pltpu.VMEM((rows, d), low),
        pltpu.VMEM((rows, d), low),
        pltpu.VMEM((h, rows, d), low),
        pltpu.VMEM((h, rows, d), low),
        pltpu.SemaphoreType.DMA((9,)),
        pltpu.SemaphoreType.DMA((10,)),
        pltpu.SemaphoreType.DMA((10,)),
    ]
    flops = 2 * h * total * depth * d
    if outer:
        width = feed.shape[-1]
        flops += 2 * h * total * depth * width
        out_shape.append(jax.ShapeDtypeStruct((width, depth), low))
        out_specs.append(pl.BlockSpec(memory_space=pl.ANY))
        scratch += [
            pltpu.VMEM((2, 8, h, rows, 256), low),
            pltpu.VMEM((2, 256, depth), low),
            pltpu.VMEM((256, h * total), low),
            pltpu.SemaphoreType.DMA((2, 8)),
            pltpu.SemaphoreType.DMA((2,)),
        ]
    result = pl.pallas_call(
        functools.partial(product_kernel, rows, flip, outer),
        out_shape=out_shape,
        in_specs=[pl.BlockSpec(memory_space=pl.ANY)] * (3 if outer else 2),
        out_specs=out_specs,
        scratch_shapes=scratch,
        compiler_params=pltpu.CompilerParams(
            collective_id=cid,
            has_side_effects=True,
            vmem_limit_bytes=(52 if outer else 60) << 20,
        ),
        cost_estimate=pl.CostEstimate(
            flops=flops, bytes_accessed=130_000_000, transcendentals=0
        ),
        name="product_sum",
    )(*((left, right, feed) if outer else (left, right)))
    return result if outer else result[0]


def fold_small_kernel(
    rows, p_ref, g_ref, o_ref, k_ref, own, sibs, dx, dy, rx, ry, local_sem, send, recv,
    gown, gsibs, grx, glocal, gsend, grecv,
):
    c, sib, xn, yn = partners()
    m = c % 4
    m_sib = m + 1 - 2 * (m % 2)
    m_x = m + 2 - 4 * (m // 2)
    m_diag = m_sib + (m_x - m)
    wide = jnp.float32

    def push(i, src, dst, dev):
        return pltpu.make_async_remote_copy(
            src_ref=src,
            dst_ref=dst,
            send_sem=gsend.at[i],
            recv_sem=grecv.at[i],
            device_id={"col": dev},
            device_id_type=MESH,
        )

    steps = fold_steps(rows, p_ref, own, sibs, dx, dy, rx, ry, local_sem, send, recv)
    next(steps)
    loads = [
        pltpu.make_async_copy(g_ref.at[d], gown.at[j], glocal.at[j])
        for j, d in enumerate((m_x, m))
    ]
    for load in loads:
        load.start()
    greet((sib, xn, yn))
    sides = [push(j, g_ref.at[d], gsibs.at[j], sib) for j, d in enumerate((m_diag, m_sib))]
    sides[0].start()
    next(steps)
    sides[1].start()
    tall = k_ref.shape[0] // 4
    loads[0].wait()
    sides[0].wait_recv()

    @pl.loop(0, 4)
    def _(i):
        r = pl.ds(pl.multiple_of(i * tall, tall), tall)
        gown[0, r, :] = (gown[0, r, :].astype(wide) + gsibs[0, r, :].astype(wide)).astype(
            gown.dtype
        )

    over = push(2, gown.at[0], grx, xn)
    over.start()
    last = None
    for step in steps:
        last = step if step is not None else last
    fold_finish(rows, o_ref, own, rx, ry, *last)
    loads[1].wait()
    sides[1].wait_recv()
    over.wait_recv()

    @pl.loop(0, 4)
    def _(i):
        r = pl.ds(pl.multiple_of(i * tall, tall), tall)
        k_ref[r, :] = (
            gown[1, r, :].astype(wide) + gsibs[1, r, :].astype(wide) + grx[r, :].astype(wide)
        )

    for copy in (*sides, over):
        copy.wait_send()


def fold_small(p, g, cid):
    h, total, d = p.shape
    rows = total // 8
    share, tall, _ = g.shape
    return pl.pallas_call(
        functools.partial(fold_small_kernel, rows),
        out_shape=(
            jax.ShapeDtypeStruct((h, rows, d), jnp.float32),
            jax.ShapeDtypeStruct((tall, d), jnp.float32),
        ),
        in_specs=[pl.BlockSpec(memory_space=pl.ANY)] * 2,
        out_specs=[pl.BlockSpec(memory_space=pltpu.VMEM)] * 2,
        scratch_shapes=fold_scratch(h, rows, d, p.dtype)
        + [
            pltpu.VMEM((2, tall, d), g.dtype),
            pltpu.VMEM((2, tall, d), g.dtype),
            pltpu.VMEM((tall, d), g.dtype),
            pltpu.SemaphoreType.DMA((2,)),
            pltpu.SemaphoreType.DMA((3,)),
            pltpu.SemaphoreType.DMA((3,)),
        ],
        compiler_params=pltpu.CompilerParams(
            collective_id=cid, has_side_effects=True, vmem_limit_bytes=40 << 20
        ),
        cost_estimate=pl.CostEstimate(flops=0, bytes_accessed=60_000_000, transcendentals=0),
        name="fold_small",
    )(p, g)


def open_kernel(
    rows, tiers, x_ref, q_ref, w_ref, g_ref, u_ref, *refs
):
    small = refs[:5]
    o_ref, sa_ref, qa_ref, wa_ref, both_ref = refs[5:10]
    tokens, stacked, both_buf, in_sem, local_sem, send, recv, line_send, line_recv = refs[10:]
    c, sib, xn, yn = partners()
    diag = yn + (xn - c)
    r = lax.axis_index("row")
    last = tiers - 1
    weights = []
    for src, dst in ((stacked, sa_ref), (q_ref, qa_ref), (w_ref, wa_ref)):
        cut = src.shape[0] // 32 * 16
        weights += [(src, dst, pl.ds(0, cut)), (src, dst, pl.ds(cut, src.shape[0] - cut))]
    pieces = len(weights)

    def slot(half, who):
        return o_ref.at[half, pl.ds(pl.multiple_of(who * rows, rows), rows), :]

    def both(who):
        return o_ref.at[:, pl.ds(pl.multiple_of(who * rows, rows), rows), :]

    started = []

    def push(src, dst, **dev):
        i = len(started)
        copy = pltpu.make_async_remote_copy(
            src_ref=src,
            dst_ref=dst,
            send_sem=send.at[i],
            recv_sem=recv.at[i],
            device_id=dev,
            device_id_type=MESH,
        )
        copy.start()
        started.append(copy)
        return copy

    width = g_ref.shape[1]
    first = [pltpu.make_async_copy(x_ref, tokens, in_sem.at[0])]
    base = 0
    for i, ref in enumerate(small):
        tall = ref.shape[0]
        first.append(
            pltpu.make_async_copy(ref, stacked.at[pl.ds(base, tall)], in_sem.at[1 + i])
        )
        base += tall
    later = [
        pltpu.make_async_copy(g_ref, both_buf.at[:, pl.ds(0, width)], in_sem.at[6]),
        pltpu.make_async_copy(u_ref, both_buf.at[:, pl.ds(width, width)], in_sem.at[7]),
    ]
    for copy in (*first, *later):
        copy.start()
    local = [
        pltpu.make_async_copy(tokens, both(c), local_sem.at[0]),
        pltpu.make_async_copy(stacked, sa_ref.at[r], local_sem.at[1]),
        pltpu.make_async_copy(q_ref, qa_ref.at[r], local_sem.at[2]),
        pltpu.make_async_copy(w_ref, wa_ref.at[r], local_sem.at[3]),
        pltpu.make_async_copy(both_buf, both_ref, local_sem.at[4]),
    ]
    barrier = pltpu.get_barrier_semaphore()
    for d in (sib, xn, yn):
        pl.semaphore_signal(barrier, inc=1, device_id={"col": d}, device_id_type=MESH)

    @pl.when(r < last)
    def _():
        pl.semaphore_signal(barrier, inc=1, device_id={"row": r + 1}, device_id_type=MESH)

    @pl.when(r > 0)
    def _():
        pl.semaphore_signal(barrier, inc=1, device_id={"row": r - 1}, device_id_type=MESH)

    @pl.when((r > 0) & (r < last))
    def _():
        pl.semaphore_wait(barrier, 5)

    @pl.when((r == 0) | (r == last))
    def _():
        pl.semaphore_wait(barrier, 4)

    def passing(way, hop, j):
        src, dst, cut = weights[j]
        whose = r - hop if way == 0 else r + hop
        return pltpu.make_async_remote_copy(
            src_ref=src.at[cut] if hop == 0 else dst.at[whose, cut],
            dst_ref=dst.at[whose, cut],
            send_sem=line_send.at[way, hop, j],
            recv_sem=line_recv.at[way, hop, j],
            device_id={"row": r + 1 if way == 0 else r - 1},
            device_id_type=MESH,
        )

    def going(way, hop):
        return (r < last) & (r >= hop) if way == 0 else (r > 0) & (r + hop <= last)

    def coming(way, hop):
        return r > hop if way == 0 else r + hop < last

    def forward(hop, j):
        for way in range(2):
            if hop > 0:

                @pl.when(coming(way, hop - 1))
                def _():
                    passing(way, hop - 1, j).wait_recv()

            @pl.when(going(way, hop))
            def _():
                passing(way, hop, j).start()

    for copy in first:
        copy.wait()
    x0 = push(tokens.at[0], slot(0, c), col=xn)
    y1 = push(tokens.at[1], slot(1, c), col=yn)
    for j in range(pieces):
        forward(0, j)
    x1 = push(tokens.at[1], slot(1, c), col=xn)
    y0 = push(tokens.at[0], slot(0, c), col=yn)
    push(tokens, both(c), col=sib)
    for copy in later:
        copy.wait()
    for copy in local:
        copy.start()
    forward(1, 0)
    forward(1, 1)
    x0.wait_recv()
    fy = push(slot(0, xn), slot(0, xn), col=yn)
    push(slot(0, xn), slot(0, xn), col=sib)
    y1.wait_recv()
    fx = push(slot(1, yn), slot(1, yn), col=xn)
    push(slot(1, yn), slot(1, yn), col=sib)
    for j in range(2, pieces):
        forward(1, j)
    x1.wait_recv()
    push(slot(1, xn), slot(1, xn), col=sib)
    y0.wait_recv()
    push(slot(0, yn), slot(0, yn), col=sib)
    for hop in range(2, last):
        for j in range(pieces):
            forward(hop, j)
    fy.wait_recv()
    push(slot(0, diag), slot(0, diag), col=sib)
    fx.wait_recv()
    push(slot(1, diag), slot(1, diag), col=sib)
    for copy in started:
        if not any(copy is other for other in (x0, y1, x1, y0, fy, fx)):
            copy.wait_recv()
    for j in range(pieces):
        for way in range(2):

            @pl.when(coming(way, last - 1))
            def _():
                passing(way, last - 1, j).wait_recv()

            for hop in range(last):

                @pl.when(going(way, hop))
                def _():
                    passing(way, hop, j).wait_send()

    for copy in started:
        copy.wait_send()
    for copy in local:
        copy.wait()


def open_all(x, query, output, gate, up, small, tiers, cid):
    h, rows, d = x.shape
    low = x.dtype
    stack = (sum(piece.shape[0] for piece in small), small[0].shape[1])
    both = (gate.shape[0], 2 * gate.shape[1])
    return pl.pallas_call(
        functools.partial(open_kernel, rows, tiers),
        out_shape=(
            jax.ShapeDtypeStruct((h, 8 * rows, d), low),
            jax.ShapeDtypeStruct((tiers, *stack), low),
            jax.ShapeDtypeStruct((tiers, *query.shape), low),
            jax.ShapeDtypeStruct((tiers, *output.shape), low),
            jax.ShapeDtypeStruct(both, low),
        ),
        in_specs=[pl.BlockSpec(memory_space=pl.ANY)] * 10,
        out_specs=[pl.BlockSpec(memory_space=pl.ANY)] * 5,
        scratch_shapes=[
            pltpu.VMEM(x.shape, low),
            pltpu.VMEM(stack, low),
            pltpu.VMEM(both, low),
            pltpu.SemaphoreType.DMA((8,)),
            pltpu.SemaphoreType.DMA((5,)),
            pltpu.SemaphoreType.DMA((13,)),
            pltpu.SemaphoreType.DMA((13,)),
            pltpu.SemaphoreType.DMA((2, tiers - 1, 6)),
            pltpu.SemaphoreType.DMA((2, tiers - 1, 6)),
        ],
        compiler_params=pltpu.CompilerParams(
            collective_id=cid, has_side_effects=True, vmem_limit_bytes=16 << 20
        ),
        cost_estimate=pl.CostEstimate(flops=0, bytes_accessed=200_000_000, transcendentals=0),
        name="open_all",
    )(x, query, output, gate, up, *small)


def share_kernel(near, s_ref, sa_ref, held, local_sem, send, recv):
    c, sib, xn, yn = partners()
    diag = yn + (xn - c)
    height = s_ref.shape[1]
    started = []

    def part(ref, first):
        return ref.at[:, pl.ds(0, near) if first else pl.ds(near, height - near), :]

    def push(who, first, dev, own=False):
        i = len(started)
        dst = part(sa_ref.at[who], first)
        copy = pltpu.make_async_remote_copy(
            src_ref=part(held, first) if own else dst,
            dst_ref=dst,
            send_sem=send.at[i],
            recv_sem=recv.at[i],
            device_id={"col": dev},
            device_id_type=MESH,
        )
        copy.start()
        started.append(copy)
        return copy

    fetch = pltpu.make_async_copy(s_ref, held, local_sem.at[0])
    fetch.start()
    mine = pltpu.make_async_copy(held, sa_ref.at[c], local_sem.at[1])
    greet((sib, xn, yn))
    fetch.wait()
    rx = push(c, False, xn, own=True)
    ry = push(c, False, yn, own=True)
    kx = push(c, True, xn, own=True)
    push(c, True, sib, own=True)
    push(c, False, sib, own=True)
    mine.start()
    rx.wait_recv()
    fd = push(xn, False, yn)
    push(xn, False, sib)
    ry.wait_recv()
    push(yn, False, sib)
    fd.wait_recv()
    push(diag, False, sib)
    kx.wait_recv()
    push(xn, True, sib)
    for copy in started:
        if not any(copy is other for other in (kx, rx, ry, fd)):
            copy.wait_recv()
    for copy in started:
        copy.wait_send()
    mine.wait()


def share_small(small, near, cid):
    return pl.pallas_call(
        functools.partial(share_kernel, near),
        out_shape=jax.ShapeDtypeStruct((8, *small.shape), small.dtype),
        in_specs=[pl.BlockSpec(memory_space=pl.ANY)],
        out_specs=pl.BlockSpec(memory_space=pl.ANY),
        scratch_shapes=[
            pltpu.VMEM(small.shape, small.dtype),
            pltpu.SemaphoreType.DMA((2,)),
            pltpu.SemaphoreType.DMA((10,)),
            pltpu.SemaphoreType.DMA((10,)),
        ],
        compiler_params=pltpu.CompilerParams(collective_id=cid, has_side_effects=True),
        cost_estimate=pl.CostEstimate(flops=0, bytes_accessed=60_000_000, transcendentals=0),
        name="share_small",
    )(small)


def rounds_of(rows, x_ref, held, local_sem, send, recv, consume, prepare):
    c, sib, xn, yn = partners()
    diag = yn + (xn - c)
    step = sib - c

    def place(t, j, n=1):
        return held.at[t, pl.ds(j * rows, n * rows), :]

    started = []

    def push(src, dst, dev):
        i = len(started)
        copy = pltpu.make_async_remote_copy(
            src_ref=src,
            dst_ref=dst,
            send_sem=send.at[i],
            recv_sem=recv.at[i],
            device_id={"col": dev},
            device_id_type=MESH,
        )
        copy.start()
        started.append(copy)
        return copy

    mine = [pltpu.make_async_copy(x_ref.at[h], place(0, h), local_sem.at[h]) for h in range(2)]
    for copy in mine:
        copy.start()
    greet((sib, xn, yn))
    x0 = push(x_ref.at[0], place(1, 0), xn)
    y1 = push(x_ref.at[1], place(1, 1), yn)
    x1 = push(x_ref.at[1], place(2, 0), xn)
    y0 = push(x_ref.at[0], place(2, 1), yn)
    s0 = push(x_ref.at[0], place(0, 2), sib)
    s1 = push(x_ref.at[1], place(0, 3), sib)
    prepare(0)
    for copy in mine:
        copy.wait()
    s0.wait_recv()
    s1.wait_recv()
    consume(0, 0, ((0, c), (1, c), (0, sib), (1, sib)))
    x0.wait_recv()
    fy = push(place(1, 0), place(3, 0), yn)
    y1.wait_recv()
    fx = push(place(1, 1), place(3, 1), xn)
    prepare(1)
    t1 = push(place(1, 0, 2), place(1, 2, 2), sib)
    t1.wait_recv()
    consume(1, 0, ((0, xn), (1, yn), (0, xn + step), (1, yn + step)))
    prepare(2)
    x1.wait_recv()
    y0.wait_recv()
    t2 = push(place(2, 0, 2), place(2, 2, 2), sib)
    t2.wait_recv()
    consume(2, 0, ((1, xn), (0, yn), (1, xn + step), (0, yn + step)))
    prepare(3)
    fy.wait_recv()
    fx.wait_recv()
    t3 = push(place(3, 0, 2), place(3, 2, 2), sib)
    consume(3, 0, ((0, diag), (1, diag)))
    t3.wait_recv()
    consume(3, 2, ((0, diag + step), (1, diag + step)))
    for copy in started:
        copy.wait_send()


def piece_at(ref, rows, piece):
    half, who = piece
    return ref.at[half, pl.ds(pl.multiple_of(who * rows, rows), rows), :]


def units_back_kernel(
    rows, x_ref, w_ref, u_ref, g_ref, v_ref, p_ref, d_ref,
    held, weights, units, turned, gates, ups, grads, total_ref,
    weight_sem, load_sem, store_sem, local_sem, send, recv,
):
    c, sib, xn, yn = partners()
    diag = yn + (xn - c)
    step = sib - c
    wide = jnp.float32
    width = w_ref.shape[0]
    d = w_ref.shape[1]
    plan = (
        ((0, c), (1, c), (0, sib), (1, sib)),
        ((0, xn), (1, yn), (0, xn + step), (1, yn + step)),
        ((1, xn), (0, yn), (1, xn + step), (0, yn + step)),
        ((0, diag), (1, diag), (0, diag + step), (1, diag + step)),
    )
    fetch = pltpu.make_async_copy(w_ref, weights, weight_sem)
    fetch.start()

    def loads(t):
        copies = []
        for j, piece in enumerate(plan[t]):
            for k, (src, dst) in enumerate(((u_ref, units), (g_ref, gates), (v_ref, ups))):
                copies.append(
                    pltpu.make_async_copy(
                        piece_at(src, rows, piece),
                        dst.at[t % 2, pl.ds(j * rows, rows), :],
                        load_sem.at[t % 2, j, k],
                    )
                )
        return copies

    def stores(t, first=0, count=4):
        return [
            pltpu.make_async_copy(
                grads.at[t % 2, pl.ds(j * rows, rows), :],
                piece_at(p_ref, rows, plan[t][j]),
                store_sem.at[t % 2, j],
            )
            for j in range(first, first + count)
        ]

    for copy in loads(0):
        copy.start()

    tile = 256

    def prepare(t):
        if t == 0:
            fetch.wait()
        if t < 3:
            for copy in loads(t + 1):
                copy.start()
        for copy in loads(t):
            copy.wait()

        @pl.loop(0, width // tile)
        def _(n):
            cut = pl.ds(pl.multiple_of(n * tile, tile), tile)
            gate = gates[t % 2, :, cut]
            square = gate * gate
            bent = jnp.tanh(CURVE * (gate + BEND * gate * square))
            rise = 0.5 * (1.0 + bent)
            slope = rise + (0.5 * CURVE) * gate * (1.0 - bent * bent) * (1.0 + 3.0 * BEND * square)
            gates[t % 2, :, cut] = ups[t % 2, :, cut] * slope
            ups[t % 2, :, cut] = gate * rise
            turned[cut, :] = units[t % 2, :, cut].T

    def consume(t, first, pieces):
        if t >= 2 and first == 0:
            for copy in stores(t - 2):
                copy.wait()
        span = slice(first * rows, (first + len(pieces)) * rows)

        @pl.loop(0, width // 512)
        def _(n):
            cut = pl.ds(pl.multiple_of(n * 512, 512), 512)
            grad = lax.dot_general(
                held[t, span, :],
                weights[cut, :],
                (((1,), (1,)), ((), ())),
                preferred_element_type=wide,
            )
            grads[t % 2, span, cut] = (grad * gates[t % 2, span, cut]).astype(grads.dtype)
            cut_up = pl.ds(pl.multiple_of(width + n * 512, 512), 512)
            grads[t % 2, span, cut_up] = (grad * ups[t % 2, span, cut]).astype(grads.dtype)

        for copy in stores(t, first, len(pieces)):
            copy.start()

        @pl.loop(0, d // 512)
        def _(n):
            cut = pl.ds(pl.multiple_of(n * 512, 512), 512)
            value = jnp.dot(turned[:, span], held[t, span, cut], preferred_element_type=wide)
            if t > 0:
                value = value + total_ref[:, cut]
            if first == 0:
                total_ref[:, cut] = value
            else:
                d_ref[:, cut] = value.astype(d_ref.dtype)

    rounds_of(rows, x_ref, held, local_sem, send, recv, consume, prepare)
    for copy in (*stores(2), *stores(3)):
        copy.wait()


def units_back(x, down, units, gate, up, cid):
    h, rows, d = x.shape
    width = down.shape[0]
    low = x.dtype
    return pl.pallas_call(
        functools.partial(units_back_kernel, rows),
        out_shape=(
            jax.ShapeDtypeStruct((h, 8 * rows, 2 * width), low),
            jax.ShapeDtypeStruct((width, d), low),
        ),
        in_specs=[pl.BlockSpec(memory_space=pl.ANY)] * 5,
        out_specs=[
            pl.BlockSpec(memory_space=pl.ANY),
            pl.BlockSpec(memory_space=pltpu.VMEM),
        ],
        scratch_shapes=[
            pltpu.VMEM((4, 4 * rows, d), low),
            pltpu.VMEM((width, d), low),
            pltpu.VMEM((2, 4 * rows, width), low),
            pltpu.VMEM((width, 4 * rows), low),
            pltpu.VMEM((2, 4 * rows, width), jnp.float32),
            pltpu.VMEM((2, 4 * rows, width), jnp.float32),
            pltpu.VMEM((2, 4 * rows, 2 * width), low),
            pltpu.VMEM((width, d), jnp.float32),
            pltpu.SemaphoreType.DMA,
            pltpu.SemaphoreType.DMA((2, 4, 3)),
            pltpu.SemaphoreType.DMA((2, 4)),
            pltpu.SemaphoreType.DMA((2,)),
            pltpu.SemaphoreType.DMA((11,)),
            pltpu.SemaphoreType.DMA((11,)),
        ],
        compiler_params=pltpu.CompilerParams(
            collective_id=cid, has_side_effects=True, vmem_limit_bytes=52 << 20
        ),
        cost_estimate=pl.CostEstimate(
            flops=64 * h * rows * width * d, bytes_accessed=130_000_000, transcendentals=0
        ),
        name="units_back",
    )(x, down, units, gate, up)


def heads_back_kernel(
    rows, scale, x_ref, w_ref, m_ref, q_ref, k_ref, v_ref, s_ref, gq_ref, gk_ref, gv_ref, d_ref,
    held, weights, mixed, queries, keys, values, seen, total_ref, load_sem, local_sem, send, recv,
):
    wide = jnp.float32
    d = w_ref.shape[1]
    low = weights.dtype
    pairs = (
        (w_ref, weights), (q_ref, queries), (k_ref, keys), (v_ref, values), (s_ref, seen),
        (m_ref, mixed),
    )
    loads = [
        pltpu.make_async_copy(src, dst, load_sem.at[i]) for i, (src, dst) in enumerate(pairs)
    ]
    for copy in loads:
        copy.start()
    back = (((1,), (1,)), ((), ()))

    def prepare(t):
        if t == 0:
            for copy in loads:
                copy.wait()
            gk_ref[...] = jnp.zeros_like(gk_ref)
            gv_ref[...] = jnp.zeros_like(gv_ref)

    def consume(t, first, pieces):
        part = slice(first * rows, (first + len(pieces)) * rows)
        grad_mixed = lax.dot_general(
            held[t, part, :], weights[...], back, preferred_element_type=wide
        )
        grad_mixed = grad_mixed.astype(low)
        spans = []
        for j, (half, who) in enumerate(pieces):
            span = pl.ds(pl.multiple_of(who * rows, rows), rows)
            spans.append(mixed[half, span, :])
            query = queries[half, span, :]
            grad = grad_mixed[j * rows : (j + 1) * rows]
            score = lax.dot_general(query, keys[half], back, preferred_element_type=wide) * scale
            score = jnp.where(seen[half, span, :] > 0, score, NEGATIVE)
            power = jnp.exp(score - jnp.max(score, axis=-1, keepdims=True))
            prob = power / jnp.sum(power, axis=-1, keepdims=True)
            slope = lax.dot_general(grad, values[half], back, preferred_element_type=wide)
            mean = jnp.sum(prob * slope, axis=-1, keepdims=True)
            flow = (prob * (slope - mean)).astype(low)
            gq_ref[half, span, :] = jnp.dot(flow, keys[half], preferred_element_type=wide) * scale
            gk_ref[half] += jnp.dot(flow.T, query, preferred_element_type=wide) * scale
            gv_ref[half] += jnp.dot(prob.astype(low).T, grad, preferred_element_type=wide)
        turned = jnp.concatenate(spans, axis=0).T

        @pl.loop(0, d // 512)
        def _(n):
            cut = pl.ds(pl.multiple_of(n * 512, 512), 512)
            value = jnp.dot(turned, held[t, part, cut], preferred_element_type=wide)
            if t > 0:
                value = value + total_ref[:, cut]
            if first == 0:
                total_ref[:, cut] = value
            else:
                d_ref[:, cut] = value.astype(d_ref.dtype)

    rounds_of(rows, x_ref, held, local_sem, send, recv, consume, prepare)


def heads_back(x, output, mixed, query, key, value, visible, scale, cid):
    h, rows, d = x.shape
    low = x.dtype
    grad = jax.ShapeDtypeStruct(query.shape, jnp.float32)
    return pl.pallas_call(
        functools.partial(heads_back_kernel, rows, scale),
        out_shape=(grad, grad, grad, jax.ShapeDtypeStruct(output.shape, low)),
        in_specs=[pl.BlockSpec(memory_space=pl.ANY)] * 7,
        out_specs=[pl.BlockSpec(memory_space=pltpu.VMEM)] * 4,
        scratch_shapes=[
            pltpu.VMEM((4, 4 * rows, d), low),
            pltpu.VMEM(output.shape, low),
            pltpu.VMEM(mixed.shape, low),
            pltpu.VMEM(query.shape, low),
            pltpu.VMEM(query.shape, low),
            pltpu.VMEM(query.shape, low),
            pltpu.VMEM(visible.shape, visible.dtype),
            pltpu.VMEM(output.shape, jnp.float32),
            pltpu.SemaphoreType.DMA((6,)),
            pltpu.SemaphoreType.DMA((2,)),
            pltpu.SemaphoreType.DMA((11,)),
            pltpu.SemaphoreType.DMA((11,)),
        ],
        compiler_params=pltpu.CompilerParams(
            collective_id=cid, has_side_effects=True, vmem_limit_bytes=60 << 20
        ),
        cost_estimate=pl.CostEstimate(
            flops=20_000_000_000, bytes_accessed=130_000_000, transcendentals=0
        ),
        name="heads_back",
    )(x, output, mixed, query, key, value, visible)


def total_kernel(x_ref, o_ref, sums, got, tier_sums, send, recv):
    c, sib, xn, yn = partners()
    r = lax.axis_index("row")
    tiers = lax.axis_size("row")
    others = [lax.rem(r + k, tiers) for k in range(1, tiers)]
    barrier = pltpu.get_barrier_semaphore()
    for d in (sib, xn, yn):
        pl.semaphore_signal(barrier, inc=1, device_id={"col": d}, device_id_type=MESH)
    for d in others:
        pl.semaphore_signal(barrier, inc=1, device_id={"row": d}, device_id_type=MESH)
    pl.semaphore_wait(barrier, 3 + len(others))
    sums[0] = x_ref[...]
    for i, dev in enumerate((sib, xn, yn)):
        copy = pltpu.make_async_remote_copy(
            src_ref=sums.at[i],
            dst_ref=got.at[i],
            send_sem=send.at[i],
            recv_sem=recv.at[i],
            device_id={"col": dev},
            device_id_type=MESH,
        )
        copy.start()
        copy.wait()
        sums[i + 1] = sums[i] + got[i]
    tier_sums[r] = sums[3]
    copies = []
    for k, d in enumerate(others):
        copy = pltpu.make_async_remote_copy(
            src_ref=sums.at[3],
            dst_ref=tier_sums.at[r],
            send_sem=send.at[3 + k],
            recv_sem=recv.at[3 + k],
            device_id={"row": d},
            device_id_type=MESH,
        )
        copy.start()
        copies.append(copy)
    for copy in copies:
        copy.wait()
    result = tier_sums[0]
    for k in range(1, tiers):
        result = result + tier_sums[k]
    o_ref[...] = result


def total(x, tiers, cid):
    return pl.pallas_call(
        total_kernel,
        out_shape=jax.ShapeDtypeStruct(x.shape, x.dtype),
        in_specs=[pl.BlockSpec(memory_space=pltpu.VMEM)],
        out_specs=pl.BlockSpec(memory_space=pltpu.VMEM),
        scratch_shapes=[
            pltpu.VMEM((4, *x.shape), x.dtype),
            pltpu.VMEM((3, *x.shape), x.dtype),
            pltpu.VMEM((tiers, *x.shape), x.dtype),
            pltpu.SemaphoreType.DMA((2 + tiers,)),
            pltpu.SemaphoreType.DMA((2 + tiers,)),
        ],
        compiler_params=pltpu.CompilerParams(collective_id=cid, has_side_effects=True),
        cost_estimate=pl.CostEstimate(flops=0, bytes_accessed=40_000_000, transcendentals=0),
        name="total",
    )(x)


def after(value, *earlier):
    return lax.optimization_barrier((value, *earlier))[0]


def general_body(
    hidden,
    per_layer,
    lengths,
    block_ids,
    out_grad,
    query_weight,
    key_weight,
    value_weight,
    output_weight,
    gate_weight,
    up_weight,
    down_weight,
    laurel_left,
    laurel_right,
    layer_gate,
    layer_proj,
    norm_gains,
    head_gains,
):
    local_rows = hidden.shape[0]
    seq_groups = hidden.shape[1]
    col_index = lax.axis_index("col")
    row_index = lax.axis_index("row")
    all_lengths = lengths
    lengths = lax.dynamic_slice_in_dim(all_lengths, row_index * seq_groups, seq_groups, 0)
    (
        query_cols,
        key_cols,
        value_cols,
        output_rows,
        gate_cols,
        up_cols,
        down_rows,
        left_cols,
        right_rows,
        gate_layer_cols,
        proj_layer_rows,
    ) = (
        lax.all_gather(query_weight, "row", axis=0, tiled=True),
        lax.all_gather(key_weight, "row", axis=0, tiled=True),
        lax.all_gather(value_weight, "row", axis=0, tiled=True),
        lax.all_gather(output_weight, "row", axis=1, tiled=True),
        lax.all_gather(gate_weight, "row", axis=0, tiled=True),
        lax.all_gather(up_weight, "row", axis=0, tiled=True),
        lax.all_gather(down_weight, "row", axis=1, tiled=True),
        lax.all_gather(laurel_left, "row", axis=0, tiled=True),
        lax.all_gather(laurel_right, "row", axis=1, tiled=True),
        lax.all_gather(layer_gate, "row", axis=0, tiled=True),
        lax.all_gather(layer_proj, "row", axis=1, tiled=True),
    )
    (
        query_full,
        key_full,
        value_full,
        output_full,
        left_full,
        right_full,
        gate_layer_full,
        proj_layer_full,
    ) = (
        lax.all_gather(query_cols, "col", axis=1, tiled=True),
        lax.all_gather(key_cols, "col", axis=1, tiled=True),
        lax.all_gather(value_cols, "col", axis=1, tiled=True),
        lax.all_gather(output_rows, "col", axis=0, tiled=True),
        lax.all_gather(left_cols, "col", axis=1, tiled=True),
        lax.all_gather(right_rows, "col", axis=0, tiled=True),
        lax.all_gather(gate_layer_cols, "col", axis=1, tiled=True),
        lax.all_gather(proj_layer_rows, "col", axis=0, tiled=True),
    )
    paired = jnp.concatenate([gate_cols, up_cols], axis=1)
    unit_width = gate_cols.shape[1]
    first_position = col_index * local_rows
    positions = first_position + jnp.arange(local_rows, dtype=jnp.int32)
    live_mask = positions[:, None] < lengths[None, :]
    keep_mask = live_mask.astype(jnp.float32)[:, :, None]
    reach_back = (WINDOW + local_rows - 2) // local_rows
    reach_ahead = (BLOCK + local_rows - 2) // local_rows
    key_span = (reach_back + 1 + reach_ahead) * local_rows
    key_position = first_position - reach_back * local_rows + jnp.arange(key_span, dtype=jnp.int32)
    filler_low = jnp.full((seq_groups, reach_back * local_rows), FAR_BLOCK, jnp.int32)
    filler_high = jnp.full((seq_groups, reach_ahead * local_rows), FAR_BLOCK, jnp.int32)
    padded_blocks = jnp.concatenate([filler_low, block_ids, filler_high], axis=1)
    key_blocks = lax.dynamic_slice_in_dim(padded_blocks, first_position, key_span, 1)
    query_blocks = lax.dynamic_slice_in_dim(block_ids, first_position, local_rows, 1)
    key_live = (key_position[None, :] >= 0) & (key_position[None, :] < lengths[:, None])
    query_live = positions[None, :] < lengths[:, None]
    distance = positions[:, None] - key_position[None, :]
    nearby = (query_blocks[:, :, None] >= key_blocks[:, None, :]) & (distance < WINDOW)[None]
    nearby = nearby & query_live[:, :, None] & key_live[:, None, :]
    visible = (nearby | (distance == 0)[None])[:, None, None]
    residual = hidden.astype(jnp.float32)
    normed_value, input_back = jax.vjp(input_norm, residual, norm_gains)
    normed_low = normed_value.astype(jnp.bfloat16)
    half_width = HD // 2
    frequency = jnp.exp(jnp.arange(half_width, dtype=jnp.float32) * (-2.0 * math.log(10000.0) / HD))
    angles = (positions.astype(jnp.float32)[:, None] * frequency[None, :])[:, None, None, :]

    def prepare(query_in, key_in, value_in, gain_rows):
        return (
            rotate(root_norm(query_in, gain_rows[0]), angles),
            rotate(root_norm(key_in, gain_rows[1]), angles),
            plain_norm(value_in),
        )

    query_raw = matmul_last(normed_low, query_full).reshape(local_rows, seq_groups, H, HD)
    key_raw = matmul_last(normed_low, key_full).reshape(local_rows, seq_groups, KV, HD)
    value_raw = matmul_last(normed_low, value_full).reshape(local_rows, seq_groups, KV, HD)
    (query_value, key_value, value_value), head_back = jax.vjp(
        prepare, query_raw, key_raw, value_raw, head_gains
    )
    query_low = query_value.astype(jnp.bfloat16).reshape(local_rows, seq_groups, KV, H // KV, HD)
    key_low = key_value.astype(jnp.bfloat16)
    value_low = value_value.astype(jnp.bfloat16)
    offsets = list(range(reach_back, -reach_ahead - 1, -1))
    key_parts = []
    value_parts = []
    for offset in offsets:
        if offset == 0:
            key_parts.append(key_low)
            value_parts.append(value_low)
        else:
            moved_key, moved_value = passed_along((key_low, value_low), "col", offset)
            key_parts.append(moved_key)
            value_parts.append(moved_value)
    near_keys = jnp.concatenate(key_parts, axis=0)
    near_values = jnp.concatenate(value_parts, axis=0)
    score_scale = HD ** (-0.5)

    def score_all():
        raw_scores = (
            jnp.einsum(
                "psjgd,esjd->sjgpe", query_low, near_keys, preferred_element_type=jnp.float32
            )
            * score_scale
        )
        return jnp.where(visible, raw_scores, NEGATIVE)

    scores = score_all()
    row_max = jnp.max(scores, axis=-1, keepdims=True)
    exponent = jnp.exp(scores - row_max)
    row_total = jnp.sum(exponent, axis=-1, keepdims=True)
    attn_prob = exponent / row_total
    log_total = row_max + jnp.log(row_total)
    mixed_heads = jnp.einsum(
        "sjgpe,esjd->psjgd",
        attn_prob.astype(jnp.bfloat16),
        near_values,
        preferred_element_type=jnp.float32,
    )
    mixed_low = mixed_heads.reshape(local_rows, seq_groups, H * HD).astype(jnp.bfloat16)
    out_proj = matmul_last(mixed_low, output_full)
    laurel_mid = matmul_last(normed_low, left_full).astype(jnp.bfloat16)
    low_rank = matmul_last(laurel_mid, right_full)
    (after_attention, feed_normed), middle_back = jax.vjp(
        middle, residual, out_proj, low_rank, normed_low.astype(jnp.float32), norm_gains
    )
    feed_low = feed_normed.astype(jnp.bfloat16)
    gate_up = matmul_last(lax.all_gather(feed_low, "col", axis=0, tiled=True), paired)
    unit_value, gate_back = jax.vjp(
        gated_product, gate_up[..., :unit_width], gate_up[..., unit_width:]
    )
    units_low = unit_value.astype(jnp.bfloat16)
    summed = lax.psum_scatter(
        matmul_last(units_low, down_rows), "col", scatter_dimension=0, tiled=True
    )
    after_feed, feed_back = jax.vjp(feed_join, after_attention, summed, norm_gains)
    feed_round = after_feed.astype(jnp.bfloat16)
    layer_pre = matmul_last(feed_round, gate_layer_full)
    layer_input = per_layer.astype(jnp.float32)
    layer_value, layer_back = jax.vjp(gated_product, layer_pre, layer_input)
    layer_low = layer_value.astype(jnp.bfloat16)
    projected = matmul_last(layer_low, proj_layer_full)
    out_value, final_back = jax.vjp(final_join, after_feed, projected, norm_gains)
    square_sums = jnp.stack(
        [
            jnp.sum(keep_mask * residual * residual),
            jnp.sum(keep_mask * after_attention * after_attention),
            jnp.sum(keep_mask * after_feed * after_feed),
            jnp.sum(keep_mask * out_value * out_value),
        ]
    )
    valid_count = jnp.sum(all_lengths).astype(jnp.float32)
    cotangent = out_grad.astype(jnp.float32) * keep_mask
    grad_feed_out, grad_projected, gains_final = final_back(cotangent)
    projected_low = grad_projected.astype(jnp.bfloat16)
    grad_proj_layer = outer_sum(layer_low, projected_low)
    grad_layer_pre, grad_layer_input = layer_back(matmul_back(projected_low, proj_layer_full))
    layer_pre_low = grad_layer_pre.astype(jnp.bfloat16)
    grad_gate_layer = outer_sum(feed_round, layer_pre_low)
    grad_after_feed = grad_feed_out + matmul_back(layer_pre_low, gate_layer_full)
    grad_after_attention_a, grad_summed, gains_feed = feed_back(grad_after_feed)
    summed_low = grad_summed.astype(jnp.bfloat16)
    block_rows = lax.all_gather(summed_low, "col", axis=0, tiled=True)
    grad_down = outer_sum(units_low, block_rows)
    grad_units = matmul_back(block_rows, down_rows)
    grad_down, grad_units = (grad_down, grad_units)
    grad_gate_value, grad_up_value = gate_back(grad_units)
    grad_paired = jnp.concatenate([grad_gate_value, grad_up_value], axis=-1).astype(jnp.bfloat16)
    grad_weights_paired = outer_sum(
        lax.all_gather(feed_low, "col", axis=0, tiled=True), grad_paired
    )
    grad_feed = lax.psum_scatter(
        matmul_back(grad_paired, paired).astype(jnp.bfloat16),
        "col",
        scatter_dimension=0,
        tiled=True,
    ).astype(jnp.float32)
    grad_residual_mid, grad_out_proj, grad_low_rank, grad_normed_mid, gains_middle = middle_back(
        (grad_after_attention_a, grad_feed)
    )
    out_proj_low = grad_out_proj.astype(jnp.bfloat16)
    grad_output = outer_sum(mixed_low, out_proj_low)
    grad_mixed = matmul_back(out_proj_low, output_full).astype(jnp.bfloat16)
    grad_mixed = grad_mixed.reshape(local_rows, seq_groups, KV, H // KV, HD)
    low_rank_grad = grad_low_rank.astype(jnp.bfloat16)
    grad_right = outer_sum(laurel_mid, low_rank_grad)
    grad_laurel_mid = matmul_back(low_rank_grad, right_full).astype(jnp.bfloat16)
    grad_left = outer_sum(normed_low, grad_laurel_mid)
    scores = score_all()
    attn_prob = jnp.exp(scores - log_total)
    grad_prob = jnp.einsum(
        "psjgd,esjd->sjgpe", grad_mixed, near_values, preferred_element_type=jnp.float32
    )
    grad_scores = (
        attn_prob * (grad_prob - jnp.sum(attn_prob * grad_prob, axis=-1, keepdims=True))
    ).astype(jnp.bfloat16)
    grad_queries = (
        jnp.einsum("sjgpe,esjd->psjgd", grad_scores, near_keys, preferred_element_type=jnp.float32)
        * score_scale
    )
    grad_near_keys = (
        jnp.einsum("sjgpe,psjgd->esjd", grad_scores, query_low, preferred_element_type=jnp.float32)
        * score_scale
    )
    grad_near_values = jnp.einsum(
        "sjgpe,psjgd->esjd",
        attn_prob.astype(jnp.bfloat16),
        grad_mixed,
        preferred_element_type=jnp.float32,
    )
    grad_key_total = grad_near_keys[reach_back * local_rows : (reach_back + 1) * local_rows]
    grad_value_total = grad_near_values[reach_back * local_rows : (reach_back + 1) * local_rows]
    for slot_index, offset in enumerate(offsets):
        if offset != 0:
            piece_keys = grad_near_keys[slot_index * local_rows : (slot_index + 1) * local_rows]
            piece_values = grad_near_values[slot_index * local_rows : (slot_index + 1) * local_rows]
            back_keys, back_values = (
                passed_along(piece_keys.astype(jnp.bfloat16), "col", -offset).astype(
                    piece_keys.dtype
                ),
                passed_along(piece_values.astype(jnp.bfloat16), "col", -offset).astype(
                    piece_values.dtype
                ),
            )
            grad_key_total = grad_key_total + back_keys
            grad_value_total = grad_value_total + back_values
    grad_query_raw, grad_key_raw, grad_value_raw, grad_heads = head_back(
        (grad_queries.reshape(local_rows, seq_groups, H, HD), grad_key_total, grad_value_total)
    )
    query_grad_low = grad_query_raw.reshape(local_rows, seq_groups, H * HD).astype(jnp.bfloat16)
    key_grad_low = grad_key_raw.reshape(local_rows, seq_groups, KV * HD).astype(jnp.bfloat16)
    value_grad_low = grad_value_raw.reshape(local_rows, seq_groups, KV * HD).astype(jnp.bfloat16)
    grad_query = outer_sum(normed_low, query_grad_low)
    grad_key = outer_sum(normed_low, key_grad_low)
    grad_value = outer_sum(normed_low, value_grad_low)
    grad_normed = (
        grad_normed_mid
        + matmul_back(grad_laurel_mid, left_full)
        + matmul_back(query_grad_low, query_full)
        + matmul_back(key_grad_low, key_full)
        + matmul_back(value_grad_low, value_full)
    )
    grad_residual_in, gains_input = input_back(grad_normed)
    d_hidden = (grad_residual_mid + grad_residual_in).astype(jnp.bfloat16)
    d_per_layer = grad_layer_input.astype(jnp.bfloat16)
    grad_gains = gains_final + gains_feed + gains_middle + gains_input
    grad_gate = grad_weights_paired[:, :unit_width]
    grad_up = grad_weights_paired[:, unit_width:]
    (
        query_part,
        key_part,
        value_part,
        output_part,
        left_part,
        right_part,
        gate_layer_part,
        proj_layer_part,
    ) = (
        lax.psum_scatter(
            grad_query.astype(jnp.bfloat16), "col", scatter_dimension=1, tiled=True
        ).astype(jnp.float32),
        lax.psum_scatter(
            grad_key.astype(jnp.bfloat16), "col", scatter_dimension=1, tiled=True
        ).astype(jnp.float32),
        lax.psum_scatter(
            grad_value.astype(jnp.bfloat16), "col", scatter_dimension=1, tiled=True
        ).astype(jnp.float32),
        lax.psum_scatter(
            grad_output.astype(jnp.bfloat16), "col", scatter_dimension=0, tiled=True
        ).astype(jnp.float32),
        lax.psum_scatter(
            grad_left.astype(jnp.bfloat16), "col", scatter_dimension=1, tiled=True
        ).astype(jnp.float32),
        lax.psum_scatter(
            grad_right.astype(jnp.bfloat16), "col", scatter_dimension=0, tiled=True
        ).astype(jnp.float32),
        lax.psum_scatter(
            grad_gate_layer.astype(jnp.bfloat16), "col", scatter_dimension=1, tiled=True
        ).astype(jnp.float32),
        lax.psum_scatter(
            grad_proj_layer.astype(jnp.bfloat16), "col", scatter_dimension=0, tiled=True
        ).astype(jnp.float32),
    )
    (
        d_query_weight,
        d_key_weight,
        d_value_weight,
        d_output_weight,
        d_gate_weight,
        d_up_weight,
        d_down_weight,
        d_laurel_left,
        d_laurel_right,
        d_layer_gate,
        d_layer_proj,
    ) = (
        lax.psum_scatter(
            query_part.astype(jnp.bfloat16), "row", scatter_dimension=0, tiled=True
        ).astype(jnp.float32),
        lax.psum_scatter(
            key_part.astype(jnp.bfloat16), "row", scatter_dimension=0, tiled=True
        ).astype(jnp.float32),
        lax.psum_scatter(
            value_part.astype(jnp.bfloat16), "row", scatter_dimension=0, tiled=True
        ).astype(jnp.float32),
        lax.psum_scatter(
            output_part.astype(jnp.bfloat16), "row", scatter_dimension=1, tiled=True
        ).astype(jnp.float32),
        lax.psum_scatter(
            grad_gate.astype(jnp.bfloat16), "row", scatter_dimension=0, tiled=True
        ).astype(jnp.float32),
        lax.psum_scatter(
            grad_up.astype(jnp.bfloat16), "row", scatter_dimension=0, tiled=True
        ).astype(jnp.float32),
        lax.psum_scatter(
            grad_down.astype(jnp.bfloat16), "row", scatter_dimension=1, tiled=True
        ).astype(jnp.float32),
        lax.psum_scatter(
            left_part.astype(jnp.bfloat16), "row", scatter_dimension=0, tiled=True
        ).astype(jnp.float32),
        lax.psum_scatter(
            right_part.astype(jnp.bfloat16), "row", scatter_dimension=1, tiled=True
        ).astype(jnp.float32),
        lax.psum_scatter(
            gate_layer_part.astype(jnp.bfloat16), "row", scatter_dimension=0, tiled=True
        ).astype(jnp.float32),
        lax.psum_scatter(
            proj_layer_part.astype(jnp.bfloat16), "row", scatter_dimension=1, tiled=True
        ).astype(jnp.float32),
    )
    d_norm_gains, d_head_gains, total_squares = lax.psum(
        (grad_gains, grad_heads, square_sums), ("row", "col")
    )
    stats = jnp.sqrt(total_squares / (valid_count * D))
    output = out_value.astype(jnp.bfloat16)
    return (
        output,
        stats,
        d_hidden,
        d_per_layer,
        d_query_weight,
        d_key_weight,
        d_value_weight,
        d_output_weight,
        d_gate_weight,
        d_up_weight,
        d_down_weight,
        d_laurel_left,
        d_laurel_right,
        d_layer_gate,
        d_layer_proj,
        d_norm_gains,
        d_head_gains,
    )


def swap(array):
    return jnp.swapaxes(array, 0, 1)


def heads_body(
    hidden,
    per_layer,
    lengths,
    block_ids,
    out_grad,
    query_weight,
    key_weight,
    value_weight,
    output_weight,
    gate_weight,
    up_weight,
    down_weight,
    laurel_left,
    laurel_right,
    layer_gate,
    layer_proj,
    norm_gains,
    head_gains,
):
    low = jnp.bfloat16
    rows = hidden.shape[0]
    groups = hidden.shape[1]
    cols = lax.axis_size("col")
    seq = rows * cols
    share = cols // KV
    col_index = lax.axis_index("col")
    row_index = lax.axis_index("row")
    all_lengths = lengths
    lengths = lax.dynamic_slice_in_dim(all_lengths, row_index * groups, groups, 0)

    laurel = jnp.concatenate([laurel_left.T, laurel_right], axis=0)
    small = [key_weight.T, value_weight.T, layer_gate.T, layer_proj, laurel]
    heights = [key_weight.shape[1], value_weight.shape[1], layer_gate.shape[1]]
    heights += [layer_proj.shape[0], laurel_left.shape[1], laurel_right.shape[0]]
    edges = [sum(heights[:i]) for i in range(len(heights) + 1)]
    unit_width = gate_weight.shape[1]
    residual = swap(hidden).astype(jnp.float32)
    normed_value, input_back = jax.vjp(input_norm, residual, norm_gains)
    normed_low = normed_value.astype(low)
    tiers = lax.axis_size("row")
    normed_all, small_row, query_full, output_full, both_weights = open_all(
        normed_low, query_weight, output_weight, gate_weight, up_weight, small, tiers, 1
    )
    small_all = share_small(small_row, heights[0] + heights[1], 8)
    paired = lax.all_gather(both_weights, "row", axis=0, tiled=True)
    down_full = lax.all_gather(after(down_weight, normed_all), "row", axis=1, tiled=True)
    query_full = query_full.reshape(D, HD).T
    output_full = jnp.swapaxes(output_full, 0, 1).reshape(HD, D)
    pieces = [small_all[:, :, a:b] for a, b in zip(edges[:-1], edges[1:])]
    group_start = (col_index // share) * share

    def joined(piece):
        return jnp.swapaxes(piece, 1, 2).reshape(-1, D)

    key_full, value_full = (
        joined(lax.dynamic_slice_in_dim(piece, group_start, share, 0)) for piece in pieces[:2]
    )
    gate_layer_full, proj_layer_full, left_full, right_full = (
        joined(piece) for piece in pieces[2:]
    )
    head_weights = jnp.concatenate([query_full, key_full, value_full], axis=0)

    positions = jnp.arange(seq, dtype=jnp.int32)
    mine = col_index * rows + jnp.arange(rows, dtype=jnp.int32)
    keep_mask = (mine[None, :] < lengths[:, None]).astype(jnp.float32)[:, :, None]
    live = positions[None, :] < lengths[:, None]
    distance = positions[:, None] - positions[None, :]
    nearby = (block_ids[:, :, None] >= block_ids[:, None, :]) & (distance < WINDOW)[None]
    nearby = nearby & live[:, :, None] & live[:, None, :]
    visible = nearby | (distance == 0)[None]

    half_width = HD // 2
    frequency = jnp.exp(jnp.arange(half_width, dtype=jnp.float32) * (-2.0 * math.log(10000.0) / HD))
    angles = (positions.astype(jnp.float32)[:, None] * frequency[None, :])[None]

    def prepare(query_in, key_in, value_in, gain_rows):
        return (
            rotate(root_norm(query_in, gain_rows[0]), angles),
            rotate(root_norm(key_in, gain_rows[1]), angles),
            plain_norm(value_in),
        )

    head_raw = matmul_back(normed_all, head_weights)
    query_raw, key_raw, value_raw = jnp.split(head_raw, 3, axis=-1)
    (query_value, key_value, value_value), head_back = jax.vjp(
        prepare, query_raw, key_raw, value_raw, head_gains
    )
    query_low = query_value.astype(low)
    key_low = key_value.astype(low)
    value_low = value_value.astype(low)
    score_scale = HD ** (-0.5)

    def score_all():
        raw_scores = (
            jnp.einsum("spd,sed->spe", query_low, key_low, preferred_element_type=jnp.float32)
            * score_scale
        )
        return jnp.where(visible, raw_scores, NEGATIVE)

    scores = score_all()
    row_max = jnp.max(scores, axis=-1, keepdims=True)
    exponent = jnp.exp(scores - row_max)
    row_total = jnp.sum(exponent, axis=-1, keepdims=True)
    attn_prob = exponent / row_total
    mixed_low = jnp.einsum(
        "spe,sed->spd", attn_prob.astype(low), value_low, preferred_element_type=jnp.float32
    ).astype(low)
    out_proj = product_sum(mixed_low, output_full, False, 2)
    laurel_mid = matmul_back(normed_low, left_full).astype(low)
    low_rank = matmul_last(laurel_mid, right_full)
    (after_attention, feed_normed), middle_back = jax.vjp(
        middle, residual, out_proj, low_rank, normed_low.astype(jnp.float32), norm_gains
    )
    feed_all = spread(feed_normed.astype(low), 0)
    gate_value = matmul_last(feed_all, paired[:, :unit_width])
    up_value = matmul_last(feed_all, paired[:, unit_width:])
    units_low = gated_product(gate_value, up_value).astype(low)
    units_low, query_low, key_low, value_low, seen, head_weights = lax.optimization_barrier(
        (units_low, query_low, key_low, value_low, visible.astype(jnp.float32), head_weights)
    )
    summed = product_sum(units_low, down_full, False, 5)
    after_feed, feed_back = jax.vjp(feed_join, after_attention, summed, norm_gains)
    feed_round = after_feed.astype(low)
    layer_pre = matmul_back(feed_round, gate_layer_full)
    layer_input = swap(per_layer).astype(jnp.float32)
    layer_value, layer_back = jax.vjp(gated_product, layer_pre, layer_input)
    layer_low = layer_value.astype(low)
    projected = matmul_last(layer_low, proj_layer_full)
    out_value, final_back = jax.vjp(final_join, after_feed, projected, norm_gains)
    square_sums = jnp.stack(
        [
            jnp.sum(keep_mask * residual * residual),
            jnp.sum(keep_mask * after_attention * after_attention),
            jnp.sum(keep_mask * after_feed * after_feed),
            jnp.sum(keep_mask * out_value * out_value),
        ]
    )
    valid_count = jnp.sum(all_lengths).astype(jnp.float32)

    cotangent = swap(out_grad).astype(jnp.float32) * keep_mask
    grad_feed_out, grad_projected, gains_final = final_back(cotangent)
    projected_low = grad_projected.astype(low)
    grad_proj_layer = outer_sum(layer_low, projected_low)
    grad_layer_pre, grad_layer_input = layer_back(matmul_back(projected_low, proj_layer_full))
    layer_pre_low = grad_layer_pre.astype(low)
    grad_gate_layer = outer_sum(layer_pre_low, feed_round)
    grad_after_feed = grad_feed_out + matmul_last(layer_pre_low, gate_layer_full)
    grad_after_attention_a, grad_summed, gains_feed = feed_back(grad_after_feed)
    grad_paired, grad_down = units_back(
        grad_summed.astype(low), down_full, units_low, gate_value, up_value, 9
    )
    d_down_weight = lax.psum_scatter(grad_down, "row", scatter_dimension=1, tiled=True)
    grad_feed, grad_both = product_sum(grad_paired, paired, True, 6, feed_all)
    d_both = lax.psum_scatter(grad_both, "row", scatter_dimension=0, tiled=True)
    grad_residual_mid, grad_out_proj, grad_low_rank, grad_normed_mid, gains_middle = middle_back(
        (grad_after_attention_a, grad_feed)
    )
    grad_queries, grad_keys, grad_values, grad_output = heads_back(
        after(grad_out_proj.astype(low), d_down_weight),
        output_full,
        mixed_low,
        query_low,
        key_low,
        value_low,
        seen,
        score_scale,
        10,
    )
    low_rank_grad = grad_low_rank.astype(low)
    grad_right = outer_sum(laurel_mid, low_rank_grad)
    grad_laurel_mid = matmul_back(low_rank_grad, right_full).astype(low)
    grad_left = outer_sum(grad_laurel_mid, normed_low)
    grad_query_raw, grad_key_raw, grad_value_raw, grad_heads = head_back(
        (grad_queries, grad_keys, grad_values)
    )
    head_grads = jnp.concatenate([grad_query_raw, grad_key_raw, grad_value_raw], axis=-1)
    head_grads = head_grads.astype(low)
    grad_head_weights = outer_sum(head_grads, normed_all).astype(low)
    grad_query, grad_key, grad_value = jnp.split(grad_head_weights, 3, axis=0)
    grad_group = jnp.concatenate(
        [grad_key.reshape(share, -1, D), grad_value.reshape(share, -1, D)], axis=1
    )
    grad_rest = jnp.concatenate(
        [
            piece.astype(low).reshape(cols, -1, D)
            for piece in (grad_gate_layer, grad_proj_layer, grad_left, grad_right)
        ],
        axis=1,
    )
    half = grad_rest.shape[1] // 2
    grad_rest = jnp.swapaxes(grad_rest.reshape(cols, 2, half, D), 0, 1)
    rest_part, group_part = fold_small(grad_rest.reshape(2, cols * half, D), grad_group, 3)
    parts = jnp.concatenate(
        [grad_output, grad_query, group_part.astype(low), rest_part.astype(low).reshape(-1, D)],
        axis=0,
    )
    grad_normed = product_sum(after(head_grads, parts), head_weights, False, 7)
    parts = after(parts, d_both, grad_normed)
    parts_out = lax.psum_scatter(parts, "row", scatter_dimension=1, tiled=True).astype(jnp.float32)
    d_output_weight = parts_out[:HD]
    d_query_weight = parts_out[HD : 2 * HD].T
    small_out = parts_out[2 * HD :]
    small_parts = [small_out[a:b] for a, b in zip(edges[:-1], edges[1:])]
    grad_normed = grad_normed + grad_normed_mid + matmul_last(grad_laurel_mid, left_full)
    grad_residual_in, gains_input = input_back(grad_normed)
    d_hidden = swap((grad_residual_mid + grad_residual_in).astype(low))
    d_per_layer = swap(grad_layer_input.astype(low))
    grad_gains = gains_final + gains_feed + gains_middle + gains_input
    extra = jnp.concatenate([grad_heads.reshape(-1), square_sums])
    extra = jnp.pad(extra, (0, 2 * D - extra.shape[0])).reshape(2, D)
    all_sums = jnp.concatenate([grad_gains, extra], axis=0)
    totals = total(after(all_sums, parts), tiers, 4)
    d_down_weight = after(d_down_weight, totals).astype(jnp.float32)
    d_both = after(d_both, totals).astype(jnp.float32)
    d_gate_weight = d_both[:, :unit_width]
    d_up_weight = d_both[:, unit_width:]
    d_norm_gains = totals[:6]
    d_head_gains = totals[6, : 2 * HD].reshape(2, HD)
    total_squares = totals[6, 2 * HD : 2 * HD + 4]
    stats = jnp.sqrt(total_squares / (valid_count * D))
    output = swap(out_value.astype(low))
    return (
        output,
        stats,
        d_hidden,
        d_per_layer,
        d_query_weight,
        small_parts[0].T,
        small_parts[1].T,
        d_output_weight,
        d_gate_weight,
        d_up_weight,
        d_down_weight,
        small_parts[4].T,
        small_parts[5],
        small_parts[2].T,
        small_parts[3],
        d_norm_gains,
        d_head_gains,
    )


def solution(mesh):
    body = heads_body if mesh.shape["col"] == H else general_body
    in_specs = (
        P("col", "row", None),
        P("col", "row", None),
        P(),
        P("row", None),
        P("col", "row", None),
        P("row", "col"),
        P("row", "col"),
        P("row", "col"),
        P("col", "row"),
        P("row", "col"),
        P("row", "col"),
        P("col", "row"),
        P("row", "col"),
        P("col", "row"),
        P("row", "col"),
        P("col", "row"),
        P(),
        P(),
    )
    out_specs = (
        P("col", "row", None),
        P(),
        P("col", "row", None),
        P("col", "row", None),
        P("row", "col"),
        P("row", "col"),
        P("row", "col"),
        P("col", "row"),
        P("row", "col"),
        P("row", "col"),
        P("col", "row"),
        P("row", "col"),
        P("col", "row"),
        P("row", "col"),
        P("col", "row"),
        P(),
        P(),
    )
    return jax.shard_map(body, mesh=mesh, in_specs=in_specs, out_specs=out_specs, check_vma=False)
```

```python
import functools
import math

import jax
import jax.numpy as jnp
from jax import lax
from jax.experimental import pallas as pl
from jax.experimental.pallas import tpu as pltpu
from jax.sharding import PartitionSpec as P

D = 2048
H = 8
KV = 2
HD = 256
WINDOW = 512
BLOCK = 256


EPSILON = 1e-06
FAR_BLOCK = 1 << 30
NEGATIVE = -1e30
HALF_ROOT = 1.0 / math.sqrt(2.0)
CURVE = math.sqrt(2.0 / math.pi)
BEND = 0.044715


MESH = pl.DeviceIdType.MESH


def passed_along(value, axis, steps):
    count = lax.axis_size(axis)
    initial, last = (max(0, -steps), min(count, count - steps))
    return lax.ppermute(value, axis, [(source, source + steps) for source in range(initial, last)])


def root_norm(values, gain_row):
    return (
        values * lax.rsqrt(jnp.mean(values * values, axis=-1, keepdims=True) + EPSILON) * gain_row
    )


def plain_norm(values):
    return values * lax.rsqrt(jnp.mean(values * values, axis=-1, keepdims=True) + EPSILON)


def smooth_gate(values):
    return jax.nn.gelu(values, approximate=True)


def rotate(values, angles):
    half_width = values.shape[-1] // 2
    leading = values[..., :half_width]
    trailing = values[..., half_width:]
    cosine = jnp.cos(angles)
    sine_part = jnp.sin(angles)
    return jnp.concatenate(
        [leading * cosine - trailing * sine_part, trailing * cosine + leading * sine_part], axis=-1
    )


def matmul_last(first_array, second_array):
    return lax.dot_general(
        first_array,
        second_array,
        (((first_array.ndim - 1,), (0,)), ((), ())),
        preferred_element_type=jnp.float32,
    )


def matmul_back(first_array, second_array):
    return lax.dot_general(
        first_array,
        second_array,
        (((first_array.ndim - 1,), (1,)), ((), ())),
        preferred_element_type=jnp.float32,
    )


def outer_sum(first_array, second_array):
    return lax.dot_general(
        first_array, second_array, (((0, 1), (0, 1)), ((), ())), preferred_element_type=jnp.float32
    )


def input_norm(residual, gain_rows):
    return root_norm(residual, gain_rows[0])


def middle(residual, out_proj, low_rank, normed, gain_rows):
    merged = (
        residual + root_norm(out_proj, gain_rows[1]) + normed + root_norm(low_rank, gain_rows[4])
    ) * HALF_ROOT
    return (merged, root_norm(merged, gain_rows[2]))


def feed_join(merged, summed, gain_rows):
    return merged + root_norm(summed, gain_rows[3])


def final_join(merged, projected, gain_rows):
    return merged + root_norm(projected, gain_rows[5])


def gated_product(first_array, second_array):
    return smooth_gate(first_array) * second_array


def partners():
    c = lax.axis_index("col")
    sib = c + 1 - 2 * (c % 2)
    xn = c + 2 - 4 * ((c // 2) % 2)
    yn = c + 4 - 8 * (c // 4)
    return c, sib, xn, yn

def greet(devs):
    barrier = pltpu.get_barrier_semaphore()
    for d in devs:
        pl.semaphore_signal(barrier, inc=1, device_id={"col": d}, device_id_type=MESH)
    pl.semaphore_wait(barrier, len(devs))

def spread_kernel(rows, x_ref, o_ref, local_sem, send, recv):
    c, sib, xn, yn = partners()
    def slot(half, who):
        return o_ref.at[half, pl.ds(pl.multiple_of(who * rows, rows), rows), :]
    def both(who):
        return o_ref.at[:, pl.ds(pl.multiple_of(who * rows, rows), rows), :]
    def push(i, src, dst, dev):
        return pltpu.make_async_remote_copy(src_ref=src, dst_ref=dst, send_sem=send.at[i], recv_sem=recv.at[i], device_id={"col": dev}, device_id_type=MESH)
    mine = pltpu.make_async_copy(x_ref, both(c), local_sem)
    mine.start()
    greet((sib, xn, yn))
    x0 = push(0, x_ref.at[0], slot(0, c), xn)
    y1 = push(1, x_ref.at[1], slot(1, c), yn)
    x1 = push(2, x_ref.at[1], slot(1, c), xn)
    y0 = push(3, x_ref.at[0], slot(0, c), yn)
    s = push(4, x_ref, both(c), sib)
    x0.start(); y1.start(); x1.start(); y0.start(); s.start()
    diag = yn + (xn - c)
    x0.wait_recv()
    fy = push(5, slot(0, xn), slot(0, xn), yn)
    fy.start()
    sx0 = push(6, slot(0, xn), slot(0, xn), sib)
    sx0.start()
    y1.wait_recv()
    fx = push(7, slot(1, yn), slot(1, yn), xn)
    fx.start()
    sy1 = push(8, slot(1, yn), slot(1, yn), sib)
    sy1.start()
    x1.wait_recv()
    sx1 = push(9, slot(1, xn), slot(1, xn), sib)
    sx1.start()
    y0.wait_recv()
    sy0 = push(10, slot(0, yn), slot(0, yn), sib)
    sy0.start()
    fy.wait_recv()
    sd0 = push(11, slot(0, diag), slot(0, diag), sib)
    sd0.start()
    fx.wait_recv()
    sd1 = push(12, slot(1, diag), slot(1, diag), sib)
    sd1.start()
    for cp in (s, sx0, sy1, sx1, sy0, sd0, sd1):
        cp.wait_recv()
    for cp in (x0, y1, x1, y0, s, fy, sx0, fx, sy1, sx1, sy0, sd0, sd1):
        cp.wait_send()
    mine.wait()

def spread(x, cid=0):
    h, rows, d = x.shape
    return pl.pallas_call(
        functools.partial(spread_kernel, rows),
        out_shape=jax.ShapeDtypeStruct((h, 8 * rows, d), x.dtype),
        in_specs=[pl.BlockSpec(memory_space=pl.ANY)],
        out_specs=pl.BlockSpec(memory_space=pl.ANY),
        scratch_shapes=[pltpu.SemaphoreType.DMA, pltpu.SemaphoreType.DMA((13,)), pltpu.SemaphoreType.DMA((13,))],
        compiler_params=pltpu.CompilerParams(collective_id=cid, has_side_effects=True),
        cost_estimate=pl.CostEstimate(flops=0, bytes_accessed=120_000_000, transcendentals=0),
        name="spread",
    )(x)

def fold_steps(rows, p_ref, own, sibs, dx, dy, rx, ry, local_sem, send, recv):
    c, sib, xn, yn = partners()
    diag = yn + (xn - c)
    wide = jnp.float32
    tall = 32 if rows % 32 == 0 else 8

    def blk(who):
        return p_ref.at[:, pl.ds(pl.multiple_of(who * rows, rows), rows), :]

    def push(i, src, dst, dev):
        return pltpu.make_async_remote_copy(
            src_ref=src,
            dst_ref=dst,
            send_sem=send.at[i],
            recv_sem=recv.at[i],
            device_id={"col": dev},
            device_id_type=MESH,
        )

    def add(dst, src):
        @pl.loop(0, rows // tall)
        def _(i):
            r = pl.ds(pl.multiple_of(i * tall, tall), tall)
            dst[r, :] = (dst[r, :].astype(wide) + src[r, :].astype(wide)).astype(dst.dtype)

    def pair(j):
        add(own.at[j, 0], sibs.at[j, 0])
        add(own.at[j, 1], sibs.at[j, 1])

    dests = (diag, xn, yn, c)
    loads = [pltpu.make_async_copy(blk(d), own.at[j], local_sem.at[j]) for j, d in enumerate(dests)]
    for load in loads:
        load.start()
    yield None
    sides = [push(j, blk(d + (sib - c)), sibs.at[j], sib) for j, d in enumerate(dests)]
    for side in sides:
        side.start()
    yield None
    loads[0].wait()
    sides[0].wait_recv()
    pair(0)
    a = push(4, own.at[0, 0], dx, xn)
    b = push(5, own.at[0, 1], dy, yn)
    a.start()
    b.start()
    yield None
    loads[1].wait()
    sides[1].wait_recv()
    pair(1)
    x0 = push(6, own.at[1, 0], rx.at[0], xn)
    x0.start()
    yield None
    loads[2].wait()
    sides[2].wait_recv()
    pair(2)
    y1 = push(7, own.at[2, 1], ry.at[1], yn)
    y1.start()
    yield None
    a.wait_recv()
    add(own.at[2, 0], dx)
    y0 = push(8, own.at[2, 0], ry.at[0], yn)
    y0.start()
    yield None
    b.wait_recv()
    add(own.at[1, 1], dy)
    x1 = push(9, own.at[1, 1], rx.at[1], xn)
    x1.start()
    yield None
    loads[3].wait()
    sides[3].wait_recv()
    pair(3)
    yield None
    waits = ((x0, y0), (x1, y1))
    yield tall, waits, (*sides, a, b, x0, y1, y0, x1)


def fold_finish(rows, o_ref, own, rx, ry, tall, waits, sent):
    wide = jnp.float32
    for h in range(2):
        for copy in waits[h]:
            copy.wait_recv()

        @pl.loop(0, rows // tall)
        def _(i):
            r = pl.ds(pl.multiple_of(i * tall, tall), tall)
            o_ref[h, r, :] = (
                own[3, h, r, :].astype(wide) + rx[h, r, :].astype(wide) + ry[h, r, :].astype(wide)
            )

    for copy in sent:
        copy.wait_send()


def fold_scratch(h, rows, d, kind):
    return [
        pltpu.VMEM((4, h, rows, d), kind),
        pltpu.VMEM((4, h, rows, d), kind),
        pltpu.VMEM((rows, d), kind),
        pltpu.VMEM((rows, d), kind),
        pltpu.VMEM((h, rows, d), kind),
        pltpu.VMEM((h, rows, d), kind),
        pltpu.SemaphoreType.DMA((4,)),
        pltpu.SemaphoreType.DMA((10,)),
        pltpu.SemaphoreType.DMA((10,)),
    ]


def product_kernel(rows, flip, outer, *refs):
    if outer:
        a_ref, w_ref, f_ref, o_ref, g_ref = refs[:5]
        f_buf, g_buf, turned, f_sem, g_sem = refs[-5:]
        refs = refs[5:-5]
    else:
        a_ref, w_ref, o_ref = refs[:3]
        refs = refs[3:]
    a_buf, w_buf, stage, own, sibs, dx, dy, rx, ry, local_sem, send, recv = refs
    c, sib, xn, yn = partners()
    diag = yn + (xn - c)
    wide = jnp.float32
    d = o_ref.shape[-1]
    tile = 512
    tall = 32

    def push(i, src, dst, dev):
        return pltpu.make_async_remote_copy(
            src_ref=src,
            dst_ref=dst,
            send_sem=send.at[i],
            recv_sem=recv.at[i],
            device_id={"col": dev},
            device_id_type=MESH,
        )

    dests = (diag, xn, yn, c)
    step = sib - c
    weights = pltpu.make_async_copy(w_ref, w_buf, local_sem.at[8])
    weights.start()

    def load(i, who):
        return pltpu.make_async_copy(
            a_ref.at[:, pl.ds(pl.multiple_of(who * rows, rows), rows), :],
            a_buf.at[i],
            local_sem.at[i],
        )

    far = [load(j, dests[j] + step) for j in range(4)]
    near = [load(4 + j, dests[j]) for j in range(4)]
    for first, second in zip(far, near):
        first.start()
        second.start()
    owners = [d + step for d in dests] + list(dests)
    strip = 256

    def strips(n):
        cut = pl.ds(pl.multiple_of(n * strip, strip), strip)
        return [
            pltpu.make_async_copy(
                f_ref.at[:, pl.ds(pl.multiple_of(who * rows, rows), rows), cut],
                f_buf.at[lax.rem(n, 2), i],
                f_sem.at[lax.rem(n, 2), i],
            )
            for i, who in enumerate(owners)
        ]

    def strip_out(n):
        cut = pl.ds(pl.multiple_of(n * strip, strip), strip)
        slot = lax.rem(n, 2)
        return pltpu.make_async_copy(g_buf.at[slot], g_ref.at[cut, :], g_sem.at[slot])

    def outer_product():
        count = g_ref.shape[0] // strip
        depth = a_buf.shape[-1]

        @pl.loop(0, count)
        def _(n):
            slot = lax.rem(n, 2)
            for copy in strips(n):
                copy.wait()

            @pl.when(n + 1 < count)
            def _():
                for copy in strips(n + 1):
                    copy.start()

            @pl.when(n >= 2)
            def _():
                strip_out(n - 2).wait()

            turned[...] = f_buf[slot].reshape(16 * rows, strip).T

            @pl.loop(0, depth // tile)
            def _(m):
                cut = pl.ds(pl.multiple_of(m * tile, tile), tile)
                right = a_buf[:, :, :, cut].reshape(16 * rows, tile)
                value = jnp.dot(turned[...], right, preferred_element_type=wide)
                g_buf[slot, :, cut] = value.astype(g_buf.dtype)

            strip_out(n).start()

        strip_out(count - 2).wait()
        strip_out(count - 1).wait()

    if outer:
        for copy in strips(0):
            copy.start()
    greet((sib, xn, yn))
    weights.wait()

    def product(i, put):
        left = a_buf[i].reshape(2 * rows, a_buf.shape[-1])

        @pl.loop(0, d // tile)
        def _(n):
            cut = pl.ds(pl.multiple_of(n * tile, tile), tile)
            right = w_buf[cut, :] if flip else w_buf[:, cut]
            dims = (((1,), (1,)), ((), ())) if flip else (((1,), (0,)), ((), ()))
            value = lax.dot_general(left, right, dims, preferred_element_type=wide)
            put(cut, value.reshape(2, rows, tile))

    sides = [push(j, stage.at[j], sibs.at[j], sib) for j in range(4)]

    def for_sibling(j):
        far[j].wait()

        def put(cut, value):
            stage[j, :, :, cut] = value.astype(stage.dtype)

        product(j, put)
        sides[j].start()

    def for_chip(j):
        near[j].wait()
        sides[j].wait_recv()

        def put(cut, value):
            own[j, :, :, cut] = (value + sibs[j, :, :, cut].astype(wide)).astype(own.dtype)

        product(4 + j, put)

    def add(dst, src):
        @pl.loop(0, rows // tall)
        def _(i):
            r = pl.ds(pl.multiple_of(i * tall, tall), tall)
            dst[r, :] = (dst[r, :].astype(wide) + src[r, :].astype(wide)).astype(dst.dtype)

    for_sibling(0)
    near[0].wait()

    def hold(cut, value):
        o_ref[:, :, cut] = value

    product(4, hold)
    sides[0].wait_recv()
    for h in range(2):

        @pl.loop(0, rows // tall)
        def _(i):
            r = pl.ds(pl.multiple_of(i * tall, tall), tall)
            own[0, h, r, :] = (o_ref[h, r, :] + sibs[0, h, r, :].astype(wide)).astype(own.dtype)

    a = push(4, own.at[0, 0], dx, xn)
    b = push(5, own.at[0, 1], dy, yn)
    a.start()
    b.start()
    for_sibling(1)
    for_sibling(2)
    for_chip(1)
    x0 = push(6, own.at[1, 0], rx.at[0], xn)
    x0.start()
    for_sibling(3)
    for_chip(2)
    y1 = push(7, own.at[2, 1], ry.at[1], yn)
    y1.start()
    a.wait_recv()
    add(own.at[2, 0], dx)
    y0 = push(8, own.at[2, 0], ry.at[0], yn)
    y0.start()
    b.wait_recv()
    add(own.at[1, 1], dy)
    x1 = push(9, own.at[1, 1], rx.at[1], xn)
    x1.start()
    near[3].wait()
    sides[3].wait_recv()

    def put(cut, value):
        o_ref[:, :, cut] = value + sibs[3, :, :, cut].astype(wide)

    product(7, put)
    if outer:
        outer_product()
    for h, waits in enumerate(((x0, y0), (x1, y1))):
        for copy in waits:
            copy.wait_recv()

        @pl.loop(0, rows // tall)
        def _(i):
            r = pl.ds(pl.multiple_of(i * tall, tall), tall)
            o_ref[h, r, :] = o_ref[h, r, :] + rx[h, r, :].astype(wide) + ry[h, r, :].astype(wide)

    for copy in (*sides, a, b, x0, y1, y0, x1):
        copy.wait_send()


def product_sum(left, right, flip, cid, feed=None, room=44):
    h, total, depth = left.shape
    rows = total // 8
    d = right.shape[0] if flip else right.shape[1]
    low = left.dtype
    outer = feed is not None
    out_shape = [jax.ShapeDtypeStruct((h, rows, d), jnp.float32)]
    out_specs = [pl.BlockSpec(memory_space=pltpu.VMEM)]
    scratch = [
        pltpu.VMEM((8, h, rows, depth), low),
        pltpu.VMEM(right.shape, low),
        pltpu.VMEM((4, h, rows, d), low),
        pltpu.VMEM((3, h, rows, d), low),
        pltpu.VMEM((4, h, rows, d), low),
        pltpu.VMEM((rows, d), low),
        pltpu.VMEM((rows, d), low),
        pltpu.VMEM((h, rows, d), low),
        pltpu.VMEM((h, rows, d), low),
        pltpu.SemaphoreType.DMA((9,)),
        pltpu.SemaphoreType.DMA((10,)),
        pltpu.SemaphoreType.DMA((10,)),
    ]
    flops = 2 * h * total * depth * d
    if outer:
        width = feed.shape[-1]
        flops += 2 * h * total * depth * width
        out_shape.append(jax.ShapeDtypeStruct((width, depth), low))
        out_specs.append(pl.BlockSpec(memory_space=pl.ANY))
        scratch += [
            pltpu.VMEM((2, 8, h, rows, 256), low),
            pltpu.VMEM((2, 256, depth), low),
            pltpu.VMEM((256, h * total), low),
            pltpu.SemaphoreType.DMA((2, 8)),
            pltpu.SemaphoreType.DMA((2,)),
        ]
    result = pl.pallas_call(
        functools.partial(product_kernel, rows, flip, outer),
        out_shape=out_shape,
        in_specs=[pl.BlockSpec(memory_space=pl.ANY)] * (3 if outer else 2),
        out_specs=out_specs,
        scratch_shapes=scratch,
        compiler_params=pltpu.CompilerParams(
            collective_id=cid,
            has_side_effects=True,
            vmem_limit_bytes=(52 if outer else room) << 20,
        ),
        cost_estimate=pl.CostEstimate(
            flops=flops, bytes_accessed=130_000_000, transcendentals=0
        ),
        name="product_sum",
    )(*((left, right, feed) if outer else (left, right)))
    return result if outer else result[0]


def fold_small_kernel(
    rows, p_ref, g_ref, o_ref, k_ref, own, sibs, dx, dy, rx, ry, local_sem, send, recv,
    gown, gsibs, grx, glocal, gsend, grecv,
):
    c, sib, xn, yn = partners()
    m = c % 4
    m_sib = m + 1 - 2 * (m % 2)
    m_x = m + 2 - 4 * (m // 2)
    m_diag = m_sib + (m_x - m)
    wide = jnp.float32

    def push(i, src, dst, dev):
        return pltpu.make_async_remote_copy(
            src_ref=src,
            dst_ref=dst,
            send_sem=gsend.at[i],
            recv_sem=grecv.at[i],
            device_id={"col": dev},
            device_id_type=MESH,
        )

    steps = fold_steps(rows, p_ref, own, sibs, dx, dy, rx, ry, local_sem, send, recv)
    next(steps)
    loads = [
        pltpu.make_async_copy(g_ref.at[d], gown.at[j], glocal.at[j])
        for j, d in enumerate((m_x, m))
    ]
    for load in loads:
        load.start()
    greet((sib, xn, yn))
    sides = [push(j, g_ref.at[d], gsibs.at[j], sib) for j, d in enumerate((m_diag, m_sib))]
    sides[0].start()
    next(steps)
    sides[1].start()
    tall = k_ref.shape[0] // 4
    loads[0].wait()
    sides[0].wait_recv()

    @pl.loop(0, 4)
    def _(i):
        r = pl.ds(pl.multiple_of(i * tall, tall), tall)
        gown[0, r, :] = (gown[0, r, :].astype(wide) + gsibs[0, r, :].astype(wide)).astype(
            gown.dtype
        )

    over = push(2, gown.at[0], grx, xn)
    over.start()
    last = None
    for step in steps:
        last = step if step is not None else last
    fold_finish(rows, o_ref, own, rx, ry, *last)
    loads[1].wait()
    sides[1].wait_recv()
    over.wait_recv()

    @pl.loop(0, 4)
    def _(i):
        r = pl.ds(pl.multiple_of(i * tall, tall), tall)
        k_ref[r, :] = (
            gown[1, r, :].astype(wide) + gsibs[1, r, :].astype(wide) + grx[r, :].astype(wide)
        )

    for copy in (*sides, over):
        copy.wait_send()


def fold_small(p, g, cid):
    h, total, d = p.shape
    rows = total // 8
    share, tall, _ = g.shape
    return pl.pallas_call(
        functools.partial(fold_small_kernel, rows),
        out_shape=(
            jax.ShapeDtypeStruct((h, rows, d), jnp.float32),
            jax.ShapeDtypeStruct((tall, d), jnp.float32),
        ),
        in_specs=[pl.BlockSpec(memory_space=pl.ANY)] * 2,
        out_specs=[pl.BlockSpec(memory_space=pltpu.VMEM)] * 2,
        scratch_shapes=fold_scratch(h, rows, d, p.dtype)
        + [
            pltpu.VMEM((2, tall, d), g.dtype),
            pltpu.VMEM((2, tall, d), g.dtype),
            pltpu.VMEM((tall, d), g.dtype),
            pltpu.SemaphoreType.DMA((2,)),
            pltpu.SemaphoreType.DMA((3,)),
            pltpu.SemaphoreType.DMA((3,)),
        ],
        compiler_params=pltpu.CompilerParams(
            collective_id=cid, has_side_effects=True, vmem_limit_bytes=40 << 20
        ),
        cost_estimate=pl.CostEstimate(flops=0, bytes_accessed=60_000_000, transcendentals=0),
        name="fold_small",
    )(p, g)


def open_kernel(
    rows, tiers, x_ref, q_ref, w_ref, g_ref, u_ref, *refs
):
    small = refs[:5]
    o_ref, sa_ref, qa_ref, wa_ref, both_ref = refs[5:10]
    tokens, stacked, both_buf, in_sem, local_sem, send, recv, line_send, line_recv = refs[10:]
    c, sib, xn, yn = partners()
    diag = yn + (xn - c)
    r = lax.axis_index("row")
    last = tiers - 1
    weights = []
    for src, dst in ((stacked, sa_ref), (q_ref, qa_ref), (w_ref, wa_ref)):
        cut = src.shape[0] // 32 * 16
        weights += [(src, dst, pl.ds(0, cut)), (src, dst, pl.ds(cut, src.shape[0] - cut))]
    pieces = len(weights)

    def slot(half, who):
        return o_ref.at[half, pl.ds(pl.multiple_of(who * rows, rows), rows), :]

    def both(who):
        return o_ref.at[:, pl.ds(pl.multiple_of(who * rows, rows), rows), :]

    started = []

    def push(src, dst, **dev):
        i = len(started)
        copy = pltpu.make_async_remote_copy(
            src_ref=src,
            dst_ref=dst,
            send_sem=send.at[i],
            recv_sem=recv.at[i],
            device_id=dev,
            device_id_type=MESH,
        )
        copy.start()
        started.append(copy)
        return copy

    width = g_ref.shape[1]
    first = [pltpu.make_async_copy(x_ref, tokens, in_sem.at[0])]
    base = 0
    for i, ref in enumerate(small):
        tall = ref.shape[0]
        first.append(
            pltpu.make_async_copy(ref, stacked.at[pl.ds(base, tall)], in_sem.at[1 + i])
        )
        base += tall
    later = [
        pltpu.make_async_copy(g_ref, both_buf.at[:, pl.ds(0, width)], in_sem.at[6]),
        pltpu.make_async_copy(u_ref, both_buf.at[:, pl.ds(width, width)], in_sem.at[7]),
    ]
    for copy in (*first, *later):
        copy.start()
    local = [
        pltpu.make_async_copy(tokens, both(c), local_sem.at[0]),
        pltpu.make_async_copy(stacked, sa_ref.at[r], local_sem.at[1]),
        pltpu.make_async_copy(q_ref, qa_ref.at[r], local_sem.at[2]),
        pltpu.make_async_copy(w_ref, wa_ref.at[r], local_sem.at[3]),
        pltpu.make_async_copy(both_buf, both_ref, local_sem.at[4]),
    ]
    barrier = pltpu.get_barrier_semaphore()
    for d in (sib, xn, yn):
        pl.semaphore_signal(barrier, inc=1, device_id={"col": d}, device_id_type=MESH)

    @pl.when(r < last)
    def _():
        pl.semaphore_signal(barrier, inc=1, device_id={"row": r + 1}, device_id_type=MESH)

    @pl.when(r > 0)
    def _():
        pl.semaphore_signal(barrier, inc=1, device_id={"row": r - 1}, device_id_type=MESH)

    @pl.when((r > 0) & (r < last))
    def _():
        pl.semaphore_wait(barrier, 5)

    @pl.when((r == 0) | (r == last))
    def _():
        pl.semaphore_wait(barrier, 4)

    def passing(way, hop, j):
        src, dst, cut = weights[j]
        whose = r - hop if way == 0 else r + hop
        return pltpu.make_async_remote_copy(
            src_ref=src.at[cut] if hop == 0 else dst.at[whose, cut],
            dst_ref=dst.at[whose, cut],
            send_sem=line_send.at[way, hop, j],
            recv_sem=line_recv.at[way, hop, j],
            device_id={"row": r + 1 if way == 0 else r - 1},
            device_id_type=MESH,
        )

    def going(way, hop):
        return (r < last) & (r >= hop) if way == 0 else (r > 0) & (r + hop <= last)

    def coming(way, hop):
        return r > hop if way == 0 else r + hop < last

    def forward(hop, j):
        for way in range(2):
            if hop > 0:

                @pl.when(coming(way, hop - 1))
                def _():
                    passing(way, hop - 1, j).wait_recv()

            @pl.when(going(way, hop))
            def _():
                passing(way, hop, j).start()

    for copy in first:
        copy.wait()
    x0 = push(tokens.at[0], slot(0, c), col=xn)
    y1 = push(tokens.at[1], slot(1, c), col=yn)
    for j in range(pieces):
        forward(0, j)
    x1 = push(tokens.at[1], slot(1, c), col=xn)
    y0 = push(tokens.at[0], slot(0, c), col=yn)
    push(tokens, both(c), col=sib)
    for copy in later:
        copy.wait()
    for copy in local:
        copy.start()
    forward(1, 0)
    forward(1, 1)
    x0.wait_recv()
    fy = push(slot(0, xn), slot(0, xn), col=yn)
    push(slot(0, xn), slot(0, xn), col=sib)
    y1.wait_recv()
    fx = push(slot(1, yn), slot(1, yn), col=xn)
    push(slot(1, yn), slot(1, yn), col=sib)
    for j in range(2, pieces):
        forward(1, j)
    x1.wait_recv()
    push(slot(1, xn), slot(1, xn), col=sib)
    y0.wait_recv()
    push(slot(0, yn), slot(0, yn), col=sib)
    for hop in range(2, last):
        for j in range(pieces):
            forward(hop, j)
    fy.wait_recv()
    push(slot(0, diag), slot(0, diag), col=sib)
    fx.wait_recv()
    push(slot(1, diag), slot(1, diag), col=sib)
    for copy in started:
        if not any(copy is other for other in (x0, y1, x1, y0, fy, fx)):
            copy.wait_recv()
    for j in range(pieces):
        for way in range(2):

            @pl.when(coming(way, last - 1))
            def _():
                passing(way, last - 1, j).wait_recv()

            for hop in range(last):

                @pl.when(going(way, hop))
                def _():
                    passing(way, hop, j).wait_send()

    for copy in started:
        copy.wait_send()
    for copy in local:
        copy.wait()


def open_all(x, query, output, gate, up, small, tiers, cid):
    h, rows, d = x.shape
    low = x.dtype
    stack = (sum(piece.shape[0] for piece in small), small[0].shape[1])
    both = (gate.shape[0], 2 * gate.shape[1])
    return pl.pallas_call(
        functools.partial(open_kernel, rows, tiers),
        out_shape=(
            jax.ShapeDtypeStruct((h, 8 * rows, d), low),
            jax.ShapeDtypeStruct((tiers, *stack), low),
            jax.ShapeDtypeStruct((tiers, *query.shape), low),
            jax.ShapeDtypeStruct((tiers, *output.shape), low),
            jax.ShapeDtypeStruct(both, low),
        ),
        in_specs=[pl.BlockSpec(memory_space=pl.ANY)] * 10,
        out_specs=[pl.BlockSpec(memory_space=pl.ANY)] * 5,
        scratch_shapes=[
            pltpu.VMEM(x.shape, low),
            pltpu.VMEM(stack, low),
            pltpu.VMEM(both, low),
            pltpu.SemaphoreType.DMA((8,)),
            pltpu.SemaphoreType.DMA((5,)),
            pltpu.SemaphoreType.DMA((13,)),
            pltpu.SemaphoreType.DMA((13,)),
            pltpu.SemaphoreType.DMA((2, tiers - 1, 6)),
            pltpu.SemaphoreType.DMA((2, tiers - 1, 6)),
        ],
        compiler_params=pltpu.CompilerParams(
            collective_id=cid, has_side_effects=True, vmem_limit_bytes=60 << 20
        ),
        cost_estimate=pl.CostEstimate(flops=0, bytes_accessed=200_000_000, transcendentals=0),
        name="open_all",
    )(x, query, output, gate, up, *small)


def share_kernel(near, s_ref, sa_ref, held, local_sem, send, recv):
    c, sib, xn, yn = partners()
    diag = yn + (xn - c)
    height = s_ref.shape[1]
    started = []

    def part(ref, first):
        return ref.at[:, pl.ds(0, near) if first else pl.ds(near, height - near), :]

    def push(who, first, dev, own=False):
        i = len(started)
        dst = part(sa_ref.at[who], first)
        copy = pltpu.make_async_remote_copy(
            src_ref=part(held, first) if own else dst,
            dst_ref=dst,
            send_sem=send.at[i],
            recv_sem=recv.at[i],
            device_id={"col": dev},
            device_id_type=MESH,
        )
        copy.start()
        started.append(copy)
        return copy

    fetch = pltpu.make_async_copy(s_ref, held, local_sem.at[0])
    fetch.start()
    mine = pltpu.make_async_copy(held, sa_ref.at[c], local_sem.at[1])
    greet((sib, xn, yn))
    fetch.wait()
    rx = push(c, False, xn, own=True)
    ry = push(c, False, yn, own=True)
    kx = push(c, True, xn, own=True)
    push(c, True, sib, own=True)
    push(c, False, sib, own=True)
    mine.start()
    rx.wait_recv()
    fd = push(xn, False, yn)
    push(xn, False, sib)
    ry.wait_recv()
    push(yn, False, sib)
    fd.wait_recv()
    push(diag, False, sib)
    kx.wait_recv()
    push(xn, True, sib)
    for copy in started:
        if not any(copy is other for other in (kx, rx, ry, fd)):
            copy.wait_recv()
    for copy in started:
        copy.wait_send()
    mine.wait()


def share_small(small, near, cid):
    return pl.pallas_call(
        functools.partial(share_kernel, near),
        out_shape=jax.ShapeDtypeStruct((8, *small.shape), small.dtype),
        in_specs=[pl.BlockSpec(memory_space=pl.ANY)],
        out_specs=pl.BlockSpec(memory_space=pl.ANY),
        scratch_shapes=[
            pltpu.VMEM(small.shape, small.dtype),
            pltpu.SemaphoreType.DMA((2,)),
            pltpu.SemaphoreType.DMA((10,)),
            pltpu.SemaphoreType.DMA((10,)),
        ],
        compiler_params=pltpu.CompilerParams(collective_id=cid, has_side_effects=True),
        cost_estimate=pl.CostEstimate(flops=0, bytes_accessed=60_000_000, transcendentals=0),
        name="share_small",
    )(small)


def rounds_of(rows, x_ref, held, local_sem, send, recv, consume, prepare):
    c, sib, xn, yn = partners()
    diag = yn + (xn - c)
    step = sib - c

    def place(t, j, n=1):
        return held.at[t, pl.ds(j * rows, n * rows), :]

    started = []

    def push(src, dst, dev):
        i = len(started)
        copy = pltpu.make_async_remote_copy(
            src_ref=src,
            dst_ref=dst,
            send_sem=send.at[i],
            recv_sem=recv.at[i],
            device_id={"col": dev},
            device_id_type=MESH,
        )
        copy.start()
        started.append(copy)
        return copy

    mine = [pltpu.make_async_copy(x_ref.at[h], place(0, h), local_sem.at[h]) for h in range(2)]
    for copy in mine:
        copy.start()
    greet((sib, xn, yn))
    x0 = push(x_ref.at[0], place(1, 0), xn)
    y1 = push(x_ref.at[1], place(1, 1), yn)
    x1 = push(x_ref.at[1], place(2, 0), xn)
    y0 = push(x_ref.at[0], place(2, 1), yn)
    s0 = push(x_ref.at[0], place(0, 2), sib)
    s1 = push(x_ref.at[1], place(0, 3), sib)
    prepare(0)
    for copy in mine:
        copy.wait()
    s0.wait_recv()
    s1.wait_recv()
    consume(0, 0, ((0, c), (1, c), (0, sib), (1, sib)))
    x0.wait_recv()
    fy = push(place(1, 0), place(3, 0), yn)
    y1.wait_recv()
    fx = push(place(1, 1), place(3, 1), xn)
    prepare(1)
    t1 = push(place(1, 0, 2), place(1, 2, 2), sib)
    t1.wait_recv()
    consume(1, 0, ((0, xn), (1, yn), (0, xn + step), (1, yn + step)))
    prepare(2)
    x1.wait_recv()
    y0.wait_recv()
    t2 = push(place(2, 0, 2), place(2, 2, 2), sib)
    t2.wait_recv()
    consume(2, 0, ((1, xn), (0, yn), (1, xn + step), (0, yn + step)))
    prepare(3)
    fy.wait_recv()
    fx.wait_recv()
    t3 = push(place(3, 0, 2), place(3, 2, 2), sib)
    consume(3, 0, ((0, diag), (1, diag)))
    t3.wait_recv()
    consume(3, 2, ((0, diag + step), (1, diag + step)))
    for copy in started:
        copy.wait_send()


def piece_at(ref, rows, piece):
    half, who = piece
    return ref.at[half, pl.ds(pl.multiple_of(who * rows, rows), rows), :]


def units_back_kernel(
    rows, x_ref, w_ref, u_ref, g_ref, v_ref, p_ref, d_ref,
    held, weights, units, turned, gates, ups, grads, total_ref,
    weight_sem, load_sem, store_sem, local_sem, send, recv,
):
    c, sib, xn, yn = partners()
    diag = yn + (xn - c)
    step = sib - c
    wide = jnp.float32
    width = w_ref.shape[0]
    d = w_ref.shape[1]
    plan = (
        ((0, c), (1, c), (0, sib), (1, sib)),
        ((0, xn), (1, yn), (0, xn + step), (1, yn + step)),
        ((1, xn), (0, yn), (1, xn + step), (0, yn + step)),
        ((0, diag), (1, diag), (0, diag + step), (1, diag + step)),
    )
    fetch = pltpu.make_async_copy(w_ref, weights, weight_sem)
    fetch.start()

    def loads(t):
        copies = []
        for j, piece in enumerate(plan[t]):
            for k, (src, dst) in enumerate(((u_ref, units), (g_ref, gates), (v_ref, ups))):
                copies.append(
                    pltpu.make_async_copy(
                        piece_at(src, rows, piece),
                        dst.at[t % 2, pl.ds(j * rows, rows), :],
                        load_sem.at[t % 2, j, k],
                    )
                )
        return copies

    def stores(t, first=0, count=4):
        return [
            pltpu.make_async_copy(
                grads.at[t % 2, pl.ds(j * rows, rows), :],
                piece_at(p_ref, rows, plan[t][j]),
                store_sem.at[t % 2, j],
            )
            for j in range(first, first + count)
        ]

    for copy in loads(0):
        copy.start()

    tile = 256

    def prepare(t):
        if t == 0:
            fetch.wait()
        if t < 3:
            for copy in loads(t + 1):
                copy.start()
        for copy in loads(t):
            copy.wait()

        @pl.loop(0, width // tile)
        def _(n):
            cut = pl.ds(pl.multiple_of(n * tile, tile), tile)
            gate = gates[t % 2, :, cut]
            square = gate * gate
            bent = jnp.tanh(CURVE * (gate + BEND * gate * square))
            rise = 0.5 * (1.0 + bent)
            slope = rise + (0.5 * CURVE) * gate * (1.0 - bent * bent) * (1.0 + 3.0 * BEND * square)
            gates[t % 2, :, cut] = ups[t % 2, :, cut] * slope
            ups[t % 2, :, cut] = gate * rise
            turned[cut, :] = units[t % 2, :, cut].T

    def consume(t, first, pieces):
        if t >= 2 and first == 0:
            for copy in stores(t - 2):
                copy.wait()
        span = slice(first * rows, (first + len(pieces)) * rows)

        @pl.loop(0, width // 512)
        def _(n):
            cut = pl.ds(pl.multiple_of(n * 512, 512), 512)
            grad = lax.dot_general(
                held[t, span, :],
                weights[cut, :],
                (((1,), (1,)), ((), ())),
                preferred_element_type=wide,
            )
            grads[t % 2, span, cut] = (grad * gates[t % 2, span, cut]).astype(grads.dtype)
            cut_up = pl.ds(pl.multiple_of(width + n * 512, 512), 512)
            grads[t % 2, span, cut_up] = (grad * ups[t % 2, span, cut]).astype(grads.dtype)

        for copy in stores(t, first, len(pieces)):
            copy.start()

        block = d_ref.shape[-1]

        @pl.loop(0, d // block)
        def _(n):
            cut = pl.ds(pl.multiple_of(n * block, block), block)
            value = jnp.dot(turned[:, span], held[t, span, cut], preferred_element_type=wide)
            if t > 0:
                value = value + total_ref[:, cut]
            if first == 0:
                total_ref[:, cut] = value
            else:
                d_ref[n] = value.astype(d_ref.dtype)

    rounds_of(rows, x_ref, held, local_sem, send, recv, consume, prepare)
    for copy in (*stores(2), *stores(3)):
        copy.wait()


def units_back(x, down, units, gate, up, tiers, cid):
    h, rows, d = x.shape
    width = down.shape[0]
    low = x.dtype
    return pl.pallas_call(
        functools.partial(units_back_kernel, rows),
        out_shape=(
            jax.ShapeDtypeStruct((h, 8 * rows, 2 * width), low),
            jax.ShapeDtypeStruct((tiers, width, d // tiers), low),
        ),
        in_specs=[pl.BlockSpec(memory_space=pl.ANY)] * 5,
        out_specs=[
            pl.BlockSpec(memory_space=pl.ANY),
            pl.BlockSpec(memory_space=pltpu.VMEM),
        ],
        scratch_shapes=[
            pltpu.VMEM((4, 4 * rows, d), low),
            pltpu.VMEM((width, d), low),
            pltpu.VMEM((2, 4 * rows, width), low),
            pltpu.VMEM((width, 4 * rows), low),
            pltpu.VMEM((2, 4 * rows, width), jnp.float32),
            pltpu.VMEM((2, 4 * rows, width), jnp.float32),
            pltpu.VMEM((2, 4 * rows, 2 * width), low),
            pltpu.VMEM((width, d), jnp.float32),
            pltpu.SemaphoreType.DMA,
            pltpu.SemaphoreType.DMA((2, 4, 3)),
            pltpu.SemaphoreType.DMA((2, 4)),
            pltpu.SemaphoreType.DMA((2,)),
            pltpu.SemaphoreType.DMA((11,)),
            pltpu.SemaphoreType.DMA((11,)),
        ],
        compiler_params=pltpu.CompilerParams(
            collective_id=cid, has_side_effects=True, vmem_limit_bytes=52 << 20
        ),
        cost_estimate=pl.CostEstimate(
            flops=64 * h * rows * width * d, bytes_accessed=130_000_000, transcendentals=0
        ),
        name="units_back",
    )(x, down, units, gate, up)


def heads_back_kernel(
    rows, scale, x_ref, w_ref, m_ref, q_ref, k_ref, v_ref, s_ref, gq_ref, gk_ref, gv_ref, d_ref,
    held, weights, mixed, queries, keys, values, seen, total_ref, load_sem, local_sem, send, recv,
):
    wide = jnp.float32
    d = w_ref.shape[1]
    low = weights.dtype
    pairs = (
        (w_ref, weights), (q_ref, queries), (k_ref, keys), (v_ref, values), (s_ref, seen),
        (m_ref, mixed),
    )
    loads = [
        pltpu.make_async_copy(src, dst, load_sem.at[i]) for i, (src, dst) in enumerate(pairs)
    ]
    for copy in loads:
        copy.start()
    back = (((1,), (1,)), ((), ()))

    def prepare(t):
        if t == 0:
            for copy in loads:
                copy.wait()
            gk_ref[...] = jnp.zeros_like(gk_ref)
            gv_ref[...] = jnp.zeros_like(gv_ref)

    def consume(t, first, pieces):
        part = slice(first * rows, (first + len(pieces)) * rows)
        grad_mixed = lax.dot_general(
            held[t, part, :], weights[...], back, preferred_element_type=wide
        )
        grad_mixed = grad_mixed.astype(low)
        spans = []
        for j, (half, who) in enumerate(pieces):
            span = pl.ds(pl.multiple_of(who * rows, rows), rows)
            spans.append(mixed[half, span, :])
            query = queries[half, span, :]
            grad = grad_mixed[j * rows : (j + 1) * rows]
            score = lax.dot_general(query, keys[half], back, preferred_element_type=wide) * scale
            score = jnp.where(seen[half, span, :] > 0, score, NEGATIVE)
            power = jnp.exp(score - jnp.max(score, axis=-1, keepdims=True))
            prob = power / jnp.sum(power, axis=-1, keepdims=True)
            slope = lax.dot_general(grad, values[half], back, preferred_element_type=wide)
            mean = jnp.sum(prob * slope, axis=-1, keepdims=True)
            flow = (prob * (slope - mean)).astype(low)
            gq_ref[half, span, :] = jnp.dot(flow, keys[half], preferred_element_type=wide) * scale
            gk_ref[half] += jnp.dot(flow.T, query, preferred_element_type=wide) * scale
            gv_ref[half] += jnp.dot(prob.astype(low).T, grad, preferred_element_type=wide)
        turned = jnp.concatenate(spans, axis=0).T

        block = d_ref.shape[-1]

        @pl.loop(0, d // block)
        def _(n):
            cut = pl.ds(pl.multiple_of(n * block, block), block)
            value = jnp.dot(turned, held[t, part, cut], preferred_element_type=wide)
            if t > 0:
                value = value + total_ref[:, cut]
            if first == 0:
                total_ref[:, cut] = value
            else:
                d_ref[n] = value.astype(d_ref.dtype)

    rounds_of(rows, x_ref, held, local_sem, send, recv, consume, prepare)


def heads_back(x, output, mixed, query, key, value, visible, scale, tiers, cid):
    h, rows, d = x.shape
    low = x.dtype
    grad = jax.ShapeDtypeStruct(query.shape, jnp.float32)
    return pl.pallas_call(
        functools.partial(heads_back_kernel, rows, scale),
        out_shape=(
            grad,
            grad,
            grad,
            jax.ShapeDtypeStruct((tiers, output.shape[0], d // tiers), low),
        ),
        in_specs=[pl.BlockSpec(memory_space=pl.ANY)] * 7,
        out_specs=[pl.BlockSpec(memory_space=pltpu.VMEM)] * 4,
        scratch_shapes=[
            pltpu.VMEM((4, 4 * rows, d), low),
            pltpu.VMEM(output.shape, low),
            pltpu.VMEM(mixed.shape, low),
            pltpu.VMEM(query.shape, low),
            pltpu.VMEM(query.shape, low),
            pltpu.VMEM(query.shape, low),
            pltpu.VMEM(visible.shape, visible.dtype),
            pltpu.VMEM(output.shape, jnp.float32),
            pltpu.SemaphoreType.DMA((6,)),
            pltpu.SemaphoreType.DMA((2,)),
            pltpu.SemaphoreType.DMA((11,)),
            pltpu.SemaphoreType.DMA((11,)),
        ],
        compiler_params=pltpu.CompilerParams(
            collective_id=cid, has_side_effects=True, vmem_limit_bytes=60 << 20
        ),
        cost_estimate=pl.CostEstimate(
            flops=20_000_000_000, bytes_accessed=130_000_000, transcendentals=0
        ),
        name="heads_back",
    )(x, output, mixed, query, key, value, visible)


def total_kernel(x_ref, o_ref, sums, got, tier_sums, send, recv):
    c, sib, xn, yn = partners()
    r = lax.axis_index("row")
    tiers = lax.axis_size("row")
    others = [lax.rem(r + k, tiers) for k in range(1, tiers)]
    barrier = pltpu.get_barrier_semaphore()
    for d in (sib, xn, yn):
        pl.semaphore_signal(barrier, inc=1, device_id={"col": d}, device_id_type=MESH)
    for d in others:
        pl.semaphore_signal(barrier, inc=1, device_id={"row": d}, device_id_type=MESH)
    pl.semaphore_wait(barrier, 3 + len(others))
    sums[0] = x_ref[...]
    for i, dev in enumerate((sib, xn, yn)):
        copy = pltpu.make_async_remote_copy(
            src_ref=sums.at[i],
            dst_ref=got.at[i],
            send_sem=send.at[i],
            recv_sem=recv.at[i],
            device_id={"col": dev},
            device_id_type=MESH,
        )
        copy.start()
        copy.wait()
        sums[i + 1] = sums[i] + got[i]
    tier_sums[r] = sums[3]
    copies = []
    for k, d in enumerate(others):
        copy = pltpu.make_async_remote_copy(
            src_ref=sums.at[3],
            dst_ref=tier_sums.at[r],
            send_sem=send.at[3 + k],
            recv_sem=recv.at[3 + k],
            device_id={"row": d},
            device_id_type=MESH,
        )
        copy.start()
        copies.append(copy)
    for copy in copies:
        copy.wait()
    result = tier_sums[0]
    for k in range(1, tiers):
        result = result + tier_sums[k]
    o_ref[...] = result


def total(x, tiers, cid):
    return pl.pallas_call(
        total_kernel,
        out_shape=jax.ShapeDtypeStruct(x.shape, x.dtype),
        in_specs=[pl.BlockSpec(memory_space=pltpu.VMEM)],
        out_specs=pl.BlockSpec(memory_space=pltpu.VMEM),
        scratch_shapes=[
            pltpu.VMEM((4, *x.shape), x.dtype),
            pltpu.VMEM((3, *x.shape), x.dtype),
            pltpu.VMEM((tiers, *x.shape), x.dtype),
            pltpu.SemaphoreType.DMA((2 + tiers,)),
            pltpu.SemaphoreType.DMA((2 + tiers,)),
        ],
        compiler_params=pltpu.CompilerParams(collective_id=cid, has_side_effects=True),
        cost_estimate=pl.CostEstimate(flops=0, bytes_accessed=40_000_000, transcendentals=0),
        name="total",
    )(x)


def after(value, *earlier):
    return lax.optimization_barrier((value, *earlier))[0]


def general_body(
    hidden,
    per_layer,
    lengths,
    block_ids,
    out_grad,
    query_weight,
    key_weight,
    value_weight,
    output_weight,
    gate_weight,
    up_weight,
    down_weight,
    laurel_left,
    laurel_right,
    layer_gate,
    layer_proj,
    norm_gains,
    head_gains,
):
    local_rows = hidden.shape[0]
    seq_groups = hidden.shape[1]
    col_index = lax.axis_index("col")
    row_index = lax.axis_index("row")
    all_lengths = lengths
    lengths = lax.dynamic_slice_in_dim(all_lengths, row_index * seq_groups, seq_groups, 0)
    (
        query_cols,
        key_cols,
        value_cols,
        output_rows,
        gate_cols,
        up_cols,
        down_rows,
        left_cols,
        right_rows,
        gate_layer_cols,
        proj_layer_rows,
    ) = (
        lax.all_gather(query_weight, "row", axis=0, tiled=True),
        lax.all_gather(key_weight, "row", axis=0, tiled=True),
        lax.all_gather(value_weight, "row", axis=0, tiled=True),
        lax.all_gather(output_weight, "row", axis=1, tiled=True),
        lax.all_gather(gate_weight, "row", axis=0, tiled=True),
        lax.all_gather(up_weight, "row", axis=0, tiled=True),
        lax.all_gather(down_weight, "row", axis=1, tiled=True),
        lax.all_gather(laurel_left, "row", axis=0, tiled=True),
        lax.all_gather(laurel_right, "row", axis=1, tiled=True),
        lax.all_gather(layer_gate, "row", axis=0, tiled=True),
        lax.all_gather(layer_proj, "row", axis=1, tiled=True),
    )
    (
        query_full,
        key_full,
        value_full,
        output_full,
        left_full,
        right_full,
        gate_layer_full,
        proj_layer_full,
    ) = (
        lax.all_gather(query_cols, "col", axis=1, tiled=True),
        lax.all_gather(key_cols, "col", axis=1, tiled=True),
        lax.all_gather(value_cols, "col", axis=1, tiled=True),
        lax.all_gather(output_rows, "col", axis=0, tiled=True),
        lax.all_gather(left_cols, "col", axis=1, tiled=True),
        lax.all_gather(right_rows, "col", axis=0, tiled=True),
        lax.all_gather(gate_layer_cols, "col", axis=1, tiled=True),
        lax.all_gather(proj_layer_rows, "col", axis=0, tiled=True),
    )
    paired = jnp.concatenate([gate_cols, up_cols], axis=1)
    unit_width = gate_cols.shape[1]
    first_position = col_index * local_rows
    positions = first_position + jnp.arange(local_rows, dtype=jnp.int32)
    live_mask = positions[:, None] < lengths[None, :]
    keep_mask = live_mask.astype(jnp.float32)[:, :, None]
    reach_back = (WINDOW + local_rows - 2) // local_rows
    reach_ahead = (BLOCK + local_rows - 2) // local_rows
    key_span = (reach_back + 1 + reach_ahead) * local_rows
    key_position = first_position - reach_back * local_rows + jnp.arange(key_span, dtype=jnp.int32)
    filler_low = jnp.full((seq_groups, reach_back * local_rows), FAR_BLOCK, jnp.int32)
    filler_high = jnp.full((seq_groups, reach_ahead * local_rows), FAR_BLOCK, jnp.int32)
    padded_blocks = jnp.concatenate([filler_low, block_ids, filler_high], axis=1)
    key_blocks = lax.dynamic_slice_in_dim(padded_blocks, first_position, key_span, 1)
    query_blocks = lax.dynamic_slice_in_dim(block_ids, first_position, local_rows, 1)
    key_live = (key_position[None, :] >= 0) & (key_position[None, :] < lengths[:, None])
    query_live = positions[None, :] < lengths[:, None]
    distance = positions[:, None] - key_position[None, :]
    nearby = (query_blocks[:, :, None] >= key_blocks[:, None, :]) & (distance < WINDOW)[None]
    nearby = nearby & query_live[:, :, None] & key_live[:, None, :]
    visible = (nearby | (distance == 0)[None])[:, None, None]
    residual = hidden.astype(jnp.float32)
    normed_value, input_back = jax.vjp(input_norm, residual, norm_gains)
    normed_low = normed_value.astype(jnp.bfloat16)
    half_width = HD // 2
    frequency = jnp.exp(jnp.arange(half_width, dtype=jnp.float32) * (-2.0 * math.log(10000.0) / HD))
    angles = (positions.astype(jnp.float32)[:, None] * frequency[None, :])[:, None, None, :]

    def prepare(query_in, key_in, value_in, gain_rows):
        return (
            rotate(root_norm(query_in, gain_rows[0]), angles),
            rotate(root_norm(key_in, gain_rows[1]), angles),
            plain_norm(value_in),
        )

    query_raw = matmul_last(normed_low, query_full).reshape(local_rows, seq_groups, H, HD)
    key_raw = matmul_last(normed_low, key_full).reshape(local_rows, seq_groups, KV, HD)
    value_raw = matmul_last(normed_low, value_full).reshape(local_rows, seq_groups, KV, HD)
    (query_value, key_value, value_value), head_back = jax.vjp(
        prepare, query_raw, key_raw, value_raw, head_gains
    )
    query_low = query_value.astype(jnp.bfloat16).reshape(local_rows, seq_groups, KV, H // KV, HD)
    key_low = key_value.astype(jnp.bfloat16)
    value_low = value_value.astype(jnp.bfloat16)
    offsets = list(range(reach_back, -reach_ahead - 1, -1))
    key_parts = []
    value_parts = []
    for offset in offsets:
        if offset == 0:
            key_parts.append(key_low)
            value_parts.append(value_low)
        else:
            moved_key, moved_value = passed_along((key_low, value_low), "col", offset)
            key_parts.append(moved_key)
            value_parts.append(moved_value)
    near_keys = jnp.concatenate(key_parts, axis=0)
    near_values = jnp.concatenate(value_parts, axis=0)
    score_scale = HD ** (-0.5)

    def score_all():
        raw_scores = (
            jnp.einsum(
                "psjgd,esjd->sjgpe", query_low, near_keys, preferred_element_type=jnp.float32
            )
            * score_scale
        )
        return jnp.where(visible, raw_scores, NEGATIVE)

    scores = score_all()
    row_max = jnp.max(scores, axis=-1, keepdims=True)
    exponent = jnp.exp(scores - row_max)
    row_total = jnp.sum(exponent, axis=-1, keepdims=True)
    attn_prob = exponent / row_total
    log_total = row_max + jnp.log(row_total)
    mixed_heads = jnp.einsum(
        "sjgpe,esjd->psjgd",
        attn_prob.astype(jnp.bfloat16),
        near_values,
        preferred_element_type=jnp.float32,
    )
    mixed_low = mixed_heads.reshape(local_rows, seq_groups, H * HD).astype(jnp.bfloat16)
    out_proj = matmul_last(mixed_low, output_full)
    laurel_mid = matmul_last(normed_low, left_full).astype(jnp.bfloat16)
    low_rank = matmul_last(laurel_mid, right_full)
    (after_attention, feed_normed), middle_back = jax.vjp(
        middle, residual, out_proj, low_rank, normed_low.astype(jnp.float32), norm_gains
    )
    feed_low = feed_normed.astype(jnp.bfloat16)
    gate_up = matmul_last(lax.all_gather(feed_low, "col", axis=0, tiled=True), paired)
    unit_value, gate_back = jax.vjp(
        gated_product, gate_up[..., :unit_width], gate_up[..., unit_width:]
    )
    units_low = unit_value.astype(jnp.bfloat16)
    summed = lax.psum_scatter(
        matmul_last(units_low, down_rows), "col", scatter_dimension=0, tiled=True
    )
    after_feed, feed_back = jax.vjp(feed_join, after_attention, summed, norm_gains)
    feed_round = after_feed.astype(jnp.bfloat16)
    layer_pre = matmul_last(feed_round, gate_layer_full)
    layer_input = per_layer.astype(jnp.float32)
    layer_value, layer_back = jax.vjp(gated_product, layer_pre, layer_input)
    layer_low = layer_value.astype(jnp.bfloat16)
    projected = matmul_last(layer_low, proj_layer_full)
    out_value, final_back = jax.vjp(final_join, after_feed, projected, norm_gains)
    square_sums = jnp.stack(
        [
            jnp.sum(keep_mask * residual * residual),
            jnp.sum(keep_mask * after_attention * after_attention),
            jnp.sum(keep_mask * after_feed * after_feed),
            jnp.sum(keep_mask * out_value * out_value),
        ]
    )
    valid_count = jnp.sum(all_lengths).astype(jnp.float32)
    cotangent = out_grad.astype(jnp.float32) * keep_mask
    grad_feed_out, grad_projected, gains_final = final_back(cotangent)
    projected_low = grad_projected.astype(jnp.bfloat16)
    grad_proj_layer = outer_sum(layer_low, projected_low)
    grad_layer_pre, grad_layer_input = layer_back(matmul_back(projected_low, proj_layer_full))
    layer_pre_low = grad_layer_pre.astype(jnp.bfloat16)
    grad_gate_layer = outer_sum(feed_round, layer_pre_low)
    grad_after_feed = grad_feed_out + matmul_back(layer_pre_low, gate_layer_full)
    grad_after_attention_a, grad_summed, gains_feed = feed_back(grad_after_feed)
    summed_low = grad_summed.astype(jnp.bfloat16)
    block_rows = lax.all_gather(summed_low, "col", axis=0, tiled=True)
    grad_down = outer_sum(units_low, block_rows)
    grad_units = matmul_back(block_rows, down_rows)
    grad_down, grad_units = (grad_down, grad_units)
    grad_gate_value, grad_up_value = gate_back(grad_units)
    grad_paired = jnp.concatenate([grad_gate_value, grad_up_value], axis=-1).astype(jnp.bfloat16)
    grad_weights_paired = outer_sum(
        lax.all_gather(feed_low, "col", axis=0, tiled=True), grad_paired
    )
    grad_feed = lax.psum_scatter(
        matmul_back(grad_paired, paired).astype(jnp.bfloat16),
        "col",
        scatter_dimension=0,
        tiled=True,
    ).astype(jnp.float32)
    grad_residual_mid, grad_out_proj, grad_low_rank, grad_normed_mid, gains_middle = middle_back(
        (grad_after_attention_a, grad_feed)
    )
    out_proj_low = grad_out_proj.astype(jnp.bfloat16)
    grad_output = outer_sum(mixed_low, out_proj_low)
    grad_mixed = matmul_back(out_proj_low, output_full).astype(jnp.bfloat16)
    grad_mixed = grad_mixed.reshape(local_rows, seq_groups, KV, H // KV, HD)
    low_rank_grad = grad_low_rank.astype(jnp.bfloat16)
    grad_right = outer_sum(laurel_mid, low_rank_grad)
    grad_laurel_mid = matmul_back(low_rank_grad, right_full).astype(jnp.bfloat16)
    grad_left = outer_sum(normed_low, grad_laurel_mid)
    scores = score_all()
    attn_prob = jnp.exp(scores - log_total)
    grad_prob = jnp.einsum(
        "psjgd,esjd->sjgpe", grad_mixed, near_values, preferred_element_type=jnp.float32
    )
    grad_scores = (
        attn_prob * (grad_prob - jnp.sum(attn_prob * grad_prob, axis=-1, keepdims=True))
    ).astype(jnp.bfloat16)
    grad_queries = (
        jnp.einsum("sjgpe,esjd->psjgd", grad_scores, near_keys, preferred_element_type=jnp.float32)
        * score_scale
    )
    grad_near_keys = (
        jnp.einsum("sjgpe,psjgd->esjd", grad_scores, query_low, preferred_element_type=jnp.float32)
        * score_scale
    )
    grad_near_values = jnp.einsum(
        "sjgpe,psjgd->esjd",
        attn_prob.astype(jnp.bfloat16),
        grad_mixed,
        preferred_element_type=jnp.float32,
    )
    grad_key_total = grad_near_keys[reach_back * local_rows : (reach_back + 1) * local_rows]
    grad_value_total = grad_near_values[reach_back * local_rows : (reach_back + 1) * local_rows]
    for slot_index, offset in enumerate(offsets):
        if offset != 0:
            piece_keys = grad_near_keys[slot_index * local_rows : (slot_index + 1) * local_rows]
            piece_values = grad_near_values[slot_index * local_rows : (slot_index + 1) * local_rows]
            back_keys, back_values = (
                passed_along(piece_keys.astype(jnp.bfloat16), "col", -offset).astype(
                    piece_keys.dtype
                ),
                passed_along(piece_values.astype(jnp.bfloat16), "col", -offset).astype(
                    piece_values.dtype
                ),
            )
            grad_key_total = grad_key_total + back_keys
            grad_value_total = grad_value_total + back_values
    grad_query_raw, grad_key_raw, grad_value_raw, grad_heads = head_back(
        (grad_queries.reshape(local_rows, seq_groups, H, HD), grad_key_total, grad_value_total)
    )
    query_grad_low = grad_query_raw.reshape(local_rows, seq_groups, H * HD).astype(jnp.bfloat16)
    key_grad_low = grad_key_raw.reshape(local_rows, seq_groups, KV * HD).astype(jnp.bfloat16)
    value_grad_low = grad_value_raw.reshape(local_rows, seq_groups, KV * HD).astype(jnp.bfloat16)
    grad_query = outer_sum(normed_low, query_grad_low)
    grad_key = outer_sum(normed_low, key_grad_low)
    grad_value = outer_sum(normed_low, value_grad_low)
    grad_normed = (
        grad_normed_mid
        + matmul_back(grad_laurel_mid, left_full)
        + matmul_back(query_grad_low, query_full)
        + matmul_back(key_grad_low, key_full)
        + matmul_back(value_grad_low, value_full)
    )
    grad_residual_in, gains_input = input_back(grad_normed)
    d_hidden = (grad_residual_mid + grad_residual_in).astype(jnp.bfloat16)
    d_per_layer = grad_layer_input.astype(jnp.bfloat16)
    grad_gains = gains_final + gains_feed + gains_middle + gains_input
    grad_gate = grad_weights_paired[:, :unit_width]
    grad_up = grad_weights_paired[:, unit_width:]
    (
        query_part,
        key_part,
        value_part,
        output_part,
        left_part,
        right_part,
        gate_layer_part,
        proj_layer_part,
    ) = (
        lax.psum_scatter(
            grad_query.astype(jnp.bfloat16), "col", scatter_dimension=1, tiled=True
        ).astype(jnp.float32),
        lax.psum_scatter(
            grad_key.astype(jnp.bfloat16), "col", scatter_dimension=1, tiled=True
        ).astype(jnp.float32),
        lax.psum_scatter(
            grad_value.astype(jnp.bfloat16), "col", scatter_dimension=1, tiled=True
        ).astype(jnp.float32),
        lax.psum_scatter(
            grad_output.astype(jnp.bfloat16), "col", scatter_dimension=0, tiled=True
        ).astype(jnp.float32),
        lax.psum_scatter(
            grad_left.astype(jnp.bfloat16), "col", scatter_dimension=1, tiled=True
        ).astype(jnp.float32),
        lax.psum_scatter(
            grad_right.astype(jnp.bfloat16), "col", scatter_dimension=0, tiled=True
        ).astype(jnp.float32),
        lax.psum_scatter(
            grad_gate_layer.astype(jnp.bfloat16), "col", scatter_dimension=1, tiled=True
        ).astype(jnp.float32),
        lax.psum_scatter(
            grad_proj_layer.astype(jnp.bfloat16), "col", scatter_dimension=0, tiled=True
        ).astype(jnp.float32),
    )
    (
        d_query_weight,
        d_key_weight,
        d_value_weight,
        d_output_weight,
        d_gate_weight,
        d_up_weight,
        d_down_weight,
        d_laurel_left,
        d_laurel_right,
        d_layer_gate,
        d_layer_proj,
    ) = (
        lax.psum_scatter(
            query_part.astype(jnp.bfloat16), "row", scatter_dimension=0, tiled=True
        ).astype(jnp.float32),
        lax.psum_scatter(
            key_part.astype(jnp.bfloat16), "row", scatter_dimension=0, tiled=True
        ).astype(jnp.float32),
        lax.psum_scatter(
            value_part.astype(jnp.bfloat16), "row", scatter_dimension=0, tiled=True
        ).astype(jnp.float32),
        lax.psum_scatter(
            output_part.astype(jnp.bfloat16), "row", scatter_dimension=1, tiled=True
        ).astype(jnp.float32),
        lax.psum_scatter(
            grad_gate.astype(jnp.bfloat16), "row", scatter_dimension=0, tiled=True
        ).astype(jnp.float32),
        lax.psum_scatter(
            grad_up.astype(jnp.bfloat16), "row", scatter_dimension=0, tiled=True
        ).astype(jnp.float32),
        lax.psum_scatter(
            grad_down.astype(jnp.bfloat16), "row", scatter_dimension=1, tiled=True
        ).astype(jnp.float32),
        lax.psum_scatter(
            left_part.astype(jnp.bfloat16), "row", scatter_dimension=0, tiled=True
        ).astype(jnp.float32),
        lax.psum_scatter(
            right_part.astype(jnp.bfloat16), "row", scatter_dimension=1, tiled=True
        ).astype(jnp.float32),
        lax.psum_scatter(
            gate_layer_part.astype(jnp.bfloat16), "row", scatter_dimension=0, tiled=True
        ).astype(jnp.float32),
        lax.psum_scatter(
            proj_layer_part.astype(jnp.bfloat16), "row", scatter_dimension=1, tiled=True
        ).astype(jnp.float32),
    )
    d_norm_gains, d_head_gains, total_squares = lax.psum(
        (grad_gains, grad_heads, square_sums), ("row", "col")
    )
    stats = jnp.sqrt(total_squares / (valid_count * D))
    output = out_value.astype(jnp.bfloat16)
    return (
        output,
        stats,
        d_hidden,
        d_per_layer,
        d_query_weight,
        d_key_weight,
        d_value_weight,
        d_output_weight,
        d_gate_weight,
        d_up_weight,
        d_down_weight,
        d_laurel_left,
        d_laurel_right,
        d_layer_gate,
        d_layer_proj,
        d_norm_gains,
        d_head_gains,
    )


def swap(array):
    return jnp.swapaxes(array, 0, 1)


def heads_body(
    hidden,
    per_layer,
    lengths,
    block_ids,
    out_grad,
    query_weight,
    key_weight,
    value_weight,
    output_weight,
    gate_weight,
    up_weight,
    down_weight,
    laurel_left,
    laurel_right,
    layer_gate,
    layer_proj,
    norm_gains,
    head_gains,
):
    low = jnp.bfloat16
    rows = hidden.shape[0]
    groups = hidden.shape[1]
    cols = lax.axis_size("col")
    seq = rows * cols
    share = cols // KV
    col_index = lax.axis_index("col")
    row_index = lax.axis_index("row")
    all_lengths = lengths
    lengths = lax.dynamic_slice_in_dim(all_lengths, row_index * groups, groups, 0)

    laurel = jnp.concatenate([laurel_left.T, laurel_right], axis=0)
    small = [key_weight.T, value_weight.T, layer_gate.T, layer_proj, laurel]
    heights = [key_weight.shape[1], value_weight.shape[1], layer_gate.shape[1]]
    heights += [layer_proj.shape[0], laurel_left.shape[1], laurel_right.shape[0]]
    edges = [sum(heights[:i]) for i in range(len(heights) + 1)]
    unit_width = gate_weight.shape[1]
    residual = swap(hidden).astype(jnp.float32)
    normed_value, input_back = jax.vjp(input_norm, residual, norm_gains)
    normed_low = normed_value.astype(low)
    tiers = lax.axis_size("row")
    normed_all, small_row, query_full, output_full, both_weights = open_all(
        normed_low, query_weight, output_weight, gate_weight, up_weight, small, tiers, 1
    )
    small_all = share_small(small_row, heights[0] + heights[1], 8)
    paired = lax.all_gather(both_weights, "row", axis=0, tiled=True)
    down_full = lax.all_gather(after(down_weight, normed_all), "row", axis=1, tiled=True)
    query_full = query_full.reshape(D, HD).T
    output_full = jnp.swapaxes(output_full, 0, 1).reshape(HD, D)
    pieces = [small_all[:, :, a:b] for a, b in zip(edges[:-1], edges[1:])]
    group_start = (col_index // share) * share

    def joined(piece):
        return jnp.swapaxes(piece, 1, 2).reshape(-1, D)

    key_full, value_full = (
        joined(lax.dynamic_slice_in_dim(piece, group_start, share, 0)) for piece in pieces[:2]
    )
    gate_layer_full, proj_layer_full, left_full, right_full = (
        joined(piece) for piece in pieces[2:]
    )
    head_weights = jnp.concatenate([query_full, key_full, value_full], axis=0)

    positions = jnp.arange(seq, dtype=jnp.int32)
    mine = col_index * rows + jnp.arange(rows, dtype=jnp.int32)
    keep_mask = (mine[None, :] < lengths[:, None]).astype(jnp.float32)[:, :, None]
    live = positions[None, :] < lengths[:, None]
    distance = positions[:, None] - positions[None, :]
    nearby = (block_ids[:, :, None] >= block_ids[:, None, :]) & (distance < WINDOW)[None]
    nearby = nearby & live[:, :, None] & live[:, None, :]
    visible = nearby | (distance == 0)[None]

    half_width = HD // 2
    frequency = jnp.exp(jnp.arange(half_width, dtype=jnp.float32) * (-2.0 * math.log(10000.0) / HD))
    angles = (positions.astype(jnp.float32)[:, None] * frequency[None, :])[None]

    def prepare(query_in, key_in, value_in, gain_rows):
        return (
            rotate(root_norm(query_in, gain_rows[0]), angles),
            rotate(root_norm(key_in, gain_rows[1]), angles),
            plain_norm(value_in),
        )

    head_raw = matmul_back(normed_all, head_weights)
    query_raw, key_raw, value_raw = jnp.split(head_raw, 3, axis=-1)
    (query_value, key_value, value_value), head_back = jax.vjp(
        prepare, query_raw, key_raw, value_raw, head_gains
    )
    query_low = query_value.astype(low)
    key_low = key_value.astype(low)
    value_low = value_value.astype(low)
    score_scale = HD ** (-0.5)

    def score_all():
        raw_scores = (
            jnp.einsum("spd,sed->spe", query_low, key_low, preferred_element_type=jnp.float32)
            * score_scale
        )
        return jnp.where(visible, raw_scores, NEGATIVE)

    scores = score_all()
    row_max = jnp.max(scores, axis=-1, keepdims=True)
    exponent = jnp.exp(scores - row_max)
    row_total = jnp.sum(exponent, axis=-1, keepdims=True)
    attn_prob = exponent / row_total
    mixed_low = jnp.einsum(
        "spe,sed->spd", attn_prob.astype(low), value_low, preferred_element_type=jnp.float32
    ).astype(low)
    out_proj = product_sum(mixed_low, output_full, False, 2)
    laurel_mid = matmul_back(normed_low, left_full).astype(low)
    low_rank = matmul_last(laurel_mid, right_full)
    (after_attention, feed_normed), middle_back = jax.vjp(
        middle, residual, out_proj, low_rank, normed_low.astype(jnp.float32), norm_gains
    )
    feed_all = spread(feed_normed.astype(low), 0)
    gate_value = matmul_last(feed_all, paired[:, :unit_width])
    up_value = matmul_last(feed_all, paired[:, unit_width:])
    units_low = gated_product(gate_value, up_value).astype(low)
    units_low, query_low, key_low, value_low, seen, head_weights = lax.optimization_barrier(
        (units_low, query_low, key_low, value_low, visible.astype(jnp.float32), head_weights)
    )
    summed = product_sum(units_low, down_full, False, 5)
    after_feed, feed_back = jax.vjp(feed_join, after_attention, summed, norm_gains)
    feed_round = after_feed.astype(low)
    layer_pre = matmul_back(feed_round, gate_layer_full)
    layer_input = swap(per_layer).astype(jnp.float32)
    layer_value, layer_back = jax.vjp(gated_product, layer_pre, layer_input)
    layer_low = layer_value.astype(low)
    projected = matmul_last(layer_low, proj_layer_full)
    out_value, final_back = jax.vjp(final_join, after_feed, projected, norm_gains)
    square_sums = jnp.stack(
        [
            jnp.sum(keep_mask * residual * residual),
            jnp.sum(keep_mask * after_attention * after_attention),
            jnp.sum(keep_mask * after_feed * after_feed),
            jnp.sum(keep_mask * out_value * out_value),
        ]
    )
    valid_count = jnp.sum(all_lengths).astype(jnp.float32)

    cotangent = swap(out_grad).astype(jnp.float32) * keep_mask
    grad_feed_out, grad_projected, gains_final = final_back(cotangent)
    projected_low = grad_projected.astype(low)
    grad_proj_layer = outer_sum(layer_low, projected_low)
    grad_layer_pre, grad_layer_input = layer_back(matmul_back(projected_low, proj_layer_full))
    layer_pre_low = grad_layer_pre.astype(low)
    grad_gate_layer = outer_sum(layer_pre_low, feed_round)
    grad_after_feed = grad_feed_out + matmul_last(layer_pre_low, gate_layer_full)
    grad_after_attention_a, grad_summed, gains_feed = feed_back(grad_after_feed)
    grad_paired, grad_down = units_back(
        grad_summed.astype(low), down_full, units_low, gate_value, up_value, tiers, 9
    )
    d_down_weight = lax.psum_scatter(grad_down, "row", scatter_dimension=0)
    grad_feed, grad_both = product_sum(grad_paired, paired, True, 6, feed_all)
    d_both = lax.psum_scatter(grad_both, "row", scatter_dimension=0, tiled=True)
    grad_residual_mid, grad_out_proj, grad_low_rank, grad_normed_mid, gains_middle = middle_back(
        (grad_after_attention_a, grad_feed)
    )
    grad_queries, grad_keys, grad_values, grad_output = heads_back(
        after(grad_out_proj.astype(low), d_down_weight),
        output_full,
        mixed_low,
        query_low,
        key_low,
        value_low,
        seen,
        score_scale,
        tiers,
        10,
    )
    low_rank_grad = grad_low_rank.astype(low)
    grad_right = outer_sum(laurel_mid, low_rank_grad)
    grad_laurel_mid = matmul_back(low_rank_grad, right_full).astype(low)
    grad_left = outer_sum(grad_laurel_mid, normed_low)
    grad_query_raw, grad_key_raw, grad_value_raw, grad_heads = head_back(
        (grad_queries, grad_keys, grad_values)
    )
    head_grads = jnp.concatenate([grad_query_raw, grad_key_raw, grad_value_raw], axis=-1)
    head_grads = head_grads.astype(low)
    grad_head_weights = outer_sum(head_grads, normed_all).astype(low)
    grad_query, grad_key, grad_value = jnp.split(grad_head_weights, 3, axis=0)
    grad_group = jnp.concatenate(
        [grad_key.reshape(share, -1, D), grad_value.reshape(share, -1, D)], axis=1
    )
    grad_rest = jnp.concatenate(
        [
            piece.astype(low).reshape(cols, -1, D)
            for piece in (grad_gate_layer, grad_proj_layer, grad_left, grad_right)
        ],
        axis=1,
    )
    half = grad_rest.shape[1] // 2
    grad_rest = jnp.swapaxes(grad_rest.reshape(cols, 2, half, D), 0, 1)
    rest_part, group_part = fold_small(grad_rest.reshape(2, cols * half, D), grad_group, 3)

    def by_row(array):
        return jnp.swapaxes(array.astype(low).reshape(-1, tiers, D // tiers), 0, 1)

    parts = jnp.concatenate(
        [grad_output, by_row(grad_query), by_row(group_part), by_row(rest_part)], axis=1
    )
    grad_normed = product_sum(after(head_grads, parts), head_weights, False, 7, room=60)
    parts = after(parts, d_both, grad_normed)
    parts_out = lax.psum_scatter(parts, "row", scatter_dimension=0).astype(jnp.float32)
    d_output_weight = parts_out[:HD]
    d_query_weight = parts_out[HD : 2 * HD].T
    small_out = parts_out[2 * HD :]
    small_parts = [small_out[a:b] for a, b in zip(edges[:-1], edges[1:])]
    grad_normed = grad_normed + grad_normed_mid + matmul_last(grad_laurel_mid, left_full)
    grad_residual_in, gains_input = input_back(grad_normed)
    d_hidden = swap((grad_residual_mid + grad_residual_in).astype(low))
    d_per_layer = swap(grad_layer_input.astype(low))
    grad_gains = gains_final + gains_feed + gains_middle + gains_input
    extra = jnp.concatenate([grad_heads.reshape(-1), square_sums])
    extra = jnp.pad(extra, (0, 2 * D - extra.shape[0])).reshape(2, D)
    all_sums = jnp.concatenate([grad_gains, extra], axis=0)
    totals = total(after(all_sums, parts), tiers, 4)
    d_down_weight = after(d_down_weight, totals).astype(jnp.float32)
    d_both = after(d_both, totals).astype(jnp.float32)
    d_gate_weight = d_both[:, :unit_width]
    d_up_weight = d_both[:, unit_width:]
    d_norm_gains = totals[:6]
    d_head_gains = totals[6, : 2 * HD].reshape(2, HD)
    total_squares = totals[6, 2 * HD : 2 * HD + 4]
    stats = jnp.sqrt(total_squares / (valid_count * D))
    output = swap(out_value.astype(low))
    return (
        output,
        stats,
        d_hidden,
        d_per_layer,
        d_query_weight,
        small_parts[0].T,
        small_parts[1].T,
        d_output_weight,
        d_gate_weight,
        d_up_weight,
        d_down_weight,
        small_parts[4].T,
        small_parts[5],
        small_parts[2].T,
        small_parts[3],
        d_norm_gains,
        d_head_gains,
    )


def solution(mesh):
    body = heads_body if mesh.shape["col"] == H else general_body
    in_specs = (
        P("col", "row", None),
        P("col", "row", None),
        P(),
        P("row", None),
        P("col", "row", None),
        P("row", "col"),
        P("row", "col"),
        P("row", "col"),
        P("col", "row"),
        P("row", "col"),
        P("row", "col"),
        P("col", "row"),
        P("row", "col"),
        P("col", "row"),
        P("row", "col"),
        P("col", "row"),
        P(),
        P(),
    )
    out_specs = (
        P("col", "row", None),
        P(),
        P("col", "row", None),
        P("col", "row", None),
        P("row", "col"),
        P("row", "col"),
        P("row", "col"),
        P("col", "row"),
        P("row", "col"),
        P("row", "col"),
        P("col", "row"),
        P("row", "col"),
        P("col", "row"),
        P("row", "col"),
        P("col", "row"),
        P(),
        P(),
    )
    return jax.shard_map(body, mesh=mesh, in_specs=in_specs, out_specs=out_specs, check_vma=False)
```

```python
import functools
import math

import jax
import jax.numpy as jnp
from jax import lax
from jax.experimental import pallas as pl
from jax.experimental.pallas import tpu as pltpu
from jax.sharding import PartitionSpec as P

D = 2048
H = 8
KV = 2
HD = 256
WINDOW = 512
BLOCK = 256


EPSILON = 1e-06
FAR_BLOCK = 1 << 30
NEGATIVE = -1e30
HALF_ROOT = 1.0 / math.sqrt(2.0)
CURVE = math.sqrt(2.0 / math.pi)
BEND = 0.044715


MESH = pl.DeviceIdType.MESH


def passed_along(value, axis, steps):
    count = lax.axis_size(axis)
    initial, last = (max(0, -steps), min(count, count - steps))
    return lax.ppermute(value, axis, [(source, source + steps) for source in range(initial, last)])


def root_norm(values, gain_row):
    return (
        values * lax.rsqrt(jnp.mean(values * values, axis=-1, keepdims=True) + EPSILON) * gain_row
    )


def plain_norm(values):
    return values * lax.rsqrt(jnp.mean(values * values, axis=-1, keepdims=True) + EPSILON)


def smooth_gate(values):
    return jax.nn.gelu(values, approximate=True)


def rotate(values, angles):
    half_width = values.shape[-1] // 2
    leading = values[..., :half_width]
    trailing = values[..., half_width:]
    cosine = jnp.cos(angles)
    sine_part = jnp.sin(angles)
    return jnp.concatenate(
        [leading * cosine - trailing * sine_part, trailing * cosine + leading * sine_part], axis=-1
    )


def matmul_last(first_array, second_array):
    return lax.dot_general(
        first_array,
        second_array,
        (((first_array.ndim - 1,), (0,)), ((), ())),
        preferred_element_type=jnp.float32,
    )


def matmul_back(first_array, second_array):
    return lax.dot_general(
        first_array,
        second_array,
        (((first_array.ndim - 1,), (1,)), ((), ())),
        preferred_element_type=jnp.float32,
    )


def outer_sum(first_array, second_array):
    return lax.dot_general(
        first_array, second_array, (((0, 1), (0, 1)), ((), ())), preferred_element_type=jnp.float32
    )


def input_norm(residual, gain_rows):
    return root_norm(residual, gain_rows[0])


def middle(residual, out_proj, low_rank, normed, gain_rows):
    merged = (
        residual + root_norm(out_proj, gain_rows[1]) + normed + root_norm(low_rank, gain_rows[4])
    ) * HALF_ROOT
    return (merged, root_norm(merged, gain_rows[2]))


def feed_join(merged, summed, gain_rows):
    return merged + root_norm(summed, gain_rows[3])


def final_join(merged, projected, gain_rows):
    return merged + root_norm(projected, gain_rows[5])


def gated_product(first_array, second_array):
    return smooth_gate(first_array) * second_array


def partners():
    c = lax.axis_index("col")
    sib = c + 1 - 2 * (c % 2)
    xn = c + 2 - 4 * ((c // 2) % 2)
    yn = c + 4 - 8 * (c // 4)
    return c, sib, xn, yn

def greet(devs):
    barrier = pltpu.get_barrier_semaphore()
    for d in devs:
        pl.semaphore_signal(barrier, inc=1, device_id={"col": d}, device_id_type=MESH)
    pl.semaphore_wait(barrier, len(devs))

def spread_kernel(rows, x_ref, o_ref, local_sem, send, recv):
    c, sib, xn, yn = partners()
    def slot(half, who):
        return o_ref.at[half, pl.ds(pl.multiple_of(who * rows, rows), rows), :]
    def both(who):
        return o_ref.at[:, pl.ds(pl.multiple_of(who * rows, rows), rows), :]
    def push(i, src, dst, dev):
        return pltpu.make_async_remote_copy(src_ref=src, dst_ref=dst, send_sem=send.at[i], recv_sem=recv.at[i], device_id={"col": dev}, device_id_type=MESH)
    mine = pltpu.make_async_copy(x_ref, both(c), local_sem)
    mine.start()
    greet((sib, xn, yn))
    x0 = push(0, x_ref.at[0], slot(0, c), xn)
    y1 = push(1, x_ref.at[1], slot(1, c), yn)
    x1 = push(2, x_ref.at[1], slot(1, c), xn)
    y0 = push(3, x_ref.at[0], slot(0, c), yn)
    s = push(4, x_ref, both(c), sib)
    x0.start(); y1.start(); x1.start(); y0.start(); s.start()
    diag = yn + (xn - c)
    x0.wait_recv()
    fy = push(5, slot(0, xn), slot(0, xn), yn)
    fy.start()
    sx0 = push(6, slot(0, xn), slot(0, xn), sib)
    sx0.start()
    y1.wait_recv()
    fx = push(7, slot(1, yn), slot(1, yn), xn)
    fx.start()
    sy1 = push(8, slot(1, yn), slot(1, yn), sib)
    sy1.start()
    x1.wait_recv()
    sx1 = push(9, slot(1, xn), slot(1, xn), sib)
    sx1.start()
    y0.wait_recv()
    sy0 = push(10, slot(0, yn), slot(0, yn), sib)
    sy0.start()
    fy.wait_recv()
    sd0 = push(11, slot(0, diag), slot(0, diag), sib)
    sd0.start()
    fx.wait_recv()
    sd1 = push(12, slot(1, diag), slot(1, diag), sib)
    sd1.start()
    for cp in (s, sx0, sy1, sx1, sy0, sd0, sd1):
        cp.wait_recv()
    for cp in (x0, y1, x1, y0, s, fy, sx0, fx, sy1, sx1, sy0, sd0, sd1):
        cp.wait_send()
    mine.wait()

def spread(x, cid=0):
    h, rows, d = x.shape
    return pl.pallas_call(
        functools.partial(spread_kernel, rows),
        out_shape=jax.ShapeDtypeStruct((h, 8 * rows, d), x.dtype),
        in_specs=[pl.BlockSpec(memory_space=pl.ANY)],
        out_specs=pl.BlockSpec(memory_space=pl.ANY),
        scratch_shapes=[pltpu.SemaphoreType.DMA, pltpu.SemaphoreType.DMA((13,)), pltpu.SemaphoreType.DMA((13,))],
        compiler_params=pltpu.CompilerParams(collective_id=cid, has_side_effects=True),
        cost_estimate=pl.CostEstimate(flops=0, bytes_accessed=120_000_000, transcendentals=0),
        name="spread",
    )(x)

def fold_steps(rows, p_ref, own, sibs, dx, dy, rx, ry, local_sem, send, recv):
    c, sib, xn, yn = partners()
    diag = yn + (xn - c)
    wide = jnp.float32
    tall = 32 if rows % 32 == 0 else 8

    def blk(who):
        return p_ref.at[:, pl.ds(pl.multiple_of(who * rows, rows), rows), :]

    def push(i, src, dst, dev):
        return pltpu.make_async_remote_copy(
            src_ref=src,
            dst_ref=dst,
            send_sem=send.at[i],
            recv_sem=recv.at[i],
            device_id={"col": dev},
            device_id_type=MESH,
        )

    def add(dst, src):
        @pl.loop(0, rows // tall)
        def _(i):
            r = pl.ds(pl.multiple_of(i * tall, tall), tall)
            dst[r, :] = (dst[r, :].astype(wide) + src[r, :].astype(wide)).astype(dst.dtype)

    def pair(j):
        add(own.at[j, 0], sibs.at[j, 0])
        add(own.at[j, 1], sibs.at[j, 1])

    dests = (diag, xn, yn, c)
    loads = [pltpu.make_async_copy(blk(d), own.at[j], local_sem.at[j]) for j, d in enumerate(dests)]
    for load in loads:
        load.start()
    yield None
    sides = [push(j, blk(d + (sib - c)), sibs.at[j], sib) for j, d in enumerate(dests)]
    for side in sides:
        side.start()
    yield None
    loads[0].wait()
    sides[0].wait_recv()
    pair(0)
    a = push(4, own.at[0, 0], dx, xn)
    b = push(5, own.at[0, 1], dy, yn)
    a.start()
    b.start()
    yield None
    loads[1].wait()
    sides[1].wait_recv()
    pair(1)
    x0 = push(6, own.at[1, 0], rx.at[0], xn)
    x0.start()
    yield None
    loads[2].wait()
    sides[2].wait_recv()
    pair(2)
    y1 = push(7, own.at[2, 1], ry.at[1], yn)
    y1.start()
    yield None
    a.wait_recv()
    add(own.at[2, 0], dx)
    y0 = push(8, own.at[2, 0], ry.at[0], yn)
    y0.start()
    yield None
    b.wait_recv()
    add(own.at[1, 1], dy)
    x1 = push(9, own.at[1, 1], rx.at[1], xn)
    x1.start()
    yield None
    loads[3].wait()
    sides[3].wait_recv()
    pair(3)
    yield None
    waits = ((x0, y0), (x1, y1))
    yield tall, waits, (*sides, a, b, x0, y1, y0, x1)


def fold_finish(rows, o_ref, own, rx, ry, tall, waits, sent):
    wide = jnp.float32
    for h in range(2):
        for copy in waits[h]:
            copy.wait_recv()

        @pl.loop(0, rows // tall)
        def _(i):
            r = pl.ds(pl.multiple_of(i * tall, tall), tall)
            o_ref[h, r, :] = (
                own[3, h, r, :].astype(wide) + rx[h, r, :].astype(wide) + ry[h, r, :].astype(wide)
            )

    for copy in sent:
        copy.wait_send()


def fold_scratch(h, rows, d, kind):
    return [
        pltpu.VMEM((4, h, rows, d), kind),
        pltpu.VMEM((4, h, rows, d), kind),
        pltpu.VMEM((rows, d), kind),
        pltpu.VMEM((rows, d), kind),
        pltpu.VMEM((h, rows, d), kind),
        pltpu.VMEM((h, rows, d), kind),
        pltpu.SemaphoreType.DMA((4,)),
        pltpu.SemaphoreType.DMA((10,)),
        pltpu.SemaphoreType.DMA((10,)),
    ]


def product_kernel(rows, flip, outer, *refs):
    if outer:
        a_ref, w_ref, f_ref, o_ref, g_ref = refs[:5]
        f_buf, g_buf, turned, f_sem, g_sem = refs[-5:]
        refs = refs[5:-5]
    else:
        a_ref, w_ref, o_ref = refs[:3]
        refs = refs[3:]
    a_buf, w_buf, stage, own, sibs, dx, dy, rx, ry, local_sem, send, recv = refs
    c, sib, xn, yn = partners()
    diag = yn + (xn - c)
    wide = jnp.float32
    d = o_ref.shape[-1]
    tile = 512
    tall = 32

    def push(i, src, dst, dev):
        return pltpu.make_async_remote_copy(
            src_ref=src,
            dst_ref=dst,
            send_sem=send.at[i],
            recv_sem=recv.at[i],
            device_id={"col": dev},
            device_id_type=MESH,
        )

    dests = (diag, xn, yn, c)
    step = sib - c
    weights = pltpu.make_async_copy(w_ref, w_buf, local_sem.at[8])
    weights.start()

    def load(i, who):
        return pltpu.make_async_copy(
            a_ref.at[:, pl.ds(pl.multiple_of(who * rows, rows), rows), :],
            a_buf.at[i],
            local_sem.at[i],
        )

    far = [load(j, dests[j] + step) for j in range(4)]
    near = [load(4 + j, dests[j]) for j in range(4)]
    for first, second in zip(far, near):
        first.start()
        second.start()
    owners = [d + step for d in dests] + list(dests)
    strip = 256

    def strips(n):
        cut = pl.ds(pl.multiple_of(n * strip, strip), strip)
        return [
            pltpu.make_async_copy(
                f_ref.at[:, pl.ds(pl.multiple_of(who * rows, rows), rows), cut],
                f_buf.at[lax.rem(n, 2), i],
                f_sem.at[lax.rem(n, 2), i],
            )
            for i, who in enumerate(owners)
        ]

    def strip_out(n):
        cut = pl.ds(pl.multiple_of(n * strip, strip), strip)
        slot = lax.rem(n, 2)
        return pltpu.make_async_copy(g_buf.at[slot], g_ref.at[cut, :], g_sem.at[slot])

    def outer_product():
        count = g_ref.shape[0] // strip
        depth = a_buf.shape[-1]

        @pl.loop(0, count)
        def _(n):
            slot = lax.rem(n, 2)
            for copy in strips(n):
                copy.wait()

            @pl.when(n + 1 < count)
            def _():
                for copy in strips(n + 1):
                    copy.start()

            @pl.when(n >= 2)
            def _():
                strip_out(n - 2).wait()

            turned[...] = f_buf[slot].reshape(16 * rows, strip).T

            @pl.loop(0, depth // tile)
            def _(m):
                cut = pl.ds(pl.multiple_of(m * tile, tile), tile)
                right = a_buf[:, :, :, cut].reshape(16 * rows, tile)
                value = jnp.dot(turned[...], right, preferred_element_type=wide)
                g_buf[slot, :, cut] = value.astype(g_buf.dtype)

            strip_out(n).start()

        strip_out(count - 2).wait()
        strip_out(count - 1).wait()

    if outer:
        for copy in strips(0):
            copy.start()
    greet((sib, xn, yn))
    weights.wait()

    def product(i, put):
        left = a_buf[i].reshape(2 * rows, a_buf.shape[-1])

        @pl.loop(0, d // tile)
        def _(n):
            cut = pl.ds(pl.multiple_of(n * tile, tile), tile)
            right = w_buf[cut, :] if flip else w_buf[:, cut]
            dims = (((1,), (1,)), ((), ())) if flip else (((1,), (0,)), ((), ()))
            value = lax.dot_general(left, right, dims, preferred_element_type=wide)
            put(cut, value.reshape(2, rows, tile))

    sides = [push(j, stage.at[j], sibs.at[j], sib) for j in range(4)]

    def for_sibling(j):
        far[j].wait()

        def put(cut, value):
            stage[j, :, :, cut] = value.astype(stage.dtype)

        product(j, put)
        sides[j].start()

    def for_chip(j):
        near[j].wait()
        sides[j].wait_recv()

        def put(cut, value):
            own[j, :, :, cut] = (value + sibs[j, :, :, cut].astype(wide)).astype(own.dtype)

        product(4 + j, put)

    def add(dst, src):
        @pl.loop(0, rows // tall)
        def _(i):
            r = pl.ds(pl.multiple_of(i * tall, tall), tall)
            dst[r, :] = (dst[r, :].astype(wide) + src[r, :].astype(wide)).astype(dst.dtype)

    for_sibling(0)
    near[0].wait()

    def hold(cut, value):
        o_ref[:, :, cut] = value

    product(4, hold)
    sides[0].wait_recv()
    for h in range(2):

        @pl.loop(0, rows // tall)
        def _(i):
            r = pl.ds(pl.multiple_of(i * tall, tall), tall)
            own[0, h, r, :] = (o_ref[h, r, :] + sibs[0, h, r, :].astype(wide)).astype(own.dtype)

    a = push(4, own.at[0, 0], dx, xn)
    b = push(5, own.at[0, 1], dy, yn)
    a.start()
    b.start()
    for_sibling(1)
    for_sibling(2)
    for_chip(1)
    x0 = push(6, own.at[1, 0], rx.at[0], xn)
    x0.start()
    for_sibling(3)
    for_chip(2)
    y1 = push(7, own.at[2, 1], ry.at[1], yn)
    y1.start()
    a.wait_recv()
    add(own.at[2, 0], dx)
    y0 = push(8, own.at[2, 0], ry.at[0], yn)
    y0.start()
    b.wait_recv()
    add(own.at[1, 1], dy)
    x1 = push(9, own.at[1, 1], rx.at[1], xn)
    x1.start()
    near[3].wait()
    sides[3].wait_recv()

    def put(cut, value):
        o_ref[:, :, cut] = value + sibs[3, :, :, cut].astype(wide)

    product(7, put)
    if outer:
        outer_product()
    for h, waits in enumerate(((x0, y0), (x1, y1))):
        for copy in waits:
            copy.wait_recv()

        @pl.loop(0, rows // tall)
        def _(i):
            r = pl.ds(pl.multiple_of(i * tall, tall), tall)
            o_ref[h, r, :] = o_ref[h, r, :] + rx[h, r, :].astype(wide) + ry[h, r, :].astype(wide)

    for copy in (*sides, a, b, x0, y1, y0, x1):
        copy.wait_send()


def product_sum(left, right, flip, cid, feed=None, room=44):
    h, total, depth = left.shape
    rows = total // 8
    d = right.shape[0] if flip else right.shape[1]
    low = left.dtype
    outer = feed is not None
    out_shape = [jax.ShapeDtypeStruct((h, rows, d), jnp.float32)]
    out_specs = [pl.BlockSpec(memory_space=pltpu.VMEM)]
    scratch = [
        pltpu.VMEM((8, h, rows, depth), low),
        pltpu.VMEM(right.shape, low),
        pltpu.VMEM((4, h, rows, d), low),
        pltpu.VMEM((3, h, rows, d), low),
        pltpu.VMEM((4, h, rows, d), low),
        pltpu.VMEM((rows, d), low),
        pltpu.VMEM((rows, d), low),
        pltpu.VMEM((h, rows, d), low),
        pltpu.VMEM((h, rows, d), low),
        pltpu.SemaphoreType.DMA((9,)),
        pltpu.SemaphoreType.DMA((10,)),
        pltpu.SemaphoreType.DMA((10,)),
    ]
    flops = 2 * h * total * depth * d
    if outer:
        width = feed.shape[-1]
        flops += 2 * h * total * depth * width
        out_shape.append(jax.ShapeDtypeStruct((width, depth), low))
        out_specs.append(pl.BlockSpec(memory_space=pl.ANY))
        scratch += [
            pltpu.VMEM((2, 8, h, rows, 256), low),
            pltpu.VMEM((2, 256, depth), low),
            pltpu.VMEM((256, h * total), low),
            pltpu.SemaphoreType.DMA((2, 8)),
            pltpu.SemaphoreType.DMA((2,)),
        ]
    result = pl.pallas_call(
        functools.partial(product_kernel, rows, flip, outer),
        out_shape=out_shape,
        in_specs=[pl.BlockSpec(memory_space=pl.ANY)] * (3 if outer else 2),
        out_specs=out_specs,
        scratch_shapes=scratch,
        compiler_params=pltpu.CompilerParams(
            collective_id=cid,
            has_side_effects=True,
            vmem_limit_bytes=(52 if outer else room) << 20,
        ),
        cost_estimate=pl.CostEstimate(
            flops=flops, bytes_accessed=130_000_000, transcendentals=0
        ),
        name="product_sum",
    )(*((left, right, feed) if outer else (left, right)))
    return result if outer else result[0]


def fold_small_kernel(
    rows, p_ref, g_ref, o_ref, k_ref, own, sibs, dx, dy, rx, ry, local_sem, send, recv,
    gown, gsibs, grx, glocal, gsend, grecv,
):
    c, sib, xn, yn = partners()
    m = c % 4
    m_sib = m + 1 - 2 * (m % 2)
    m_x = m + 2 - 4 * (m // 2)
    m_diag = m_sib + (m_x - m)
    wide = jnp.float32

    def push(i, src, dst, dev):
        return pltpu.make_async_remote_copy(
            src_ref=src,
            dst_ref=dst,
            send_sem=gsend.at[i],
            recv_sem=grecv.at[i],
            device_id={"col": dev},
            device_id_type=MESH,
        )

    steps = fold_steps(rows, p_ref, own, sibs, dx, dy, rx, ry, local_sem, send, recv)
    next(steps)
    loads = [
        pltpu.make_async_copy(g_ref.at[d], gown.at[j], glocal.at[j])
        for j, d in enumerate((m_x, m))
    ]
    for load in loads:
        load.start()
    greet((sib, xn, yn))
    sides = [push(j, g_ref.at[d], gsibs.at[j], sib) for j, d in enumerate((m_diag, m_sib))]
    sides[0].start()
    next(steps)
    sides[1].start()
    tall = k_ref.shape[0] // 4
    loads[0].wait()
    sides[0].wait_recv()

    @pl.loop(0, 4)
    def _(i):
        r = pl.ds(pl.multiple_of(i * tall, tall), tall)
        gown[0, r, :] = (gown[0, r, :].astype(wide) + gsibs[0, r, :].astype(wide)).astype(
            gown.dtype
        )

    over = push(2, gown.at[0], grx, xn)
    over.start()
    last = None
    for step in steps:
        last = step if step is not None else last
    fold_finish(rows, o_ref, own, rx, ry, *last)
    loads[1].wait()
    sides[1].wait_recv()
    over.wait_recv()

    @pl.loop(0, 4)
    def _(i):
        r = pl.ds(pl.multiple_of(i * tall, tall), tall)
        k_ref[r, :] = (
            gown[1, r, :].astype(wide) + gsibs[1, r, :].astype(wide) + grx[r, :].astype(wide)
        )

    for copy in (*sides, over):
        copy.wait_send()


def fold_small(p, g, cid):
    h, total, d = p.shape
    rows = total // 8
    share, tall, _ = g.shape
    return pl.pallas_call(
        functools.partial(fold_small_kernel, rows),
        out_shape=(
            jax.ShapeDtypeStruct((h, rows, d), jnp.float32),
            jax.ShapeDtypeStruct((tall, d), jnp.float32),
        ),
        in_specs=[pl.BlockSpec(memory_space=pl.ANY)] * 2,
        out_specs=[pl.BlockSpec(memory_space=pltpu.VMEM)] * 2,
        scratch_shapes=fold_scratch(h, rows, d, p.dtype)
        + [
            pltpu.VMEM((2, tall, d), g.dtype),
            pltpu.VMEM((2, tall, d), g.dtype),
            pltpu.VMEM((tall, d), g.dtype),
            pltpu.SemaphoreType.DMA((2,)),
            pltpu.SemaphoreType.DMA((3,)),
            pltpu.SemaphoreType.DMA((3,)),
        ],
        compiler_params=pltpu.CompilerParams(
            collective_id=cid, has_side_effects=True, vmem_limit_bytes=40 << 20
        ),
        cost_estimate=pl.CostEstimate(flops=0, bytes_accessed=60_000_000, transcendentals=0),
        name="fold_small",
    )(p, g)


def open_kernel(
    rows, tiers, x_ref, q_ref, w_ref, g_ref, u_ref, *refs
):
    small = refs[:5]
    o_ref, sa_ref, qa_ref, wa_ref, both_ref = refs[5:10]
    tokens, stacked, both_buf, in_sem, local_sem, send, recv, line_send, line_recv = refs[10:]
    c, sib, xn, yn = partners()
    diag = yn + (xn - c)
    r = lax.axis_index("row")
    last = tiers - 1
    weights = []
    for src, dst in ((stacked, sa_ref), (q_ref, qa_ref), (w_ref, wa_ref)):
        cut = src.shape[0] // 32 * 16
        weights += [(src, dst, pl.ds(0, cut)), (src, dst, pl.ds(cut, src.shape[0] - cut))]
    pieces = len(weights)

    def slot(half, who):
        return o_ref.at[half, pl.ds(pl.multiple_of(who * rows, rows), rows), :]

    def both(who):
        return o_ref.at[:, pl.ds(pl.multiple_of(who * rows, rows), rows), :]

    started = []

    def push(src, dst, **dev):
        i = len(started)
        copy = pltpu.make_async_remote_copy(
            src_ref=src,
            dst_ref=dst,
            send_sem=send.at[i],
            recv_sem=recv.at[i],
            device_id=dev,
            device_id_type=MESH,
        )
        copy.start()
        started.append(copy)
        return copy

    width = g_ref.shape[1]
    first = [pltpu.make_async_copy(x_ref, tokens, in_sem.at[0])]
    base = 0
    for i, ref in enumerate(small):
        tall = ref.shape[0]
        first.append(
            pltpu.make_async_copy(ref, stacked.at[pl.ds(base, tall)], in_sem.at[1 + i])
        )
        base += tall
    later = [
        pltpu.make_async_copy(g_ref, both_buf.at[:, pl.ds(0, width)], in_sem.at[6]),
        pltpu.make_async_copy(u_ref, both_buf.at[:, pl.ds(width, width)], in_sem.at[7]),
    ]
    for copy in (*first, *later):
        copy.start()
    local = [
        pltpu.make_async_copy(tokens, both(c), local_sem.at[0]),
        pltpu.make_async_copy(stacked, sa_ref.at[r], local_sem.at[1]),
        pltpu.make_async_copy(q_ref, qa_ref.at[r], local_sem.at[2]),
        pltpu.make_async_copy(w_ref, wa_ref.at[r], local_sem.at[3]),
        pltpu.make_async_copy(both_buf, both_ref, local_sem.at[4]),
    ]
    barrier = pltpu.get_barrier_semaphore()
    for d in (sib, xn, yn):
        pl.semaphore_signal(barrier, inc=1, device_id={"col": d}, device_id_type=MESH)

    @pl.when(r < last)
    def _():
        pl.semaphore_signal(barrier, inc=1, device_id={"row": r + 1}, device_id_type=MESH)

    @pl.when(r > 0)
    def _():
        pl.semaphore_signal(barrier, inc=1, device_id={"row": r - 1}, device_id_type=MESH)

    @pl.when((r > 0) & (r < last))
    def _():
        pl.semaphore_wait(barrier, 5)

    @pl.when((r == 0) | (r == last))
    def _():
        pl.semaphore_wait(barrier, 4)

    def passing(way, hop, j):
        src, dst, cut = weights[j]
        whose = r - hop if way == 0 else r + hop
        return pltpu.make_async_remote_copy(
            src_ref=src.at[cut] if hop == 0 else dst.at[whose, cut],
            dst_ref=dst.at[whose, cut],
            send_sem=line_send.at[way, hop, j],
            recv_sem=line_recv.at[way, hop, j],
            device_id={"row": r + 1 if way == 0 else r - 1},
            device_id_type=MESH,
        )

    def going(way, hop):
        return (r < last) & (r >= hop) if way == 0 else (r > 0) & (r + hop <= last)

    def coming(way, hop):
        return r > hop if way == 0 else r + hop < last

    def forward(hop, j):
        for way in range(2):
            if hop > 0:

                @pl.when(coming(way, hop - 1))
                def _():
                    passing(way, hop - 1, j).wait_recv()

            @pl.when(going(way, hop))
            def _():
                passing(way, hop, j).start()

    for copy in first:
        copy.wait()
    x0 = push(tokens.at[0], slot(0, c), col=xn)
    y1 = push(tokens.at[1], slot(1, c), col=yn)
    for j in range(pieces):
        forward(0, j)
    x1 = push(tokens.at[1], slot(1, c), col=xn)
    y0 = push(tokens.at[0], slot(0, c), col=yn)
    push(tokens, both(c), col=sib)
    for copy in later:
        copy.wait()
    for copy in local:
        copy.start()
    forward(1, 0)
    forward(1, 1)
    x0.wait_recv()
    fy = push(slot(0, xn), slot(0, xn), col=yn)
    push(slot(0, xn), slot(0, xn), col=sib)
    y1.wait_recv()
    fx = push(slot(1, yn), slot(1, yn), col=xn)
    push(slot(1, yn), slot(1, yn), col=sib)
    for j in range(2, pieces):
        forward(1, j)
    x1.wait_recv()
    push(slot(1, xn), slot(1, xn), col=sib)
    y0.wait_recv()
    push(slot(0, yn), slot(0, yn), col=sib)
    for hop in range(2, last):
        for j in range(pieces):
            forward(hop, j)
    fy.wait_recv()
    push(slot(0, diag), slot(0, diag), col=sib)
    fx.wait_recv()
    push(slot(1, diag), slot(1, diag), col=sib)
    for copy in started:
        if not any(copy is other for other in (x0, y1, x1, y0, fy, fx)):
            copy.wait_recv()
    for j in range(pieces):
        for way in range(2):

            @pl.when(coming(way, last - 1))
            def _():
                passing(way, last - 1, j).wait_recv()

            for hop in range(last):

                @pl.when(going(way, hop))
                def _():
                    passing(way, hop, j).wait_send()

    for copy in started:
        copy.wait_send()
    for copy in local:
        copy.wait()


def open_all(x, query, output, gate, up, small, tiers, cid):
    h, rows, d = x.shape
    low = x.dtype
    stack = (sum(piece.shape[0] for piece in small), small[0].shape[1])
    both = (gate.shape[0], 2 * gate.shape[1])
    return pl.pallas_call(
        functools.partial(open_kernel, rows, tiers),
        out_shape=(
            jax.ShapeDtypeStruct((h, 8 * rows, d), low),
            jax.ShapeDtypeStruct((tiers, *stack), low),
            jax.ShapeDtypeStruct((tiers, *query.shape), low),
            jax.ShapeDtypeStruct((tiers, *output.shape), low),
            jax.ShapeDtypeStruct(both, low),
        ),
        in_specs=[pl.BlockSpec(memory_space=pl.ANY)] * 10,
        out_specs=[pl.BlockSpec(memory_space=pl.ANY)] * 5,
        scratch_shapes=[
            pltpu.VMEM(x.shape, low),
            pltpu.VMEM(stack, low),
            pltpu.VMEM(both, low),
            pltpu.SemaphoreType.DMA((8,)),
            pltpu.SemaphoreType.DMA((5,)),
            pltpu.SemaphoreType.DMA((13,)),
            pltpu.SemaphoreType.DMA((13,)),
            pltpu.SemaphoreType.DMA((2, tiers - 1, 6)),
            pltpu.SemaphoreType.DMA((2, tiers - 1, 6)),
        ],
        compiler_params=pltpu.CompilerParams(
            collective_id=cid, has_side_effects=True, vmem_limit_bytes=60 << 20
        ),
        cost_estimate=pl.CostEstimate(flops=0, bytes_accessed=200_000_000, transcendentals=0),
        name="open_all",
    )(x, query, output, gate, up, *small)


def share_kernel(near, s_ref, sa_ref, held, local_sem, send, recv):
    c, sib, xn, yn = partners()
    diag = yn + (xn - c)
    height = s_ref.shape[1]
    started = []

    def part(ref, first):
        return ref.at[:, pl.ds(0, near) if first else pl.ds(near, height - near), :]

    def push(who, first, dev, own=False):
        i = len(started)
        dst = part(sa_ref.at[who], first)
        copy = pltpu.make_async_remote_copy(
            src_ref=part(held, first) if own else dst,
            dst_ref=dst,
            send_sem=send.at[i],
            recv_sem=recv.at[i],
            device_id={"col": dev},
            device_id_type=MESH,
        )
        copy.start()
        started.append(copy)
        return copy

    fetch = pltpu.make_async_copy(s_ref, held, local_sem.at[0])
    fetch.start()
    mine = pltpu.make_async_copy(held, sa_ref.at[c], local_sem.at[1])
    greet((sib, xn, yn))
    fetch.wait()
    rx = push(c, False, xn, own=True)
    ry = push(c, False, yn, own=True)
    kx = push(c, True, xn, own=True)
    push(c, True, sib, own=True)
    push(c, False, sib, own=True)
    mine.start()
    rx.wait_recv()
    fd = push(xn, False, yn)
    push(xn, False, sib)
    ry.wait_recv()
    push(yn, False, sib)
    fd.wait_recv()
    push(diag, False, sib)
    kx.wait_recv()
    push(xn, True, sib)
    for copy in started:
        if not any(copy is other for other in (kx, rx, ry, fd)):
            copy.wait_recv()
    for copy in started:
        copy.wait_send()
    mine.wait()


def share_small(small, near, cid):
    return pl.pallas_call(
        functools.partial(share_kernel, near),
        out_shape=jax.ShapeDtypeStruct((8, *small.shape), small.dtype),
        in_specs=[pl.BlockSpec(memory_space=pl.ANY)],
        out_specs=pl.BlockSpec(memory_space=pl.ANY),
        scratch_shapes=[
            pltpu.VMEM(small.shape, small.dtype),
            pltpu.SemaphoreType.DMA((2,)),
            pltpu.SemaphoreType.DMA((10,)),
            pltpu.SemaphoreType.DMA((10,)),
        ],
        compiler_params=pltpu.CompilerParams(collective_id=cid, has_side_effects=True),
        cost_estimate=pl.CostEstimate(flops=0, bytes_accessed=60_000_000, transcendentals=0),
        name="share_small",
    )(small)


def rounds_of(rows, x_ref, held, local_sem, send, recv, consume, prepare):
    c, sib, xn, yn = partners()
    diag = yn + (xn - c)
    step = sib - c

    def place(t, j, n=1):
        return held.at[t, pl.ds(j * rows, n * rows), :]

    started = []

    def push(src, dst, dev):
        i = len(started)
        copy = pltpu.make_async_remote_copy(
            src_ref=src,
            dst_ref=dst,
            send_sem=send.at[i],
            recv_sem=recv.at[i],
            device_id={"col": dev},
            device_id_type=MESH,
        )
        copy.start()
        started.append(copy)
        return copy

    mine = [pltpu.make_async_copy(x_ref.at[h], place(0, h), local_sem.at[h]) for h in range(2)]
    for copy in mine:
        copy.start()
    greet((sib, xn, yn))
    x0 = push(x_ref.at[0], place(1, 0), xn)
    y1 = push(x_ref.at[1], place(1, 1), yn)
    x1 = push(x_ref.at[1], place(2, 0), xn)
    y0 = push(x_ref.at[0], place(2, 1), yn)
    s0 = push(x_ref.at[0], place(0, 2), sib)
    s1 = push(x_ref.at[1], place(0, 3), sib)
    prepare(0)
    for copy in mine:
        copy.wait()
    s0.wait_recv()
    s1.wait_recv()
    consume(0, 0, ((0, c), (1, c), (0, sib), (1, sib)))
    x0.wait_recv()
    fy = push(place(1, 0), place(3, 0), yn)
    y1.wait_recv()
    fx = push(place(1, 1), place(3, 1), xn)
    prepare(1)
    t1 = push(place(1, 0, 2), place(1, 2, 2), sib)
    t1.wait_recv()
    consume(1, 0, ((0, xn), (1, yn), (0, xn + step), (1, yn + step)))
    prepare(2)
    x1.wait_recv()
    y0.wait_recv()
    t2 = push(place(2, 0, 2), place(2, 2, 2), sib)
    t2.wait_recv()
    consume(2, 0, ((1, xn), (0, yn), (1, xn + step), (0, yn + step)))
    prepare(3)
    fy.wait_recv()
    fx.wait_recv()
    t3 = push(place(3, 0, 2), place(3, 2, 2), sib)
    consume(3, 0, ((0, diag), (1, diag)))
    t3.wait_recv()
    consume(3, 2, ((0, diag + step), (1, diag + step)))
    for copy in started:
        copy.wait_send()


def piece_at(ref, rows, piece):
    half, who = piece
    return ref.at[half, pl.ds(pl.multiple_of(who * rows, rows), rows), :]


def units_back_kernel(
    rows, x_ref, w_ref, u_ref, g_ref, v_ref, p_ref, d_ref,
    held, weights, units, turned, gates, ups, grads, total_ref,
    weight_sem, load_sem, store_sem, local_sem, send, recv,
):
    c, sib, xn, yn = partners()
    diag = yn + (xn - c)
    step = sib - c
    wide = jnp.float32
    width = w_ref.shape[0]
    d = w_ref.shape[1]
    plan = (
        ((0, c), (1, c), (0, sib), (1, sib)),
        ((0, xn), (1, yn), (0, xn + step), (1, yn + step)),
        ((1, xn), (0, yn), (1, xn + step), (0, yn + step)),
        ((0, diag), (1, diag), (0, diag + step), (1, diag + step)),
    )
    fetch = pltpu.make_async_copy(w_ref, weights, weight_sem)
    fetch.start()

    def loads(t):
        copies = []
        for j, piece in enumerate(plan[t]):
            for k, (src, dst) in enumerate(((u_ref, units), (g_ref, gates), (v_ref, ups))):
                copies.append(
                    pltpu.make_async_copy(
                        piece_at(src, rows, piece),
                        dst.at[t % 2, pl.ds(j * rows, rows), :],
                        load_sem.at[t % 2, j, k],
                    )
                )
        return copies

    def stores(t, first=0, count=4):
        return [
            pltpu.make_async_copy(
                grads.at[t % 2, pl.ds(j * rows, rows), :],
                piece_at(p_ref, rows, plan[t][j]),
                store_sem.at[t % 2, j],
            )
            for j in range(first, first + count)
        ]

    for copy in loads(0):
        copy.start()

    tile = 256

    def prepare(t):
        if t == 0:
            fetch.wait()
        if t < 3:
            for copy in loads(t + 1):
                copy.start()
        for copy in loads(t):
            copy.wait()

        @pl.loop(0, width // tile)
        def _(n):
            cut = pl.ds(pl.multiple_of(n * tile, tile), tile)
            gate = gates[t % 2, :, cut]
            square = gate * gate
            bent = jnp.tanh(CURVE * (gate + BEND * gate * square))
            rise = 0.5 * (1.0 + bent)
            slope = rise + (0.5 * CURVE) * gate * (1.0 - bent * bent) * (1.0 + 3.0 * BEND * square)
            gates[t % 2, :, cut] = ups[t % 2, :, cut] * slope
            ups[t % 2, :, cut] = gate * rise
            turned[cut, :] = units[t % 2, :, cut].T

    def consume(t, first, pieces):
        if t >= 2 and first == 0:
            for copy in stores(t - 2):
                copy.wait()
        span = slice(first * rows, (first + len(pieces)) * rows)

        @pl.loop(0, width // 512)
        def _(n):
            cut = pl.ds(pl.multiple_of(n * 512, 512), 512)
            grad = lax.dot_general(
                held[t, span, :],
                weights[cut, :],
                (((1,), (1,)), ((), ())),
                preferred_element_type=wide,
            )
            grads[t % 2, span, cut] = (grad * gates[t % 2, span, cut]).astype(grads.dtype)
            cut_up = pl.ds(pl.multiple_of(width + n * 512, 512), 512)
            grads[t % 2, span, cut_up] = (grad * ups[t % 2, span, cut]).astype(grads.dtype)

        for copy in stores(t, first, len(pieces)):
            copy.start()

        block = d_ref.shape[-1]

        @pl.loop(0, d // block)
        def _(n):
            cut = pl.ds(pl.multiple_of(n * block, block), block)
            value = jnp.dot(turned[:, span], held[t, span, cut], preferred_element_type=wide)
            if t > 0:
                value = value + total_ref[:, cut]
            if first == 0:
                total_ref[:, cut] = value
            else:
                d_ref[n] = value.astype(d_ref.dtype)

    rounds_of(rows, x_ref, held, local_sem, send, recv, consume, prepare)
    for copy in (*stores(2), *stores(3)):
        copy.wait()


def units_back(x, down, units, gate, up, tiers, cid):
    h, rows, d = x.shape
    width = down.shape[0]
    low = x.dtype
    return pl.pallas_call(
        functools.partial(units_back_kernel, rows),
        out_shape=(
            jax.ShapeDtypeStruct((h, 8 * rows, 2 * width), low),
            jax.ShapeDtypeStruct((tiers, width, d // tiers), low),
        ),
        in_specs=[pl.BlockSpec(memory_space=pl.ANY)] * 5,
        out_specs=[
            pl.BlockSpec(memory_space=pl.ANY),
            pl.BlockSpec(memory_space=pltpu.VMEM),
        ],
        scratch_shapes=[
            pltpu.VMEM((4, 4 * rows, d), low),
            pltpu.VMEM((width, d), low),
            pltpu.VMEM((2, 4 * rows, width), low),
            pltpu.VMEM((width, 4 * rows), low),
            pltpu.VMEM((2, 4 * rows, width), jnp.float32),
            pltpu.VMEM((2, 4 * rows, width), jnp.float32),
            pltpu.VMEM((2, 4 * rows, 2 * width), low),
            pltpu.VMEM((width, d), jnp.float32),
            pltpu.SemaphoreType.DMA,
            pltpu.SemaphoreType.DMA((2, 4, 3)),
            pltpu.SemaphoreType.DMA((2, 4)),
            pltpu.SemaphoreType.DMA((2,)),
            pltpu.SemaphoreType.DMA((11,)),
            pltpu.SemaphoreType.DMA((11,)),
        ],
        compiler_params=pltpu.CompilerParams(
            collective_id=cid, has_side_effects=True, vmem_limit_bytes=52 << 20
        ),
        cost_estimate=pl.CostEstimate(
            flops=64 * h * rows * width * d, bytes_accessed=130_000_000, transcendentals=0
        ),
        name="units_back",
    )(x, down, units, gate, up)


def heads_back_kernel(
    rows, scale, x_ref, w_ref, m_ref, q_ref, k_ref, v_ref, s_ref, gq_ref, gk_ref, gv_ref, d_ref,
    held, weights, mixed, queries, keys, values, seen, total_ref, load_sem, local_sem, send, recv,
):
    wide = jnp.float32
    d = w_ref.shape[1]
    low = weights.dtype
    pairs = (
        (w_ref, weights), (q_ref, queries), (k_ref, keys), (v_ref, values), (s_ref, seen),
        (m_ref, mixed),
    )
    loads = [
        pltpu.make_async_copy(src, dst, load_sem.at[i]) for i, (src, dst) in enumerate(pairs)
    ]
    for copy in loads:
        copy.start()
    back = (((1,), (1,)), ((), ()))

    def prepare(t):
        if t == 0:
            for copy in loads:
                copy.wait()
            gk_ref[...] = jnp.zeros_like(gk_ref)
            gv_ref[...] = jnp.zeros_like(gv_ref)

    def consume(t, first, pieces):
        part = slice(first * rows, (first + len(pieces)) * rows)
        grad_mixed = lax.dot_general(
            held[t, part, :], weights[...], back, preferred_element_type=wide
        )
        grad_mixed = grad_mixed.astype(low)
        spans = []
        for j, (half, who) in enumerate(pieces):
            span = pl.ds(pl.multiple_of(who * rows, rows), rows)
            spans.append(mixed[half, span, :])
            query = queries[half, span, :]
            grad = grad_mixed[j * rows : (j + 1) * rows]
            score = lax.dot_general(query, keys[half], back, preferred_element_type=wide) * scale
            score = jnp.where(seen[half, span, :] > 0, score, NEGATIVE)
            power = jnp.exp(score - jnp.max(score, axis=-1, keepdims=True))
            prob = power / jnp.sum(power, axis=-1, keepdims=True)
            slope = lax.dot_general(grad, values[half], back, preferred_element_type=wide)
            mean = jnp.sum(prob * slope, axis=-1, keepdims=True)
            flow = (prob * (slope - mean)).astype(low)
            gq_ref[half, span, :] = jnp.dot(flow, keys[half], preferred_element_type=wide) * scale
            gk_ref[half] += jnp.dot(flow.T, query, preferred_element_type=wide) * scale
            gv_ref[half] += jnp.dot(prob.astype(low).T, grad, preferred_element_type=wide)
        turned = jnp.concatenate(spans, axis=0).T

        @pl.loop(0, d // 512)
        def _(n):
            cut = pl.ds(pl.multiple_of(n * 512, 512), 512)
            value = jnp.dot(turned, held[t, part, cut], preferred_element_type=wide)
            if t > 0:
                value = value + total_ref[:, cut]
            if first == 0:
                total_ref[:, cut] = value
            else:
                d_ref[:, cut] = value.astype(d_ref.dtype)

    rounds_of(rows, x_ref, held, local_sem, send, recv, consume, prepare)


def heads_back(x, output, mixed, query, key, value, visible, scale, cid):
    h, rows, d = x.shape
    low = x.dtype
    grad = jax.ShapeDtypeStruct(query.shape, jnp.float32)
    return pl.pallas_call(
        functools.partial(heads_back_kernel, rows, scale),
        out_shape=(grad, grad, grad, jax.ShapeDtypeStruct(output.shape, low)),
        in_specs=[pl.BlockSpec(memory_space=pl.ANY)] * 7,
        out_specs=[pl.BlockSpec(memory_space=pltpu.VMEM)] * 4,
        scratch_shapes=[
            pltpu.VMEM((4, 4 * rows, d), low),
            pltpu.VMEM(output.shape, low),
            pltpu.VMEM(mixed.shape, low),
            pltpu.VMEM(query.shape, low),
            pltpu.VMEM(query.shape, low),
            pltpu.VMEM(query.shape, low),
            pltpu.VMEM(visible.shape, visible.dtype),
            pltpu.VMEM(output.shape, jnp.float32),
            pltpu.SemaphoreType.DMA((6,)),
            pltpu.SemaphoreType.DMA((2,)),
            pltpu.SemaphoreType.DMA((11,)),
            pltpu.SemaphoreType.DMA((11,)),
        ],
        compiler_params=pltpu.CompilerParams(
            collective_id=cid, has_side_effects=True, vmem_limit_bytes=60 << 20
        ),
        cost_estimate=pl.CostEstimate(
            flops=20_000_000_000, bytes_accessed=130_000_000, transcendentals=0
        ),
        name="heads_back",
    )(x, output, mixed, query, key, value, visible)


def total_kernel(x_ref, o_ref, sums, got, tier_sums, send, recv):
    c, sib, xn, yn = partners()
    r = lax.axis_index("row")
    tiers = lax.axis_size("row")
    others = [lax.rem(r + k, tiers) for k in range(1, tiers)]
    barrier = pltpu.get_barrier_semaphore()
    for d in (sib, xn, yn):
        pl.semaphore_signal(barrier, inc=1, device_id={"col": d}, device_id_type=MESH)
    for d in others:
        pl.semaphore_signal(barrier, inc=1, device_id={"row": d}, device_id_type=MESH)
    pl.semaphore_wait(barrier, 3 + len(others))
    sums[0] = x_ref[...]
    for i, dev in enumerate((sib, xn, yn)):
        copy = pltpu.make_async_remote_copy(
            src_ref=sums.at[i],
            dst_ref=got.at[i],
            send_sem=send.at[i],
            recv_sem=recv.at[i],
            device_id={"col": dev},
            device_id_type=MESH,
        )
        copy.start()
        copy.wait()
        sums[i + 1] = sums[i] + got[i]
    tier_sums[r] = sums[3]
    copies = []
    for k, d in enumerate(others):
        copy = pltpu.make_async_remote_copy(
            src_ref=sums.at[3],
            dst_ref=tier_sums.at[r],
            send_sem=send.at[3 + k],
            recv_sem=recv.at[3 + k],
            device_id={"row": d},
            device_id_type=MESH,
        )
        copy.start()
        copies.append(copy)
    for copy in copies:
        copy.wait()
    result = tier_sums[0]
    for k in range(1, tiers):
        result = result + tier_sums[k]
    o_ref[...] = result


def total(x, tiers, cid):
    return pl.pallas_call(
        total_kernel,
        out_shape=jax.ShapeDtypeStruct(x.shape, x.dtype),
        in_specs=[pl.BlockSpec(memory_space=pltpu.VMEM)],
        out_specs=pl.BlockSpec(memory_space=pltpu.VMEM),
        scratch_shapes=[
            pltpu.VMEM((4, *x.shape), x.dtype),
            pltpu.VMEM((3, *x.shape), x.dtype),
            pltpu.VMEM((tiers, *x.shape), x.dtype),
            pltpu.SemaphoreType.DMA((2 + tiers,)),
            pltpu.SemaphoreType.DMA((2 + tiers,)),
        ],
        compiler_params=pltpu.CompilerParams(collective_id=cid, has_side_effects=True),
        cost_estimate=pl.CostEstimate(flops=0, bytes_accessed=40_000_000, transcendentals=0),
        name="total",
    )(x)


def after(value, *earlier):
    return lax.optimization_barrier((value, *earlier))[0]


def general_body(
    hidden,
    per_layer,
    lengths,
    block_ids,
    out_grad,
    query_weight,
    key_weight,
    value_weight,
    output_weight,
    gate_weight,
    up_weight,
    down_weight,
    laurel_left,
    laurel_right,
    layer_gate,
    layer_proj,
    norm_gains,
    head_gains,
):
    local_rows = hidden.shape[0]
    seq_groups = hidden.shape[1]
    col_index = lax.axis_index("col")
    row_index = lax.axis_index("row")
    all_lengths = lengths
    lengths = lax.dynamic_slice_in_dim(all_lengths, row_index * seq_groups, seq_groups, 0)
    (
        query_cols,
        key_cols,
        value_cols,
        output_rows,
        gate_cols,
        up_cols,
        down_rows,
        left_cols,
        right_rows,
        gate_layer_cols,
        proj_layer_rows,
    ) = (
        lax.all_gather(query_weight, "row", axis=0, tiled=True),
        lax.all_gather(key_weight, "row", axis=0, tiled=True),
        lax.all_gather(value_weight, "row", axis=0, tiled=True),
        lax.all_gather(output_weight, "row", axis=1, tiled=True),
        lax.all_gather(gate_weight, "row", axis=0, tiled=True),
        lax.all_gather(up_weight, "row", axis=0, tiled=True),
        lax.all_gather(down_weight, "row", axis=1, tiled=True),
        lax.all_gather(laurel_left, "row", axis=0, tiled=True),
        lax.all_gather(laurel_right, "row", axis=1, tiled=True),
        lax.all_gather(layer_gate, "row", axis=0, tiled=True),
        lax.all_gather(layer_proj, "row", axis=1, tiled=True),
    )
    (
        query_full,
        key_full,
        value_full,
        output_full,
        left_full,
        right_full,
        gate_layer_full,
        proj_layer_full,
    ) = (
        lax.all_gather(query_cols, "col", axis=1, tiled=True),
        lax.all_gather(key_cols, "col", axis=1, tiled=True),
        lax.all_gather(value_cols, "col", axis=1, tiled=True),
        lax.all_gather(output_rows, "col", axis=0, tiled=True),
        lax.all_gather(left_cols, "col", axis=1, tiled=True),
        lax.all_gather(right_rows, "col", axis=0, tiled=True),
        lax.all_gather(gate_layer_cols, "col", axis=1, tiled=True),
        lax.all_gather(proj_layer_rows, "col", axis=0, tiled=True),
    )
    paired = jnp.concatenate([gate_cols, up_cols], axis=1)
    unit_width = gate_cols.shape[1]
    first_position = col_index * local_rows
    positions = first_position + jnp.arange(local_rows, dtype=jnp.int32)
    live_mask = positions[:, None] < lengths[None, :]
    keep_mask = live_mask.astype(jnp.float32)[:, :, None]
    reach_back = (WINDOW + local_rows - 2) // local_rows
    reach_ahead = (BLOCK + local_rows - 2) // local_rows
    key_span = (reach_back + 1 + reach_ahead) * local_rows
    key_position = first_position - reach_back * local_rows + jnp.arange(key_span, dtype=jnp.int32)
    filler_low = jnp.full((seq_groups, reach_back * local_rows), FAR_BLOCK, jnp.int32)
    filler_high = jnp.full((seq_groups, reach_ahead * local_rows), FAR_BLOCK, jnp.int32)
    padded_blocks = jnp.concatenate([filler_low, block_ids, filler_high], axis=1)
    key_blocks = lax.dynamic_slice_in_dim(padded_blocks, first_position, key_span, 1)
    query_blocks = lax.dynamic_slice_in_dim(block_ids, first_position, local_rows, 1)
    key_live = (key_position[None, :] >= 0) & (key_position[None, :] < lengths[:, None])
    query_live = positions[None, :] < lengths[:, None]
    distance = positions[:, None] - key_position[None, :]
    nearby = (query_blocks[:, :, None] >= key_blocks[:, None, :]) & (distance < WINDOW)[None]
    nearby = nearby & query_live[:, :, None] & key_live[:, None, :]
    visible = (nearby | (distance == 0)[None])[:, None, None]
    residual = hidden.astype(jnp.float32)
    normed_value, input_back = jax.vjp(input_norm, residual, norm_gains)
    normed_low = normed_value.astype(jnp.bfloat16)
    half_width = HD // 2
    frequency = jnp.exp(jnp.arange(half_width, dtype=jnp.float32) * (-2.0 * math.log(10000.0) / HD))
    angles = (positions.astype(jnp.float32)[:, None] * frequency[None, :])[:, None, None, :]

    def prepare(query_in, key_in, value_in, gain_rows):
        return (
            rotate(root_norm(query_in, gain_rows[0]), angles),
            rotate(root_norm(key_in, gain_rows[1]), angles),
            plain_norm(value_in),
        )

    query_raw = matmul_last(normed_low, query_full).reshape(local_rows, seq_groups, H, HD)
    key_raw = matmul_last(normed_low, key_full).reshape(local_rows, seq_groups, KV, HD)
    value_raw = matmul_last(normed_low, value_full).reshape(local_rows, seq_groups, KV, HD)
    (query_value, key_value, value_value), head_back = jax.vjp(
        prepare, query_raw, key_raw, value_raw, head_gains
    )
    query_low = query_value.astype(jnp.bfloat16).reshape(local_rows, seq_groups, KV, H // KV, HD)
    key_low = key_value.astype(jnp.bfloat16)
    value_low = value_value.astype(jnp.bfloat16)
    offsets = list(range(reach_back, -reach_ahead - 1, -1))
    key_parts = []
    value_parts = []
    for offset in offsets:
        if offset == 0:
            key_parts.append(key_low)
            value_parts.append(value_low)
        else:
            moved_key, moved_value = passed_along((key_low, value_low), "col", offset)
            key_parts.append(moved_key)
            value_parts.append(moved_value)
    near_keys = jnp.concatenate(key_parts, axis=0)
    near_values = jnp.concatenate(value_parts, axis=0)
    score_scale = HD ** (-0.5)

    def score_all():
        raw_scores = (
            jnp.einsum(
                "psjgd,esjd->sjgpe", query_low, near_keys, preferred_element_type=jnp.float32
            )
            * score_scale
        )
        return jnp.where(visible, raw_scores, NEGATIVE)

    scores = score_all()
    row_max = jnp.max(scores, axis=-1, keepdims=True)
    exponent = jnp.exp(scores - row_max)
    row_total = jnp.sum(exponent, axis=-1, keepdims=True)
    attn_prob = exponent / row_total
    log_total = row_max + jnp.log(row_total)
    mixed_heads = jnp.einsum(
        "sjgpe,esjd->psjgd",
        attn_prob.astype(jnp.bfloat16),
        near_values,
        preferred_element_type=jnp.float32,
    )
    mixed_low = mixed_heads.reshape(local_rows, seq_groups, H * HD).astype(jnp.bfloat16)
    out_proj = matmul_last(mixed_low, output_full)
    laurel_mid = matmul_last(normed_low, left_full).astype(jnp.bfloat16)
    low_rank = matmul_last(laurel_mid, right_full)
    (after_attention, feed_normed), middle_back = jax.vjp(
        middle, residual, out_proj, low_rank, normed_low.astype(jnp.float32), norm_gains
    )
    feed_low = feed_normed.astype(jnp.bfloat16)
    gate_up = matmul_last(lax.all_gather(feed_low, "col", axis=0, tiled=True), paired)
    unit_value, gate_back = jax.vjp(
        gated_product, gate_up[..., :unit_width], gate_up[..., unit_width:]
    )
    units_low = unit_value.astype(jnp.bfloat16)
    summed = lax.psum_scatter(
        matmul_last(units_low, down_rows), "col", scatter_dimension=0, tiled=True
    )
    after_feed, feed_back = jax.vjp(feed_join, after_attention, summed, norm_gains)
    feed_round = after_feed.astype(jnp.bfloat16)
    layer_pre = matmul_last(feed_round, gate_layer_full)
    layer_input = per_layer.astype(jnp.float32)
    layer_value, layer_back = jax.vjp(gated_product, layer_pre, layer_input)
    layer_low = layer_value.astype(jnp.bfloat16)
    projected = matmul_last(layer_low, proj_layer_full)
    out_value, final_back = jax.vjp(final_join, after_feed, projected, norm_gains)
    square_sums = jnp.stack(
        [
            jnp.sum(keep_mask * residual * residual),
            jnp.sum(keep_mask * after_attention * after_attention),
            jnp.sum(keep_mask * after_feed * after_feed),
            jnp.sum(keep_mask * out_value * out_value),
        ]
    )
    valid_count = jnp.sum(all_lengths).astype(jnp.float32)
    cotangent = out_grad.astype(jnp.float32) * keep_mask
    grad_feed_out, grad_projected, gains_final = final_back(cotangent)
    projected_low = grad_projected.astype(jnp.bfloat16)
    grad_proj_layer = outer_sum(layer_low, projected_low)
    grad_layer_pre, grad_layer_input = layer_back(matmul_back(projected_low, proj_layer_full))
    layer_pre_low = grad_layer_pre.astype(jnp.bfloat16)
    grad_gate_layer = outer_sum(feed_round, layer_pre_low)
    grad_after_feed = grad_feed_out + matmul_back(layer_pre_low, gate_layer_full)
    grad_after_attention_a, grad_summed, gains_feed = feed_back(grad_after_feed)
    summed_low = grad_summed.astype(jnp.bfloat16)
    block_rows = lax.all_gather(summed_low, "col", axis=0, tiled=True)
    grad_down = outer_sum(units_low, block_rows)
    grad_units = matmul_back(block_rows, down_rows)
    grad_down, grad_units = (grad_down, grad_units)
    grad_gate_value, grad_up_value = gate_back(grad_units)
    grad_paired = jnp.concatenate([grad_gate_value, grad_up_value], axis=-1).astype(jnp.bfloat16)
    grad_weights_paired = outer_sum(
        lax.all_gather(feed_low, "col", axis=0, tiled=True), grad_paired
    )
    grad_feed = lax.psum_scatter(
        matmul_back(grad_paired, paired).astype(jnp.bfloat16),
        "col",
        scatter_dimension=0,
        tiled=True,
    ).astype(jnp.float32)
    grad_residual_mid, grad_out_proj, grad_low_rank, grad_normed_mid, gains_middle = middle_back(
        (grad_after_attention_a, grad_feed)
    )
    out_proj_low = grad_out_proj.astype(jnp.bfloat16)
    grad_output = outer_sum(mixed_low, out_proj_low)
    grad_mixed = matmul_back(out_proj_low, output_full).astype(jnp.bfloat16)
    grad_mixed = grad_mixed.reshape(local_rows, seq_groups, KV, H // KV, HD)
    low_rank_grad = grad_low_rank.astype(jnp.bfloat16)
    grad_right = outer_sum(laurel_mid, low_rank_grad)
    grad_laurel_mid = matmul_back(low_rank_grad, right_full).astype(jnp.bfloat16)
    grad_left = outer_sum(normed_low, grad_laurel_mid)
    scores = score_all()
    attn_prob = jnp.exp(scores - log_total)
    grad_prob = jnp.einsum(
        "psjgd,esjd->sjgpe", grad_mixed, near_values, preferred_element_type=jnp.float32
    )
    grad_scores = (
        attn_prob * (grad_prob - jnp.sum(attn_prob * grad_prob, axis=-1, keepdims=True))
    ).astype(jnp.bfloat16)
    grad_queries = (
        jnp.einsum("sjgpe,esjd->psjgd", grad_scores, near_keys, preferred_element_type=jnp.float32)
        * score_scale
    )
    grad_near_keys = (
        jnp.einsum("sjgpe,psjgd->esjd", grad_scores, query_low, preferred_element_type=jnp.float32)
        * score_scale
    )
    grad_near_values = jnp.einsum(
        "sjgpe,psjgd->esjd",
        attn_prob.astype(jnp.bfloat16),
        grad_mixed,
        preferred_element_type=jnp.float32,
    )
    grad_key_total = grad_near_keys[reach_back * local_rows : (reach_back + 1) * local_rows]
    grad_value_total = grad_near_values[reach_back * local_rows : (reach_back + 1) * local_rows]
    for slot_index, offset in enumerate(offsets):
        if offset != 0:
            piece_keys = grad_near_keys[slot_index * local_rows : (slot_index + 1) * local_rows]
            piece_values = grad_near_values[slot_index * local_rows : (slot_index + 1) * local_rows]
            back_keys, back_values = (
                passed_along(piece_keys.astype(jnp.bfloat16), "col", -offset).astype(
                    piece_keys.dtype
                ),
                passed_along(piece_values.astype(jnp.bfloat16), "col", -offset).astype(
                    piece_values.dtype
                ),
            )
            grad_key_total = grad_key_total + back_keys
            grad_value_total = grad_value_total + back_values
    grad_query_raw, grad_key_raw, grad_value_raw, grad_heads = head_back(
        (grad_queries.reshape(local_rows, seq_groups, H, HD), grad_key_total, grad_value_total)
    )
    query_grad_low = grad_query_raw.reshape(local_rows, seq_groups, H * HD).astype(jnp.bfloat16)
    key_grad_low = grad_key_raw.reshape(local_rows, seq_groups, KV * HD).astype(jnp.bfloat16)
    value_grad_low = grad_value_raw.reshape(local_rows, seq_groups, KV * HD).astype(jnp.bfloat16)
    grad_query = outer_sum(normed_low, query_grad_low)
    grad_key = outer_sum(normed_low, key_grad_low)
    grad_value = outer_sum(normed_low, value_grad_low)
    grad_normed = (
        grad_normed_mid
        + matmul_back(grad_laurel_mid, left_full)
        + matmul_back(query_grad_low, query_full)
        + matmul_back(key_grad_low, key_full)
        + matmul_back(value_grad_low, value_full)
    )
    grad_residual_in, gains_input = input_back(grad_normed)
    d_hidden = (grad_residual_mid + grad_residual_in).astype(jnp.bfloat16)
    d_per_layer = grad_layer_input.astype(jnp.bfloat16)
    grad_gains = gains_final + gains_feed + gains_middle + gains_input
    grad_gate = grad_weights_paired[:, :unit_width]
    grad_up = grad_weights_paired[:, unit_width:]
    (
        query_part,
        key_part,
        value_part,
        output_part,
        left_part,
        right_part,
        gate_layer_part,
        proj_layer_part,
    ) = (
        lax.psum_scatter(
            grad_query.astype(jnp.bfloat16), "col", scatter_dimension=1, tiled=True
        ).astype(jnp.float32),
        lax.psum_scatter(
            grad_key.astype(jnp.bfloat16), "col", scatter_dimension=1, tiled=True
        ).astype(jnp.float32),
        lax.psum_scatter(
            grad_value.astype(jnp.bfloat16), "col", scatter_dimension=1, tiled=True
        ).astype(jnp.float32),
        lax.psum_scatter(
            grad_output.astype(jnp.bfloat16), "col", scatter_dimension=0, tiled=True
        ).astype(jnp.float32),
        lax.psum_scatter(
            grad_left.astype(jnp.bfloat16), "col", scatter_dimension=1, tiled=True
        ).astype(jnp.float32),
        lax.psum_scatter(
            grad_right.astype(jnp.bfloat16), "col", scatter_dimension=0, tiled=True
        ).astype(jnp.float32),
        lax.psum_scatter(
            grad_gate_layer.astype(jnp.bfloat16), "col", scatter_dimension=1, tiled=True
        ).astype(jnp.float32),
        lax.psum_scatter(
            grad_proj_layer.astype(jnp.bfloat16), "col", scatter_dimension=0, tiled=True
        ).astype(jnp.float32),
    )
    (
        d_query_weight,
        d_key_weight,
        d_value_weight,
        d_output_weight,
        d_gate_weight,
        d_up_weight,
        d_down_weight,
        d_laurel_left,
        d_laurel_right,
        d_layer_gate,
        d_layer_proj,
    ) = (
        lax.psum_scatter(
            query_part.astype(jnp.bfloat16), "row", scatter_dimension=0, tiled=True
        ).astype(jnp.float32),
        lax.psum_scatter(
            key_part.astype(jnp.bfloat16), "row", scatter_dimension=0, tiled=True
        ).astype(jnp.float32),
        lax.psum_scatter(
            value_part.astype(jnp.bfloat16), "row", scatter_dimension=0, tiled=True
        ).astype(jnp.float32),
        lax.psum_scatter(
            output_part.astype(jnp.bfloat16), "row", scatter_dimension=1, tiled=True
        ).astype(jnp.float32),
        lax.psum_scatter(
            grad_gate.astype(jnp.bfloat16), "row", scatter_dimension=0, tiled=True
        ).astype(jnp.float32),
        lax.psum_scatter(
            grad_up.astype(jnp.bfloat16), "row", scatter_dimension=0, tiled=True
        ).astype(jnp.float32),
        lax.psum_scatter(
            grad_down.astype(jnp.bfloat16), "row", scatter_dimension=1, tiled=True
        ).astype(jnp.float32),
        lax.psum_scatter(
            left_part.astype(jnp.bfloat16), "row", scatter_dimension=0, tiled=True
        ).astype(jnp.float32),
        lax.psum_scatter(
            right_part.astype(jnp.bfloat16), "row", scatter_dimension=1, tiled=True
        ).astype(jnp.float32),
        lax.psum_scatter(
            gate_layer_part.astype(jnp.bfloat16), "row", scatter_dimension=0, tiled=True
        ).astype(jnp.float32),
        lax.psum_scatter(
            proj_layer_part.astype(jnp.bfloat16), "row", scatter_dimension=1, tiled=True
        ).astype(jnp.float32),
    )
    d_norm_gains, d_head_gains, total_squares = lax.psum(
        (grad_gains, grad_heads, square_sums), ("row", "col")
    )
    stats = jnp.sqrt(total_squares / (valid_count * D))
    output = out_value.astype(jnp.bfloat16)
    return (
        output,
        stats,
        d_hidden,
        d_per_layer,
        d_query_weight,
        d_key_weight,
        d_value_weight,
        d_output_weight,
        d_gate_weight,
        d_up_weight,
        d_down_weight,
        d_laurel_left,
        d_laurel_right,
        d_layer_gate,
        d_layer_proj,
        d_norm_gains,
        d_head_gains,
    )


def swap(array):
    return jnp.swapaxes(array, 0, 1)


def heads_body(
    hidden,
    per_layer,
    lengths,
    block_ids,
    out_grad,
    query_weight,
    key_weight,
    value_weight,
    output_weight,
    gate_weight,
    up_weight,
    down_weight,
    laurel_left,
    laurel_right,
    layer_gate,
    layer_proj,
    norm_gains,
    head_gains,
):
    low = jnp.bfloat16
    rows = hidden.shape[0]
    groups = hidden.shape[1]
    cols = lax.axis_size("col")
    seq = rows * cols
    share = cols // KV
    col_index = lax.axis_index("col")
    row_index = lax.axis_index("row")
    all_lengths = lengths
    lengths = lax.dynamic_slice_in_dim(all_lengths, row_index * groups, groups, 0)

    laurel = jnp.concatenate([laurel_left.T, laurel_right], axis=0)
    small = [key_weight.T, value_weight.T, layer_gate.T, layer_proj, laurel]
    heights = [key_weight.shape[1], value_weight.shape[1], layer_gate.shape[1]]
    heights += [layer_proj.shape[0], laurel_left.shape[1], laurel_right.shape[0]]
    edges = [sum(heights[:i]) for i in range(len(heights) + 1)]
    unit_width = gate_weight.shape[1]
    residual = swap(hidden).astype(jnp.float32)
    normed_value, input_back = jax.vjp(input_norm, residual, norm_gains)
    normed_low = normed_value.astype(low)
    tiers = lax.axis_size("row")
    normed_all, small_row, query_full, output_full, both_weights = open_all(
        normed_low, query_weight, output_weight, gate_weight, up_weight, small, tiers, 1
    )
    small_all = share_small(small_row, heights[0] + heights[1], 8)
    paired = lax.all_gather(both_weights, "row", axis=0, tiled=True)
    down_full = lax.all_gather(after(down_weight, normed_all), "row", axis=1, tiled=True)
    query_full = query_full.reshape(D, HD).T
    output_full = jnp.swapaxes(output_full, 0, 1).reshape(HD, D)
    pieces = [small_all[:, :, a:b] for a, b in zip(edges[:-1], edges[1:])]
    group_start = (col_index // share) * share

    def joined(piece):
        return jnp.swapaxes(piece, 1, 2).reshape(-1, D)

    key_full, value_full = (
        joined(lax.dynamic_slice_in_dim(piece, group_start, share, 0)) for piece in pieces[:2]
    )
    gate_layer_full, proj_layer_full, left_full, right_full = (
        joined(piece) for piece in pieces[2:]
    )
    head_weights = jnp.concatenate([query_full, key_full, value_full], axis=0)

    positions = jnp.arange(seq, dtype=jnp.int32)
    mine = col_index * rows + jnp.arange(rows, dtype=jnp.int32)
    keep_mask = (mine[None, :] < lengths[:, None]).astype(jnp.float32)[:, :, None]
    live = positions[None, :] < lengths[:, None]
    distance = positions[:, None] - positions[None, :]
    nearby = (block_ids[:, :, None] >= block_ids[:, None, :]) & (distance < WINDOW)[None]
    nearby = nearby & live[:, :, None] & live[:, None, :]
    visible = nearby | (distance == 0)[None]

    half_width = HD // 2
    frequency = jnp.exp(jnp.arange(half_width, dtype=jnp.float32) * (-2.0 * math.log(10000.0) / HD))
    angles = (positions.astype(jnp.float32)[:, None] * frequency[None, :])[None]

    def prepare(query_in, key_in, value_in, gain_rows):
        return (
            rotate(root_norm(query_in, gain_rows[0]), angles),
            rotate(root_norm(key_in, gain_rows[1]), angles),
            plain_norm(value_in),
        )

    head_raw = matmul_back(normed_all, head_weights)
    query_raw, key_raw, value_raw = jnp.split(head_raw, 3, axis=-1)
    (query_value, key_value, value_value), head_back = jax.vjp(
        prepare, query_raw, key_raw, value_raw, head_gains
    )
    query_low = query_value.astype(low)
    key_low = key_value.astype(low)
    value_low = value_value.astype(low)
    score_scale = HD ** (-0.5)

    def score_all():
        raw_scores = (
            jnp.einsum("spd,sed->spe", query_low, key_low, preferred_element_type=jnp.float32)
            * score_scale
        )
        return jnp.where(visible, raw_scores, NEGATIVE)

    scores = score_all()
    row_max = jnp.max(scores, axis=-1, keepdims=True)
    exponent = jnp.exp(scores - row_max)
    row_total = jnp.sum(exponent, axis=-1, keepdims=True)
    attn_prob = exponent / row_total
    mixed_low = jnp.einsum(
        "spe,sed->spd", attn_prob.astype(low), value_low, preferred_element_type=jnp.float32
    ).astype(low)
    out_proj = product_sum(mixed_low, output_full, False, 2)
    laurel_mid = matmul_back(normed_low, left_full).astype(low)
    low_rank = matmul_last(laurel_mid, right_full)
    (after_attention, feed_normed), middle_back = jax.vjp(
        middle, residual, out_proj, low_rank, normed_low.astype(jnp.float32), norm_gains
    )
    feed_all = spread(feed_normed.astype(low), 0)
    gate_value = matmul_last(feed_all, paired[:, :unit_width])
    up_value = matmul_last(feed_all, paired[:, unit_width:])
    units_low = gated_product(gate_value, up_value).astype(low)
    units_low, query_low, key_low, value_low, seen, head_weights = lax.optimization_barrier(
        (units_low, query_low, key_low, value_low, visible.astype(jnp.float32), head_weights)
    )
    summed = product_sum(units_low, down_full, False, 5, room=44)
    after_feed, feed_back = jax.vjp(feed_join, after_attention, summed, norm_gains)
    feed_round = after_feed.astype(low)
    layer_pre = matmul_back(feed_round, gate_layer_full)
    layer_input = swap(per_layer).astype(jnp.float32)
    layer_value, layer_back = jax.vjp(gated_product, layer_pre, layer_input)
    layer_low = layer_value.astype(low)
    projected = matmul_last(layer_low, proj_layer_full)
    out_value, final_back = jax.vjp(final_join, after_feed, projected, norm_gains)
    square_sums = jnp.stack(
        [
            jnp.sum(keep_mask * residual * residual),
            jnp.sum(keep_mask * after_attention * after_attention),
            jnp.sum(keep_mask * after_feed * after_feed),
            jnp.sum(keep_mask * out_value * out_value),
        ]
    )
    valid_count = jnp.sum(all_lengths).astype(jnp.float32)

    cotangent = swap(out_grad).astype(jnp.float32) * keep_mask
    grad_feed_out, grad_projected, gains_final = final_back(cotangent)
    projected_low = grad_projected.astype(low)
    grad_proj_layer = outer_sum(layer_low, projected_low)
    grad_layer_pre, grad_layer_input = layer_back(matmul_back(projected_low, proj_layer_full))
    layer_pre_low = grad_layer_pre.astype(low)
    grad_gate_layer = outer_sum(layer_pre_low, feed_round)
    grad_after_feed = grad_feed_out + matmul_last(layer_pre_low, gate_layer_full)
    grad_after_attention_a, grad_summed, gains_feed = feed_back(grad_after_feed)
    grad_paired, grad_down = units_back(
        grad_summed.astype(low), down_full, units_low, gate_value, up_value, tiers, 9
    )
    d_down_weight = lax.psum_scatter(grad_down, "row", scatter_dimension=0)
    grad_feed, grad_both = product_sum(grad_paired, paired, True, 6, feed_all)
    d_both = lax.psum_scatter(grad_both, "row", scatter_dimension=0, tiled=True)
    grad_residual_mid, grad_out_proj, grad_low_rank, grad_normed_mid, gains_middle = middle_back(
        (grad_after_attention_a, grad_feed)
    )
    grad_queries, grad_keys, grad_values, grad_output = heads_back(
        after(grad_out_proj.astype(low), d_down_weight),
        output_full,
        mixed_low,
        query_low,
        key_low,
        value_low,
        seen,
        score_scale,
        10,
    )
    low_rank_grad = grad_low_rank.astype(low)
    grad_right = outer_sum(laurel_mid, low_rank_grad)
    grad_laurel_mid = matmul_back(low_rank_grad, right_full).astype(low)
    grad_left = outer_sum(grad_laurel_mid, normed_low)
    grad_query_raw, grad_key_raw, grad_value_raw, grad_heads = head_back(
        (grad_queries, grad_keys, grad_values)
    )
    head_grads = jnp.concatenate([grad_query_raw, grad_key_raw, grad_value_raw], axis=-1)
    head_grads = head_grads.astype(low)
    grad_head_weights = outer_sum(head_grads, normed_all).astype(low)
    grad_query, grad_key, grad_value = jnp.split(grad_head_weights, 3, axis=0)
    grad_group = jnp.concatenate(
        [grad_key.reshape(share, -1, D), grad_value.reshape(share, -1, D)], axis=1
    )
    grad_rest = jnp.concatenate(
        [
            piece.astype(low).reshape(cols, -1, D)
            for piece in (grad_gate_layer, grad_proj_layer, grad_left, grad_right)
        ],
        axis=1,
    )
    half = grad_rest.shape[1] // 2
    grad_rest = jnp.swapaxes(grad_rest.reshape(cols, 2, half, D), 0, 1)
    rest_part, group_part = fold_small(grad_rest.reshape(2, cols * half, D), grad_group, 3)
    parts = jnp.concatenate(
        [grad_output, grad_query, group_part.astype(low), rest_part.astype(low).reshape(-1, D)],
        axis=0,
    )
    grad_normed = product_sum(after(head_grads, parts), head_weights, False, 7, room=60)
    parts = after(parts, d_both, grad_normed)
    parts_out = lax.psum_scatter(parts, "row", scatter_dimension=1, tiled=True).astype(jnp.float32)
    d_output_weight = parts_out[:HD]
    d_query_weight = parts_out[HD : 2 * HD].T
    small_out = parts_out[2 * HD :]
    small_parts = [small_out[a:b] for a, b in zip(edges[:-1], edges[1:])]
    grad_normed = grad_normed + grad_normed_mid + matmul_last(grad_laurel_mid, left_full)
    grad_residual_in, gains_input = input_back(grad_normed)
    d_hidden = swap((grad_residual_mid + grad_residual_in).astype(low))
    d_per_layer = swap(grad_layer_input.astype(low))
    grad_gains = gains_final + gains_feed + gains_middle + gains_input
    extra = jnp.concatenate([grad_heads.reshape(-1), square_sums])
    extra = jnp.pad(extra, (0, 2 * D - extra.shape[0])).reshape(2, D)
    all_sums = jnp.concatenate([grad_gains, extra], axis=0)
    totals = total(after(all_sums, parts), tiers, 4)
    d_down_weight = after(d_down_weight, totals).astype(jnp.float32)
    d_both = after(d_both, totals).astype(jnp.float32)
    d_gate_weight = d_both[:, :unit_width]
    d_up_weight = d_both[:, unit_width:]
    d_norm_gains = totals[:6]
    d_head_gains = totals[6, : 2 * HD].reshape(2, HD)
    total_squares = totals[6, 2 * HD : 2 * HD + 4]
    stats = jnp.sqrt(total_squares / (valid_count * D))
    output = swap(out_value.astype(low))
    return (
        output,
        stats,
        d_hidden,
        d_per_layer,
        d_query_weight,
        small_parts[0].T,
        small_parts[1].T,
        d_output_weight,
        d_gate_weight,
        d_up_weight,
        d_down_weight,
        small_parts[4].T,
        small_parts[5],
        small_parts[2].T,
        small_parts[3],
        d_norm_gains,
        d_head_gains,
    )


def solution(mesh):
    body = heads_body if mesh.shape["col"] == H else general_body
    in_specs = (
        P("col", "row", None),
        P("col", "row", None),
        P(),
        P("row", None),
        P("col", "row", None),
        P("row", "col"),
        P("row", "col"),
        P("row", "col"),
        P("col", "row"),
        P("row", "col"),
        P("row", "col"),
        P("col", "row"),
        P("row", "col"),
        P("col", "row"),
        P("row", "col"),
        P("col", "row"),
        P(),
        P(),
    )
    out_specs = (
        P("col", "row", None),
        P(),
        P("col", "row", None),
        P("col", "row", None),
        P("row", "col"),
        P("row", "col"),
        P("row", "col"),
        P("col", "row"),
        P("row", "col"),
        P("row", "col"),
        P("col", "row"),
        P("row", "col"),
        P("col", "row"),
        P("row", "col"),
        P("col", "row"),
        P(),
        P(),
    )
    return jax.shard_map(body, mesh=mesh, in_specs=in_specs, out_specs=out_specs, check_vma=False)
```

```python
import functools
import math

import jax
import jax.numpy as jnp
from jax import lax
from jax.experimental import pallas as pl
from jax.experimental.pallas import tpu as pltpu
from jax.sharding import PartitionSpec as P

D = 2048
H = 8
KV = 2
HD = 256
WINDOW = 512
BLOCK = 256


EPSILON = 1e-06
FAR_BLOCK = 1 << 30
NEGATIVE = -1e30
HALF_ROOT = 1.0 / math.sqrt(2.0)
CURVE = math.sqrt(2.0 / math.pi)
BEND = 0.044715


MESH = pl.DeviceIdType.MESH


def passed_along(value, axis, steps):
    count = lax.axis_size(axis)
    initial, last = (max(0, -steps), min(count, count - steps))
    return lax.ppermute(value, axis, [(source, source + steps) for source in range(initial, last)])


def root_norm(values, gain_row):
    return (
        values * lax.rsqrt(jnp.mean(values * values, axis=-1, keepdims=True) + EPSILON) * gain_row
    )


def plain_norm(values):
    return values * lax.rsqrt(jnp.mean(values * values, axis=-1, keepdims=True) + EPSILON)


def smooth_gate(values):
    return jax.nn.gelu(values, approximate=True)


def rotate(values, angles):
    half_width = values.shape[-1] // 2
    leading = values[..., :half_width]
    trailing = values[..., half_width:]
    cosine = jnp.cos(angles)
    sine_part = jnp.sin(angles)
    return jnp.concatenate(
        [leading * cosine - trailing * sine_part, trailing * cosine + leading * sine_part], axis=-1
    )


def matmul_last(first_array, second_array):
    return lax.dot_general(
        first_array,
        second_array,
        (((first_array.ndim - 1,), (0,)), ((), ())),
        preferred_element_type=jnp.float32,
    )


def matmul_back(first_array, second_array):
    return lax.dot_general(
        first_array,
        second_array,
        (((first_array.ndim - 1,), (1,)), ((), ())),
        preferred_element_type=jnp.float32,
    )


def outer_sum(first_array, second_array):
    return lax.dot_general(
        first_array, second_array, (((0, 1), (0, 1)), ((), ())), preferred_element_type=jnp.float32
    )


def input_norm(residual, gain_rows):
    return root_norm(residual, gain_rows[0])


def middle(residual, out_proj, low_rank, normed, gain_rows):
    merged = (
        residual + root_norm(out_proj, gain_rows[1]) + normed + root_norm(low_rank, gain_rows[4])
    ) * HALF_ROOT
    return (merged, root_norm(merged, gain_rows[2]))


def feed_join(merged, summed, gain_rows):
    return merged + root_norm(summed, gain_rows[3])


def final_join(merged, projected, gain_rows):
    return merged + root_norm(projected, gain_rows[5])


def gated_product(first_array, second_array):
    return smooth_gate(first_array) * second_array


def partners():
    c = lax.axis_index("col")
    sib = c + 1 - 2 * (c % 2)
    xn = c + 2 - 4 * ((c // 2) % 2)
    yn = c + 4 - 8 * (c // 4)
    return c, sib, xn, yn

def greet(devs):
    barrier = pltpu.get_barrier_semaphore()
    for d in devs:
        pl.semaphore_signal(barrier, inc=1, device_id={"col": d}, device_id_type=MESH)
    pl.semaphore_wait(barrier, len(devs))

def spread_kernel(rows, x_ref, o_ref, local_sem, send, recv):
    c, sib, xn, yn = partners()
    def slot(half, who):
        return o_ref.at[half, pl.ds(pl.multiple_of(who * rows, rows), rows), :]
    def both(who):
        return o_ref.at[:, pl.ds(pl.multiple_of(who * rows, rows), rows), :]
    def push(i, src, dst, dev):
        return pltpu.make_async_remote_copy(src_ref=src, dst_ref=dst, send_sem=send.at[i], recv_sem=recv.at[i], device_id={"col": dev}, device_id_type=MESH)
    mine = pltpu.make_async_copy(x_ref, both(c), local_sem)
    mine.start()
    greet((sib, xn, yn))
    x0 = push(0, x_ref.at[0], slot(0, c), xn)
    y1 = push(1, x_ref.at[1], slot(1, c), yn)
    x1 = push(2, x_ref.at[1], slot(1, c), xn)
    y0 = push(3, x_ref.at[0], slot(0, c), yn)
    s = push(4, x_ref, both(c), sib)
    x0.start(); y1.start(); x1.start(); y0.start(); s.start()
    diag = yn + (xn - c)
    x0.wait_recv()
    fy = push(5, slot(0, xn), slot(0, xn), yn)
    fy.start()
    sx0 = push(6, slot(0, xn), slot(0, xn), sib)
    sx0.start()
    y1.wait_recv()
    fx = push(7, slot(1, yn), slot(1, yn), xn)
    fx.start()
    sy1 = push(8, slot(1, yn), slot(1, yn), sib)
    sy1.start()
    x1.wait_recv()
    sx1 = push(9, slot(1, xn), slot(1, xn), sib)
    sx1.start()
    y0.wait_recv()
    sy0 = push(10, slot(0, yn), slot(0, yn), sib)
    sy0.start()
    fy.wait_recv()
    sd0 = push(11, slot(0, diag), slot(0, diag), sib)
    sd0.start()
    fx.wait_recv()
    sd1 = push(12, slot(1, diag), slot(1, diag), sib)
    sd1.start()
    for cp in (s, sx0, sy1, sx1, sy0, sd0, sd1):
        cp.wait_recv()
    for cp in (x0, y1, x1, y0, s, fy, sx0, fx, sy1, sx1, sy0, sd0, sd1):
        cp.wait_send()
    mine.wait()

def spread(x, cid=0):
    h, rows, d = x.shape
    return pl.pallas_call(
        functools.partial(spread_kernel, rows),
        out_shape=jax.ShapeDtypeStruct((h, 8 * rows, d), x.dtype),
        in_specs=[pl.BlockSpec(memory_space=pl.ANY)],
        out_specs=pl.BlockSpec(memory_space=pl.ANY),
        scratch_shapes=[pltpu.SemaphoreType.DMA, pltpu.SemaphoreType.DMA((13,)), pltpu.SemaphoreType.DMA((13,))],
        compiler_params=pltpu.CompilerParams(collective_id=cid, has_side_effects=True),
        cost_estimate=pl.CostEstimate(flops=0, bytes_accessed=120_000_000, transcendentals=0),
        name="spread",
    )(x)

def fold_steps(rows, p_ref, own, sibs, dx, dy, rx, ry, local_sem, send, recv):
    c, sib, xn, yn = partners()
    diag = yn + (xn - c)
    wide = jnp.float32
    tall = 32 if rows % 32 == 0 else 8

    def blk(who):
        return p_ref.at[:, pl.ds(pl.multiple_of(who * rows, rows), rows), :]

    def push(i, src, dst, dev):
        return pltpu.make_async_remote_copy(
            src_ref=src,
            dst_ref=dst,
            send_sem=send.at[i],
            recv_sem=recv.at[i],
            device_id={"col": dev},
            device_id_type=MESH,
        )

    def add(dst, src):
        @pl.loop(0, rows // tall)
        def _(i):
            r = pl.ds(pl.multiple_of(i * tall, tall), tall)
            dst[r, :] = (dst[r, :].astype(wide) + src[r, :].astype(wide)).astype(dst.dtype)

    def pair(j):
        add(own.at[j, 0], sibs.at[j, 0])
        add(own.at[j, 1], sibs.at[j, 1])

    dests = (diag, xn, yn, c)
    loads = [pltpu.make_async_copy(blk(d), own.at[j], local_sem.at[j]) for j, d in enumerate(dests)]
    for load in loads:
        load.start()
    yield None
    sides = [push(j, blk(d + (sib - c)), sibs.at[j], sib) for j, d in enumerate(dests)]
    for side in sides:
        side.start()
    yield None
    loads[0].wait()
    sides[0].wait_recv()
    pair(0)
    a = push(4, own.at[0, 0], dx, xn)
    b = push(5, own.at[0, 1], dy, yn)
    a.start()
    b.start()
    yield None
    loads[1].wait()
    sides[1].wait_recv()
    pair(1)
    x0 = push(6, own.at[1, 0], rx.at[0], xn)
    x0.start()
    yield None
    loads[2].wait()
    sides[2].wait_recv()
    pair(2)
    y1 = push(7, own.at[2, 1], ry.at[1], yn)
    y1.start()
    yield None
    a.wait_recv()
    add(own.at[2, 0], dx)
    y0 = push(8, own.at[2, 0], ry.at[0], yn)
    y0.start()
    yield None
    b.wait_recv()
    add(own.at[1, 1], dy)
    x1 = push(9, own.at[1, 1], rx.at[1], xn)
    x1.start()
    yield None
    loads[3].wait()
    sides[3].wait_recv()
    pair(3)
    yield None
    waits = ((x0, y0), (x1, y1))
    yield tall, waits, (*sides, a, b, x0, y1, y0, x1)


def fold_finish(rows, o_ref, own, rx, ry, tall, waits, sent):
    wide = jnp.float32
    for h in range(2):
        for copy in waits[h]:
            copy.wait_recv()

        @pl.loop(0, rows // tall)
        def _(i):
            r = pl.ds(pl.multiple_of(i * tall, tall), tall)
            o_ref[h, r, :] = (
                own[3, h, r, :].astype(wide) + rx[h, r, :].astype(wide) + ry[h, r, :].astype(wide)
            )

    for copy in sent:
        copy.wait_send()


def fold_scratch(h, rows, d, kind):
    return [
        pltpu.VMEM((4, h, rows, d), kind),
        pltpu.VMEM((4, h, rows, d), kind),
        pltpu.VMEM((rows, d), kind),
        pltpu.VMEM((rows, d), kind),
        pltpu.VMEM((h, rows, d), kind),
        pltpu.VMEM((h, rows, d), kind),
        pltpu.SemaphoreType.DMA((4,)),
        pltpu.SemaphoreType.DMA((10,)),
        pltpu.SemaphoreType.DMA((10,)),
    ]


def product_kernel(rows, flip, outer, *refs):
    if outer:
        a_ref, w_ref, f_ref, o_ref, g_ref = refs[:5]
        f_buf, g_buf, turned, f_sem, g_sem = refs[-5:]
        refs = refs[5:-5]
    else:
        a_ref, w_ref, o_ref = refs[:3]
        refs = refs[3:]
    a_buf, w_buf, stage, own, sibs, dx, dy, rx, ry, local_sem, send, recv = refs
    c, sib, xn, yn = partners()
    diag = yn + (xn - c)
    wide = jnp.float32
    d = o_ref.shape[-1]
    tile = 512
    tall = 32

    def push(i, src, dst, dev):
        return pltpu.make_async_remote_copy(
            src_ref=src,
            dst_ref=dst,
            send_sem=send.at[i],
            recv_sem=recv.at[i],
            device_id={"col": dev},
            device_id_type=MESH,
        )

    dests = (diag, xn, yn, c)
    step = sib - c
    weights = pltpu.make_async_copy(w_ref, w_buf, local_sem.at[8])
    weights.start()

    def load(i, who):
        return pltpu.make_async_copy(
            a_ref.at[:, pl.ds(pl.multiple_of(who * rows, rows), rows), :],
            a_buf.at[i],
            local_sem.at[i],
        )

    far = [load(j, dests[j] + step) for j in range(4)]
    near = [load(4 + j, dests[j]) for j in range(4)]
    for first, second in zip(far, near):
        first.start()
        second.start()
    owners = [d + step for d in dests] + list(dests)
    strip = 256

    def strips(n):
        cut = pl.ds(pl.multiple_of(n * strip, strip), strip)
        return [
            pltpu.make_async_copy(
                f_ref.at[:, pl.ds(pl.multiple_of(who * rows, rows), rows), cut],
                f_buf.at[lax.rem(n, 2), i],
                f_sem.at[lax.rem(n, 2), i],
            )
            for i, who in enumerate(owners)
        ]

    def strip_out(n):
        cut = pl.ds(pl.multiple_of(n * strip, strip), strip)
        slot = lax.rem(n, 2)
        return pltpu.make_async_copy(g_buf.at[slot], g_ref.at[cut, :], g_sem.at[slot])

    def outer_product():
        count = g_ref.shape[0] // strip
        depth = a_buf.shape[-1]

        @pl.loop(0, count)
        def _(n):
            slot = lax.rem(n, 2)
            for copy in strips(n):
                copy.wait()

            @pl.when(n + 1 < count)
            def _():
                for copy in strips(n + 1):
                    copy.start()

            @pl.when(n >= 2)
            def _():
                strip_out(n - 2).wait()

            turned[...] = f_buf[slot].reshape(16 * rows, strip).T

            @pl.loop(0, depth // tile)
            def _(m):
                cut = pl.ds(pl.multiple_of(m * tile, tile), tile)
                right = a_buf[:, :, :, cut].reshape(16 * rows, tile)
                value = jnp.dot(turned[...], right, preferred_element_type=wide)
                g_buf[slot, :, cut] = value.astype(g_buf.dtype)

            strip_out(n).start()

        strip_out(count - 2).wait()
        strip_out(count - 1).wait()

    if outer:
        for copy in strips(0):
            copy.start()
    greet((sib, xn, yn))
    weights.wait()

    def product(i, put):
        left = a_buf[i].reshape(2 * rows, a_buf.shape[-1])

        @pl.loop(0, d // tile)
        def _(n):
            cut = pl.ds(pl.multiple_of(n * tile, tile), tile)
            right = w_buf[cut, :] if flip else w_buf[:, cut]
            dims = (((1,), (1,)), ((), ())) if flip else (((1,), (0,)), ((), ()))
            value = lax.dot_general(left, right, dims, preferred_element_type=wide)
            put(cut, value.reshape(2, rows, tile))

    sides = [push(j, stage.at[j], sibs.at[j], sib) for j in range(4)]

    def for_sibling(j):
        far[j].wait()

        def put(cut, value):
            stage[j, :, :, cut] = value.astype(stage.dtype)

        product(j, put)
        sides[j].start()

    def for_chip(j):
        near[j].wait()
        sides[j].wait_recv()

        def put(cut, value):
            own[j, :, :, cut] = (value + sibs[j, :, :, cut].astype(wide)).astype(own.dtype)

        product(4 + j, put)

    def add(dst, src):
        @pl.loop(0, rows // tall)
        def _(i):
            r = pl.ds(pl.multiple_of(i * tall, tall), tall)
            dst[r, :] = (dst[r, :].astype(wide) + src[r, :].astype(wide)).astype(dst.dtype)

    for_sibling(0)
    near[0].wait()

    def hold(cut, value):
        o_ref[:, :, cut] = value

    product(4, hold)
    sides[0].wait_recv()
    for h in range(2):

        @pl.loop(0, rows // tall)
        def _(i):
            r = pl.ds(pl.multiple_of(i * tall, tall), tall)
            own[0, h, r, :] = (o_ref[h, r, :] + sibs[0, h, r, :].astype(wide)).astype(own.dtype)

    a = push(4, own.at[0, 0], dx, xn)
    b = push(5, own.at[0, 1], dy, yn)
    a.start()
    b.start()
    for_sibling(1)
    for_sibling(2)
    for_chip(1)
    x0 = push(6, own.at[1, 0], rx.at[0], xn)
    x0.start()
    for_sibling(3)
    for_chip(2)
    y1 = push(7, own.at[2, 1], ry.at[1], yn)
    y1.start()
    a.wait_recv()
    add(own.at[2, 0], dx)
    y0 = push(8, own.at[2, 0], ry.at[0], yn)
    y0.start()
    b.wait_recv()
    add(own.at[1, 1], dy)
    x1 = push(9, own.at[1, 1], rx.at[1], xn)
    x1.start()
    near[3].wait()
    sides[3].wait_recv()

    def put(cut, value):
        o_ref[:, :, cut] = value + sibs[3, :, :, cut].astype(wide)

    product(7, put)
    if outer:
        outer_product()
    for h, waits in enumerate(((x0, y0), (x1, y1))):
        for copy in waits:
            copy.wait_recv()

        @pl.loop(0, rows // tall)
        def _(i):
            r = pl.ds(pl.multiple_of(i * tall, tall), tall)
            o_ref[h, r, :] = o_ref[h, r, :] + rx[h, r, :].astype(wide) + ry[h, r, :].astype(wide)

    for copy in (*sides, a, b, x0, y1, y0, x1):
        copy.wait_send()


def product_sum(left, right, flip, cid, feed=None, room=44):
    h, total, depth = left.shape
    rows = total // 8
    d = right.shape[0] if flip else right.shape[1]
    low = left.dtype
    outer = feed is not None
    out_shape = [jax.ShapeDtypeStruct((h, rows, d), jnp.float32)]
    out_specs = [pl.BlockSpec(memory_space=pltpu.VMEM)]
    scratch = [
        pltpu.VMEM((8, h, rows, depth), low),
        pltpu.VMEM(right.shape, low),
        pltpu.VMEM((4, h, rows, d), low),
        pltpu.VMEM((3, h, rows, d), low),
        pltpu.VMEM((4, h, rows, d), low),
        pltpu.VMEM((rows, d), low),
        pltpu.VMEM((rows, d), low),
        pltpu.VMEM((h, rows, d), low),
        pltpu.VMEM((h, rows, d), low),
        pltpu.SemaphoreType.DMA((9,)),
        pltpu.SemaphoreType.DMA((10,)),
        pltpu.SemaphoreType.DMA((10,)),
    ]
    flops = 2 * h * total * depth * d
    if outer:
        width = feed.shape[-1]
        flops += 2 * h * total * depth * width
        out_shape.append(jax.ShapeDtypeStruct((width, depth), low))
        out_specs.append(pl.BlockSpec(memory_space=pl.ANY))
        scratch += [
            pltpu.VMEM((2, 8, h, rows, 256), low),
            pltpu.VMEM((2, 256, depth), low),
            pltpu.VMEM((256, h * total), low),
            pltpu.SemaphoreType.DMA((2, 8)),
            pltpu.SemaphoreType.DMA((2,)),
        ]
    result = pl.pallas_call(
        functools.partial(product_kernel, rows, flip, outer),
        out_shape=out_shape,
        in_specs=[pl.BlockSpec(memory_space=pl.ANY)] * (3 if outer else 2),
        out_specs=out_specs,
        scratch_shapes=scratch,
        compiler_params=pltpu.CompilerParams(
            collective_id=cid,
            has_side_effects=True,
            vmem_limit_bytes=(52 if outer else room) << 20,
        ),
        cost_estimate=pl.CostEstimate(
            flops=flops, bytes_accessed=130_000_000, transcendentals=0
        ),
        name="product_sum",
    )(*((left, right, feed) if outer else (left, right)))
    return result if outer else result[0]


def fold_small_kernel(
    rows, p_ref, g_ref, o_ref, k_ref, own, sibs, dx, dy, rx, ry, local_sem, send, recv,
    gown, gsibs, grx, glocal, gsend, grecv,
):
    c, sib, xn, yn = partners()
    m = c % 4
    m_sib = m + 1 - 2 * (m % 2)
    m_x = m + 2 - 4 * (m // 2)
    m_diag = m_sib + (m_x - m)
    wide = jnp.float32

    def push(i, src, dst, dev):
        return pltpu.make_async_remote_copy(
            src_ref=src,
            dst_ref=dst,
            send_sem=gsend.at[i],
            recv_sem=grecv.at[i],
            device_id={"col": dev},
            device_id_type=MESH,
        )

    steps = fold_steps(rows, p_ref, own, sibs, dx, dy, rx, ry, local_sem, send, recv)
    next(steps)
    loads = [
        pltpu.make_async_copy(g_ref.at[d], gown.at[j], glocal.at[j])
        for j, d in enumerate((m_x, m))
    ]
    for load in loads:
        load.start()
    greet((sib, xn, yn))
    sides = [push(j, g_ref.at[d], gsibs.at[j], sib) for j, d in enumerate((m_diag, m_sib))]
    sides[0].start()
    next(steps)
    sides[1].start()
    tall = k_ref.shape[0] // 4
    loads[0].wait()
    sides[0].wait_recv()

    @pl.loop(0, 4)
    def _(i):
        r = pl.ds(pl.multiple_of(i * tall, tall), tall)
        gown[0, r, :] = (gown[0, r, :].astype(wide) + gsibs[0, r, :].astype(wide)).astype(
            gown.dtype
        )

    over = push(2, gown.at[0], grx, xn)
    over.start()
    last = None
    for step in steps:
        last = step if step is not None else last
    fold_finish(rows, o_ref, own, rx, ry, *last)
    loads[1].wait()
    sides[1].wait_recv()
    over.wait_recv()

    @pl.loop(0, 4)
    def _(i):
        r = pl.ds(pl.multiple_of(i * tall, tall), tall)
        k_ref[r, :] = (
            gown[1, r, :].astype(wide) + gsibs[1, r, :].astype(wide) + grx[r, :].astype(wide)
        )

    for copy in (*sides, over):
        copy.wait_send()


def fold_small(p, g, cid):
    h, total, d = p.shape
    rows = total // 8
    share, tall, _ = g.shape
    return pl.pallas_call(
        functools.partial(fold_small_kernel, rows),
        out_shape=(
            jax.ShapeDtypeStruct((h, rows, d), jnp.float32),
            jax.ShapeDtypeStruct((tall, d), jnp.float32),
        ),
        in_specs=[pl.BlockSpec(memory_space=pl.ANY)] * 2,
        out_specs=[pl.BlockSpec(memory_space=pltpu.VMEM)] * 2,
        scratch_shapes=fold_scratch(h, rows, d, p.dtype)
        + [
            pltpu.VMEM((2, tall, d), g.dtype),
            pltpu.VMEM((2, tall, d), g.dtype),
            pltpu.VMEM((tall, d), g.dtype),
            pltpu.SemaphoreType.DMA((2,)),
            pltpu.SemaphoreType.DMA((3,)),
            pltpu.SemaphoreType.DMA((3,)),
        ],
        compiler_params=pltpu.CompilerParams(
            collective_id=cid, has_side_effects=True, vmem_limit_bytes=40 << 20
        ),
        cost_estimate=pl.CostEstimate(flops=0, bytes_accessed=60_000_000, transcendentals=0),
        name="fold_small",
    )(p, g)


def open_kernel(
    rows, tiers, x_ref, q_ref, w_ref, g_ref, u_ref, *refs
):
    small = refs[:5]
    o_ref, sa_ref, qa_ref, wa_ref, both_ref = refs[5:10]
    tokens, stacked, both_buf, in_sem, local_sem, send, recv, line_send, line_recv = refs[10:]
    c, sib, xn, yn = partners()
    diag = yn + (xn - c)
    r = lax.axis_index("row")
    last = tiers - 1
    weights = []
    for src, dst in ((stacked, sa_ref), (q_ref, qa_ref), (w_ref, wa_ref)):
        cut = src.shape[0] // 32 * 16
        weights += [(src, dst, pl.ds(0, cut)), (src, dst, pl.ds(cut, src.shape[0] - cut))]
    pieces = len(weights)

    def slot(half, who):
        return o_ref.at[half, pl.ds(pl.multiple_of(who * rows, rows), rows), :]

    def both(who):
        return o_ref.at[:, pl.ds(pl.multiple_of(who * rows, rows), rows), :]

    started = []

    def push(src, dst, **dev):
        i = len(started)
        copy = pltpu.make_async_remote_copy(
            src_ref=src,
            dst_ref=dst,
            send_sem=send.at[i],
            recv_sem=recv.at[i],
            device_id=dev,
            device_id_type=MESH,
        )
        copy.start()
        started.append(copy)
        return copy

    width = g_ref.shape[1]
    first = [pltpu.make_async_copy(x_ref, tokens, in_sem.at[0])]
    base = 0
    for i, ref in enumerate(small):
        tall = ref.shape[0]
        first.append(
            pltpu.make_async_copy(ref, stacked.at[pl.ds(base, tall)], in_sem.at[1 + i])
        )
        base += tall
    later = [
        pltpu.make_async_copy(g_ref, both_buf.at[:, pl.ds(0, width)], in_sem.at[6]),
        pltpu.make_async_copy(u_ref, both_buf.at[:, pl.ds(width, width)], in_sem.at[7]),
    ]
    for copy in (*first, *later):
        copy.start()
    local = [
        pltpu.make_async_copy(tokens, both(c), local_sem.at[0]),
        pltpu.make_async_copy(stacked, sa_ref.at[r], local_sem.at[1]),
        pltpu.make_async_copy(q_ref, qa_ref.at[r], local_sem.at[2]),
        pltpu.make_async_copy(w_ref, wa_ref.at[r], local_sem.at[3]),
        pltpu.make_async_copy(both_buf, both_ref, local_sem.at[4]),
    ]
    barrier = pltpu.get_barrier_semaphore()
    for d in (sib, xn, yn):
        pl.semaphore_signal(barrier, inc=1, device_id={"col": d}, device_id_type=MESH)

    @pl.when(r < last)
    def _():
        pl.semaphore_signal(barrier, inc=1, device_id={"row": r + 1}, device_id_type=MESH)

    @pl.when(r > 0)
    def _():
        pl.semaphore_signal(barrier, inc=1, device_id={"row": r - 1}, device_id_type=MESH)

    @pl.when((r > 0) & (r < last))
    def _():
        pl.semaphore_wait(barrier, 5)

    @pl.when((r == 0) | (r == last))
    def _():
        pl.semaphore_wait(barrier, 4)

    def passing(way, hop, j):
        src, dst, cut = weights[j]
        whose = r - hop if way == 0 else r + hop
        return pltpu.make_async_remote_copy(
            src_ref=src.at[cut] if hop == 0 else dst.at[whose, cut],
            dst_ref=dst.at[whose, cut],
            send_sem=line_send.at[way, hop, j],
            recv_sem=line_recv.at[way, hop, j],
            device_id={"row": r + 1 if way == 0 else r - 1},
            device_id_type=MESH,
        )

    def going(way, hop):
        return (r < last) & (r >= hop) if way == 0 else (r > 0) & (r + hop <= last)

    def coming(way, hop):
        return r > hop if way == 0 else r + hop < last

    def forward(hop, j):
        for way in range(2):
            if hop > 0:

                @pl.when(coming(way, hop - 1))
                def _():
                    passing(way, hop - 1, j).wait_recv()

            @pl.when(going(way, hop))
            def _():
                passing(way, hop, j).start()

    for copy in first:
        copy.wait()
    x0 = push(tokens.at[0], slot(0, c), col=xn)
    y1 = push(tokens.at[1], slot(1, c), col=yn)
    for j in range(pieces):
        forward(0, j)
    x1 = push(tokens.at[1], slot(1, c), col=xn)
    y0 = push(tokens.at[0], slot(0, c), col=yn)
    push(tokens, both(c), col=sib)
    for copy in later:
        copy.wait()
    for copy in local:
        copy.start()
    forward(1, 0)
    forward(1, 1)
    x0.wait_recv()
    fy = push(slot(0, xn), slot(0, xn), col=yn)
    push(slot(0, xn), slot(0, xn), col=sib)
    y1.wait_recv()
    fx = push(slot(1, yn), slot(1, yn), col=xn)
    push(slot(1, yn), slot(1, yn), col=sib)
    for j in range(2, pieces):
        forward(1, j)
    x1.wait_recv()
    push(slot(1, xn), slot(1, xn), col=sib)
    y0.wait_recv()
    push(slot(0, yn), slot(0, yn), col=sib)
    for hop in range(2, last):
        for j in range(pieces):
            forward(hop, j)
    fy.wait_recv()
    push(slot(0, diag), slot(0, diag), col=sib)
    fx.wait_recv()
    push(slot(1, diag), slot(1, diag), col=sib)
    for copy in started:
        if not any(copy is other for other in (x0, y1, x1, y0, fy, fx)):
            copy.wait_recv()
    for j in range(pieces):
        for way in range(2):

            @pl.when(coming(way, last - 1))
            def _():
                passing(way, last - 1, j).wait_recv()

            for hop in range(last):

                @pl.when(going(way, hop))
                def _():
                    passing(way, hop, j).wait_send()

    for copy in started:
        copy.wait_send()
    for copy in local:
        copy.wait()


def open_all(x, query, output, gate, up, small, tiers, cid):
    h, rows, d = x.shape
    low = x.dtype
    stack = (sum(piece.shape[0] for piece in small), small[0].shape[1])
    both = (gate.shape[0], 2 * gate.shape[1])
    return pl.pallas_call(
        functools.partial(open_kernel, rows, tiers),
        out_shape=(
            jax.ShapeDtypeStruct((h, 8 * rows, d), low),
            jax.ShapeDtypeStruct((tiers, *stack), low),
            jax.ShapeDtypeStruct((tiers, *query.shape), low),
            jax.ShapeDtypeStruct((tiers, *output.shape), low),
            jax.ShapeDtypeStruct(both, low),
        ),
        in_specs=[pl.BlockSpec(memory_space=pl.ANY)] * 10,
        out_specs=[pl.BlockSpec(memory_space=pl.ANY)] * 5,
        scratch_shapes=[
            pltpu.VMEM(x.shape, low),
            pltpu.VMEM(stack, low),
            pltpu.VMEM(both, low),
            pltpu.SemaphoreType.DMA((8,)),
            pltpu.SemaphoreType.DMA((5,)),
            pltpu.SemaphoreType.DMA((13,)),
            pltpu.SemaphoreType.DMA((13,)),
            pltpu.SemaphoreType.DMA((2, tiers - 1, 6)),
            pltpu.SemaphoreType.DMA((2, tiers - 1, 6)),
        ],
        compiler_params=pltpu.CompilerParams(
            collective_id=cid, has_side_effects=True, vmem_limit_bytes=60 << 20
        ),
        cost_estimate=pl.CostEstimate(flops=0, bytes_accessed=200_000_000, transcendentals=0),
        name="open_all",
    )(x, query, output, gate, up, *small)


def share_kernel(near, s_ref, sa_ref, held, local_sem, send, recv):
    c, sib, xn, yn = partners()
    diag = yn + (xn - c)
    height = s_ref.shape[1]
    started = []

    def part(ref, first):
        return ref.at[:, pl.ds(0, near) if first else pl.ds(near, height - near), :]

    def push(who, first, dev, own=False):
        i = len(started)
        dst = part(sa_ref.at[who], first)
        copy = pltpu.make_async_remote_copy(
            src_ref=part(held, first) if own else dst,
            dst_ref=dst,
            send_sem=send.at[i],
            recv_sem=recv.at[i],
            device_id={"col": dev},
            device_id_type=MESH,
        )
        copy.start()
        started.append(copy)
        return copy

    fetch = pltpu.make_async_copy(s_ref, held, local_sem.at[0])
    fetch.start()
    mine = pltpu.make_async_copy(held, sa_ref.at[c], local_sem.at[1])
    greet((sib, xn, yn))
    fetch.wait()
    rx = push(c, False, xn, own=True)
    ry = push(c, False, yn, own=True)
    kx = push(c, True, xn, own=True)
    push(c, True, sib, own=True)
    push(c, False, sib, own=True)
    mine.start()
    rx.wait_recv()
    fd = push(xn, False, yn)
    push(xn, False, sib)
    ry.wait_recv()
    push(yn, False, sib)
    fd.wait_recv()
    push(diag, False, sib)
    kx.wait_recv()
    push(xn, True, sib)
    for copy in started:
        if not any(copy is other for other in (kx, rx, ry, fd)):
            copy.wait_recv()
    for copy in started:
        copy.wait_send()
    mine.wait()


def share_small(small, near, cid):
    return pl.pallas_call(
        functools.partial(share_kernel, near),
        out_shape=jax.ShapeDtypeStruct((8, *small.shape), small.dtype),
        in_specs=[pl.BlockSpec(memory_space=pl.ANY)],
        out_specs=pl.BlockSpec(memory_space=pl.ANY),
        scratch_shapes=[
            pltpu.VMEM(small.shape, small.dtype),
            pltpu.SemaphoreType.DMA((2,)),
            pltpu.SemaphoreType.DMA((10,)),
            pltpu.SemaphoreType.DMA((10,)),
        ],
        compiler_params=pltpu.CompilerParams(collective_id=cid, has_side_effects=True),
        cost_estimate=pl.CostEstimate(flops=0, bytes_accessed=60_000_000, transcendentals=0),
        name="share_small",
    )(small)


def rounds_of(rows, x_ref, held, local_sem, send, recv, consume, prepare):
    c, sib, xn, yn = partners()
    diag = yn + (xn - c)
    step = sib - c

    def place(t, j, n=1):
        return held.at[t, pl.ds(j * rows, n * rows), :]

    started = []

    def push(src, dst, dev):
        i = len(started)
        copy = pltpu.make_async_remote_copy(
            src_ref=src,
            dst_ref=dst,
            send_sem=send.at[i],
            recv_sem=recv.at[i],
            device_id={"col": dev},
            device_id_type=MESH,
        )
        copy.start()
        started.append(copy)
        return copy

    mine = [pltpu.make_async_copy(x_ref.at[h], place(0, h), local_sem.at[h]) for h in range(2)]
    for copy in mine:
        copy.start()
    greet((sib, xn, yn))
    x0 = push(x_ref.at[0], place(1, 0), xn)
    y1 = push(x_ref.at[1], place(1, 1), yn)
    x1 = push(x_ref.at[1], place(2, 0), xn)
    y0 = push(x_ref.at[0], place(2, 1), yn)
    s0 = push(x_ref.at[0], place(0, 2), sib)
    s1 = push(x_ref.at[1], place(0, 3), sib)
    prepare(0)
    for copy in mine:
        copy.wait()
    s0.wait_recv()
    s1.wait_recv()
    consume(0, 0, ((0, c), (1, c), (0, sib), (1, sib)))
    x0.wait_recv()
    fy = push(place(1, 0), place(3, 0), yn)
    y1.wait_recv()
    fx = push(place(1, 1), place(3, 1), xn)
    prepare(1)
    t1 = push(place(1, 0, 2), place(1, 2, 2), sib)
    t1.wait_recv()
    consume(1, 0, ((0, xn), (1, yn), (0, xn + step), (1, yn + step)))
    prepare(2)
    x1.wait_recv()
    y0.wait_recv()
    t2 = push(place(2, 0, 2), place(2, 2, 2), sib)
    t2.wait_recv()
    consume(2, 0, ((1, xn), (0, yn), (1, xn + step), (0, yn + step)))
    prepare(3)
    fy.wait_recv()
    fx.wait_recv()
    t3 = push(place(3, 0, 2), place(3, 2, 2), sib)
    consume(3, 0, ((0, diag), (1, diag)))
    t3.wait_recv()
    consume(3, 2, ((0, diag + step), (1, diag + step)))
    for copy in started:
        copy.wait_send()


def piece_at(ref, rows, piece):
    half, who = piece
    return ref.at[half, pl.ds(pl.multiple_of(who * rows, rows), rows), :]


def units_back_kernel(
    rows, x_ref, w_ref, u_ref, g_ref, v_ref, p_ref, d_ref,
    held, weights, units, turned, gates, ups, grads, total_ref,
    weight_sem, load_sem, store_sem, local_sem, send, recv,
):
    c, sib, xn, yn = partners()
    diag = yn + (xn - c)
    step = sib - c
    wide = jnp.float32
    width = w_ref.shape[0]
    d = w_ref.shape[1]
    plan = (
        ((0, c), (1, c), (0, sib), (1, sib)),
        ((0, xn), (1, yn), (0, xn + step), (1, yn + step)),
        ((1, xn), (0, yn), (1, xn + step), (0, yn + step)),
        ((0, diag), (1, diag), (0, diag + step), (1, diag + step)),
    )
    fetch = pltpu.make_async_copy(w_ref, weights, weight_sem)
    fetch.start()

    def loads(t):
        copies = []
        for j, piece in enumerate(plan[t]):
            for k, (src, dst) in enumerate(((u_ref, units), (g_ref, gates), (v_ref, ups))):
                copies.append(
                    pltpu.make_async_copy(
                        piece_at(src, rows, piece),
                        dst.at[t % 2, pl.ds(j * rows, rows), :],
                        load_sem.at[t % 2, j, k],
                    )
                )
        return copies

    def stores(t, first=0, count=4):
        return [
            pltpu.make_async_copy(
                grads.at[t % 2, pl.ds(j * rows, rows), :],
                piece_at(p_ref, rows, plan[t][j]),
                store_sem.at[t % 2, j],
            )
            for j in range(first, first + count)
        ]

    for copy in loads(0):
        copy.start()

    tile = 256

    def prepare(t):
        if t == 0:
            fetch.wait()
        if t < 3:
            for copy in loads(t + 1):
                copy.start()
        for copy in loads(t):
            copy.wait()

        @pl.loop(0, width // tile)
        def _(n):
            cut = pl.ds(pl.multiple_of(n * tile, tile), tile)
            gate = gates[t % 2, :, cut]
            square = gate * gate
            bent = jnp.tanh(CURVE * (gate + BEND * gate * square))
            rise = 0.5 * (1.0 + bent)
            slope = rise + (0.5 * CURVE) * gate * (1.0 - bent * bent) * (1.0 + 3.0 * BEND * square)
            gates[t % 2, :, cut] = ups[t % 2, :, cut] * slope
            ups[t % 2, :, cut] = gate * rise
            turned[cut, :] = units[t % 2, :, cut].T

    def consume(t, first, pieces):
        if t >= 2 and first == 0:
            for copy in stores(t - 2):
                copy.wait()
        span = slice(first * rows, (first + len(pieces)) * rows)

        @pl.loop(0, width // 512)
        def _(n):
            cut = pl.ds(pl.multiple_of(n * 512, 512), 512)
            grad = lax.dot_general(
                held[t, span, :],
                weights[cut, :],
                (((1,), (1,)), ((), ())),
                preferred_element_type=wide,
            )
            grads[t % 2, span, cut] = (grad * gates[t % 2, span, cut]).astype(grads.dtype)
            cut_up = pl.ds(pl.multiple_of(width + n * 512, 512), 512)
            grads[t % 2, span, cut_up] = (grad * ups[t % 2, span, cut]).astype(grads.dtype)

        for copy in stores(t, first, len(pieces)):
            copy.start()

        block = d_ref.shape[-1]

        @pl.loop(0, d // block)
        def _(n):
            cut = pl.ds(pl.multiple_of(n * block, block), block)
            value = jnp.dot(turned[:, span], held[t, span, cut], preferred_element_type=wide)
            if t > 0:
                value = value + total_ref[:, cut]
            if first == 0:
                total_ref[:, cut] = value
            else:
                d_ref[n] = value.astype(d_ref.dtype)

    rounds_of(rows, x_ref, held, local_sem, send, recv, consume, prepare)
    for copy in (*stores(2), *stores(3)):
        copy.wait()


def units_back(x, down, units, gate, up, tiers, cid):
    h, rows, d = x.shape
    width = down.shape[0]
    low = x.dtype
    return pl.pallas_call(
        functools.partial(units_back_kernel, rows),
        out_shape=(
            jax.ShapeDtypeStruct((h, 8 * rows, 2 * width), low),
            jax.ShapeDtypeStruct((tiers, width, d // tiers), low),
        ),
        in_specs=[pl.BlockSpec(memory_space=pl.ANY)] * 5,
        out_specs=[
            pl.BlockSpec(memory_space=pl.ANY),
            pl.BlockSpec(memory_space=pltpu.VMEM),
        ],
        scratch_shapes=[
            pltpu.VMEM((4, 4 * rows, d), low),
            pltpu.VMEM((width, d), low),
            pltpu.VMEM((2, 4 * rows, width), low),
            pltpu.VMEM((width, 4 * rows), low),
            pltpu.VMEM((2, 4 * rows, width), jnp.float32),
            pltpu.VMEM((2, 4 * rows, width), jnp.float32),
            pltpu.VMEM((2, 4 * rows, 2 * width), low),
            pltpu.VMEM((width, d), jnp.float32),
            pltpu.SemaphoreType.DMA,
            pltpu.SemaphoreType.DMA((2, 4, 3)),
            pltpu.SemaphoreType.DMA((2, 4)),
            pltpu.SemaphoreType.DMA((2,)),
            pltpu.SemaphoreType.DMA((11,)),
            pltpu.SemaphoreType.DMA((11,)),
        ],
        compiler_params=pltpu.CompilerParams(
            collective_id=cid, has_side_effects=True, vmem_limit_bytes=52 << 20
        ),
        cost_estimate=pl.CostEstimate(
            flops=64 * h * rows * width * d, bytes_accessed=130_000_000, transcendentals=0
        ),
        name="units_back",
    )(x, down, units, gate, up)


def heads_back_kernel(
    rows, scale, x_ref, w_ref, m_ref, q_ref, k_ref, v_ref, s_ref, gq_ref, gk_ref, gv_ref, d_ref,
    held, weights, mixed, queries, keys, values, seen, total_ref, load_sem, local_sem, send, recv,
):
    wide = jnp.float32
    d = w_ref.shape[1]
    low = weights.dtype
    pairs = (
        (w_ref, weights), (q_ref, queries), (k_ref, keys), (v_ref, values), (s_ref, seen),
        (m_ref, mixed),
    )
    loads = [
        pltpu.make_async_copy(src, dst, load_sem.at[i]) for i, (src, dst) in enumerate(pairs)
    ]
    for copy in loads:
        copy.start()
    back = (((1,), (1,)), ((), ()))

    def prepare(t):
        if t == 0:
            for copy in loads:
                copy.wait()
            gk_ref[...] = jnp.zeros_like(gk_ref)
            gv_ref[...] = jnp.zeros_like(gv_ref)

    def consume(t, first, pieces):
        part = slice(first * rows, (first + len(pieces)) * rows)
        grad_mixed = lax.dot_general(
            held[t, part, :], weights[...], back, preferred_element_type=wide
        )
        grad_mixed = grad_mixed.astype(low)
        spans = []
        for j, (half, who) in enumerate(pieces):
            span = pl.ds(pl.multiple_of(who * rows, rows), rows)
            spans.append(mixed[half, span, :])
            query = queries[half, span, :]
            grad = grad_mixed[j * rows : (j + 1) * rows]
            score = lax.dot_general(query, keys[half], back, preferred_element_type=wide) * scale
            score = jnp.where(seen[half, span, :] > 0, score, NEGATIVE)
            power = jnp.exp(score - jnp.max(score, axis=-1, keepdims=True))
            prob = power / jnp.sum(power, axis=-1, keepdims=True)
            slope = lax.dot_general(grad, values[half], back, preferred_element_type=wide)
            mean = jnp.sum(prob * slope, axis=-1, keepdims=True)
            flow = (prob * (slope - mean)).astype(low)
            gq_ref[half, span, :] = jnp.dot(flow, keys[half], preferred_element_type=wide) * scale
            gk_ref[half] += jnp.dot(flow.T, query, preferred_element_type=wide) * scale
            gv_ref[half] += jnp.dot(prob.astype(low).T, grad, preferred_element_type=wide)
        turned = jnp.concatenate(spans, axis=0).T

        @pl.loop(0, d // 512)
        def _(n):
            cut = pl.ds(pl.multiple_of(n * 512, 512), 512)
            value = jnp.dot(turned, held[t, part, cut], preferred_element_type=wide)
            if t > 0:
                value = value + total_ref[:, cut]
            if first == 0:
                total_ref[:, cut] = value
            else:
                d_ref[:, cut] = value.astype(d_ref.dtype)

    rounds_of(rows, x_ref, held, local_sem, send, recv, consume, prepare)


def heads_back(x, output, mixed, query, key, value, visible, scale, cid):
    h, rows, d = x.shape
    low = x.dtype
    grad = jax.ShapeDtypeStruct(query.shape, jnp.float32)
    return pl.pallas_call(
        functools.partial(heads_back_kernel, rows, scale),
        out_shape=(grad, grad, grad, jax.ShapeDtypeStruct(output.shape, low)),
        in_specs=[pl.BlockSpec(memory_space=pl.ANY)] * 7,
        out_specs=[pl.BlockSpec(memory_space=pltpu.VMEM)] * 4,
        scratch_shapes=[
            pltpu.VMEM((4, 4 * rows, d), low),
            pltpu.VMEM(output.shape, low),
            pltpu.VMEM(mixed.shape, low),
            pltpu.VMEM(query.shape, low),
            pltpu.VMEM(query.shape, low),
            pltpu.VMEM(query.shape, low),
            pltpu.VMEM(visible.shape, visible.dtype),
            pltpu.VMEM(output.shape, jnp.float32),
            pltpu.SemaphoreType.DMA((6,)),
            pltpu.SemaphoreType.DMA((2,)),
            pltpu.SemaphoreType.DMA((11,)),
            pltpu.SemaphoreType.DMA((11,)),
        ],
        compiler_params=pltpu.CompilerParams(
            collective_id=cid, has_side_effects=True, vmem_limit_bytes=60 << 20
        ),
        cost_estimate=pl.CostEstimate(
            flops=20_000_000_000, bytes_accessed=130_000_000, transcendentals=0
        ),
        name="heads_back",
    )(x, output, mixed, query, key, value, visible)


def total_kernel(x_ref, o_ref, sums, got, tier_sums, send, recv):
    c, sib, xn, yn = partners()
    r = lax.axis_index("row")
    tiers = lax.axis_size("row")
    others = [lax.rem(r + k, tiers) for k in range(1, tiers)]
    barrier = pltpu.get_barrier_semaphore()
    for d in (sib, xn, yn):
        pl.semaphore_signal(barrier, inc=1, device_id={"col": d}, device_id_type=MESH)
    for d in others:
        pl.semaphore_signal(barrier, inc=1, device_id={"row": d}, device_id_type=MESH)
    pl.semaphore_wait(barrier, 3 + len(others))
    sums[0] = x_ref[...]
    for i, dev in enumerate((sib, xn, yn)):
        copy = pltpu.make_async_remote_copy(
            src_ref=sums.at[i],
            dst_ref=got.at[i],
            send_sem=send.at[i],
            recv_sem=recv.at[i],
            device_id={"col": dev},
            device_id_type=MESH,
        )
        copy.start()
        copy.wait()
        sums[i + 1] = sums[i] + got[i]
    tier_sums[r] = sums[3]
    copies = []
    for k, d in enumerate(others):
        copy = pltpu.make_async_remote_copy(
            src_ref=sums.at[3],
            dst_ref=tier_sums.at[r],
            send_sem=send.at[3 + k],
            recv_sem=recv.at[3 + k],
            device_id={"row": d},
            device_id_type=MESH,
        )
        copy.start()
        copies.append(copy)
    for copy in copies:
        copy.wait()
    result = tier_sums[0]
    for k in range(1, tiers):
        result = result + tier_sums[k]
    o_ref[...] = result


def total(x, tiers, cid):
    return pl.pallas_call(
        total_kernel,
        out_shape=jax.ShapeDtypeStruct(x.shape, x.dtype),
        in_specs=[pl.BlockSpec(memory_space=pltpu.VMEM)],
        out_specs=pl.BlockSpec(memory_space=pltpu.VMEM),
        scratch_shapes=[
            pltpu.VMEM((4, *x.shape), x.dtype),
            pltpu.VMEM((3, *x.shape), x.dtype),
            pltpu.VMEM((tiers, *x.shape), x.dtype),
            pltpu.SemaphoreType.DMA((2 + tiers,)),
            pltpu.SemaphoreType.DMA((2 + tiers,)),
        ],
        compiler_params=pltpu.CompilerParams(collective_id=cid, has_side_effects=True),
        cost_estimate=pl.CostEstimate(flops=0, bytes_accessed=40_000_000, transcendentals=0),
        name="total",
    )(x)


def after(value, *earlier):
    return lax.optimization_barrier((value, *earlier))[0]


def general_body(
    hidden,
    per_layer,
    lengths,
    block_ids,
    out_grad,
    query_weight,
    key_weight,
    value_weight,
    output_weight,
    gate_weight,
    up_weight,
    down_weight,
    laurel_left,
    laurel_right,
    layer_gate,
    layer_proj,
    norm_gains,
    head_gains,
):
    local_rows = hidden.shape[0]
    seq_groups = hidden.shape[1]
    col_index = lax.axis_index("col")
    row_index = lax.axis_index("row")
    all_lengths = lengths
    lengths = lax.dynamic_slice_in_dim(all_lengths, row_index * seq_groups, seq_groups, 0)
    (
        query_cols,
        key_cols,
        value_cols,
        output_rows,
        gate_cols,
        up_cols,
        down_rows,
        left_cols,
        right_rows,
        gate_layer_cols,
        proj_layer_rows,
    ) = (
        lax.all_gather(query_weight, "row", axis=0, tiled=True),
        lax.all_gather(key_weight, "row", axis=0, tiled=True),
        lax.all_gather(value_weight, "row", axis=0, tiled=True),
        lax.all_gather(output_weight, "row", axis=1, tiled=True),
        lax.all_gather(gate_weight, "row", axis=0, tiled=True),
        lax.all_gather(up_weight, "row", axis=0, tiled=True),
        lax.all_gather(down_weight, "row", axis=1, tiled=True),
        lax.all_gather(laurel_left, "row", axis=0, tiled=True),
        lax.all_gather(laurel_right, "row", axis=1, tiled=True),
        lax.all_gather(layer_gate, "row", axis=0, tiled=True),
        lax.all_gather(layer_proj, "row", axis=1, tiled=True),
    )
    (
        query_full,
        key_full,
        value_full,
        output_full,
        left_full,
        right_full,
        gate_layer_full,
        proj_layer_full,
    ) = (
        lax.all_gather(query_cols, "col", axis=1, tiled=True),
        lax.all_gather(key_cols, "col", axis=1, tiled=True),
        lax.all_gather(value_cols, "col", axis=1, tiled=True),
        lax.all_gather(output_rows, "col", axis=0, tiled=True),
        lax.all_gather(left_cols, "col", axis=1, tiled=True),
        lax.all_gather(right_rows, "col", axis=0, tiled=True),
        lax.all_gather(gate_layer_cols, "col", axis=1, tiled=True),
        lax.all_gather(proj_layer_rows, "col", axis=0, tiled=True),
    )
    paired = jnp.concatenate([gate_cols, up_cols], axis=1)
    unit_width = gate_cols.shape[1]
    first_position = col_index * local_rows
    positions = first_position + jnp.arange(local_rows, dtype=jnp.int32)
    live_mask = positions[:, None] < lengths[None, :]
    keep_mask = live_mask.astype(jnp.float32)[:, :, None]
    reach_back = (WINDOW + local_rows - 2) // local_rows
    reach_ahead = (BLOCK + local_rows - 2) // local_rows
    key_span = (reach_back + 1 + reach_ahead) * local_rows
    key_position = first_position - reach_back * local_rows + jnp.arange(key_span, dtype=jnp.int32)
    filler_low = jnp.full((seq_groups, reach_back * local_rows), FAR_BLOCK, jnp.int32)
    filler_high = jnp.full((seq_groups, reach_ahead * local_rows), FAR_BLOCK, jnp.int32)
    padded_blocks = jnp.concatenate([filler_low, block_ids, filler_high], axis=1)
    key_blocks = lax.dynamic_slice_in_dim(padded_blocks, first_position, key_span, 1)
    query_blocks = lax.dynamic_slice_in_dim(block_ids, first_position, local_rows, 1)
    key_live = (key_position[None, :] >= 0) & (key_position[None, :] < lengths[:, None])
    query_live = positions[None, :] < lengths[:, None]
    distance = positions[:, None] - key_position[None, :]
    nearby = (query_blocks[:, :, None] >= key_blocks[:, None, :]) & (distance < WINDOW)[None]
    nearby = nearby & query_live[:, :, None] & key_live[:, None, :]
    visible = (nearby | (distance == 0)[None])[:, None, None]
    residual = hidden.astype(jnp.float32)
    normed_value, input_back = jax.vjp(input_norm, residual, norm_gains)
    normed_low = normed_value.astype(jnp.bfloat16)
    half_width = HD // 2
    frequency = jnp.exp(jnp.arange(half_width, dtype=jnp.float32) * (-2.0 * math.log(10000.0) / HD))
    angles = (positions.astype(jnp.float32)[:, None] * frequency[None, :])[:, None, None, :]

    def prepare(query_in, key_in, value_in, gain_rows):
        return (
            rotate(root_norm(query_in, gain_rows[0]), angles),
            rotate(root_norm(key_in, gain_rows[1]), angles),
            plain_norm(value_in),
        )

    query_raw = matmul_last(normed_low, query_full).reshape(local_rows, seq_groups, H, HD)
    key_raw = matmul_last(normed_low, key_full).reshape(local_rows, seq_groups, KV, HD)
    value_raw = matmul_last(normed_low, value_full).reshape(local_rows, seq_groups, KV, HD)
    (query_value, key_value, value_value), head_back = jax.vjp(
        prepare, query_raw, key_raw, value_raw, head_gains
    )
    query_low = query_value.astype(jnp.bfloat16).reshape(local_rows, seq_groups, KV, H // KV, HD)
    key_low = key_value.astype(jnp.bfloat16)
    value_low = value_value.astype(jnp.bfloat16)
    offsets = list(range(reach_back, -reach_ahead - 1, -1))
    key_parts = []
    value_parts = []
    for offset in offsets:
        if offset == 0:
            key_parts.append(key_low)
            value_parts.append(value_low)
        else:
            moved_key, moved_value = passed_along((key_low, value_low), "col", offset)
            key_parts.append(moved_key)
            value_parts.append(moved_value)
    near_keys = jnp.concatenate(key_parts, axis=0)
    near_values = jnp.concatenate(value_parts, axis=0)
    score_scale = HD ** (-0.5)

    def score_all():
        raw_scores = (
            jnp.einsum(
                "psjgd,esjd->sjgpe", query_low, near_keys, preferred_element_type=jnp.float32
            )
            * score_scale
        )
        return jnp.where(visible, raw_scores, NEGATIVE)

    scores = score_all()
    row_max = jnp.max(scores, axis=-1, keepdims=True)
    exponent = jnp.exp(scores - row_max)
    row_total = jnp.sum(exponent, axis=-1, keepdims=True)
    attn_prob = exponent / row_total
    log_total = row_max + jnp.log(row_total)
    mixed_heads = jnp.einsum(
        "sjgpe,esjd->psjgd",
        attn_prob.astype(jnp.bfloat16),
        near_values,
        preferred_element_type=jnp.float32,
    )
    mixed_low = mixed_heads.reshape(local_rows, seq_groups, H * HD).astype(jnp.bfloat16)
    out_proj = matmul_last(mixed_low, output_full)
    laurel_mid = matmul_last(normed_low, left_full).astype(jnp.bfloat16)
    low_rank = matmul_last(laurel_mid, right_full)
    (after_attention, feed_normed), middle_back = jax.vjp(
        middle, residual, out_proj, low_rank, normed_low.astype(jnp.float32), norm_gains
    )
    feed_low = feed_normed.astype(jnp.bfloat16)
    gate_up = matmul_last(lax.all_gather(feed_low, "col", axis=0, tiled=True), paired)
    unit_value, gate_back = jax.vjp(
        gated_product, gate_up[..., :unit_width], gate_up[..., unit_width:]
    )
    units_low = unit_value.astype(jnp.bfloat16)
    summed = lax.psum_scatter(
        matmul_last(units_low, down_rows), "col", scatter_dimension=0, tiled=True
    )
    after_feed, feed_back = jax.vjp(feed_join, after_attention, summed, norm_gains)
    feed_round = after_feed.astype(jnp.bfloat16)
    layer_pre = matmul_last(feed_round, gate_layer_full)
    layer_input = per_layer.astype(jnp.float32)
    layer_value, layer_back = jax.vjp(gated_product, layer_pre, layer_input)
    layer_low = layer_value.astype(jnp.bfloat16)
    projected = matmul_last(layer_low, proj_layer_full)
    out_value, final_back = jax.vjp(final_join, after_feed, projected, norm_gains)
    square_sums = jnp.stack(
        [
            jnp.sum(keep_mask * residual * residual),
            jnp.sum(keep_mask * after_attention * after_attention),
            jnp.sum(keep_mask * after_feed * after_feed),
            jnp.sum(keep_mask * out_value * out_value),
        ]
    )
    valid_count = jnp.sum(all_lengths).astype(jnp.float32)
    cotangent = out_grad.astype(jnp.float32) * keep_mask
    grad_feed_out, grad_projected, gains_final = final_back(cotangent)
    projected_low = grad_projected.astype(jnp.bfloat16)
    grad_proj_layer = outer_sum(layer_low, projected_low)
    grad_layer_pre, grad_layer_input = layer_back(matmul_back(projected_low, proj_layer_full))
    layer_pre_low = grad_layer_pre.astype(jnp.bfloat16)
    grad_gate_layer = outer_sum(feed_round, layer_pre_low)
    grad_after_feed = grad_feed_out + matmul_back(layer_pre_low, gate_layer_full)
    grad_after_attention_a, grad_summed, gains_feed = feed_back(grad_after_feed)
    summed_low = grad_summed.astype(jnp.bfloat16)
    block_rows = lax.all_gather(summed_low, "col", axis=0, tiled=True)
    grad_down = outer_sum(units_low, block_rows)
    grad_units = matmul_back(block_rows, down_rows)
    grad_down, grad_units = (grad_down, grad_units)
    grad_gate_value, grad_up_value = gate_back(grad_units)
    grad_paired = jnp.concatenate([grad_gate_value, grad_up_value], axis=-1).astype(jnp.bfloat16)
    grad_weights_paired = outer_sum(
        lax.all_gather(feed_low, "col", axis=0, tiled=True), grad_paired
    )
    grad_feed = lax.psum_scatter(
        matmul_back(grad_paired, paired).astype(jnp.bfloat16),
        "col",
        scatter_dimension=0,
        tiled=True,
    ).astype(jnp.float32)
    grad_residual_mid, grad_out_proj, grad_low_rank, grad_normed_mid, gains_middle = middle_back(
        (grad_after_attention_a, grad_feed)
    )
    out_proj_low = grad_out_proj.astype(jnp.bfloat16)
    grad_output = outer_sum(mixed_low, out_proj_low)
    grad_mixed = matmul_back(out_proj_low, output_full).astype(jnp.bfloat16)
    grad_mixed = grad_mixed.reshape(local_rows, seq_groups, KV, H // KV, HD)
    low_rank_grad = grad_low_rank.astype(jnp.bfloat16)
    grad_right = outer_sum(laurel_mid, low_rank_grad)
    grad_laurel_mid = matmul_back(low_rank_grad, right_full).astype(jnp.bfloat16)
    grad_left = outer_sum(normed_low, grad_laurel_mid)
    scores = score_all()
    attn_prob = jnp.exp(scores - log_total)
    grad_prob = jnp.einsum(
        "psjgd,esjd->sjgpe", grad_mixed, near_values, preferred_element_type=jnp.float32
    )
    grad_scores = (
        attn_prob * (grad_prob - jnp.sum(attn_prob * grad_prob, axis=-1, keepdims=True))
    ).astype(jnp.bfloat16)
    grad_queries = (
        jnp.einsum("sjgpe,esjd->psjgd", grad_scores, near_keys, preferred_element_type=jnp.float32)
        * score_scale
    )
    grad_near_keys = (
        jnp.einsum("sjgpe,psjgd->esjd", grad_scores, query_low, preferred_element_type=jnp.float32)
        * score_scale
    )
    grad_near_values = jnp.einsum(
        "sjgpe,psjgd->esjd",
        attn_prob.astype(jnp.bfloat16),
        grad_mixed,
        preferred_element_type=jnp.float32,
    )
    grad_key_total = grad_near_keys[reach_back * local_rows : (reach_back + 1) * local_rows]
    grad_value_total = grad_near_values[reach_back * local_rows : (reach_back + 1) * local_rows]
    for slot_index, offset in enumerate(offsets):
        if offset != 0:
            piece_keys = grad_near_keys[slot_index * local_rows : (slot_index + 1) * local_rows]
            piece_values = grad_near_values[slot_index * local_rows : (slot_index + 1) * local_rows]
            back_keys, back_values = (
                passed_along(piece_keys.astype(jnp.bfloat16), "col", -offset).astype(
                    piece_keys.dtype
                ),
                passed_along(piece_values.astype(jnp.bfloat16), "col", -offset).astype(
                    piece_values.dtype
                ),
            )
            grad_key_total = grad_key_total + back_keys
            grad_value_total = grad_value_total + back_values
    grad_query_raw, grad_key_raw, grad_value_raw, grad_heads = head_back(
        (grad_queries.reshape(local_rows, seq_groups, H, HD), grad_key_total, grad_value_total)
    )
    query_grad_low = grad_query_raw.reshape(local_rows, seq_groups, H * HD).astype(jnp.bfloat16)
    key_grad_low = grad_key_raw.reshape(local_rows, seq_groups, KV * HD).astype(jnp.bfloat16)
    value_grad_low = grad_value_raw.reshape(local_rows, seq_groups, KV * HD).astype(jnp.bfloat16)
    grad_query = outer_sum(normed_low, query_grad_low)
    grad_key = outer_sum(normed_low, key_grad_low)
    grad_value = outer_sum(normed_low, value_grad_low)
    grad_normed = (
        grad_normed_mid
        + matmul_back(grad_laurel_mid, left_full)
        + matmul_back(query_grad_low, query_full)
        + matmul_back(key_grad_low, key_full)
        + matmul_back(value_grad_low, value_full)
    )
    grad_residual_in, gains_input = input_back(grad_normed)
    d_hidden = (grad_residual_mid + grad_residual_in).astype(jnp.bfloat16)
    d_per_layer = grad_layer_input.astype(jnp.bfloat16)
    grad_gains = gains_final + gains_feed + gains_middle + gains_input
    grad_gate = grad_weights_paired[:, :unit_width]
    grad_up = grad_weights_paired[:, unit_width:]
    (
        query_part,
        key_part,
        value_part,
        output_part,
        left_part,
        right_part,
        gate_layer_part,
        proj_layer_part,
    ) = (
        lax.psum_scatter(
            grad_query.astype(jnp.bfloat16), "col", scatter_dimension=1, tiled=True
        ).astype(jnp.float32),
        lax.psum_scatter(
            grad_key.astype(jnp.bfloat16), "col", scatter_dimension=1, tiled=True
        ).astype(jnp.float32),
        lax.psum_scatter(
            grad_value.astype(jnp.bfloat16), "col", scatter_dimension=1, tiled=True
        ).astype(jnp.float32),
        lax.psum_scatter(
            grad_output.astype(jnp.bfloat16), "col", scatter_dimension=0, tiled=True
        ).astype(jnp.float32),
        lax.psum_scatter(
            grad_left.astype(jnp.bfloat16), "col", scatter_dimension=1, tiled=True
        ).astype(jnp.float32),
        lax.psum_scatter(
            grad_right.astype(jnp.bfloat16), "col", scatter_dimension=0, tiled=True
        ).astype(jnp.float32),
        lax.psum_scatter(
            grad_gate_layer.astype(jnp.bfloat16), "col", scatter_dimension=1, tiled=True
        ).astype(jnp.float32),
        lax.psum_scatter(
            grad_proj_layer.astype(jnp.bfloat16), "col", scatter_dimension=0, tiled=True
        ).astype(jnp.float32),
    )
    (
        d_query_weight,
        d_key_weight,
        d_value_weight,
        d_output_weight,
        d_gate_weight,
        d_up_weight,
        d_down_weight,
        d_laurel_left,
        d_laurel_right,
        d_layer_gate,
        d_layer_proj,
    ) = (
        lax.psum_scatter(
            query_part.astype(jnp.bfloat16), "row", scatter_dimension=0, tiled=True
        ).astype(jnp.float32),
        lax.psum_scatter(
            key_part.astype(jnp.bfloat16), "row", scatter_dimension=0, tiled=True
        ).astype(jnp.float32),
        lax.psum_scatter(
            value_part.astype(jnp.bfloat16), "row", scatter_dimension=0, tiled=True
        ).astype(jnp.float32),
        lax.psum_scatter(
            output_part.astype(jnp.bfloat16), "row", scatter_dimension=1, tiled=True
        ).astype(jnp.float32),
        lax.psum_scatter(
            grad_gate.astype(jnp.bfloat16), "row", scatter_dimension=0, tiled=True
        ).astype(jnp.float32),
        lax.psum_scatter(
            grad_up.astype(jnp.bfloat16), "row", scatter_dimension=0, tiled=True
        ).astype(jnp.float32),
        lax.psum_scatter(
            grad_down.astype(jnp.bfloat16), "row", scatter_dimension=1, tiled=True
        ).astype(jnp.float32),
        lax.psum_scatter(
            left_part.astype(jnp.bfloat16), "row", scatter_dimension=0, tiled=True
        ).astype(jnp.float32),
        lax.psum_scatter(
            right_part.astype(jnp.bfloat16), "row", scatter_dimension=1, tiled=True
        ).astype(jnp.float32),
        lax.psum_scatter(
            gate_layer_part.astype(jnp.bfloat16), "row", scatter_dimension=0, tiled=True
        ).astype(jnp.float32),
        lax.psum_scatter(
            proj_layer_part.astype(jnp.bfloat16), "row", scatter_dimension=1, tiled=True
        ).astype(jnp.float32),
    )
    d_norm_gains, d_head_gains, total_squares = lax.psum(
        (grad_gains, grad_heads, square_sums), ("row", "col")
    )
    stats = jnp.sqrt(total_squares / (valid_count * D))
    output = out_value.astype(jnp.bfloat16)
    return (
        output,
        stats,
        d_hidden,
        d_per_layer,
        d_query_weight,
        d_key_weight,
        d_value_weight,
        d_output_weight,
        d_gate_weight,
        d_up_weight,
        d_down_weight,
        d_laurel_left,
        d_laurel_right,
        d_layer_gate,
        d_layer_proj,
        d_norm_gains,
        d_head_gains,
    )


def swap(array):
    return jnp.swapaxes(array, 0, 1)


def heads_body(
    hidden,
    per_layer,
    lengths,
    block_ids,
    out_grad,
    query_weight,
    key_weight,
    value_weight,
    output_weight,
    gate_weight,
    up_weight,
    down_weight,
    laurel_left,
    laurel_right,
    layer_gate,
    layer_proj,
    norm_gains,
    head_gains,
):
    low = jnp.bfloat16
    rows = hidden.shape[0]
    groups = hidden.shape[1]
    cols = lax.axis_size("col")
    seq = rows * cols
    share = cols // KV
    col_index = lax.axis_index("col")
    row_index = lax.axis_index("row")
    all_lengths = lengths
    lengths = lax.dynamic_slice_in_dim(all_lengths, row_index * groups, groups, 0)

    laurel = jnp.concatenate([laurel_left.T, laurel_right], axis=0)
    small = [key_weight.T, value_weight.T, layer_gate.T, layer_proj, laurel]
    heights = [key_weight.shape[1], value_weight.shape[1], layer_gate.shape[1]]
    heights += [layer_proj.shape[0], laurel_left.shape[1], laurel_right.shape[0]]
    edges = [sum(heights[:i]) for i in range(len(heights) + 1)]
    unit_width = gate_weight.shape[1]
    residual = swap(hidden).astype(jnp.float32)
    normed_value, input_back = jax.vjp(input_norm, residual, norm_gains)
    normed_low = normed_value.astype(low)
    tiers = lax.axis_size("row")
    normed_all, small_row, query_full, output_full, both_weights = open_all(
        normed_low, query_weight, output_weight, gate_weight, up_weight, small, tiers, 1
    )
    small_all = share_small(small_row, heights[0] + heights[1], 8)
    paired = lax.all_gather(both_weights, "row", axis=0, tiled=True)
    down_full = lax.all_gather(after(down_weight, normed_all), "row", axis=1, tiled=True)
    late_gains = after(norm_gains, normed_all)
    query_full = query_full.reshape(D, HD).T
    output_full = jnp.swapaxes(output_full, 0, 1).reshape(HD, D)
    pieces = [small_all[:, :, a:b] for a, b in zip(edges[:-1], edges[1:])]
    group_start = (col_index // share) * share

    def joined(piece):
        return jnp.swapaxes(piece, 1, 2).reshape(-1, D)

    key_full, value_full = (
        joined(lax.dynamic_slice_in_dim(piece, group_start, share, 0)) for piece in pieces[:2]
    )
    gate_layer_full, proj_layer_full, left_full, right_full = (
        joined(piece) for piece in pieces[2:]
    )
    head_weights = jnp.concatenate([query_full, key_full, value_full], axis=0)

    positions = jnp.arange(seq, dtype=jnp.int32)
    mine = col_index * rows + jnp.arange(rows, dtype=jnp.int32)
    keep_mask = (mine[None, :] < lengths[:, None]).astype(jnp.float32)[:, :, None]
    live = positions[None, :] < lengths[:, None]
    distance = positions[:, None] - positions[None, :]
    nearby = (block_ids[:, :, None] >= block_ids[:, None, :]) & (distance < WINDOW)[None]
    nearby = nearby & live[:, :, None] & live[:, None, :]
    visible = nearby | (distance == 0)[None]

    half_width = HD // 2
    frequency = jnp.exp(jnp.arange(half_width, dtype=jnp.float32) * (-2.0 * math.log(10000.0) / HD))
    angles = (positions.astype(jnp.float32)[:, None] * frequency[None, :])[None]

    def prepare(query_in, key_in, value_in, gain_rows):
        return (
            rotate(root_norm(query_in, gain_rows[0]), angles),
            rotate(root_norm(key_in, gain_rows[1]), angles),
            plain_norm(value_in),
        )

    head_raw = matmul_back(normed_all, head_weights)
    query_raw, key_raw, value_raw = jnp.split(head_raw, 3, axis=-1)
    (query_value, key_value, value_value), head_back = jax.vjp(
        prepare, query_raw, key_raw, value_raw, head_gains
    )
    query_low = query_value.astype(low)
    key_low = key_value.astype(low)
    value_low = value_value.astype(low)
    score_scale = HD ** (-0.5)

    def score_all():
        raw_scores = (
            jnp.einsum("spd,sed->spe", query_low, key_low, preferred_element_type=jnp.float32)
            * score_scale
        )
        return jnp.where(visible, raw_scores, NEGATIVE)

    scores = score_all()
    row_max = jnp.max(scores, axis=-1, keepdims=True)
    exponent = jnp.exp(scores - row_max)
    row_total = jnp.sum(exponent, axis=-1, keepdims=True)
    attn_prob = exponent / row_total
    mixed_low = jnp.einsum(
        "spe,sed->spd", attn_prob.astype(low), value_low, preferred_element_type=jnp.float32
    ).astype(low)
    out_proj = product_sum(mixed_low, output_full, False, 2)
    laurel_mid = matmul_back(normed_low, left_full).astype(low)
    low_rank = matmul_last(laurel_mid, right_full)
    (after_attention, feed_normed), middle_back = jax.vjp(
        middle, residual, out_proj, low_rank, normed_low.astype(jnp.float32), late_gains
    )
    feed_all = spread(feed_normed.astype(low), 0)
    gate_value = matmul_last(feed_all, paired[:, :unit_width])
    up_value = matmul_last(feed_all, paired[:, unit_width:])
    units_low = gated_product(gate_value, up_value).astype(low)
    units_low, query_low, key_low, value_low, seen, head_weights = lax.optimization_barrier(
        (units_low, query_low, key_low, value_low, visible.astype(jnp.float32), head_weights)
    )
    summed = product_sum(units_low, down_full, False, 5, room=44)
    after_feed, feed_back = jax.vjp(feed_join, after_attention, summed, late_gains)
    feed_round = after_feed.astype(low)
    layer_pre = matmul_back(feed_round, gate_layer_full)
    layer_input = swap(per_layer).astype(jnp.float32)
    layer_value, layer_back = jax.vjp(gated_product, layer_pre, layer_input)
    layer_low = layer_value.astype(low)
    projected = matmul_last(layer_low, proj_layer_full)
    out_value, final_back = jax.vjp(final_join, after_feed, projected, late_gains)
    square_sums = jnp.stack(
        [
            jnp.sum(keep_mask * residual * residual),
            jnp.sum(keep_mask * after_attention * after_attention),
            jnp.sum(keep_mask * after_feed * after_feed),
            jnp.sum(keep_mask * out_value * out_value),
        ]
    )
    valid_count = jnp.sum(all_lengths).astype(jnp.float32)

    cotangent = swap(out_grad).astype(jnp.float32) * keep_mask
    grad_feed_out, grad_projected, gains_final = final_back(cotangent)
    projected_low = grad_projected.astype(low)
    grad_proj_layer = outer_sum(layer_low, projected_low)
    grad_layer_pre, grad_layer_input = layer_back(matmul_back(projected_low, proj_layer_full))
    layer_pre_low = grad_layer_pre.astype(low)
    grad_gate_layer = outer_sum(layer_pre_low, feed_round)
    grad_after_feed = grad_feed_out + matmul_last(layer_pre_low, gate_layer_full)
    grad_after_attention_a, grad_summed, gains_feed = feed_back(grad_after_feed)
    grad_paired, grad_down = units_back(
        grad_summed.astype(low), down_full, units_low, gate_value, up_value, tiers, 9
    )
    d_down_weight = lax.psum_scatter(grad_down, "row", scatter_dimension=0)
    grad_feed, grad_both = product_sum(grad_paired, paired, True, 6, feed_all)
    d_both = lax.psum_scatter(grad_both, "row", scatter_dimension=0, tiled=True)
    grad_residual_mid, grad_out_proj, grad_low_rank, grad_normed_mid, gains_middle = middle_back(
        (grad_after_attention_a, grad_feed)
    )
    grad_queries, grad_keys, grad_values, grad_output = heads_back(
        after(grad_out_proj.astype(low), d_down_weight),
        output_full,
        mixed_low,
        query_low,
        key_low,
        value_low,
        seen,
        score_scale,
        10,
    )
    low_rank_grad = grad_low_rank.astype(low)
    grad_right = outer_sum(laurel_mid, low_rank_grad)
    grad_laurel_mid = matmul_back(low_rank_grad, right_full).astype(low)
    grad_left = outer_sum(grad_laurel_mid, normed_low)
    grad_query_raw, grad_key_raw, grad_value_raw, grad_heads = head_back(
        (grad_queries, grad_keys, grad_values)
    )
    head_grads = jnp.concatenate([grad_query_raw, grad_key_raw, grad_value_raw], axis=-1)
    head_grads = head_grads.astype(low)
    grad_head_weights = outer_sum(head_grads, normed_all).astype(low)
    grad_query, grad_key, grad_value = jnp.split(grad_head_weights, 3, axis=0)
    grad_group = jnp.concatenate(
        [grad_key.reshape(share, -1, D), grad_value.reshape(share, -1, D)], axis=1
    )
    grad_rest = jnp.concatenate(
        [
            piece.astype(low).reshape(cols, -1, D)
            for piece in (grad_gate_layer, grad_proj_layer, grad_left, grad_right)
        ],
        axis=1,
    )
    half = grad_rest.shape[1] // 2
    grad_rest = jnp.swapaxes(grad_rest.reshape(cols, 2, half, D), 0, 1)
    rest_part, group_part = fold_small(grad_rest.reshape(2, cols * half, D), grad_group, 3)
    parts = jnp.concatenate(
        [grad_output, grad_query, group_part.astype(low), rest_part.astype(low).reshape(-1, D)],
        axis=0,
    )
    grad_normed = product_sum(after(head_grads, parts), head_weights, False, 7, room=60)
    parts = after(parts, d_both, grad_normed)
    parts_out = lax.psum_scatter(parts, "row", scatter_dimension=1, tiled=True)
    d_output_weight = parts_out[:HD].astype(jnp.float32)
    d_query_weight = parts_out[HD : 2 * HD].T.astype(jnp.float32)
    small_out = parts_out[2 * HD :]
    small_parts = [small_out[a:b].astype(jnp.float32) for a, b in zip(edges[:-1], edges[1:])]
    grad_normed = grad_normed + grad_normed_mid + matmul_last(grad_laurel_mid, left_full)
    grad_residual_in, gains_input = input_back(grad_normed)
    d_hidden = swap((grad_residual_mid + grad_residual_in).astype(low))
    d_per_layer = swap(grad_layer_input.astype(low))
    grad_gains = gains_final + gains_feed + gains_middle + gains_input
    extra = jnp.concatenate([grad_heads.reshape(-1), square_sums])
    extra = jnp.pad(extra, (0, 2 * D - extra.shape[0])).reshape(2, D)
    all_sums = jnp.concatenate([grad_gains, extra], axis=0)
    totals = total(after(all_sums, parts), tiers, 4)
    d_down_weight = after(d_down_weight, totals).astype(jnp.float32)
    d_both = after(d_both, totals).astype(jnp.float32)
    d_gate_weight = d_both[:, :unit_width]
    d_up_weight = d_both[:, unit_width:]
    d_norm_gains = totals[:6]
    d_head_gains = totals[6, : 2 * HD].reshape(2, HD)
    total_squares = totals[6, 2 * HD : 2 * HD + 4]
    stats = jnp.sqrt(total_squares / (valid_count * D))
    output = swap(out_value.astype(low))
    return (
        output,
        stats,
        d_hidden,
        d_per_layer,
        d_query_weight,
        small_parts[0].T,
        small_parts[1].T,
        d_output_weight,
        d_gate_weight,
        d_up_weight,
        d_down_weight,
        small_parts[4].T,
        small_parts[5],
        small_parts[2].T,
        small_parts[3],
        d_norm_gains,
        d_head_gains,
    )


def solution(mesh):
    body = heads_body if mesh.shape["col"] == H else general_body
    in_specs = (
        P("col", "row", None),
        P("col", "row", None),
        P(),
        P("row", None),
        P("col", "row", None),
        P("row", "col"),
        P("row", "col"),
        P("row", "col"),
        P("col", "row"),
        P("row", "col"),
        P("row", "col"),
        P("col", "row"),
        P("row", "col"),
        P("col", "row"),
        P("row", "col"),
        P("col", "row"),
        P(),
        P(),
    )
    out_specs = (
        P("col", "row", None),
        P(),
        P("col", "row", None),
        P("col", "row", None),
        P("row", "col"),
        P("row", "col"),
        P("row", "col"),
        P("col", "row"),
        P("row", "col"),
        P("row", "col"),
        P("col", "row"),
        P("row", "col"),
        P("col", "row"),
        P("row", "col"),
        P("col", "row"),
        P(),
        P(),
    )
    return jax.shard_map(body, mesh=mesh, in_specs=in_specs, out_specs=out_specs, check_vma=False)
```
